32 devices in a mesh: fsdp: 2 (over x), ctx: 4 (over y, core), tp: 4 (over z).
Axes of the slice: x: 2, y: 2, z: 4, core: 2. Of those that a mesh axis runs over, the one named last changes fastest.
Arguments:
- tokens: bfloat16 [8192, 1024], P(('fsdp', 'ctx', 'tp')), may hold values from -6 to 6
- out_grad: bfloat16 [8192, 1024], P(('fsdp', 'ctx', 'tp')), may hold values from -6 to 6
- routes: int32 [8192, 8], P(('fsdp', 'ctx', 'tp')), may hold values from 0 to 31, all different within a row; in each aligned block of 256 rows (0 to 255, 256 to 511, ...) at most 96 rows name the same one
- parents: int32 [64], replicated, may hold values from -1 to 30, as said below
- adapter_set: int32 [2], replicated, may hold values from 0 to 7
- gain_a: bfloat16 [1024], replicated, may hold values from 0.5 to 1.5
- gain_b: bfloat16 [1024], replicated, may hold values from 0.5 to 1.5
- w_query: bfloat16 [1024, 1024], P('fsdp', 'tp'), may hold values from -0.75 to 0.75
- key_projection_matrix: bfloat16 [1024, 512], P('fsdp', 'tp'), may hold values from -0.75 to 0.75
- value_projection_matrix: bfloat16 [1024, 512], P('fsdp', 'tp'), may hold values from -0.1875 to 0.1875
- w_output: bfloat16 [1024, 1024], P('tp', 'fsdp'), may hold values from -3 to 3
- w_router: bfloat16 [1024, 32], replicated, may hold values from -0.09375 to 0.09375
- w_gate: bfloat16 [32, 1024, 512], P('ctx', 'fsdp'), may hold values from -0.1875 to 0.1875
- w_up: bfloat16 [32, 1024, 512], P('ctx', 'fsdp'), may hold values from -0.1875 to 0.1875
- w_down: bfloat16 [32, 512, 1024], P('ctx', 'fsdp'), may hold values from -4 to 4
- query_in: bfloat16 [1024, 128], replicated, may hold values from -0.1875 to 0.1875
- query_out: bfloat16 [128, 1024], replicated, may hold values from -1.5 to 1.5
- key_in: bfloat16 [1024, 128], replicated, may hold values from -0.1875 to 0.1875
- key_second_factor: bfloat16 [128, 512], replicated, may hold values from -1.5 to 1.5
- value_in: bfloat16 [1024, 128], replicated, may hold values from -0.1875 to 0.1875
- value_second_factor: bfloat16 [128, 512], replicated, may hold values from -1.5 to 1.5
- out_in: bfloat16 [1024, 128], replicated, may hold values from -0.1875 to 0.1875
- out_out: bfloat16 [128, 1024], replicated, may hold values from -6 to 6
- gate_in: bfloat16 [32, 1024, 128], P('ctx'), may hold values from -0.1875 to 0.1875
- gate_out: bfloat16 [32, 128, 512], P('ctx'), may hold values from -1.5 to 1.5
- up_in: bfloat16 [32, 1024, 128], P('ctx'), may hold values from -0.1875 to 0.1875
- up_out: bfloat16 [32, 128, 512], P('ctx'), may hold values from -1.5 to 1.5
- down_in: bfloat16 [32, 512, 128], P('ctx'), may hold values from -0.25 to 0.25
- down_out: bfloat16 [32, 128, 1024], P('ctx'), may hold values from -6 to 6
Outputs:
- output: bfloat16 [8192, 1024], P(('fsdp', 'ctx', 'tp'))
- input_grad: bfloat16 [8192, 1024], P(('fsdp', 'ctx', 'tp'))
- query_in_grad: float32 [1024, 128], replicated
- query_out_grad: float32 [128, 1024], replicated
- key_in_grad: float32 [1024, 128], replicated
- key_out_grad: float32 [128, 512], replicated
- value_in_grad: float32 [1024, 128], replicated
- value_out_grad: float32 [128, 512], replicated
- out_in_grad: float32 [1024, 128], replicated
- out_out_grad: float32 [128, 1024], replicated
- gate_in_grad: float32 [32, 1024, 128], P('ctx')
- gate_out_grad: float32 [32, 128, 512], P('ctx')
- up_in_grad: float32 [32, 1024, 128], P('ctx')
- up_out_grad: float32 [32, 128, 512], P('ctx')
- down_in_grad: float32 [32, 512, 128], P('ctx')
- down_out_grad: float32 [32, 128, 1024], P('ctx')
The draws below stay inside these ranges and needn't reach their ends.
Inputs may be any that keep to these rules, and one draw needn't show every extreme that they name: `parents`: entry s is the index within its tree of segment s's parent; the first segment of every tree has -1 and no other segment has; every other segment's parent has a lower index in the same tree. `routes`: of the rows of one device (aligned blocks of 256 rows), at most 96 name one expert, and some block reaches 96.
All inputs are finite; a program needn't handle non-finite values.
Results may differ from the reference program's by a relative error of at most 0.029.
Values may be sent and summed in bfloat16 or wider, within the bound.
A program may use at most 320 MiB of HBM per device.

```python
import math
import jax
import jax.numpy as jnp
import numpy as np
from jax import lax

MODEL_DIMENSION = 1024
QUERY_HEAD_COUNT = 16
KEY_VALUE_HEADS = 8
HEAD_DIMENSION = 64
FF = 512
EXPERTS = 32
TOP = 8
ADAPTER_SETS = 8
ADAPTER_RANK = 16
SEG = 128
TREE_SEGS = 32
TOK_DEV = 256
CAP = 96
TOKENS = 8192
NSEG = 64
NTREES = 2


def draw_parents(key, part):
    trunk_key = jax.random.fold_in(key, 11)
    pick_key = jax.random.fold_in(key, 23)
    tree_count = NSEG // TREE_SEGS
    trunk_len = jax.random.randint(trunk_key, (tree_count, 1), TREE_SEGS // 2, TREE_SEGS - 2)
    token_positions = jnp.arange(TREE_SEGS, dtype=jnp.int32)[None, :]
    random_pick = jax.random.randint(pick_key, (tree_count, TREE_SEGS), 0, 1 << 20)
    branch_parent = trunk_len - 1 + random_pick % jnp.maximum(token_positions - trunk_len + 1, 1)
    chain_parent = token_positions - 1
    result = jnp.where(token_positions < trunk_len, chain_parent, branch_parent)
    return result.reshape(-1).astype(jnp.int32)


def steps_of(stream_key, shape, split, low, largest):
    gain = 1.0
    for dim, blocks in split:
        steps = jax.random.uniform(jax.random.fold_in(jax.random.fold_in(stream_key, 6), dim), (blocks,), jnp.float32, low / len(split), largest / len(split))
        gain = gain * jnp.repeat(jnp.exp(steps), shape[dim] // blocks).reshape((-1,) + (1,) * (len(shape) - 1 - dim))
    return gain


def routed_block(own_key, own, number, rows, amount, top, limit, slope):
    ranking = jax.random.permutation(own_key, amount)
    crowded, common = portions_of(amount, rows * top, limit, slope, True), portions_of(amount, rows * top, limit, slope, False)
    places = jnp.arange(amount)

    def named(sizes, rotation):
        used = int((sizes > 0).sum())
        fixed = max(1, used // 4)
        shifted = fixed + (places - fixed + rotation * (used - fixed)) % max(1, amount - fixed)
        return jnp.zeros((amount,), jnp.int32).at[ranking[jnp.where(places < fixed, places, shifted)]].set(jnp.asarray(sizes, jnp.int32))

    sizes = jnp.where(number % 4 == 0, named(crowded, number // 4), named(common, number - number // 4 - 1))
    mixed = jax.random.permutation(jax.random.fold_in(own, 3), amount)
    donor, receiver = mixed[0:amount // 2 * 2:2], mixed[1:amount // 2 * 2:2]
    margin = jnp.minimum(sizes[donor] - 1, limit - sizes[receiver]) // 2
    margin = jnp.where((donor == ranking[0]) | (receiver == ranking[0]) | (sizes[receiver] == 0), 0, jnp.maximum(margin, 0))
    shifted = jax.random.randint(jax.random.fold_in(own, 4), (amount // 2,), 0, 1 << 20) % (margin + 1)
    sizes = sizes.at[donor].add(-shifted).at[receiver].add(shifted)
    labels = jnp.searchsorted(jnp.cumsum(sizes), jnp.arange(rows * top), side="right").astype(jnp.int32)
    table = labels.reshape(top, rows).T
    table = table[jax.random.permutation(jax.random.fold_in(own, 1), rows)]
    rotation = jax.random.randint(jax.random.fold_in(own, 2), (rows, 1), 0, top)
    return jnp.take_along_axis(table, (jnp.arange(top)[None, :] + rotation) % top, axis=1)


def portions_of(count, total, bound, skew, full):
    weights = [(1 << 20) // math.isqrt(standing ** skew) + 1 for standing in range(1, count + 1)]
    largest = bound if full else min(bound, max(-(-total // count), total * weights[0] // sum(weights)))
    least = 1 if total - largest >= count - 1 else 0
    counts, spare = [largest] + [least] * (count - 1), total - largest - least * (count - 1)
    while spare > 0:
        movable = [i for i in range(1, count) if counts[i] < largest] or [i for i in range(1, count) if counts[i] < bound]
        mass, remaining = sum([weights[i] for i in movable]), spare
        for i in movable:
            addition = min(bound - counts[i], max(1, remaining * weights[i] // mass), spare)
            counts[i] = counts[i] + addition
            spare = spare - addition
    return np.array(counts)


def gaussian(rng, shape, scale, reach, pieces=(), kind=jnp.bfloat16):
    array = jax.random.normal(rng, shape, jnp.float32) * scale
    if len(pieces) > 0:
        array = steps_of(rng, shape, pieces, -0.22, 0.18) * array
    return jnp.clip(array, min=-reach, max=reach).astype(kind)


def setup_inputs(seed: int = 0) -> dict:
    splits = jax.random.split(jax.random.key(seed), 30)
    tokens = gaussian(splits[0], (TOKENS, MODEL_DIMENSION), 1.0, 6.0, ((0, 32),))
    out_grad = gaussian(splits[1], (TOKENS, MODEL_DIMENSION), 1.0, 6.0, ((0, 32),))
    routes_keys = jax.random.split(jax.random.fold_in(splits[2], 1), TOKENS // TOK_DEV)
    routes_turns = jax.random.permutation(jax.random.fold_in(splits[2], 3), TOKENS // TOK_DEV)
    routes = jax.vmap(lambda own, number: routed_block(jax.random.fold_in(splits[2], 2), own, number, TOK_DEV, EXPERTS, TOP, CAP, 1))(routes_keys, routes_turns).reshape((TOKENS, TOP))
    parents = draw_parents(jax.random.fold_in(splits[29], 71), 0)
    adapter_set = jax.random.randint(splits[4], (NTREES,), 0, ADAPTER_SETS).astype(jnp.int32)
    gain_a = jnp.clip(1.0 + 0.1 * jax.random.normal(splits[5], (MODEL_DIMENSION,), jnp.float32), 0.5, 1.5).astype(jnp.bfloat16)
    gain_b = jnp.clip(1.0 + 0.1 * jax.random.normal(splits[6], (MODEL_DIMENSION,), jnp.float32), 0.5, 1.5).astype(jnp.bfloat16)
    w_query = gaussian(splits[7], (MODEL_DIMENSION, QUERY_HEAD_COUNT * HEAD_DIMENSION), (MODEL_DIMENSION // 16) ** -0.5, 0.75, ((0, 2), (1, 4)))
    key_projection_matrix = gaussian(splits[8], (MODEL_DIMENSION, KEY_VALUE_HEADS * HEAD_DIMENSION), (MODEL_DIMENSION // 16) ** -0.5, 0.75, ((0, 2), (1, 4)))
    value_projection_matrix = gaussian(splits[9], (MODEL_DIMENSION, KEY_VALUE_HEADS * HEAD_DIMENSION), MODEL_DIMENSION ** -0.5, 0.1875, ((0, 2), (1, 4)))
    w_output = gaussian(splits[10], (QUERY_HEAD_COUNT * HEAD_DIMENSION, MODEL_DIMENSION), 4 ** -0.5, 3.0, ((0, 4), (1, 2)))
    w_router = gaussian(splits[11], (MODEL_DIMENSION, EXPERTS), (4 * MODEL_DIMENSION) ** -0.5, 0.09375)
    w_gate = gaussian(splits[12], (EXPERTS, MODEL_DIMENSION, FF), MODEL_DIMENSION ** -0.5, 0.1875, ((0, 4), (1, 2)))
    w_up = gaussian(splits[13], (EXPERTS, MODEL_DIMENSION, FF), MODEL_DIMENSION ** -0.5, 0.1875, ((0, 4), (1, 2)))
    w_down = gaussian(splits[14], (EXPERTS, FF, MODEL_DIMENSION), 2 ** -0.5, 4.0, ((0, 4), (1, 2)))
    query_in = gaussian(splits[15], (MODEL_DIMENSION, ADAPTER_SETS * ADAPTER_RANK), MODEL_DIMENSION ** -0.5, 0.1875)
    query_out = gaussian(splits[16], (ADAPTER_SETS * ADAPTER_RANK, QUERY_HEAD_COUNT * HEAD_DIMENSION), ADAPTER_RANK ** -0.5, 1.5)
    key_in = gaussian(splits[17], (MODEL_DIMENSION, ADAPTER_SETS * ADAPTER_RANK), MODEL_DIMENSION ** -0.5, 0.1875)
    key_second_factor = gaussian(splits[18], (ADAPTER_SETS * ADAPTER_RANK, KEY_VALUE_HEADS * HEAD_DIMENSION), ADAPTER_RANK ** -0.5, 1.5)
    value_in = gaussian(splits[19], (MODEL_DIMENSION, ADAPTER_SETS * ADAPTER_RANK), MODEL_DIMENSION ** -0.5, 0.1875)
    value_second_factor = gaussian(splits[20], (ADAPTER_SETS * ADAPTER_RANK, KEY_VALUE_HEADS * HEAD_DIMENSION), ADAPTER_RANK ** -0.5, 1.5)
    out_in = gaussian(splits[21], (QUERY_HEAD_COUNT * HEAD_DIMENSION, ADAPTER_SETS * ADAPTER_RANK), (QUERY_HEAD_COUNT * HEAD_DIMENSION) ** -0.5, 0.1875)
    out_out = gaussian(splits[22], (ADAPTER_SETS * ADAPTER_RANK, MODEL_DIMENSION), 1 ** -0.5, 6.0)
    gate_in = gaussian(splits[23], (EXPERTS, MODEL_DIMENSION, ADAPTER_SETS * ADAPTER_RANK), MODEL_DIMENSION ** -0.5, 0.1875, ((0, 4),))
    gate_out = gaussian(splits[24], (EXPERTS, ADAPTER_SETS * ADAPTER_RANK, FF), ADAPTER_RANK ** -0.5, 1.5, ((0, 4),))
    up_in = gaussian(splits[25], (EXPERTS, MODEL_DIMENSION, ADAPTER_SETS * ADAPTER_RANK), MODEL_DIMENSION ** -0.5, 0.1875, ((0, 4),))
    up_out = gaussian(splits[26], (EXPERTS, ADAPTER_SETS * ADAPTER_RANK, FF), ADAPTER_RANK ** -0.5, 1.5, ((0, 4),))
    down_in = gaussian(splits[27], (EXPERTS, FF, ADAPTER_SETS * ADAPTER_RANK), FF ** -0.5, 0.25, ((0, 4),))
    down_out = gaussian(splits[28], (EXPERTS, ADAPTER_SETS * ADAPTER_RANK, MODEL_DIMENSION), 1 ** -0.5, 6.0, ((0, 4),))
    return {"tokens": tokens, "out_grad": out_grad, "routes": routes, "parents": parents, "adapter_set": adapter_set, "gain_a": gain_a, "gain_b": gain_b, "w_query": w_query, "key_projection_matrix": key_projection_matrix, "value_projection_matrix": value_projection_matrix, "w_output": w_output, "w_router": w_router, "w_gate": w_gate, "w_up": w_up, "w_down": w_down, "query_in": query_in, "query_out": query_out, "key_in": key_in, "key_second_factor": key_second_factor, "value_in": value_in, "value_second_factor": value_second_factor, "out_in": out_in, "out_out": out_out, "gate_in": gate_in, "gate_out": gate_out, "up_in": up_in, "up_out": up_out, "down_in": down_in, "down_out": down_out}


@jax.custom_vjp
def reduced_rows(v):
    return lax.optimization_barrier(v.astype(jnp.bfloat16)).astype(jnp.float32)

@jax.custom_vjp
def low_back(v):
    return v

def low_keep(v):
    return (reduced_rows(v), None)

def low_pass(kept, grad):
    return (grad,)

def back_keep(v):
    return (v, None)

def back_low(kept, grad):
    return (reduced_rows(grad),)
reduced_rows.defvjp(low_keep, low_pass)
low_back.defvjp(back_keep, back_low)
RESIDUAL_SCALE = 0.22
SCORE_SCALE = 0.015625
EPSILON = 1e-06
ROPE_BASE = 10000.0
MASKED = -1e+30

def forward_backward(value):
    return reduced_rows(low_back(value))

def precise_product(left_arg, right_arg):
    return jnp.dot(left_arg, right_arg, precision=lax.Precision.HIGHEST, preferred_element_type=jnp.float32)

def rms_scale(values, gain_row):
    return values * lax.rsqrt(lax.optimization_barrier(jnp.mean(values * values, axis=-1, keepdims=True)) + EPSILON) * gain_row

def apply_rotary(values, token_positions):
    half_width = values.shape[-1] // 2
    freqs = ROPE_BASE ** (-(jnp.arange(half_width, dtype=jnp.float32) * 2.0) / values.shape[-1])
    angles = token_positions[:, None] * freqs[None, :]
    cosine = jnp.cos(angles)[:, None, :]
    sine = jnp.sin(angles)[:, None, :]
    first_half = values[..., :half_width]
    second_half = values[..., half_width:]
    return jnp.concatenate([first_half * cosine - second_half * sine, second_half * cosine + first_half * sine], axis=-1)

def tree_links(tree_parents):
    seg_count = tree_parents.shape[0]
    columns = jnp.arange(seg_count, dtype=jnp.int32)
    current = tree_parents
    ancestors = jnp.zeros((seg_count, seg_count), jnp.float32)
    for climb_step in range(seg_count):
        hit_table = current[:, None] == columns[None, :]
        ancestors = ancestors + hit_table.astype(jnp.float32)
        current = lax.optimization_barrier(jnp.sum(hit_table.astype(jnp.int32) * (tree_parents[None, :] + 1), axis=1)) - 1
    return (ancestors, lax.optimization_barrier(jnp.sum(ancestors, axis=1)))

def reference(tokens, out_grad, routes, parents, adapter_set, gain_a, gain_b, w_query, key_projection_matrix, value_projection_matrix, w_output, w_router, w_gate, w_up, w_down, query_in, query_out, key_in, key_second_factor, value_in, value_second_factor, out_in, out_out, gate_in, gate_out, up_in, up_out, down_in, down_out):
    gain_one = gain_a.astype(jnp.float32)
    gain_two = gain_b.astype(jnp.float32)
    query_full = w_query.astype(jnp.float32)
    key_full = key_projection_matrix.astype(jnp.float32)
    value_complete = value_projection_matrix.astype(jnp.float32)
    output_full = w_output.astype(jnp.float32)
    router_full = w_router.astype(jnp.float32)
    gate_full = w_gate.astype(jnp.float32)
    up_full = w_up.astype(jnp.float32)
    down_full = w_down.astype(jnp.float32)
    tree_length = TREE_SEGS * SEG
    flat_routes = routes.reshape(-1)
    most_rows = TOKENS // TOK_DEV * CAP

    def expert_slots(expert):
        slot_order = jnp.argsort((flat_routes != expert).astype(jnp.int32), stable=True)[:most_rows].astype(jnp.int32)
        filled = jnp.sum((flat_routes == expert).astype(jnp.int32))
        slot_live = (jnp.arange(most_rows, dtype=jnp.int32) < filled).astype(jnp.float32)
        return (slot_order, slot_live)
    slot_orders, slot_lives = lax.map(expert_slots, jnp.arange(EXPERTS, dtype=jnp.int32))
    token_set = adapter_set[jnp.arange(TOKENS, dtype=jnp.int32) // tree_length]
    set_column = jnp.arange(ADAPTER_SETS * ADAPTER_RANK, dtype=jnp.int32) // ADAPTER_RANK

    def forward(inputs, adapters):
        query_in_f, query_out_f, key_in_f, key_out_f, value_in_f, value_second_factor_float, out_in_f, out_out_f, gate_in_f, gate_out_f, up_in_f, up_out_f, down_in_f, down_out_f = adapters

        def tree_step(packed):
            rows_in, chosen, tree_parents = packed
            mask_columns = (set_column == chosen).astype(jnp.float32)
            ancestors, seg_depth = tree_links(tree_parents)
            segment = jnp.arange(tree_length, dtype=jnp.int32) // SEG
            offset = jnp.arange(tree_length, dtype=jnp.int32) % SEG
            token_positions = seg_depth[segment] * SEG + offset.astype(jnp.float32)
            normalized_rows = reduced_rows(rms_scale(rows_in, gain_one))
            query_reduced = forward_backward(precise_product(normalized_rows, query_in_f)) * mask_columns
            key_reduced = forward_backward(precise_product(normalized_rows, key_in_f)) * mask_columns
            value_reduced = forward_backward(precise_product(normalized_rows, value_in_f)) * mask_columns
            query_pre = low_back(precise_product(normalized_rows, query_full) + precise_product(query_reduced, query_out_f))
            key_unrotated = low_back(precise_product(normalized_rows, key_full) + precise_product(key_reduced, key_out_f))
            queries = reduced_rows(apply_rotary(query_pre.reshape(tree_length, QUERY_HEAD_COUNT, HEAD_DIMENSION), token_positions))
            rotated_keys = reduced_rows(apply_rotary(key_unrotated.reshape(tree_length, KEY_VALUE_HEADS, HEAD_DIMENSION), token_positions))
            every_value = forward_backward(precise_product(normalized_rows, value_complete) + precise_product(value_reduced, value_second_factor_float)).reshape(tree_length, KEY_VALUE_HEADS, HEAD_DIMENSION)
            expanded_keys = jnp.repeat(rotated_keys, QUERY_HEAD_COUNT // KEY_VALUE_HEADS, axis=1)
            expanded_values = jnp.repeat(every_value, QUERY_HEAD_COUNT // KEY_VALUE_HEADS, axis=1)
            block_rows = math.gcd(tree_length, 512)

            def attend(row_start):
                query_block = lax.dynamic_slice_in_dim(queries, row_start, block_rows, 0)
                seg_block = lax.dynamic_slice_in_dim(segment, row_start, block_rows, 0)
                off_block = lax.dynamic_slice_in_dim(offset, row_start, block_rows, 0)
                linked = ancestors[seg_block][:, segment] > 0.5
                same_seg = (seg_block[:, None] == segment[None, :]) & (offset[None, :] <= off_block[:, None])
                allowed = linked | same_seg
                scores = low_back(jnp.einsum('qhd,khd->hqk', query_block, expanded_keys, precision=lax.Precision.HIGHEST) * SCORE_SCALE)
                scores = jnp.where(allowed[None], scores, MASKED)
                prob_table = reduced_rows(jax.nn.softmax(scores, axis=-1))
                return jnp.einsum('hqk,khd->qhd', prob_table, expanded_values, precision=lax.Precision.HIGHEST)
            starts = jnp.arange(tree_length // block_rows, dtype=jnp.int32) * block_rows
            attention_result = forward_backward(lax.map(jax.checkpoint(attend), starts).reshape(tree_length, QUERY_HEAD_COUNT * HEAD_DIMENSION))
            output_reduced = forward_backward(precise_product(attention_result, out_in_f)) * mask_columns
            branch = low_back(precise_product(attention_result, output_full) + precise_product(output_reduced, out_out_f))
            return rows_in + RESIDUAL_SCALE * branch
        middle = lax.map(tree_step, (inputs.reshape(NTREES, tree_length, MODEL_DIMENSION), adapter_set, parents.reshape(NTREES, TREE_SEGS))).reshape(TOKENS, MODEL_DIMENSION)
        normed_two = reduced_rows(rms_scale(middle, gain_two))
        logits = precise_product(normed_two, router_full)
        gate_weights = jax.nn.softmax(jnp.take_along_axis(logits, routes, axis=1), axis=-1)

        def expert_rows(packed):
            slot_order, slot_live, gate_weight, up_weight, down_weight, gate_first, gate_second, up_first, up_second, down_first, down_second = packed
            token_ids = slot_order // TOP
            picked_rows = low_back(normed_two[token_ids]) * slot_live[:, None]
            row_mask = (set_column[None, :] == token_set[token_ids][:, None]).astype(jnp.float32)
            gate_value = low_back(precise_product(picked_rows, gate_weight) + precise_product(forward_backward(precise_product(picked_rows, gate_first)) * row_mask, gate_second))
            up_value = low_back(precise_product(picked_rows, up_weight) + precise_product(forward_backward(precise_product(picked_rows, up_first)) * row_mask, up_second))
            active = forward_backward(jax.nn.silu(gate_value) * up_value)
            return forward_backward(precise_product(active, down_weight) + precise_product(forward_backward(precise_product(active, down_first)) * row_mask, down_second))
        produced = lax.map(jax.checkpoint(expert_rows), (slot_orders, slot_lives, gate_full, up_full, down_full, gate_in_f, gate_out_f, up_in_f, up_out_f, down_in_f, down_out_f))
        slot_gates = gate_weights.reshape(-1)[slot_orders] * slot_lives
        mixture = jnp.zeros((TOKENS, MODEL_DIMENSION), jnp.float32).at[(slot_orders // TOP).reshape(-1)].add((produced * slot_gates[:, :, None]).reshape(-1, MODEL_DIMENSION))
        return middle + RESIDUAL_SCALE * mixture
    adapters = (query_in.astype(jnp.float32), query_out.astype(jnp.float32), key_in.astype(jnp.float32), key_second_factor.astype(jnp.float32), value_in.astype(jnp.float32), value_second_factor.astype(jnp.float32), out_in.astype(jnp.float32), out_out.astype(jnp.float32), gate_in.astype(jnp.float32), gate_out.astype(jnp.float32), up_in.astype(jnp.float32), up_out.astype(jnp.float32), down_in.astype(jnp.float32), down_out.astype(jnp.float32))
    result, pullback = jax.vjp(forward, tokens.astype(jnp.float32), adapters)
    input_grad, adapter_grads = pullback(out_grad.astype(jnp.float32))
    return (result.astype(jnp.bfloat16), input_grad.astype(jnp.bfloat16), adapter_grads[0], adapter_grads[1], adapter_grads[2], adapter_grads[3], adapter_grads[4], adapter_grads[5], adapter_grads[6], adapter_grads[7], adapter_grads[8], adapter_grads[9], adapter_grads[10], adapter_grads[11], adapter_grads[12], adapter_grads[13])
```

```python
import functools
import math

import jax
import jax.numpy as jnp
from jax import lax
from jax.experimental import pallas as pl
from jax.experimental.pallas import tpu as pltpu
from jax.sharding import PartitionSpec as P

HEAD = 64
TOP = 8
RANK = 16
SEG = 128
SEGS_DEV = 8
TREE_SEGS = 32
SPAN = TREE_SEGS // SEGS_DEV
LANES = 128

RESIDUAL_SCALE = 0.22
SCORE_SCALE = 0.015625
EPSILON = 1e-06
ROPE_BASE = 10000.0
MASKED = -1e30

F32 = jnp.float32
BF16 = jnp.bfloat16

CODE = HEAD
LSE = CODE + TREE_SEGS + 1
ONES = HEAD

VMEM_LIMIT = 56 * 1024 * 1024


def dot(a, b):
    return lax.dot_general(a, b, (((1,), (0,)), ((), ())), preferred_element_type=F32)


def dot_nt(a, b):
    return lax.dot_general(a, b, (((1,), (1,)), ((), ())), preferred_element_type=F32)


def dot_tn(a, b):
    return lax.dot_general(a, b, (((0,), (0,)), ((), ())), preferred_element_type=F32)


def iota(shape, dim):
    return lax.broadcasted_iota(jnp.int32, shape, dim)


def shifted(block, axis, distance):
    devices = range(lax.axis_size(axis))
    route = [(i - distance, i) for i in devices if i - distance in devices]
    return lax.ppermute(block, axis, route)


def rms_scale(values, gain_row):
    return (
        values * lax.rsqrt(jnp.mean(values * values, axis=-1, keepdims=True) + EPSILON) * gain_row
    )


def rms_back(values, gain_row, grad):
    inv = lax.rsqrt(jnp.mean(values * values, axis=-1, keepdims=True) + EPSILON)
    scaled = grad * gain_row
    inner = jnp.mean(scaled * values, axis=-1, keepdims=True)
    return inv * scaled - values * (inv * inv * inv * inner)


def tree_links(tree_parents):
    count = tree_parents.shape[0]
    columns = jnp.arange(count, dtype=jnp.int32)
    reach = (
        (tree_parents[:, None] == columns[None, :]) | (columns[:, None] == columns[None, :])
    ).astype(BF16)
    for _ in range(max(1, (count - 1).bit_length())):
        reach = jnp.minimum(dot(reach, reach), 1.0).astype(BF16)
    reach = reach.astype(F32)
    return reach, jnp.sum(reach, axis=1) - 1.0


def swap_halves(values):
    width = values.shape[-1]
    lane = iota(values.shape, 1) % HEAD
    ahead = pltpu.roll(values, width - HEAD // 2, 1)
    behind = pltpu.roll(values, HEAD // 2, 1)
    return jnp.where(lane < HEAD // 2, -ahead, behind)


def place_table(rows, source, target):
    r, c = iota((rows, LANES), 0), iota((rows, LANES), 1)
    return ((r - source == c - target) & (c >= target) & (c < target + HEAD)).astype(BF16)


def project_kernel(normed, weights, first, second, cos, sin, codes, q_out, kv_out, lora_out):
    rows = normed[...]
    half = weights.shape[1]
    lora = dot(rows, first[...]).astype(BF16)
    lora_out[...] = lora
    pre = (
        dot(rows[:, :half], weights[0])
        + dot(rows[:, half:], weights[1])
        + dot(lora, second[...])
    )
    turn = cos.shape[1]
    parts = []
    for start in range(0, pre.shape[1] // 4 * 3, turn):
        piece = pre[:, start : start + turn]
        parts.append(piece * cos[...] + swap_halves(piece) * sin[...])
    heads = q_out.shape[0]
    width = heads * HEAD
    queries = (jnp.concatenate(parts[: width // turn], axis=1) * SCORE_SCALE).astype(BF16)
    for head in range(heads):
        place = place_table(width, head * HEAD, 0)
        q_out[head] = (dot(queries, place) + codes[...].astype(F32)).astype(BF16)
    keys = jnp.concatenate(parts[width // turn :], axis=1).astype(BF16)
    kv_out[:, : keys.shape[1]] = keys
    kv_out[:, keys.shape[1] :] = pre[:, width + keys.shape[1] :].astype(BF16)


def project(normed, weights, first, second, cos, sin, codes, heads, pairs):
    rows, width = normed.shape
    block = 256
    cols = (heads + 2 * pairs) * HEAD
    return pl.pallas_call(
        project_kernel,
        grid=(rows // block,),
        in_specs=[
            pl.BlockSpec((block, width), lambda i: (i, 0)),
            pl.BlockSpec((2, width // 2, cols), lambda i: (0, 0, 0)),
            pl.BlockSpec((width, LANES), lambda i: (0, 0)),
            pl.BlockSpec((LANES, cols), lambda i: (0, 0)),
            pl.BlockSpec((block, LANES), lambda i: (i, 0)),
            pl.BlockSpec((block, LANES), lambda i: (i, 0)),
            pl.BlockSpec((block, LANES), lambda i: (i, 0)),
        ],
        out_specs=[
            pl.BlockSpec((heads, block, LANES), lambda i: (0, i, 0)),
            pl.BlockSpec((block, 2 * pairs * HEAD), lambda i: (i, 0)),
            pl.BlockSpec((block, LANES), lambda i: (i, 0)),
        ],
        out_shape=[
            jax.ShapeDtypeStruct((heads, rows, LANES), BF16),
            jax.ShapeDtypeStruct((rows, 2 * pairs * HEAD), BF16),
            jax.ShapeDtypeStruct((rows, LANES), BF16),
        ],
        compiler_params=pltpu.CompilerParams(vmem_limit_bytes=VMEM_LIMIT),
        name="project",
    )(normed, weights, first, second, cos, sin, codes)


def build_tables(rank, kv_refs, k_aug, v_aug):
    pairs = k_aug.shape[0]
    for distance, kv in enumerate(kv_refs):

        @pl.when(distance <= rank)
        def _(distance=distance, kv=kv):
            rows, width = kv.shape
            values = kv[...]
            lane = iota((rows, LANES), 1)
            seg = (rank - distance) * SEGS_DEV + iota((rows, LANES), 0) // SEG
            key_code = ((lane - CODE == seg) | ((lane >= LSE) & (lane < LSE + 3))).astype(F32)
            one_code = ((lane == ONES) | (lane == ONES + 1)).astype(F32)
            for pair in range(pairs):
                k_place = place_table(width, pair * HEAD, 0)
                v_place = place_table(width, (pairs + pair) * HEAD, 0)
                span = pl.ds(distance * rows, rows)
                k_aug[pair, span, :] = (dot(values, k_place) + key_code).astype(BF16)
                v_aug[pair, span, :] = (dot(values, v_place) + one_code).astype(BF16)


def attend_kernel(
    rank_ref, q_ref, kv0, kv1, kv2, kv3, w_out, out_in, att_out, q_out, part_out,
    k_aug, v_aug, top, acc,
):
    step = pl.program_id(0)
    rank = rank_ref[0]
    heads, block, _ = q_ref.shape
    pairs = k_aug.shape[0]
    group = heads // pairs
    rows = kv0.shape[0]
    tall = group * block

    @pl.when(step == 0)
    def _():
        build_tables(rank, (kv0, kv1, kv2, kv3), k_aug, v_aug)

    for pair in range(pairs):
        queries = q_ref[pl.ds(pair * group, group)].reshape(tall, LANES)
        top[...] = jnp.full(top.shape, MASKED, F32)
        acc[...] = jnp.zeros(acc.shape, F32)

        def tile(start, size, causal, queries=queries, pair=pair):
            span = pl.ds(start, size)
            scores = dot_nt(queries, k_aug[pair, span, :])
            if causal:
                q_row = iota(scores.shape, 0) % block
                scores = jnp.where(iota(scores.shape, 1) <= q_row, scores, MASKED)
            before = top[...]
            now = jnp.maximum(before, jnp.max(scores, axis=1, keepdims=True))
            top[...] = now
            probs = jnp.exp(scores - now[:, :1]).astype(BF16)
            acc[...] = acc[...] * jnp.exp(before - now) + dot(probs, v_aug[pair, span, :])

        tile(pl.multiple_of(step * block, block), block, True)

        @pl.loop(0, step)
        def _(j, tile=tile):
            tile(pl.multiple_of(j * block, block), block, False)

        for distance in range(1, SPAN):

            @pl.when(distance <= rank)
            def _(distance=distance, tile=tile):
                tile(distance * rows, rows, False)

        total = acc[:, ONES : ONES + 1]
        result = (acc[...] / total).astype(BF16)
        for member in range(group):
            head = pair * group + member
            att_out[:, pl.ds(head * HEAD, HEAD)] = result[member * block : (member + 1) * block, :HEAD]
        minus = -(top[...] + jnp.log(total))
        high = minus.astype(BF16).astype(F32)
        middle = (minus - high).astype(BF16).astype(F32)
        low = minus - high - middle
        lane = iota(minus.shape, 1)
        coded = jnp.where(
            lane == LSE,
            high,
            jnp.where(
                lane == LSE + 1, middle, jnp.where(lane == LSE + 2, low, queries.astype(F32))
            ),
        )
        q_out[pl.ds(pair * group, group)] = coded.astype(BF16).reshape(group, block, LANES)

    mixed = att_out[...]
    half = w_out.shape[2]
    part_out[:, :half] = dot(mixed, w_out[0]).astype(BF16)
    part_out[:, half : 2 * half] = dot(mixed, w_out[1]).astype(BF16)
    part_out[:, 2 * half :] = dot(mixed, out_in[...]).astype(BF16)


def attend(rank, queries, kv_parts, w_out, out_in):
    heads, rows, _ = queries.shape
    block = 256
    kv_width = kv_parts[0].shape[1]
    pairs = kv_width // (2 * HEAD)
    tall = heads // pairs * block
    cols = 2 * w_out.shape[2] + LANES
    whole = lambda i, r: (0, 0)
    return pl.pallas_call(
        attend_kernel,
        grid_spec=pltpu.PrefetchScalarGridSpec(
            num_scalar_prefetch=1,
            grid=(rows // block,),
            in_specs=[pl.BlockSpec((heads, block, LANES), lambda i, r: (0, i, 0))]
            + [pl.BlockSpec((rows, kv_width), whole)] * SPAN
            + [
                pl.BlockSpec(w_out.shape, lambda i, r: (0, 0, 0)),
                pl.BlockSpec(out_in.shape, whole),
            ],
            out_specs=[
                pl.BlockSpec((block, heads * HEAD), lambda i, r: (i, 0)),
                pl.BlockSpec((heads, block, LANES), lambda i, r: (0, i, 0)),
                pl.BlockSpec((block, cols), lambda i, r: (i, 0)),
            ],
            scratch_shapes=[
                pltpu.VMEM((pairs, SPAN * rows, LANES), BF16),
                pltpu.VMEM((pairs, SPAN * rows, LANES), BF16),
                pltpu.VMEM((tall, LANES), F32),
                pltpu.VMEM((tall, LANES), F32),
            ],
        ),
        out_shape=[
            jax.ShapeDtypeStruct((rows, heads * HEAD), BF16),
            jax.ShapeDtypeStruct((heads, rows, LANES), BF16),
            jax.ShapeDtypeStruct((rows, cols), BF16),
        ],
        compiler_params=pltpu.CompilerParams(vmem_limit_bytes=VMEM_LIMIT),
        name="attend",
    )(rank, queries, *kv_parts, w_out, out_in)


def retrace_kernel(
    rank_ref, q_ref, kv0, kv1, kv2, kv3, att, branch, w_out, out_in, out_out, cos, sin,
    dq_out, own_out, far_out, in_grad,
    k_aug, v_aug, dk, dv, dq,
):
    step = pl.program_id(0)
    rank = rank_ref[0]
    heads, block, _ = q_ref.shape
    pairs = k_aug.shape[0]
    group = heads // pairs
    rows = kv0.shape[0]
    tall = group * block
    width = heads * HEAD

    @pl.when(step == 0)
    def _():
        build_tables(rank, (kv0, kv1, kv2, kv3), k_aug, v_aug)
        dk[...] = jnp.zeros(dk.shape, F32)
        dv[...] = jnp.zeros(dv.shape, F32)
        in_grad[...] = jnp.zeros(in_grad.shape, F32)

    half = w_out.shape[2]
    low_grad = dot_nt(branch[...], out_out[...]).astype(BF16)
    grads = (
        dot_nt(branch[:, :half], w_out[0])
        + dot_nt(branch[:, half:], w_out[1])
        + dot_nt(low_grad, out_in[...])
    ).astype(BF16)
    mixed = att[...]
    in_grad[...] += dot_tn(mixed, low_grad)
    product = grads.astype(F32) * mixed.astype(F32)
    wide = heads * LANES
    r, c = iota((width, wide), 0), iota((width, wide), 1)
    same = r // HEAD == c // LANES
    place = (same & (r % HEAD == c % LANES)).astype(BF16)
    spread = (same & (c % LANES >= ONES) & (c % LANES < ONES + 2)).astype(F32)
    minus = -lax.dot_general(
        product, spread, (((1,), (0,)), ((), ())),
        precision=lax.Precision.HIGHEST, preferred_element_type=F32,
    )
    high = minus.astype(BF16).astype(F32)
    lane = iota(minus.shape, 1) % LANES
    coded = dot(grads, place) + jnp.where(
        lane == ONES, high, jnp.where(lane == ONES + 1, minus - high, 0.0)
    )
    coded = coded.astype(BF16)

    pieces = []
    for pair in range(pairs):
        queries = q_ref[pl.ds(pair * group, group)].reshape(tall, LANES)
        upstream = jnp.concatenate(
            [
                coded[:, (pair * group + member) * LANES : (pair * group + member + 1) * LANES]
                for member in range(group)
            ],
            axis=0,
        )
        dq[...] = jnp.zeros(dq.shape, F32)

        def tile(start, size, causal, queries=queries, upstream=upstream, pair=pair):
            span = pl.ds(start, size)
            keys = k_aug[pair, span, :]
            probs = jnp.exp(dot_nt(keys, queries))
            if causal:
                q_row = iota(probs.shape, 1) % block
                probs = jnp.where(iota(probs.shape, 0) <= q_row, probs, 0.0)
            slopes = (probs * dot_nt(v_aug[pair, span, :], upstream)).astype(BF16)
            dv[pair, span, :] += dot(probs.astype(BF16), upstream)
            dk[pair, span, :] += dot(slopes, queries)
            dq[...] += dot_tn(slopes, keys)

        tile(pl.multiple_of(step * block, block), block, True)

        @pl.loop(0, step)
        def _(j, tile=tile):
            tile(pl.multiple_of(j * block, block), block, False)

        for distance in range(1, SPAN):

            @pl.when(distance <= rank)
            def _(distance=distance, tile=tile):
                for part in range(0, rows, rows // 2):
                    tile(distance * rows + part, rows // 2, False)

        for member in range(group):
            pieces.append(dq[member * block : (member + 1) * block, :HEAD] * SCORE_SCALE)

    for pair in range(pairs):
        turned = jnp.concatenate(pieces[pair * group : (pair + 1) * group], axis=1)
        turned = turned * cos[...] - swap_halves(turned) * sin[...]
        dq_out[:, pl.ds(pair * group * HEAD, group * HEAD)] = turned.astype(BF16)

    @pl.when(step == pl.num_programs(0) - 1)
    def _():
        for distance in range(SPAN):
            span = pl.ds(distance * rows, rows)
            joined = jnp.concatenate(
                [dk[pair, span, :HEAD] for pair in range(pairs)]
                + [dv[pair, span, :HEAD] for pair in range(pairs)],
                axis=1,
            )
            if distance == 0:
                own_out[...] = joined
            else:
                far_out[distance - 1] = joined.astype(BF16)


def retrace(rank, queries, kv_parts, att, branch, w_out, out_in, out_out, cos, sin):
    heads, rows, _ = queries.shape
    block = 256
    kv_width = kv_parts[0].shape[1]
    pairs = kv_width // (2 * HEAD)
    tall = heads // pairs * block
    width = heads * HEAD
    whole = lambda i, r: (0, 0)
    row = lambda i, r: (i, 0)
    return pl.pallas_call(
        retrace_kernel,
        grid_spec=pltpu.PrefetchScalarGridSpec(
            num_scalar_prefetch=1,
            grid=(rows // block,),
            in_specs=[pl.BlockSpec((heads, block, LANES), lambda i, r: (0, i, 0))]
            + [pl.BlockSpec((rows, kv_width), whole)] * SPAN
            + [
                pl.BlockSpec((block, width), row),
                pl.BlockSpec((block, branch.shape[1]), row),
                pl.BlockSpec(w_out.shape, lambda i, r: (0, 0, 0)),
                pl.BlockSpec(out_in.shape, whole),
                pl.BlockSpec(out_out.shape, whole),
                pl.BlockSpec((block, LANES), row),
                pl.BlockSpec((block, LANES), row),
            ],
            out_specs=[
                pl.BlockSpec((block, width), row),
                pl.BlockSpec((rows, kv_width), whole),
                pl.BlockSpec((SPAN - 1, rows, kv_width), lambda i, r: (0, 0, 0)),
                pl.BlockSpec((width, LANES), whole),
            ],
            scratch_shapes=[
                pltpu.VMEM((pairs, SPAN * rows, LANES), BF16),
                pltpu.VMEM((pairs, SPAN * rows, LANES), BF16),
                pltpu.VMEM((pairs, SPAN * rows, LANES), F32),
                pltpu.VMEM((pairs, SPAN * rows, LANES), F32),
                pltpu.VMEM((tall, LANES), F32),
            ],
        ),
        out_shape=[
            jax.ShapeDtypeStruct((rows, width), BF16),
            jax.ShapeDtypeStruct((rows, kv_width), F32),
            jax.ShapeDtypeStruct((SPAN - 1, rows, kv_width), BF16),
            jax.ShapeDtypeStruct((width, LANES), F32),
        ],
        compiler_params=pltpu.CompilerParams(vmem_limit_bytes=VMEM_LIMIT),
        name="retrace",
    )(rank, queries, *kv_parts, att, branch, w_out, out_in, out_out, cos, sin)


def unproject_kernel(
    dq, own, far1, far2, far3, lora, weights, second, cos, sin, part_out, grad_out
):
    step = pl.program_id(0)
    total = own[...] + far1[...].astype(F32) + far2[...].astype(F32) + far3[...].astype(F32)
    split = total.shape[1] // 2
    keys = total[:, :split]
    keys = keys * cos[...] - swap_halves(keys) * sin[...]
    grads = jnp.concatenate(
        [dq[...], keys.astype(BF16), total[:, split:].astype(BF16)], axis=1
    )
    half = weights.shape[1]
    part_out[:, :half] = dot_nt(grads, weights[0]).astype(BF16)
    part_out[:, half : 2 * half] = dot_nt(grads, weights[1]).astype(BF16)
    part_out[:, 2 * half :] = dot_nt(grads, second[...]).astype(BF16)

    @pl.when(step == 0)
    def _():
        grad_out[...] = jnp.zeros(grad_out.shape, F32)

    grad_out[...] += dot_tn(lora[...], grads)


def unproject(dq, own, fars, lora, weights, second, cos, sin):
    rows, width = dq.shape
    kv_width = own.shape[1]
    block = 256
    cols = weights.shape[2]
    model = 2 * weights.shape[1]
    row = lambda i: (i, 0)
    return pl.pallas_call(
        unproject_kernel,
        grid=(rows // block,),
        in_specs=[pl.BlockSpec((block, width), row)]
        + [pl.BlockSpec((block, kv_width), row)] * SPAN
        + [
            pl.BlockSpec((block, LANES), row),
            pl.BlockSpec((2, model // 2, cols), lambda i: (0, 0, 0)),
            pl.BlockSpec((LANES, cols), lambda i: (0, 0)),
            pl.BlockSpec((block, LANES), row),
            pl.BlockSpec((block, LANES), row),
        ],
        out_specs=[
            pl.BlockSpec((block, model + LANES), row),
            pl.BlockSpec((LANES, cols), lambda i: (0, 0)),
        ],
        out_shape=[
            jax.ShapeDtypeStruct((rows, model + LANES), BF16),
            jax.ShapeDtypeStruct((LANES, cols), F32),
        ],
        compiler_params=pltpu.CompilerParams(vmem_limit_bytes=VMEM_LIMIT),
        name="unproject",
    )(dq, own, *fars, lora, weights, second, cos, sin)


def expert_kernel(
    sets, base, x_ref, g_ref, routes, router, w_gate, w_up, w_down,
    gate_in, up_in, gate_out, up_out, down_in, down_out,
    mixed_out, grad_out,
    rank_rows, gate_rows, slope_rows, mix, back, xs, firsts, tall_grad,
    *, slots, sources,
):
    chunk, expert = pl.program_id(0), pl.program_id(1)
    experts = router.shape[0]
    tokens, model = x_ref.shape
    each = tokens // sources
    hidden = w_gate.shape[3]
    lanes = gate_in.shape[2]
    chosen = sets[chunk]

    @pl.when(expert == 0)
    def _():
        logits = dot_nt(router[...], x_ref[...])
        number = iota((experts, tokens), 0)
        hit = jnp.zeros((experts, tokens), F32)
        for k in range(routes.shape[0]):
            hit += (routes[k : k + 1, :] == number).astype(F32)
        kept = jnp.where(hit > 0.5, logits, MASKED)
        weights = jnp.exp(kept - jnp.max(kept, axis=0, keepdims=True)) * hit
        gate_rows[...] = weights / jnp.sum(weights, axis=0, keepdims=True)
        earlier = (iota((each, each), 0) < iota((each, each), 1)).astype(BF16)
        for s in range(sources):
            span = slice(s * each, (s + 1) * each)
            order = dot(hit[:, span].astype(BF16), earlier)
            rank_rows[:, span] = jnp.where(hit[:, span] > 0.5, order, -1.0)
        mix[...] = jnp.zeros(mix.shape, F32)
        back[...] = jnp.zeros(back.shape, F32)
        slope_rows[...] = jnp.zeros(slope_rows.shape, F32)

    row = base[0] + expert
    ranks = rank_rows[pl.ds(row, 1), :]
    gates = gate_rows[pl.ds(row, 1), :]
    slot_number = iota((slots, each), 0).astype(F32)
    picks, columns, upstreams = [], [], []
    for s in range(sources):
        span = slice(s * each, (s + 1) * each)
        pick = ranks[:, span] == slot_number
        columns.append(jnp.sum(jnp.where(pick, gates[:, span], 0.0), axis=1, keepdims=True))
        pick = pick.astype(BF16)
        picks.append(pick)
        xs[pl.ds(s * slots, slots), :] = dot(pick, x_ref[pl.ds(s * each, each), :]).astype(BF16)
        upstreams.append(dot(pick, g_ref[pl.ds(s * each, each), :]))
    gate_column = jnp.concatenate(columns, axis=0)
    upstream = RESIDUAL_SCALE * jnp.concatenate(upstreams, axis=0)

    firsts[:, :lanes] = gate_in[0]
    firsts[:, lanes:] = up_in[0]
    keep = (iota((1, 2 * lanes), 1) % lanes // RANK == chosen).astype(BF16)
    rows = xs[...]
    inner = dot(rows, firsts[...]).astype(BF16) * keep
    half = w_gate.shape[2]
    gate_value = (
        dot(rows[:, :half], w_gate[0, 0])
        + dot(rows[:, half:], w_gate[1, 0])
        + dot(inner[:, :lanes], gate_out[0])
    )
    up_value = (
        dot(rows[:, :half], w_up[0, 0])
        + dot(rows[:, half:], w_up[1, 0])
        + dot(inner[:, lanes:], up_out[0])
    )
    sigmoid = 1.0 / (1.0 + jnp.exp(-gate_value))
    silu = gate_value * sigmoid
    active = (silu * up_value).astype(BF16)
    down_inner = dot(active, down_in[0]).astype(BF16) * keep[:, :lanes]
    down_half = w_down.shape[2]
    produced = (
        dot(active[:, :down_half], w_down[0, 0])
        + dot(active[:, down_half:], w_down[1, 0])
        + dot(down_inner, down_out[0])
    ).astype(BF16).astype(F32)
    slope = jnp.sum(upstream * produced, axis=1, keepdims=True)
    sent = (gate_column * produced).astype(BF16)
    slot_grad = (gate_column * upstream).astype(BF16)

    down_inner_grad = dot_nt(slot_grad, down_out[0]).astype(BF16) * keep[:, :lanes]
    active_grad = (
        jnp.concatenate(
            [dot_nt(slot_grad, w_down[0, 0]), dot_nt(slot_grad, w_down[1, 0])], axis=1
        )
        + dot_nt(down_inner_grad, down_in[0])
    ).astype(BF16).astype(F32)
    gate_grad = (active_grad * up_value * (sigmoid + silu * (1.0 - sigmoid))).astype(BF16)
    up_grad = (active_grad * silu).astype(BF16)
    inner_grad = (
        jnp.concatenate([dot_nt(gate_grad, gate_out[0]), dot_nt(up_grad, up_out[0])], axis=1)
    ).astype(BF16) * keep
    row_grad = jnp.concatenate(
        [dot_nt(gate_grad, w_gate[h, 0]) + dot_nt(up_grad, w_up[h, 0]) for h in range(2)], axis=1
    )
    row_grad = (row_grad + dot_nt(inner_grad, firsts[...])).astype(BF16)

    for s in range(sources):
        span = slice(s * slots, (s + 1) * slots)
        spot = pl.ds(s * each, each)
        mix[spot, :] += dot_tn(picks[s], sent[span, :])
        back[spot, :] += dot_tn(picks[s], row_grad[span, :])
        slope_rows[pl.ds(expert, 1), spot] = jnp.sum(
            jnp.where(picks[s] > 0.5, slope[span, :], 0.0), axis=0, keepdims=True
        )

    own = pl.multiple_of(chosen * RANK, RANK)
    tall_grad[...] = dot_tn(inner_grad, rows)
    grad_out[0, 0, pl.ds(0, RANK), :] = tall_grad[pl.ds(own, RANK), :].astype(BF16)
    grad_out[0, 0, pl.ds(RANK, RANK), :] = tall_grad[pl.ds(lanes + own, RANK), :].astype(BF16)
    tall_grad[pl.ds(0, lanes), :hidden] = dot_tn(inner[:, :lanes], gate_grad)
    tall_grad[pl.ds(0, lanes), hidden:] = dot_tn(inner[:, lanes:], up_grad)
    grad_out[0, 0, pl.ds(2 * RANK, RANK), :] = tall_grad[pl.ds(own, RANK), :].astype(BF16)
    tall_grad[pl.ds(0, lanes), :] = dot_tn(down_inner, slot_grad)
    grad_out[0, 0, pl.ds(3 * RANK, RANK), :] = tall_grad[pl.ds(own, RANK), :].astype(BF16)
    tall_grad[pl.ds(0, lanes), :hidden] = dot_tn(down_inner_grad, active)
    tall_grad[pl.ds(0, lanes), hidden:] = jnp.zeros((lanes, model - hidden), F32)
    grad_out[0, 0, pl.ds(4 * RANK, RANK), :] = tall_grad[pl.ds(own, RANK), :].astype(BF16)

    @pl.when(expert == pl.num_programs(1) - 1)
    def _():
        mixed_out[:, :model] = mix[...].astype(BF16)
        mixed_out[:, model : 2 * model] = back[...].astype(BF16)
        turned = slope_rows[...].T
        high = turned.astype(BF16)
        low = (turned - high.astype(F32)).astype(BF16)
        local, lane = iota((LANES, LANES), 0), iota((LANES, LANES), 1)
        inside = local < pl.num_programs(1)
        first = (inside & (lane == local + base[0])).astype(BF16)
        later = (inside & (lane == local + base[0] + experts)).astype(BF16)
        mixed_out[:, 2 * model :] = (dot(high, first) + dot(low, later)).astype(BF16)


def run_experts(
    sets, base, rows, upstream, routes, router, weights, adapters, slots, sources
):
    total, model = rows.shape
    experts = router.shape[0]
    w_gate, w_up, w_down = weights
    local = w_gate.shape[1]
    trees = sets.shape[0]
    tokens = total // trees
    hidden = w_gate.shape[3]
    lanes = adapters[0].shape[2]
    cols = 2 * model + LANES
    tall = sources * slots
    piece = lambda c, e, *_: (c, 0)
    fixed = lambda c, e, *_: (0, 0)
    expert = lambda c, e, *_: (e, 0, 0)
    return pl.pallas_call(
        functools.partial(expert_kernel, slots=slots, sources=sources),
        grid_spec=pltpu.PrefetchScalarGridSpec(
            num_scalar_prefetch=2,
            grid=(trees, local),
            in_specs=[
                pl.BlockSpec((tokens, model), piece),
                pl.BlockSpec((tokens, model), piece),
                pl.BlockSpec((routes.shape[0], tokens), lambda c, e, *_: (0, c)),
                pl.BlockSpec(router.shape, fixed),
                *[
                    pl.BlockSpec((2, 1) + w.shape[2:], lambda c, e, *_: (0, e, 0, 0))
                    for w in weights
                ],
                *[pl.BlockSpec((1,) + a.shape[1:], expert) for a in adapters],
            ],
            out_specs=[
                pl.BlockSpec((tokens, cols), piece),
                pl.BlockSpec((1, 1, 5 * RANK, model), lambda c, e, *_: (c, e, 0, 0)),
            ],
            scratch_shapes=[
                pltpu.VMEM((experts, tokens), F32),
                pltpu.VMEM((experts, tokens), F32),
                pltpu.VMEM((LANES, tokens), F32),
                pltpu.VMEM((tokens, model), F32),
                pltpu.VMEM((tokens, model), F32),
                pltpu.VMEM((tall, model), BF16),
                pltpu.VMEM((model, 2 * lanes), BF16),
                pltpu.VMEM((2 * lanes, model), F32),
            ],
        ),
        out_shape=[
            jax.ShapeDtypeStruct((total, cols), BF16),
            jax.ShapeDtypeStruct((trees, local, 5 * RANK, model), BF16),
        ],
        compiler_params=pltpu.CompilerParams(vmem_limit_bytes=60 * 1024 * 1024),
        name="experts",
    )(sets, base, rows, upstream, routes, router, *weights, *adapters)


def take_set(table, chosen, axis):
    return lax.dynamic_slice_in_dim(table, chosen * RANK, RANK, axis)


def per_device(
    tokens,
    out_grad,
    routes,
    parents,
    adapter_set,
    gain_a,
    gain_b,
    w_query,
    key_projection_matrix,
    value_projection_matrix,
    w_output,
    w_router,
    w_gate,
    w_up,
    w_down,
    query_in,
    query_out,
    key_in,
    key_second_factor,
    value_in,
    value_second_factor,
    out_in,
    out_out,
    gate_in,
    gate_out,
    up_in,
    up_out,
    down_in,
    down_out,
):
    tp_rank = lax.axis_index("tp")
    ctx_rank = lax.axis_index("ctx")
    fsdp_rank = lax.axis_index("fsdp")
    ctx_count = lax.axis_size("ctx")
    tp_count = lax.axis_size("tp")
    fsdp_count = lax.axis_size("fsdp")
    tok_rows, model = tokens.shape
    q_cols = w_query.shape[1]
    kv_cols = key_projection_matrix.shape[1]
    heads, pairs = q_cols // HEAD, kv_cols // HEAD
    experts = w_router.shape[1]
    local_experts = w_gate.shape[0]
    sets = query_in.shape[1] // RANK
    slots = tok_rows * TOP * 3 // (2 * experts)
    trees = ctx_count // SPAN

    attention_shard = jnp.concatenate(
        [
            jnp.concatenate([w_query, key_projection_matrix, value_projection_matrix], axis=1),
            w_output,
        ],
        axis=0,
    )
    attention_weights = lax.all_gather(attention_shard, "fsdp")
    project_weights = attention_weights[:, : w_query.shape[0]]
    output_weights = attention_weights[:, w_query.shape[0] :]

    seg_start = (fsdp_rank * ctx_count + ctx_rank) * SEGS_DEV
    tree_index = seg_start // TREE_SEGS
    local_start = seg_start % TREE_SEGS
    rank = (local_start // SEGS_DEV).astype(jnp.int32).reshape(1)
    tree_parents = lax.dynamic_slice_in_dim(parents, tree_index * TREE_SEGS, TREE_SEGS, 0)
    reach, depth = tree_links(tree_parents)
    chosen = lax.dynamic_slice_in_dim(adapter_set, tree_index, 1, 0)[0]

    inputs = tokens.astype(F32)
    gain_one = gain_a.astype(F32)
    gain_two = gain_b.astype(F32)
    normed = rms_scale(inputs, gain_one).astype(BF16)
    normed_all = lax.all_gather(normed, "tp", axis=0, tiled=True)
    group_rows = normed_all.shape[0]

    own_reach = lax.dynamic_slice_in_dim(reach, local_start, SEGS_DEV, 0)
    codes = jnp.pad(
        jnp.where(own_reach > 0.5, 0.0, MASKED), ((0, 0), (CODE, LANES - CODE - TREE_SEGS))
    )
    codes = jnp.repeat(codes.astype(BF16), SEG, axis=0)
    own_depth = lax.dynamic_slice_in_dim(depth, local_start, SEGS_DEV, 0)
    positions = (
        own_depth[:, None] * SEG + jnp.arange(SEG, dtype=jnp.int32).astype(F32)[None, :]
    ).reshape(-1)
    half_head = HEAD // 2
    freqs = ROPE_BASE ** (-(jnp.arange(half_head, dtype=jnp.int32).astype(F32) * 2.0) / HEAD)
    angles = positions[:, None] * jnp.tile(freqs, LANES // half_head)[None, :]
    cos, sin = jnp.cos(angles), jnp.sin(angles)

    first = jnp.pad(
        jnp.concatenate(
            [take_set(t, chosen, 1) for t in (query_in, key_in, value_in)], axis=1
        ),
        ((0, 0), (0, LANES - 3 * RANK)),
    )
    q_second = lax.dynamic_slice(query_out, (chosen * RANK, tp_rank * q_cols), (RANK, q_cols))
    k_second = lax.dynamic_slice(
        key_second_factor, (chosen * RANK, tp_rank * kv_cols), (RANK, kv_cols)
    )
    v_second = lax.dynamic_slice(
        value_second_factor, (chosen * RANK, tp_rank * kv_cols), (RANK, kv_cols)
    )
    second = jnp.concatenate(
        [
            jnp.pad(q_second, ((0, 0), (0, 2 * kv_cols))),
            jnp.pad(k_second, ((0, 0), (q_cols, kv_cols))),
            jnp.pad(v_second, ((0, 0), (q_cols + kv_cols, 0))),
            jnp.zeros((LANES - 3 * RANK, q_cols + 2 * kv_cols), BF16),
        ],
        axis=0,
    )
    o_first = jnp.pad(
        lax.dynamic_slice(out_in, (tp_rank * q_cols, chosen * RANK), (q_cols, RANK)),
        ((0, 0), (0, LANES - RANK)),
    )
    o_second = jnp.pad(take_set(out_out, chosen, 0), ((0, LANES - RANK), (0, 0)))

    queries, kv, lora = project(
        normed_all, project_weights, first, second, cos, sin, codes, heads, pairs
    )
    kv_parts = [kv] + [shifted(kv, "ctx", distance) for distance in range(1, SPAN)]
    attended, queries, part = attend(rank, queries, kv_parts, output_weights, o_first)
    summed = lax.psum_scatter(part, "tp", scatter_dimension=0, tiled=True)
    o_reduced = summed[:, model:]
    middle = inputs + RESIDUAL_SCALE * (
        summed[:, :model].astype(F32)
        + jnp.dot(o_reduced, o_second, preferred_element_type=F32)
    )

    upstream_all = lax.all_gather(out_grad, "ctx", axis=0, tiled=True)
    routes_all = lax.all_gather(routes, "ctx", axis=0, tiled=True).T
    gate_full = lax.all_gather(w_gate, "fsdp")
    up_full = lax.all_gather(w_up, "fsdp")
    down_full = lax.all_gather(w_down, "fsdp")
    normed_two = rms_scale(middle, gain_two).astype(BF16)
    rows_all = lax.all_gather(normed_two, "ctx", axis=0, tiled=True)
    tree_sets = lax.dynamic_slice_in_dim(adapter_set, fsdp_rank * trees, trees, 0)
    base = (ctx_rank * local_experts).astype(jnp.int32).reshape(1)
    mixed, expert_part = run_experts(
        tree_sets,
        base,
        rows_all,
        upstream_all,
        routes_all,
        w_router.T,
        (gate_full, up_full, down_full),
        (gate_in, up_in, gate_out, up_out, down_in, down_out),
        slots,
        SPAN,
    )
    combined = lax.psum_scatter(mixed, "ctx", scatter_dimension=0, tiled=True).astype(F32)
    mixture = combined[:, :model]
    output = (middle + RESIDUAL_SCALE * mixture).astype(BF16)

    logits = jnp.dot(normed_two, w_router, preferred_element_type=F32)
    hits = jnp.sum(
        (routes[:, :, None] == jnp.arange(experts, dtype=jnp.int32)[None, None, :]).astype(F32),
        axis=1,
    )
    kept = jnp.where(hits > 0.5, logits, MASKED)
    gates = jnp.exp(kept - jnp.max(kept, axis=1, keepdims=True)) * hits
    gates = gates / jnp.sum(gates, axis=1, keepdims=True)
    slopes = (
        combined[:, 2 * model : 2 * model + experts]
        + combined[:, 2 * model + experts : 2 * model + 2 * experts]
    )
    logits_grad = gates * (slopes - jnp.sum(gates * slopes, axis=1, keepdims=True))
    normed_two_grad = combined[:, model : 2 * model] + jnp.einsum(
        "te,de->td", logits_grad, w_router.astype(F32), precision=lax.Precision.HIGHEST
    )
    upstream = out_grad.astype(F32)
    middle_grad = upstream + rms_back(middle, gain_two, normed_two_grad)
    branch_grad = (RESIDUAL_SCALE * middle_grad).astype(BF16)
    out_out_part = jnp.einsum(
        "ts,td->sd", o_reduced, branch_grad, preferred_element_type=F32
    )[:RANK]
    branch_all = lax.all_gather(branch_grad, "tp", axis=0, tiled=True)
    dq, own_grad, far_grad, out_in_part = retrace(
        rank, queries, kv_parts, attended, branch_all, output_weights, o_first, o_second, cos, sin
    )
    fars = [shifted(far_grad[d - 1], "ctx", -d) for d in range(1, SPAN)]
    part, second_part = unproject(
        dq, own_grad, fars, lora, project_weights, second, cos, sin
    )
    summed = lax.psum_scatter(part, "tp", scatter_dimension=0, tiled=True)
    reduced_grad = summed[:, model:]
    normed_grad = summed[:, :model].astype(F32) + jnp.einsum(
        "ts,ds->td", reduced_grad, first, preferred_element_type=F32
    )
    first_part = jnp.einsum(
        "ts,td->sd", reduced_grad, normed, preferred_element_type=F32
    )[: 3 * RANK]
    input_grad = (middle_grad + rms_back(inputs, gain_one, normed_grad)).astype(BF16)

    full_q = q_cols * tp_count
    full_kv = kv_cols * tp_count

    def widen(part, cols, axis, start):
        shape = list(part.shape)
        shape[axis] = cols
        return lax.dynamic_update_slice_in_dim(jnp.zeros(shape, F32), part, start, axis)

    packed = jnp.concatenate(
        [
            first_part,
            widen(out_in_part[:, :RANK].T, full_q, 1, tp_rank * q_cols),
            out_out_part,
            widen(second_part[:RANK, :q_cols], full_q, 1, tp_rank * q_cols),
            jnp.concatenate(
                [
                    widen(
                        second_part[RANK : 2 * RANK, q_cols : q_cols + kv_cols],
                        full_kv, 1, tp_rank * kv_cols,
                    ),
                    widen(
                        second_part[2 * RANK : 3 * RANK, q_cols + kv_cols :],
                        full_kv, 1, tp_rank * kv_cols,
                    ),
                ],
                axis=1,
            ),
        ],
        axis=0,
    )
    all_trees = fsdp_count * trees
    if trees > 1:
        packed = lax.psum(
            jnp.where(
                (jnp.arange(all_trees) == tree_index)[:, None, None], packed[None], 0.0
            ),
            ("fsdp", "ctx", "tp"),
        )
    else:
        packed = lax.all_gather(lax.psum(packed, ("ctx", "tp")), "fsdp")
    place = (
        adapter_set[:, None] == jnp.arange(sets, dtype=jnp.int32)[None, :]
    ).astype(F32)

    def in_rows(part):
        spread = jnp.einsum("ts,trd->srd", place, part, precision=lax.Precision.HIGHEST)
        return spread.reshape(sets * RANK, part.shape[2])

    def in_columns(part):
        return in_rows(part).T

    adapter_totals = (
        in_columns(packed[:, :RANK]),
        in_rows(packed[:, 5 * RANK : 6 * RANK]),
        in_columns(packed[:, RANK : 2 * RANK]),
        in_rows(packed[:, 6 * RANK :, :full_kv]),
        in_columns(packed[:, 2 * RANK : 3 * RANK]),
        in_rows(packed[:, 6 * RANK :, full_kv:]),
        in_columns(packed[:, 3 * RANK : 4 * RANK]),
        in_rows(packed[:, 4 * RANK : 5 * RANK]),
    )

    expert_part = lax.all_gather(lax.psum(expert_part, "tp"), "fsdp")
    expert_part = expert_part.reshape(all_trees, local_experts, 5 * RANK, model)
    hidden = w_gate.shape[2]

    def expert_rows(part):
        spread = jnp.einsum(
            "ts,terd->esrd", place.astype(BF16), part, preferred_element_type=F32
        )
        return spread.reshape(local_experts, sets * RANK, part.shape[3])

    def expert_columns(part):
        return expert_rows(part).transpose(0, 2, 1)

    return (
        output,
        input_grad,
        *adapter_totals,
        expert_columns(expert_part[:, :, :RANK]),
        expert_rows(expert_part[:, :, 2 * RANK : 3 * RANK, :hidden]),
        expert_columns(expert_part[:, :, RANK : 2 * RANK]),
        expert_rows(expert_part[:, :, 2 * RANK : 3 * RANK, hidden:]),
        expert_columns(expert_part[:, :, 4 * RANK :, :hidden]),
        expert_rows(expert_part[:, :, 3 * RANK : 4 * RANK]),
    )


def solution(mesh):
    in_specs = (
        P(("fsdp", "ctx", "tp"), None),
        P(("fsdp", "ctx", "tp"), None),
        P(("fsdp", "ctx", "tp"), None),
        P(),
        P(),
        P(),
        P(),
        P("fsdp", "tp"),
        P("fsdp", "tp"),
        P("fsdp", "tp"),
        P("tp", "fsdp"),
        P(),
        P("ctx", "fsdp", None),
        P("ctx", "fsdp", None),
        P("ctx", "fsdp", None),
        P(),
        P(),
        P(),
        P(),
        P(),
        P(),
        P(),
        P(),
        P("ctx", None, None),
        P("ctx", None, None),
        P("ctx", None, None),
        P("ctx", None, None),
        P("ctx", None, None),
        P("ctx", None, None),
    )
    out_specs = (
        P(("fsdp", "ctx", "tp"), None),
        P(("fsdp", "ctx", "tp"), None),
        P(),
        P(),
        P(),
        P(),
        P(),
        P(),
        P(),
        P(),
        P("ctx", None, None),
        P("ctx", None, None),
        P("ctx", None, None),
        P("ctx", None, None),
        P("ctx", None, None),
        P("ctx", None, None),
    )
    return jax.shard_map(
        per_device, mesh=mesh, in_specs=in_specs, out_specs=out_specs, check_vma=False
    )
```

```python
import functools
import math

import jax
import jax.numpy as jnp
from jax import lax
from jax.experimental import pallas as pl
from jax.experimental.pallas import tpu as pltpu
from jax.sharding import PartitionSpec as P

HEAD = 64
TOP = 8
RANK = 16
SEG = 128
SEGS_DEV = 8
TREE_SEGS = 32
SPAN = TREE_SEGS // SEGS_DEV
LANES = 128

RESIDUAL_SCALE = 0.22
SCORE_SCALE = 0.015625
EPSILON = 1e-06
ROPE_BASE = 10000.0
MASKED = -1e30

F32 = jnp.float32
BF16 = jnp.bfloat16

CODE = HEAD
LSE = CODE + TREE_SEGS + 1
ONES = HEAD

VMEM_LIMIT = 56 * 1024 * 1024


def dot(a, b):
    return lax.dot_general(a, b, (((1,), (0,)), ((), ())), preferred_element_type=F32)


def dot_nt(a, b):
    return lax.dot_general(a, b, (((1,), (1,)), ((), ())), preferred_element_type=F32)


def dot_tn(a, b):
    return lax.dot_general(a, b, (((0,), (0,)), ((), ())), preferred_element_type=F32)


def iota(shape, dim):
    return lax.broadcasted_iota(jnp.int32, shape, dim)


def shifted(block, axis, distance):
    devices = range(lax.axis_size(axis))
    route = [(i - distance, i) for i in devices if i - distance in devices]
    return lax.ppermute(block, axis, route)


def rms_scale(values, gain_row):
    return (
        values * lax.rsqrt(jnp.mean(values * values, axis=-1, keepdims=True) + EPSILON) * gain_row
    )


def rms_back(values, gain_row, grad):
    inv = lax.rsqrt(jnp.mean(values * values, axis=-1, keepdims=True) + EPSILON)
    scaled = grad * gain_row
    inner = jnp.mean(scaled * values, axis=-1, keepdims=True)
    return inv * scaled - values * (inv * inv * inv * inner)


def tree_links(tree_parents):
    count = tree_parents.shape[0]
    columns = jnp.arange(count, dtype=jnp.int32)
    reach = (
        (tree_parents[:, None] == columns[None, :]) | (columns[:, None] == columns[None, :])
    ).astype(BF16)
    for _ in range(max(1, (count - 1).bit_length())):
        reach = jnp.minimum(dot(reach, reach), 1.0).astype(BF16)
    reach = reach.astype(F32)
    return reach, jnp.sum(reach, axis=1) - 1.0


def swap_halves(values):
    width = values.shape[-1]
    lane = iota(values.shape, 1) % HEAD
    ahead = pltpu.roll(values, width - HEAD // 2, 1)
    behind = pltpu.roll(values, HEAD // 2, 1)
    return jnp.where(lane < HEAD // 2, -ahead, behind)


def place_table(rows, source, target):
    r, c = iota((rows, LANES), 0), iota((rows, LANES), 1)
    return ((r - source == c - target) & (c >= target) & (c < target + HEAD)).astype(BF16)


def remote(src, dst, send, recv, where):
    return pltpu.make_async_remote_copy(
        src_ref=src,
        dst_ref=dst,
        send_sem=send,
        recv_sem=recv,
        device_id=where,
        device_id_type=pl.DeviceIdType.MESH,
    )


def ring(me, step, count):
    return lax.rem(me + (step + count), count)


def aug_keys(kv, pair, pairs, first_seg, k_aug, v_aug, start):
    rows, width = kv.shape
    lane = iota((rows, LANES), 1)
    seg = first_seg + iota((rows, LANES), 0) // SEG
    key_code = ((lane - CODE == seg) | ((lane >= LSE) & (lane < LSE + 3))).astype(F32)
    one_code = ((lane == ONES) | (lane == ONES + 1)).astype(F32)
    span = pl.ds(start, rows)
    k_aug[pair, span, :] = (dot(kv, place_table(width, pair * HEAD, 0)) + key_code).astype(BF16)
    v_aug[pair, span, :] = (
        dot(kv, place_table(width, (pairs + pair) * HEAD, 0)) + one_code
    ).astype(BF16)


def forward_kernel(
    tokens, gain_one, gain_two, shard, first, second, o_first, o_second, cos, sin, codes,
    w_gate, w_up, w_down, grads, routes,
    att_out, q_out, kv_out, lora_out, middle_out, low_out, weights_out,
    gate_far, up_far, down_far, grads_all, routes_all, rows_all,
    normed_all, weights, q_aug, k_aug, v_aug, top, acc, parts, parts_in, rows_own,
    shard_sem, normed_sem, kv_sem, part_sem, far_sem, grads_sem, routes_sem, rows_sem,
    pass_sem, local_sem,
    *, tp_count, ctx_count,
):
    tp, ctx, fsdp = (lax.axis_index(name) for name in ("tp", "ctx", "fsdp"))
    rank = lax.rem(ctx, SPAN)
    block, model = tokens.shape
    heads = q_aug.shape[0]
    pairs = k_aug.shape[0]
    group = heads // pairs
    tall = group * block
    half = shard.shape[1]
    q_cols = heads * HEAD
    turn = cos.shape[1]
    chips = ctx_count // 2
    partner = ctx + 1 - 2 * lax.rem(ctx, 2)
    other = {"fsdp": 1 - fsdp}

    barrier = pltpu.get_barrier_semaphore()
    pl.semaphore_signal(barrier, 1, device_id=other, device_id_type=pl.DeviceIdType.MESH)
    for k in range(1, tp_count):
        pl.semaphore_signal(
            barrier, 1, device_id={"tp": ring(tp, k, tp_count)},
            device_id_type=pl.DeviceIdType.MESH,
        )
    for k in range(1, ctx_count):
        pl.semaphore_signal(
            barrier, 1, device_id={"ctx": ring(ctx, k, ctx_count)},
            device_id_type=pl.DeviceIdType.MESH,
        )
    pl.semaphore_wait(barrier, tp_count + ctx_count - 1)

    shard_copy = remote(shard, weights.at[fsdp], shard_sem.at[0], shard_sem.at[1], other)
    shard_copy.start()

    inputs = tokens[...].astype(F32)
    normed = rms_scale(inputs, gain_one[...]).astype(BF16)
    normed_all[tp] = normed

    def normed_copy(k):
        return remote(
            normed_all.at[tp], normed_all.at[tp], normed_sem.at[0, k - 1], normed_sem.at[1, k - 1],
            {"tp": ring(tp, k, tp_count)},
        )

    for k in range(1, tp_count):
        normed_copy(k).start()

    def side_copies(k):
        where = {"ctx": ring(ctx, k, ctx_count)}
        return (
            remote(grads, grads_all.at[ctx], grads_sem.at[0, k], grads_sem.at[1, k], where),
            remote(routes, routes_all.at[ctx], routes_sem.at[0, k], routes_sem.at[1, k], where),
        )

    own_copies = (
        pltpu.make_async_copy(grads, grads_all.at[ctx], local_sem.at[0]),
        pltpu.make_async_copy(routes, routes_all.at[ctx], local_sem.at[1]),
    )
    for copy in own_copies:
        copy.start()
    for k in range(1, ctx_count):
        for copy in side_copies(k):
            copy.start()

    weights[fsdp] = shard[...]
    shard_copy.wait()
    far_copies = [
        remote(near, far, far_sem.at[0, n], far_sem.at[1, n], other)
        for n, (near, far) in enumerate(((w_gate, gate_far), (w_up, up_far), (w_down, down_far)))
    ]
    for copy in far_copies:
        copy.start()
    weights_out[...] = weights[...]

    def kv_copy(distance, part):
        return remote(
            kv_out.at[0, part], kv_out.at[distance, part],
            kv_sem.at[0, distance - 1], kv_sem.at[1, distance - 1], {"ctx": ring(ctx, distance, ctx_count)},
        )

    @pl.loop(0, tp_count)
    def _(k):
        @pl.when(k > 0)
        def _():
            normed_copy(k).wait_recv()

        part = ring(tp, -k, tp_count)
        span = pl.ds(pl.multiple_of(part * block, block), block)
        rows = normed_all[part]
        lora = dot(rows, first[...]).astype(BF16)
        lora_out[span, :] = lora
        pre = (
            dot(rows[:, :half], weights[0, pl.ds(0, half), :])
            + dot(rows[:, half:], weights[1, pl.ds(0, half), :])
            + dot(lora, second[...])
        )
        turned = []
        for start in range(0, pre.shape[1] // 4 * 3, turn):
            piece = pre[:, start : start + turn]
            turned.append(piece * cos[span, :] + swap_halves(piece) * sin[span, :])
        queries = (
            jnp.concatenate(turned[: q_cols // turn], axis=1) * SCORE_SCALE
        ).astype(BF16)
        for head in range(heads):
            q_aug[head, span, :] = (
                dot(queries, place_table(q_cols, head * HEAD, 0)) + codes[span, :].astype(F32)
            ).astype(BF16)
        keys = jnp.concatenate(turned[q_cols // turn :], axis=1)
        kv = jnp.concatenate([keys, pre[:, q_cols + keys.shape[1] :]], axis=1).astype(BF16)
        kv_out[0, part] = kv
        for distance in range(1, SPAN):

            @pl.when(rank + distance < SPAN)
            def _(distance=distance):
                kv_copy(distance, part).start()

        for pair in range(pairs):
            aug_keys(
                kv, pair, pairs, rank * SEGS_DEV + part * (block // SEG), k_aug, v_aug,
                pl.multiple_of(part * block, block),
            )

    def tile(part, pair, start, size, causal):
        index = part * pairs + pair
        rows = pl.ds(pl.multiple_of(part * block, block), block)
        queries = q_aug[pl.ds(pair * group, group), rows, :].reshape(tall, LANES)
        span = pl.ds(start, size)
        scores = dot_nt(queries, k_aug[pair, span, :])
        if causal:
            q_row = iota(scores.shape, 0) % block
            scores = jnp.where(iota(scores.shape, 1) <= q_row, scores, MASKED)
            now = jnp.broadcast_to(jnp.max(scores, axis=1, keepdims=True), (tall, LANES))
            probs = jnp.exp(scores - now[:, :1]).astype(BF16)
            acc[index] = dot(probs, v_aug[pair, span, :])
        else:
            before = top[index]
            now = jnp.maximum(before, jnp.max(scores, axis=1, keepdims=True))
            probs = jnp.exp(scores - now[:, :1]).astype(BF16)
            acc[index] = acc[index] * jnp.exp(before - now) + dot(probs, v_aug[pair, span, :])
        top[index] = now

    @pl.loop(0, tp_count * pairs)
    def _(index):
        part, pair = index // pairs, lax.rem(index, pairs)
        tile(part, pair, pl.multiple_of(part * block, block), block, True)

        @pl.loop(0, part)
        def _(j):
            tile(part, pair, pl.multiple_of(j * block, block), block, False)

    group_rows = tp_count * block
    for distance in range(1, SPAN):

        @pl.when(distance <= rank)
        def _(distance=distance):
            remote(
                kv_out.at[0], kv_out.at[distance], kv_sem.at[0, distance - 1],
                kv_sem.at[1, distance - 1], {"ctx": ring(ctx, distance, ctx_count)},
            ).wait_recv()

            @pl.loop(0, tp_count)
            def _(part):
                kv = kv_out[distance, part]
                for pair in range(pairs):
                    aug_keys(
                        kv, pair, pairs,
                        (rank - distance) * SEGS_DEV + part * (block // SEG), k_aug, v_aug,
                        pl.multiple_of(distance * group_rows + part * block, block),
                    )

        @pl.when(distance > rank)
        def _(distance=distance):
            kv_out[distance] = jnp.zeros(kv_out.shape[1:], BF16)

    def part_copy(k):
        return remote(
            parts.at[k], parts_in.at[k], part_sem.at[0, k], part_sem.at[1, k],
            {"tp": ring(tp, k + 1, tp_count)},
        )

    @pl.loop(0, tp_count)
    def _(k):
        part = ring(tp, k + 1, tp_count)
        rows = pl.ds(pl.multiple_of(part * block, block), block)
        for pair in range(pairs):
            index = part * pairs + pair

            @pl.loop(1, rank + 1)
            def _(distance, pair=pair):
                tile(
                    part, pair, pl.multiple_of(distance * group_rows, group_rows), group_rows, False
                )

            summed = acc[index]
            total = summed[:, ONES : ONES + 1]
            result = (summed / total).astype(BF16)
            for member in range(group):
                head = pair * group + member
                att_out[rows, pl.ds(head * HEAD, HEAD)] = result[
                    member * block : (member + 1) * block, :HEAD
                ]
            minus = -(top[index] + jnp.log(total))
            high = minus.astype(BF16).astype(F32)
            middle = (minus - high).astype(BF16).astype(F32)
            lane = iota(minus.shape, 1)
            queries = q_aug[pl.ds(pair * group, group), rows, :].reshape(tall, LANES)
            coded = jnp.where(
                lane == LSE,
                high,
                jnp.where(
                    lane == LSE + 1,
                    middle,
                    jnp.where(lane == LSE + 2, minus - high - middle, queries.astype(F32)),
                ),
            )
            q_out[pl.ds(pair * group, group), rows, :] = coded.astype(BF16).reshape(
                group, block, LANES
            )
        mixed = att_out[rows, :]
        for side in range(2):
            parts[k, :, side * half : (side + 1) * half] = dot(
                mixed, weights[side, pl.ds(half, q_cols), :]
            ).astype(BF16)
        parts[k, :, model:] = dot(mixed, o_first[...]).astype(BF16)

        @pl.when(k < tp_count - 1)
        def _():
            part_copy(k).start()

    summed = parts[tp_count - 1].astype(F32)
    for k in range(tp_count - 1):
        part_copy(k).wait_recv()
        summed += parts_in[k].astype(F32)
    low = summed[:, model:].astype(BF16)
    low_out[...] = low
    middle = inputs + RESIDUAL_SCALE * (summed[:, :model] + dot(low, o_second[...]))
    middle_out[...] = middle
    rows_own[...] = rms_scale(middle, gain_two[...]).astype(BF16)

    own_rows = pltpu.make_async_copy(rows_own, rows_all.at[ctx], local_sem.at[2])
    own_rows.start()
    to_partner = remote(
        rows_own, rows_all.at[ctx], rows_sem.at[0, 0], rows_sem.at[1, 0], {"ctx": partner}
    )
    to_partner.start()

    def rows_copy(k):
        return remote(
            rows_own, rows_all.at[ctx], rows_sem.at[0, k], rows_sem.at[1, k],
            {"ctx": ring(ctx, 2 * k, ctx_count)},
        )

    def pass_copy(k):
        source = ring(ctx, -2 * k, ctx_count)
        return remote(
            rows_all.at[source], rows_all.at[source], pass_sem.at[0, k], pass_sem.at[1, k],
            {"ctx": partner},
        )

    for k in range(1, chips):
        rows_copy(k).start()
    for k in range(1, chips):
        rows_copy(k).wait_recv()
        pass_copy(k).start()

    for k in range(1, tp_count):
        normed_copy(k).wait_send()
    for k in range(tp_count - 1):
        part_copy(k).wait_send()
    for distance in range(1, SPAN):

        @pl.when(rank + distance < SPAN)
        def _(distance=distance):
            remote(
                kv_out.at[0], kv_out.at[distance], kv_sem.at[0, distance - 1],
                kv_sem.at[1, distance - 1], {"ctx": ring(ctx, distance, ctx_count)},
            ).wait_send()

    for k in range(1, ctx_count):
        for copy in side_copies(k):
            copy.wait()
    for copy in own_copies:
        copy.wait()
    own_rows.wait()
    to_partner.wait()
    for k in range(1, chips):
        rows_copy(k).wait_send()
        pass_copy(k).wait()
    for copy in far_copies:
        copy.wait()


def forward(
    tokens, gains, shard, first, second, o_first, o_second, cos, sin, codes, weights, grads,
    routes, tp_count, ctx_count,
):
    block, model = tokens.shape
    rows = tp_count * block
    heads = o_first.shape[0] // HEAD
    cols = second.shape[1]
    kv_cols = cols - heads * HEAD
    pairs = kv_cols // (2 * HEAD)
    tall = heads // pairs * block
    chips = ctx_count // 2
    vmem = pl.BlockSpec(memory_space=pltpu.VMEM)
    hbm = pl.BlockSpec(memory_space=pl.ANY)
    dma = pltpu.SemaphoreType.DMA
    part = (block, model + LANES)
    return pl.pallas_call(
        functools.partial(forward_kernel, tp_count=tp_count, ctx_count=ctx_count),
        in_specs=[vmem] * 11 + [hbm] * 5,
        out_specs=[vmem] * 7 + [hbm] * 6,
        out_shape=[
            jax.ShapeDtypeStruct((rows, heads * HEAD), BF16),
            jax.ShapeDtypeStruct((heads, rows, LANES), BF16),
            jax.ShapeDtypeStruct((SPAN, tp_count, block, kv_cols), BF16),
            jax.ShapeDtypeStruct((rows, LANES), BF16),
            jax.ShapeDtypeStruct((block, model), F32),
            jax.ShapeDtypeStruct((block, LANES), BF16),
            jax.ShapeDtypeStruct((2,) + shard.shape, BF16),
            *[jax.ShapeDtypeStruct(w.shape, BF16) for w in weights],
            jax.ShapeDtypeStruct((ctx_count,) + grads.shape, BF16),
            jax.ShapeDtypeStruct((ctx_count,) + routes.shape, jnp.int32),
            jax.ShapeDtypeStruct((ctx_count, block, model), BF16),
        ],
        scratch_shapes=[
            pltpu.VMEM((tp_count, block, model), BF16),
            pltpu.VMEM((2,) + shard.shape, BF16),
            pltpu.VMEM((heads, rows, LANES), BF16),
            pltpu.VMEM((pairs, SPAN * rows, LANES), BF16),
            pltpu.VMEM((pairs, SPAN * rows, LANES), BF16),
            pltpu.VMEM((tp_count * pairs, tall, LANES), F32),
            pltpu.VMEM((tp_count * pairs, tall, LANES), F32),
            pltpu.VMEM((tp_count,) + part, BF16),
            pltpu.VMEM((tp_count - 1,) + part, BF16),
            pltpu.VMEM((block, model), BF16),
            dma((2,)),
            dma((2, tp_count - 1)),
            dma((2, SPAN - 1)),
            dma((2, tp_count - 1)),
            dma((2, 3)),
            dma((2, ctx_count)),
            dma((2, ctx_count)),
            dma((2, chips)),
            dma((2, chips)),
            dma((3,)),
        ],
        compiler_params=pltpu.CompilerParams(
            vmem_limit_bytes=VMEM_LIMIT, collective_id=0, has_side_effects=True
        ),
        cost_estimate=pl.CostEstimate(
            flops=16 * SPAN * rows * rows * heads * LANES,
            bytes_accessed=32 * 1024 * 1024,
            transcendentals=0,
        ),
        name="forward",
    )(
        tokens, *gains, shard, first, second, o_first, o_second, cos, sin, codes, *weights,
        grads, routes,
    )


def build_tables(rank, kv_refs, k_aug, v_aug):
    pairs = k_aug.shape[0]
    for distance, kv in enumerate(kv_refs):

        @pl.when(distance <= rank)
        def _(distance=distance, kv=kv):
            values = kv[...]
            for pair in range(pairs):
                aug_keys(
                    values, pair, pairs, (rank - distance) * SEGS_DEV, k_aug, v_aug,
                    distance * values.shape[0],
                )


def retrace_kernel(
    rank_ref, q_ref, kv_ref, att, branch, w_out, out_in, out_out, cos, sin,
    dq_out, own_out, far_out, in_grad,
    k_aug, v_aug, dk, dv, dq,
):
    step = pl.program_id(0)
    rank = rank_ref[0]
    heads, block, _ = q_ref.shape
    pairs = k_aug.shape[0]
    group = heads // pairs
    rows = kv_ref.shape[1]
    tall = group * block
    width = heads * HEAD

    @pl.when(step == 0)
    def _():
        build_tables(rank, [kv_ref.at[d] for d in range(SPAN)], k_aug, v_aug)
        dk[...] = jnp.zeros(dk.shape, F32)
        dv[...] = jnp.zeros(dv.shape, F32)
        in_grad[...] = jnp.zeros(in_grad.shape, F32)

    half = w_out.shape[2]
    low_grad = dot_nt(branch[...], out_out[...]).astype(BF16)
    grads = (
        dot_nt(branch[:, :half], w_out[0])
        + dot_nt(branch[:, half:], w_out[1])
        + dot_nt(low_grad, out_in[...])
    ).astype(BF16)
    mixed = att[...]
    in_grad[...] += dot_tn(mixed, low_grad)
    product = grads.astype(F32) * mixed.astype(F32)
    wide = heads * LANES
    r, c = iota((width, wide), 0), iota((width, wide), 1)
    same = r // HEAD == c // LANES
    place = (same & (r % HEAD == c % LANES)).astype(BF16)
    spread = (same & (c % LANES >= ONES) & (c % LANES < ONES + 2)).astype(F32)
    minus = -lax.dot_general(
        product, spread, (((1,), (0,)), ((), ())),
        precision=lax.Precision.HIGHEST, preferred_element_type=F32,
    )
    high = minus.astype(BF16).astype(F32)
    lane = iota(minus.shape, 1) % LANES
    coded = dot(grads, place) + jnp.where(
        lane == ONES, high, jnp.where(lane == ONES + 1, minus - high, 0.0)
    )
    coded = coded.astype(BF16)

    pieces = []
    for pair in range(pairs):
        queries = q_ref[pl.ds(pair * group, group)].reshape(tall, LANES)
        upstream = jnp.concatenate(
            [
                coded[:, (pair * group + member) * LANES : (pair * group + member + 1) * LANES]
                for member in range(group)
            ],
            axis=0,
        )
        dq[...] = jnp.zeros(dq.shape, F32)

        def tile(start, size, causal, queries=queries, upstream=upstream, pair=pair):
            span = pl.ds(start, size)
            keys = k_aug[pair, span, :]
            probs = jnp.exp(dot_nt(keys, queries))
            if causal:
                q_row = iota(probs.shape, 1) % block
                probs = jnp.where(iota(probs.shape, 0) <= q_row, probs, 0.0)
            slopes = (probs * dot_nt(v_aug[pair, span, :], upstream)).astype(BF16)
            dv[pair, span, :] += dot(probs.astype(BF16), upstream)
            dk[pair, span, :] += dot(slopes, queries)
            dq[...] += dot_tn(slopes, keys)

        tile(pl.multiple_of(step * block, block), block, True)

        @pl.loop(0, step)
        def _(j, tile=tile):
            tile(pl.multiple_of(j * block, block), block, False)

        for distance in range(1, SPAN):

            @pl.when(distance <= rank)
            def _(distance=distance, tile=tile):
                for part in range(0, rows, rows // 2):
                    tile(distance * rows + part, rows // 2, False)

        for member in range(group):
            pieces.append(dq[member * block : (member + 1) * block, :HEAD] * SCORE_SCALE)

    for pair in range(pairs):
        turned = jnp.concatenate(pieces[pair * group : (pair + 1) * group], axis=1)
        turned = turned * cos[...] - swap_halves(turned) * sin[...]
        dq_out[:, pl.ds(pair * group * HEAD, group * HEAD)] = turned.astype(BF16)

    @pl.when(step == pl.num_programs(0) - 1)
    def _():
        for distance in range(SPAN):
            span = pl.ds(distance * rows, rows)
            joined = jnp.concatenate(
                [dk[pair, span, :HEAD] for pair in range(pairs)]
                + [dv[pair, span, :HEAD] for pair in range(pairs)],
                axis=1,
            )
            if distance == 0:
                own_out[...] = joined
            else:
                far_out[distance - 1] = joined.astype(BF16)


def retrace(rank, queries, kv_parts, att, branch, w_out, out_in, out_out, cos, sin):
    heads, rows, _ = queries.shape
    block = 256
    kv_width = kv_parts.shape[2]
    pairs = kv_width // (2 * HEAD)
    tall = heads // pairs * block
    width = heads * HEAD
    whole = lambda i, r: (0, 0)
    row = lambda i, r: (i, 0)
    return pl.pallas_call(
        retrace_kernel,
        grid_spec=pltpu.PrefetchScalarGridSpec(
            num_scalar_prefetch=1,
            grid=(rows // block,),
            in_specs=[pl.BlockSpec((heads, block, LANES), lambda i, r: (0, i, 0))]
            + [
                pl.BlockSpec(kv_parts.shape, lambda i, r: (0, 0, 0)),
                pl.BlockSpec((block, width), row),
                pl.BlockSpec((block, branch.shape[1]), row),
                pl.BlockSpec(w_out.shape, lambda i, r: (0, 0, 0)),
                pl.BlockSpec(out_in.shape, whole),
                pl.BlockSpec(out_out.shape, whole),
                pl.BlockSpec((block, LANES), row),
                pl.BlockSpec((block, LANES), row),
            ],
            out_specs=[
                pl.BlockSpec((block, width), row),
                pl.BlockSpec((rows, kv_width), whole),
                pl.BlockSpec((SPAN - 1, rows, kv_width), lambda i, r: (0, 0, 0)),
                pl.BlockSpec((width, LANES), whole),
            ],
            scratch_shapes=[
                pltpu.VMEM((pairs, SPAN * rows, LANES), BF16),
                pltpu.VMEM((pairs, SPAN * rows, LANES), BF16),
                pltpu.VMEM((pairs, SPAN * rows, LANES), F32),
                pltpu.VMEM((pairs, SPAN * rows, LANES), F32),
                pltpu.VMEM((tall, LANES), F32),
            ],
        ),
        out_shape=[
            jax.ShapeDtypeStruct((rows, width), BF16),
            jax.ShapeDtypeStruct((rows, kv_width), F32),
            jax.ShapeDtypeStruct((SPAN - 1, rows, kv_width), BF16),
            jax.ShapeDtypeStruct((width, LANES), F32),
        ],
        compiler_params=pltpu.CompilerParams(vmem_limit_bytes=VMEM_LIMIT),
        name="retrace",
        cost_estimate=pl.CostEstimate(
            flops=16 * SPAN * rows * rows * heads * LANES,
            bytes_accessed=8 * 1024 * 1024,
            transcendentals=0,
        ),
    )(rank, queries, kv_parts, att, branch, w_out, out_in, out_out, cos, sin)


def unproject_kernel(
    dq, own, far1, far2, far3, lora, weights, second, cos, sin, part_out, grad_out
):
    step = pl.program_id(0)
    total = own[...] + far1[...].astype(F32) + far2[...].astype(F32) + far3[...].astype(F32)
    split = total.shape[1] // 2
    keys = total[:, :split]
    keys = keys * cos[...] - swap_halves(keys) * sin[...]
    grads = jnp.concatenate(
        [dq[...], keys.astype(BF16), total[:, split:].astype(BF16)], axis=1
    )
    half = weights.shape[1]
    part_out[:, :half] = dot_nt(grads, weights[0]).astype(BF16)
    part_out[:, half : 2 * half] = dot_nt(grads, weights[1]).astype(BF16)
    part_out[:, 2 * half :] = dot_nt(grads, second[...]).astype(BF16)

    @pl.when(step == 0)
    def _():
        grad_out[...] = jnp.zeros(grad_out.shape, F32)

    grad_out[...] += dot_tn(lora[...], grads)


def unproject(dq, own, fars, lora, weights, second, cos, sin):
    rows, width = dq.shape
    kv_width = own.shape[1]
    block = 256
    cols = weights.shape[2]
    model = 2 * weights.shape[1]
    row = lambda i: (i, 0)
    return pl.pallas_call(
        unproject_kernel,
        grid=(rows // block,),
        in_specs=[pl.BlockSpec((block, width), row)]
        + [pl.BlockSpec((block, kv_width), row)] * SPAN
        + [
            pl.BlockSpec((block, LANES), row),
            pl.BlockSpec((2, model // 2, cols), lambda i: (0, 0, 0)),
            pl.BlockSpec((LANES, cols), lambda i: (0, 0)),
            pl.BlockSpec((block, LANES), row),
            pl.BlockSpec((block, LANES), row),
        ],
        out_specs=[
            pl.BlockSpec((block, model + LANES), row),
            pl.BlockSpec((LANES, cols), lambda i: (0, 0)),
        ],
        out_shape=[
            jax.ShapeDtypeStruct((rows, model + LANES), BF16),
            jax.ShapeDtypeStruct((LANES, cols), F32),
        ],
        compiler_params=pltpu.CompilerParams(vmem_limit_bytes=VMEM_LIMIT),
        name="unproject",
        cost_estimate=pl.CostEstimate(
            flops=2 * rows * model * (cols + 2 * LANES),
            bytes_accessed=8 * 1024 * 1024,
            transcendentals=0,
        ),
    )(dq, own, *fars, lora, weights, second, cos, sin)


def expert_kernel(
    sets, base, x_ref, g_ref, routes, router,
    w_gate, w_up, w_down, w_gate_far, w_up_far, w_down_far, gate_in, up_in, gate_out, up_out, down_in, down_out,
    mixed_out, grad_out,
    rank_rows, gate_rows, slope_rows, mix, back, xs, firsts, tall_grad,
    gate_full, up_full, down_full,
    *, slots, sources,
):
    chunk, expert = pl.program_id(0), pl.program_id(1)
    experts = router.shape[0]
    tokens, model = x_ref.shape
    each = tokens // sources
    hidden = w_gate.shape[2]
    lanes = gate_in.shape[2]
    chosen = sets[chunk]

    @pl.when(expert == 0)
    def _():
        logits = dot_nt(router[...], x_ref[...])
        number = iota((experts, tokens), 0)
        hit = jnp.zeros((experts, tokens), F32)
        for k in range(routes.shape[0]):
            hit += (routes[k : k + 1, :] == number).astype(F32)
        kept = jnp.where(hit > 0.5, logits, MASKED)
        weights = jnp.exp(kept - jnp.max(kept, axis=0, keepdims=True)) * hit
        gate_rows[...] = weights / jnp.sum(weights, axis=0, keepdims=True)
        earlier = (iota((each, each), 0) < iota((each, each), 1)).astype(BF16)
        for s in range(sources):
            span = slice(s * each, (s + 1) * each)
            order = dot(hit[:, span].astype(BF16), earlier)
            rank_rows[:, span] = jnp.where(hit[:, span] > 0.5, order, -1.0)
        mix[...] = jnp.zeros(mix.shape, F32)
        back[...] = jnp.zeros(back.shape, F32)
        slope_rows[...] = jnp.zeros(slope_rows.shape, F32)

    row = base[0] + expert
    ranks = rank_rows[pl.ds(row, 1), :]
    gates = gate_rows[pl.ds(row, 1), :]
    slot_number = iota((slots, each), 0).astype(F32)
    picks, columns, upstreams = [], [], []
    for s in range(sources):
        span = slice(s * each, (s + 1) * each)
        pick = ranks[:, span] == slot_number
        columns.append(jnp.sum(jnp.where(pick, gates[:, span], 0.0), axis=1, keepdims=True))
        pick = pick.astype(BF16)
        picks.append(pick)
        xs[pl.ds(s * slots, slots), :] = dot(pick, x_ref[pl.ds(s * each, each), :]).astype(BF16)
        upstreams.append(dot(pick, g_ref[pl.ds(s * each, each), :]))
    gate_column = jnp.concatenate(columns, axis=0)
    upstream = RESIDUAL_SCALE * jnp.concatenate(upstreams, axis=0)

    firsts[:, :lanes] = gate_in[0]
    firsts[:, lanes:] = up_in[0]
    keep = (iota((1, 2 * lanes), 1) % lanes // RANK == chosen).astype(BF16)
    rows = xs[...]
    inner = dot(rows, firsts[...]).astype(BF16) * keep
    for full, near, far in (
        (gate_full, w_gate, w_gate_far),
        (up_full, w_up, w_up_far),
        (down_full, w_down, w_down_far),
    ):
        size = near.shape[1]
        full[pl.ds(pl.multiple_of(base[1] * size, size), size), :] = near[0]
        full[pl.ds(pl.multiple_of((1 - base[1]) * size, size), size), :] = far[0]
    gate_value = dot(rows, gate_full[...]) + dot(inner[:, :lanes], gate_out[0])
    up_value = dot(rows, up_full[...]) + dot(inner[:, lanes:], up_out[0])
    sigmoid = 1.0 / (1.0 + jnp.exp(-gate_value))
    silu = gate_value * sigmoid
    active = (silu * up_value).astype(BF16)
    down_inner = dot(active, down_in[0]).astype(BF16) * keep[:, :lanes]
    produced = (
        (dot(active, down_full[...]) + dot(down_inner, down_out[0])).astype(BF16).astype(F32)
    )
    slope = jnp.sum(upstream * produced, axis=1, keepdims=True)
    sent = (gate_column * produced).astype(BF16)
    slot_grad = (gate_column * upstream).astype(BF16)

    down_inner_grad = dot_nt(slot_grad, down_out[0]).astype(BF16) * keep[:, :lanes]
    active_grad = (
        (dot_nt(slot_grad, down_full[...]) + dot_nt(down_inner_grad, down_in[0]))
        .astype(BF16)
        .astype(F32)
    )
    gate_grad = (active_grad * up_value * (sigmoid + silu * (1.0 - sigmoid))).astype(BF16)
    up_grad = (active_grad * silu).astype(BF16)
    inner_grad = (
        jnp.concatenate([dot_nt(gate_grad, gate_out[0]), dot_nt(up_grad, up_out[0])], axis=1)
    ).astype(BF16) * keep
    row_grad = (
        dot_nt(gate_grad, gate_full[...])
        + dot_nt(up_grad, up_full[...])
        + dot_nt(inner_grad, firsts[...])
    ).astype(BF16)

    for s in range(sources):
        span = slice(s * slots, (s + 1) * slots)
        spot = pl.ds(s * each, each)
        mix[spot, :] += dot_tn(picks[s], sent[span, :])
        back[spot, :] += dot_tn(picks[s], row_grad[span, :])
        slope_rows[pl.ds(expert, 1), spot] = jnp.sum(
            jnp.where(picks[s] > 0.5, slope[span, :], 0.0), axis=0, keepdims=True
        )

    own = pl.multiple_of(chosen * RANK, RANK)
    tall_grad[...] = dot_tn(inner_grad, rows)
    grad_out[0, 0, pl.ds(0, RANK), :] = tall_grad[pl.ds(own, RANK), :].astype(BF16)
    grad_out[0, 0, pl.ds(RANK, RANK), :] = tall_grad[pl.ds(lanes + own, RANK), :].astype(BF16)
    tall_grad[pl.ds(0, lanes), :hidden] = dot_tn(inner[:, :lanes], gate_grad)
    tall_grad[pl.ds(0, lanes), hidden:] = dot_tn(inner[:, lanes:], up_grad)
    grad_out[0, 0, pl.ds(2 * RANK, RANK), :] = tall_grad[pl.ds(own, RANK), :].astype(BF16)
    tall_grad[pl.ds(0, lanes), :] = dot_tn(down_inner, slot_grad)
    grad_out[0, 0, pl.ds(3 * RANK, RANK), :] = tall_grad[pl.ds(own, RANK), :].astype(BF16)
    tall_grad[pl.ds(0, lanes), :hidden] = dot_tn(down_inner_grad, active)
    tall_grad[pl.ds(0, lanes), hidden:] = jnp.zeros((lanes, model - hidden), F32)
    grad_out[0, 0, pl.ds(4 * RANK, RANK), :] = tall_grad[pl.ds(own, RANK), :].astype(BF16)

    @pl.when(expert == pl.num_programs(1) - 1)
    def _():
        mixed_out[:, :model] = mix[...].astype(BF16)
        mixed_out[:, model : 2 * model] = back[...].astype(BF16)
        turned = slope_rows[...].T
        high = turned.astype(BF16)
        low = (turned - high.astype(F32)).astype(BF16)
        local, lane = iota((LANES, LANES), 0), iota((LANES, LANES), 1)
        inside = local < pl.num_programs(1)
        first = (inside & (lane == local + base[0])).astype(BF16)
        later = (inside & (lane == local + base[0] + experts)).astype(BF16)
        mixed_out[:, 2 * model :] = (dot(high, first) + dot(low, later)).astype(BF16)


def run_experts(
    sets, base, rows, upstream, routes, router, weights, adapters, slots, sources
):
    total, model = rows.shape
    experts = router.shape[0]
    local, half, hidden = weights[0].shape
    trees = sets.shape[0]
    tokens = total // trees
    lanes = adapters[0].shape[2]
    cols = 2 * model + LANES
    tall = sources * slots
    piece = lambda c, e, *_: (c, 0)
    fixed = lambda c, e, *_: (0, 0)
    expert = lambda c, e, *_: (e, 0, 0)
    return pl.pallas_call(
        functools.partial(expert_kernel, slots=slots, sources=sources),
        grid_spec=pltpu.PrefetchScalarGridSpec(
            num_scalar_prefetch=2,
            grid=(trees, local),
            in_specs=[
                pl.BlockSpec((tokens, model), piece),
                pl.BlockSpec((tokens, model), piece),
                pl.BlockSpec((routes.shape[0], tokens), lambda c, e, *_: (0, c)),
                pl.BlockSpec(router.shape, fixed),
                *[pl.BlockSpec((1,) + a.shape[1:], expert) for a in (*weights, *adapters)],
            ],
            out_specs=[
                pl.BlockSpec((tokens, cols), piece),
                pl.BlockSpec((1, 1, 5 * RANK, model), lambda c, e, *_: (c, e, 0, 0)),
            ],
            scratch_shapes=[
                pltpu.VMEM((experts, tokens), F32),
                pltpu.VMEM((experts, tokens), F32),
                pltpu.VMEM((LANES, tokens), F32),
                pltpu.VMEM((tokens, model), F32),
                pltpu.VMEM((tokens, model), F32),
                pltpu.VMEM((tall, model), BF16),
                pltpu.VMEM((model, 2 * lanes), BF16),
                pltpu.VMEM((2 * lanes, model), F32),
                pltpu.VMEM((2 * half, hidden), BF16),
                pltpu.VMEM((2 * half, hidden), BF16),
                pltpu.VMEM((hidden, model), BF16),
            ],
        ),
        out_shape=[
            jax.ShapeDtypeStruct((total, cols), BF16),
            jax.ShapeDtypeStruct((trees, local, 5 * RANK, model), BF16),
        ],
        compiler_params=pltpu.CompilerParams(vmem_limit_bytes=60 * 1024 * 1024),
        name="experts",
        cost_estimate=pl.CostEstimate(
            flops=2 * local * total * model * model * 2,
            bytes_accessed=8 * 1024 * 1024,
            transcendentals=0,
        ),
    )(sets, base, rows, upstream, routes, router, *weights, *adapters)


def take_set(table, chosen, axis):
    return lax.dynamic_slice_in_dim(table, chosen * RANK, RANK, axis)


def per_device(
    tokens,
    out_grad,
    routes,
    parents,
    adapter_set,
    gain_a,
    gain_b,
    w_query,
    key_projection_matrix,
    value_projection_matrix,
    w_output,
    w_router,
    w_gate,
    w_up,
    w_down,
    query_in,
    query_out,
    key_in,
    key_second_factor,
    value_in,
    value_second_factor,
    out_in,
    out_out,
    gate_in,
    gate_out,
    up_in,
    up_out,
    down_in,
    down_out,
):
    tp_rank = lax.axis_index("tp")
    ctx_rank = lax.axis_index("ctx")
    fsdp_rank = lax.axis_index("fsdp")
    ctx_count = lax.axis_size("ctx")
    tp_count = lax.axis_size("tp")
    fsdp_count = lax.axis_size("fsdp")
    tok_rows, model = tokens.shape
    q_cols = w_query.shape[1]
    kv_cols = key_projection_matrix.shape[1]
    heads, pairs = q_cols // HEAD, kv_cols // HEAD
    experts = w_router.shape[1]
    local_experts = w_gate.shape[0]
    sets = query_in.shape[1] // RANK
    slots = tok_rows * TOP * 3 // (2 * experts)
    trees = ctx_count // SPAN

    attention_shard = jnp.concatenate(
        [
            jnp.concatenate([w_query, key_projection_matrix, value_projection_matrix], axis=1),
            w_output,
        ],
        axis=0,
    )

    seg_start = (fsdp_rank * ctx_count + ctx_rank) * SEGS_DEV
    tree_index = seg_start // TREE_SEGS
    local_start = seg_start % TREE_SEGS
    rank = (local_start // SEGS_DEV).astype(jnp.int32).reshape(1)
    tree_parents = lax.dynamic_slice_in_dim(parents, tree_index * TREE_SEGS, TREE_SEGS, 0)
    reach, depth = tree_links(tree_parents)
    chosen = lax.dynamic_slice_in_dim(adapter_set, tree_index, 1, 0)[0]

    inputs = tokens.astype(F32)
    gain_one = gain_a.astype(F32)
    gain_two = gain_b.astype(F32)
    normed = rms_scale(inputs, gain_one).astype(BF16)

    own_reach = lax.dynamic_slice_in_dim(reach, local_start, SEGS_DEV, 0)
    codes = jnp.pad(
        jnp.where(own_reach > 0.5, 0.0, MASKED), ((0, 0), (CODE, LANES - CODE - TREE_SEGS))
    )
    codes = jnp.repeat(codes.astype(BF16), SEG, axis=0)
    own_depth = lax.dynamic_slice_in_dim(depth, local_start, SEGS_DEV, 0)
    positions = (
        own_depth[:, None] * SEG + jnp.arange(SEG, dtype=jnp.int32).astype(F32)[None, :]
    ).reshape(-1)
    half_head = HEAD // 2
    freqs = ROPE_BASE ** (-(jnp.arange(half_head, dtype=jnp.int32).astype(F32) * 2.0) / HEAD)
    angles = positions[:, None] * jnp.tile(freqs, LANES // half_head)[None, :]
    cos, sin = jnp.cos(angles), jnp.sin(angles)

    first = jnp.pad(
        jnp.concatenate(
            [take_set(t, chosen, 1) for t in (query_in, key_in, value_in)], axis=1
        ),
        ((0, 0), (0, LANES - 3 * RANK)),
    )
    q_second = lax.dynamic_slice(query_out, (chosen * RANK, tp_rank * q_cols), (RANK, q_cols))
    k_second = lax.dynamic_slice(
        key_second_factor, (chosen * RANK, tp_rank * kv_cols), (RANK, kv_cols)
    )
    v_second = lax.dynamic_slice(
        value_second_factor, (chosen * RANK, tp_rank * kv_cols), (RANK, kv_cols)
    )
    second = jnp.concatenate(
        [
            jnp.pad(q_second, ((0, 0), (0, 2 * kv_cols))),
            jnp.pad(k_second, ((0, 0), (q_cols, kv_cols))),
            jnp.pad(v_second, ((0, 0), (q_cols + kv_cols, 0))),
            jnp.zeros((LANES - 3 * RANK, q_cols + 2 * kv_cols), BF16),
        ],
        axis=0,
    )
    o_first = jnp.pad(
        lax.dynamic_slice(out_in, (tp_rank * q_cols, chosen * RANK), (q_cols, RANK)),
        ((0, 0), (0, LANES - RANK)),
    )
    o_second = jnp.pad(take_set(out_out, chosen, 0), ((0, LANES - RANK), (0, 0)))

    (
        attended, queries, kv_parts, lora, middle, o_reduced, attention_weights,
        *far_weights, upstream_all, routes_all, rows_all,
    ) = forward(
        tokens, (gain_one[None], gain_two[None]), attention_shard, first, second,
        o_first, o_second, cos, sin, codes, (w_gate, w_up, w_down), out_grad, routes.T,
        tp_count, ctx_count,
    )
    kv_parts = kv_parts.reshape(SPAN, -1, kv_parts.shape[-1])
    project_weights = attention_weights[:, : w_query.shape[0]]
    output_weights = attention_weights[:, w_query.shape[0] :]
    upstream_all = upstream_all.reshape(-1, model)
    rows_all = rows_all.reshape(-1, model)
    routes_all = routes_all.transpose(1, 0, 2).reshape(TOP, -1)
    normed_two = rms_scale(middle, gain_two).astype(BF16)

    tree_sets = lax.dynamic_slice_in_dim(adapter_set, fsdp_rank * trees, trees, 0)
    base = jnp.stack([ctx_rank * local_experts, fsdp_rank]).astype(jnp.int32)
    mixed, expert_part = run_experts(
        tree_sets,
        base,
        rows_all,
        upstream_all,
        routes_all,
        w_router.T,
        (w_gate, w_up, w_down, *far_weights),
        (gate_in, up_in, gate_out, up_out, down_in, down_out),
        slots,
        SPAN,
    )
    combined = lax.psum_scatter(mixed, "ctx", scatter_dimension=0, tiled=True).astype(F32)
    mixture = combined[:, :model]
    output = (middle + RESIDUAL_SCALE * mixture).astype(BF16)

    logits = jnp.dot(normed_two, w_router, preferred_element_type=F32)
    hits = jnp.sum(
        (routes[:, :, None] == jnp.arange(experts, dtype=jnp.int32)[None, None, :]).astype(F32),
        axis=1,
    )
    kept = jnp.where(hits > 0.5, logits, MASKED)
    gates = jnp.exp(kept - jnp.max(kept, axis=1, keepdims=True)) * hits
    gates = gates / jnp.sum(gates, axis=1, keepdims=True)
    slopes = (
        combined[:, 2 * model : 2 * model + experts]
        + combined[:, 2 * model + experts : 2 * model + 2 * experts]
    )
    logits_grad = gates * (slopes - jnp.sum(gates * slopes, axis=1, keepdims=True))
    normed_two_grad = combined[:, model : 2 * model] + jnp.einsum(
        "te,de->td", logits_grad, w_router.astype(F32), precision=lax.Precision.HIGHEST
    )
    upstream = out_grad.astype(F32)
    middle_grad = upstream + rms_back(middle, gain_two, normed_two_grad)
    branch_grad = (RESIDUAL_SCALE * middle_grad).astype(BF16)
    out_out_part = jnp.einsum(
        "ts,td->sd", o_reduced, branch_grad, preferred_element_type=F32
    )[:RANK]
    branch_all = lax.all_gather(branch_grad, "tp", axis=0, tiled=True)
    dq, own_grad, far_grad, out_in_part = retrace(
        rank, queries, kv_parts, attended, branch_all, output_weights, o_first, o_second, cos, sin
    )
    fars = [shifted(far_grad[d - 1], "ctx", -d) for d in range(1, SPAN)]
    part, second_part = unproject(
        dq, own_grad, fars, lora, project_weights, second, cos, sin
    )
    summed = lax.psum_scatter(part, "tp", scatter_dimension=0, tiled=True)
    reduced_grad = summed[:, model:]
    normed_grad = summed[:, :model].astype(F32) + jnp.einsum(
        "ts,ds->td", reduced_grad, first, preferred_element_type=F32
    )
    first_part = jnp.einsum(
        "ts,td->sd", reduced_grad, normed, preferred_element_type=F32
    )[: 3 * RANK]
    input_grad = (middle_grad + rms_back(inputs, gain_one, normed_grad)).astype(BF16)

    full_q = q_cols * tp_count
    full_kv = kv_cols * tp_count

    def widen(part, cols, axis, start):
        shape = list(part.shape)
        shape[axis] = cols
        return lax.dynamic_update_slice_in_dim(jnp.zeros(shape, F32), part, start, axis)

    packed = jnp.concatenate(
        [
            first_part,
            widen(out_in_part[:, :RANK].T, full_q, 1, tp_rank * q_cols),
            out_out_part,
            widen(second_part[:RANK, :q_cols], full_q, 1, tp_rank * q_cols),
            jnp.concatenate(
                [
                    widen(
                        second_part[RANK : 2 * RANK, q_cols : q_cols + kv_cols],
                        full_kv, 1, tp_rank * kv_cols,
                    ),
                    widen(
                        second_part[2 * RANK : 3 * RANK, q_cols + kv_cols :],
                        full_kv, 1, tp_rank * kv_cols,
                    ),
                ],
                axis=1,
            ),
        ],
        axis=0,
    )
    all_trees = fsdp_count * trees
    if trees > 1:
        packed = lax.psum(
            jnp.where(
                (jnp.arange(all_trees) == tree_index)[:, None, None], packed[None], 0.0
            ),
            ("fsdp", "ctx", "tp"),
        )
    else:
        packed = lax.all_gather(lax.psum(packed, ("ctx", "tp")), "fsdp")
    place = (
        adapter_set[:, None] == jnp.arange(sets, dtype=jnp.int32)[None, :]
    ).astype(F32)

    def in_rows(part):
        spread = jnp.einsum("ts,trd->srd", place, part, precision=lax.Precision.HIGHEST)
        return spread.reshape(sets * RANK, part.shape[2])

    def in_columns(part):
        return in_rows(part).T

    adapter_totals = (
        in_columns(packed[:, :RANK]),
        in_rows(packed[:, 5 * RANK : 6 * RANK]),
        in_columns(packed[:, RANK : 2 * RANK]),
        in_rows(packed[:, 6 * RANK :, :full_kv]),
        in_columns(packed[:, 2 * RANK : 3 * RANK]),
        in_rows(packed[:, 6 * RANK :, full_kv:]),
        in_columns(packed[:, 3 * RANK : 4 * RANK]),
        in_rows(packed[:, 4 * RANK : 5 * RANK]),
    )

    expert_part = lax.all_gather(lax.psum(expert_part, "tp"), "fsdp")
    expert_part = expert_part.reshape(all_trees, local_experts, 5 * RANK, model)
    hidden = w_gate.shape[2]

    def expert_rows(part):
        spread = jnp.einsum(
            "ts,terd->esrd", place.astype(BF16), part, preferred_element_type=F32
        )
        return spread.reshape(local_experts, sets * RANK, part.shape[3])

    def expert_columns(part):
        return expert_rows(part).transpose(0, 2, 1)

    return (
        output,
        input_grad,
        *adapter_totals,
        expert_columns(expert_part[:, :, :RANK]),
        expert_rows(expert_part[:, :, 2 * RANK : 3 * RANK, :hidden]),
        expert_columns(expert_part[:, :, RANK : 2 * RANK]),
        expert_rows(expert_part[:, :, 2 * RANK : 3 * RANK, hidden:]),
        expert_columns(expert_part[:, :, 4 * RANK :, :hidden]),
        expert_rows(expert_part[:, :, 3 * RANK : 4 * RANK]),
    )


def solution(mesh):
    in_specs = (
        P(("fsdp", "ctx", "tp"), None),
        P(("fsdp", "ctx", "tp"), None),
        P(("fsdp", "ctx", "tp"), None),
        P(),
        P(),
        P(),
        P(),
        P("fsdp", "tp"),
        P("fsdp", "tp"),
        P("fsdp", "tp"),
        P("tp", "fsdp"),
        P(),
        P("ctx", "fsdp", None),
        P("ctx", "fsdp", None),
        P("ctx", "fsdp", None),
        P(),
        P(),
        P(),
        P(),
        P(),
        P(),
        P(),
        P(),
        P("ctx", None, None),
        P("ctx", None, None),
        P("ctx", None, None),
        P("ctx", None, None),
        P("ctx", None, None),
        P("ctx", None, None),
    )
    out_specs = (
        P(("fsdp", "ctx", "tp"), None),
        P(("fsdp", "ctx", "tp"), None),
        P(),
        P(),
        P(),
        P(),
        P(),
        P(),
        P(),
        P(),
        P("ctx", None, None),
        P("ctx", None, None),
        P("ctx", None, None),
        P("ctx", None, None),
        P("ctx", None, None),
        P("ctx", None, None),
    )
    return jax.shard_map(
        per_device, mesh=mesh, in_specs=in_specs, out_specs=out_specs, check_vma=False
    )
```

```python
import functools
import math

import jax
import jax.numpy as jnp
from jax import lax
from jax.experimental import pallas as pl
from jax.experimental.pallas import tpu as pltpu
from jax.sharding import PartitionSpec as P

HEAD = 64
TOP = 8
RANK = 16
SEG = 128
SEGS_DEV = 8
TREE_SEGS = 32
SPAN = TREE_SEGS // SEGS_DEV
LANES = 128

RESIDUAL_SCALE = 0.22
SCORE_SCALE = 0.015625
EPSILON = 1e-06
ROPE_BASE = 10000.0
MASKED = -1e30

F32 = jnp.float32
BF16 = jnp.bfloat16

CODE = HEAD
LSE = CODE + TREE_SEGS + 1
ONES = HEAD

VMEM_LIMIT = 56 * 1024 * 1024


def dot(a, b):
    return lax.dot_general(a, b, (((1,), (0,)), ((), ())), preferred_element_type=F32)


def dot_nt(a, b):
    return lax.dot_general(a, b, (((1,), (1,)), ((), ())), preferred_element_type=F32)


def dot_tn(a, b):
    return lax.dot_general(a, b, (((0,), (0,)), ((), ())), preferred_element_type=F32)


def iota(shape, dim):
    return lax.broadcasted_iota(jnp.int32, shape, dim)


def shifted(block, axis, distance):
    devices = range(lax.axis_size(axis))
    route = [(i - distance, i) for i in devices if i - distance in devices]
    return lax.ppermute(block, axis, route)


def rms_scale(values, gain_row):
    return (
        values * lax.rsqrt(jnp.mean(values * values, axis=-1, keepdims=True) + EPSILON) * gain_row
    )


def rms_back(values, gain_row, grad):
    inv = lax.rsqrt(jnp.mean(values * values, axis=-1, keepdims=True) + EPSILON)
    scaled = grad * gain_row
    inner = jnp.mean(scaled * values, axis=-1, keepdims=True)
    return inv * scaled - values * (inv * inv * inv * inner)


def tree_links(tree_parents):
    count = tree_parents.shape[0]
    columns = jnp.arange(count, dtype=jnp.int32)
    reach = (
        (tree_parents[:, None] == columns[None, :]) | (columns[:, None] == columns[None, :])
    ).astype(BF16)
    for _ in range(max(1, (count - 1).bit_length())):
        reach = jnp.minimum(dot(reach, reach), 1.0).astype(BF16)
    reach = reach.astype(F32)
    return reach, jnp.sum(reach, axis=1) - 1.0


def swap_halves(values):
    width = values.shape[-1]
    lane = iota(values.shape, 1) % HEAD
    ahead = pltpu.roll(values, width - HEAD // 2, 1)
    behind = pltpu.roll(values, HEAD // 2, 1)
    return jnp.where(lane < HEAD // 2, -ahead, behind)


def place_table(rows, source, target):
    r, c = iota((rows, LANES), 0), iota((rows, LANES), 1)
    return ((r - source == c - target) & (c >= target) & (c < target + HEAD)).astype(BF16)


def remote(src, dst, send, recv, where):
    return pltpu.make_async_remote_copy(
        src_ref=src,
        dst_ref=dst,
        send_sem=send,
        recv_sem=recv,
        device_id=where,
        device_id_type=pl.DeviceIdType.MESH,
    )


def ring(me, step, count):
    return lax.rem(me + (step + count), count)


def aug_keys(kv, pair, pairs, first_seg, k_aug, v_aug, start):
    rows, width = kv.shape
    lane = iota((rows, LANES), 1)
    seg = first_seg + iota((rows, LANES), 0) // SEG
    key_code = ((lane - CODE == seg) | ((lane >= LSE) & (lane < LSE + 3))).astype(F32)
    one_code = ((lane == ONES) | (lane == ONES + 1)).astype(F32)
    span = pl.ds(start, rows)
    k_aug[pair, span, :] = (dot(kv, place_table(width, pair * HEAD, 0)) + key_code).astype(BF16)
    v_aug[pair, span, :] = (
        dot(kv, place_table(width, (pairs + pair) * HEAD, 0)) + one_code
    ).astype(BF16)


def forward_kernel(
    tokens, gain_one, gain_two, shard, first, second, o_first, o_second, cos, sin, codes,
    w_gate, w_up, w_down, grads, routes,
    att_out, q_out, kv_out, lora_out, middle_out, low_out, weights_out, normed_all,
    gate_far, up_far, down_far, grads_all, routes_all, rows_all,
    weights, q_aug, k_aug, v_aug, top, acc, parts, parts_in, rows_own,
    shard_sem, normed_sem, kv_sem, part_sem, far_sem, grads_sem, routes_sem, rows_sem,
    pass_sem, local_sem,
    *, tp_count, ctx_count,
):
    tp, ctx, fsdp = (lax.axis_index(name) for name in ("tp", "ctx", "fsdp"))
    rank = lax.rem(ctx, SPAN)
    block, model = tokens.shape
    heads = q_aug.shape[0]
    pairs = k_aug.shape[0]
    group = heads // pairs
    tall = group * block
    half = shard.shape[1]
    q_cols = heads * HEAD
    turn = cos.shape[1]
    chips = ctx_count // 2
    partner = ctx + 1 - 2 * lax.rem(ctx, 2)
    other = {"fsdp": 1 - fsdp}

    barrier = pltpu.get_barrier_semaphore()
    pl.semaphore_signal(barrier, 1, device_id=other, device_id_type=pl.DeviceIdType.MESH)
    for k in range(1, tp_count):
        pl.semaphore_signal(
            barrier, 1, device_id={"tp": ring(tp, k, tp_count)},
            device_id_type=pl.DeviceIdType.MESH,
        )
    for k in range(1, ctx_count):
        pl.semaphore_signal(
            barrier, 1, device_id={"ctx": ring(ctx, k, ctx_count)},
            device_id_type=pl.DeviceIdType.MESH,
        )
    pl.semaphore_wait(barrier, tp_count + ctx_count - 1)

    shard_copy = remote(shard, weights.at[fsdp], shard_sem.at[0], shard_sem.at[1], other)
    shard_copy.start()

    inputs = tokens[...].astype(F32)
    normed = rms_scale(inputs, gain_one[...]).astype(BF16)
    normed_all[tp] = normed

    def normed_copy(k):
        return remote(
            normed_all.at[tp], normed_all.at[tp], normed_sem.at[0, k - 1], normed_sem.at[1, k - 1],
            {"tp": ring(tp, k, tp_count)},
        )

    for k in range(1, tp_count):
        normed_copy(k).start()

    def side_copies(k):
        where = {"ctx": ring(ctx, k, ctx_count)}
        return (
            remote(grads, grads_all.at[ctx], grads_sem.at[0, k], grads_sem.at[1, k], where),
            remote(routes, routes_all.at[ctx], routes_sem.at[0, k], routes_sem.at[1, k], where),
        )

    own_copies = (
        pltpu.make_async_copy(grads, grads_all.at[ctx], local_sem.at[0]),
        pltpu.make_async_copy(routes, routes_all.at[ctx], local_sem.at[1]),
    )
    for copy in own_copies:
        copy.start()
    for k in range(1, ctx_count):
        for copy in side_copies(k):
            copy.start()

    weights[fsdp] = shard[...]
    shard_copy.wait()
    far_copies = [
        remote(near, far, far_sem.at[0, n], far_sem.at[1, n], other)
        for n, (near, far) in enumerate(((w_gate, gate_far), (w_up, up_far), (w_down, down_far)))
    ]
    for copy in far_copies:
        copy.start()
    weights_out[...] = weights[...]

    def kv_copy(distance, part):
        return remote(
            kv_out.at[0, part], kv_out.at[distance, part],
            kv_sem.at[0, distance - 1], kv_sem.at[1, distance - 1], {"ctx": ring(ctx, distance, ctx_count)},
        )

    @pl.loop(0, tp_count)
    def _(k):
        @pl.when(k > 0)
        def _():
            normed_copy(k).wait_recv()

        part = ring(tp, -k, tp_count)
        span = pl.ds(pl.multiple_of(part * block, block), block)
        rows = normed_all[part]
        lora = dot(rows, first[...]).astype(BF16)
        lora_out[span, :] = lora
        pre = (
            dot(rows[:, :half], weights[0, pl.ds(0, half), :])
            + dot(rows[:, half:], weights[1, pl.ds(0, half), :])
            + dot(lora, second[...])
        )
        turned = []
        for start in range(0, pre.shape[1] // 4 * 3, turn):
            piece = pre[:, start : start + turn]
            turned.append(piece * cos[span, :] + swap_halves(piece) * sin[span, :])
        queries = (
            jnp.concatenate(turned[: q_cols // turn], axis=1) * SCORE_SCALE
        ).astype(BF16)
        for head in range(heads):
            q_aug[head, span, :] = (
                dot(queries, place_table(q_cols, head * HEAD, 0)) + codes[span, :].astype(F32)
            ).astype(BF16)
        keys = jnp.concatenate(turned[q_cols // turn :], axis=1)
        kv = jnp.concatenate([keys, pre[:, q_cols + keys.shape[1] :]], axis=1).astype(BF16)
        kv_out[0, part] = kv
        for distance in range(1, SPAN):

            @pl.when(rank + distance < SPAN)
            def _(distance=distance):
                kv_copy(distance, part).start()

        for pair in range(pairs):
            aug_keys(
                kv, pair, pairs, rank * SEGS_DEV + part * (block // SEG), k_aug, v_aug,
                pl.multiple_of(part * block, block),
            )

    def tile(part, pair, start, size, causal):
        index = part * pairs + pair
        rows = pl.ds(pl.multiple_of(part * block, block), block)
        queries = q_aug[pl.ds(pair * group, group), rows, :].reshape(tall, LANES)
        span = pl.ds(start, size)
        scores = dot_nt(queries, k_aug[pair, span, :])
        if causal:
            q_row = iota(scores.shape, 0) % block
            scores = jnp.where(iota(scores.shape, 1) <= q_row, scores, MASKED)
            now = jnp.broadcast_to(jnp.max(scores, axis=1, keepdims=True), (tall, LANES))
            probs = jnp.exp(scores - now[:, :1]).astype(BF16)
            acc[index] = dot(probs, v_aug[pair, span, :])
        else:
            before = top[index]
            now = jnp.maximum(before, jnp.max(scores, axis=1, keepdims=True))
            probs = jnp.exp(scores - now[:, :1]).astype(BF16)
            acc[index] = acc[index] * jnp.exp(before - now) + dot(probs, v_aug[pair, span, :])
        top[index] = now

    @pl.loop(0, tp_count * pairs)
    def _(index):
        part, pair = index // pairs, lax.rem(index, pairs)
        tile(part, pair, pl.multiple_of(part * block, block), block, True)

        @pl.loop(0, part)
        def _(j):
            tile(part, pair, pl.multiple_of(j * block, block), block, False)

    group_rows = tp_count * block
    for distance in range(1, SPAN):

        @pl.when(distance <= rank)
        def _(distance=distance):
            remote(
                kv_out.at[0], kv_out.at[distance], kv_sem.at[0, distance - 1],
                kv_sem.at[1, distance - 1], {"ctx": ring(ctx, distance, ctx_count)},
            ).wait_recv()

            @pl.loop(0, tp_count)
            def _(part):
                kv = kv_out[distance, part]
                for pair in range(pairs):
                    aug_keys(
                        kv, pair, pairs,
                        (rank - distance) * SEGS_DEV + part * (block // SEG), k_aug, v_aug,
                        pl.multiple_of(distance * group_rows + part * block, block),
                    )

        @pl.when(distance > rank)
        def _(distance=distance):
            kv_out[distance] = jnp.zeros(kv_out.shape[1:], BF16)

    def part_copy(k):
        return remote(
            parts.at[k], parts_in.at[k], part_sem.at[0, k], part_sem.at[1, k],
            {"tp": ring(tp, k + 1, tp_count)},
        )

    @pl.loop(0, tp_count)
    def _(k):
        part = ring(tp, k + 1, tp_count)
        rows = pl.ds(pl.multiple_of(part * block, block), block)
        for pair in range(pairs):
            index = part * pairs + pair

            @pl.loop(1, rank + 1)
            def _(distance, pair=pair):
                tile(
                    part, pair, pl.multiple_of(distance * group_rows, group_rows), group_rows, False
                )

            summed = acc[index]
            total = summed[:, ONES : ONES + 1]
            result = (summed / total).astype(BF16)
            for member in range(group):
                head = pair * group + member
                att_out[rows, pl.ds(head * HEAD, HEAD)] = result[
                    member * block : (member + 1) * block, :HEAD
                ]
            minus = -(top[index] + jnp.log(total))
            high = minus.astype(BF16).astype(F32)
            middle = (minus - high).astype(BF16).astype(F32)
            lane = iota(minus.shape, 1)
            queries = q_aug[pl.ds(pair * group, group), rows, :].reshape(tall, LANES)
            coded = jnp.where(
                lane == LSE,
                high,
                jnp.where(
                    lane == LSE + 1,
                    middle,
                    jnp.where(lane == LSE + 2, minus - high - middle, queries.astype(F32)),
                ),
            )
            q_out[pl.ds(pair * group, group), rows, :] = coded.astype(BF16).reshape(
                group, block, LANES
            )
        mixed = att_out[rows, :]
        for side in range(2):
            parts[k, :, side * half : (side + 1) * half] = dot(
                mixed, weights[side, pl.ds(half, q_cols), :]
            ).astype(BF16)
        parts[k, :, model:] = dot(mixed, o_first[...]).astype(BF16)

        @pl.when(k < tp_count - 1)
        def _():
            part_copy(k).start()

    summed = parts[tp_count - 1].astype(F32)
    for k in range(tp_count - 1):
        part_copy(k).wait_recv()
        summed += parts_in[k].astype(F32)
    low = summed[:, model:].astype(BF16)
    low_out[...] = low
    middle = inputs + RESIDUAL_SCALE * (summed[:, :model] + dot(low, o_second[...]))
    middle_out[...] = middle
    rows_own[...] = rms_scale(middle, gain_two[...]).astype(BF16)

    own_rows = pltpu.make_async_copy(rows_own, rows_all.at[ctx], local_sem.at[2])
    own_rows.start()
    to_partner = remote(
        rows_own, rows_all.at[ctx], rows_sem.at[0, 0], rows_sem.at[1, 0], {"ctx": partner}
    )
    to_partner.start()

    def rows_copy(k):
        return remote(
            rows_own, rows_all.at[ctx], rows_sem.at[0, k], rows_sem.at[1, k],
            {"ctx": ring(ctx, 2 * k, ctx_count)},
        )

    def pass_copy(k):
        source = ring(ctx, -2 * k, ctx_count)
        return remote(
            rows_all.at[source], rows_all.at[source], pass_sem.at[0, k], pass_sem.at[1, k],
            {"ctx": partner},
        )

    for k in range(1, chips):
        rows_copy(k).start()
    for k in range(1, chips):
        rows_copy(k).wait_recv()
        pass_copy(k).start()

    for k in range(1, tp_count):
        normed_copy(k).wait_send()
    for k in range(tp_count - 1):
        part_copy(k).wait_send()
    for distance in range(1, SPAN):

        @pl.when(rank + distance < SPAN)
        def _(distance=distance):
            remote(
                kv_out.at[0], kv_out.at[distance], kv_sem.at[0, distance - 1],
                kv_sem.at[1, distance - 1], {"ctx": ring(ctx, distance, ctx_count)},
            ).wait_send()

    for k in range(1, ctx_count):
        for copy in side_copies(k):
            copy.wait()
    for copy in own_copies:
        copy.wait()
    own_rows.wait()
    to_partner.wait()
    for k in range(1, chips):
        rows_copy(k).wait_send()
        pass_copy(k).wait()
    for copy in far_copies:
        copy.wait()


def forward(
    tokens, gains, shard, first, second, o_first, o_second, cos, sin, codes, weights, grads,
    routes, tp_count, ctx_count,
):
    block, model = tokens.shape
    rows = tp_count * block
    heads = o_first.shape[0] // HEAD
    cols = second.shape[1]
    kv_cols = cols - heads * HEAD
    pairs = kv_cols // (2 * HEAD)
    tall = heads // pairs * block
    chips = ctx_count // 2
    vmem = pl.BlockSpec(memory_space=pltpu.VMEM)
    hbm = pl.BlockSpec(memory_space=pl.ANY)
    dma = pltpu.SemaphoreType.DMA
    part = (block, model + LANES)
    return pl.pallas_call(
        functools.partial(forward_kernel, tp_count=tp_count, ctx_count=ctx_count),
        in_specs=[vmem] * 11 + [hbm] * 5,
        out_specs=[vmem] * 8 + [hbm] * 6,
        out_shape=[
            jax.ShapeDtypeStruct((rows, heads * HEAD), BF16),
            jax.ShapeDtypeStruct((heads, rows, LANES), BF16),
            jax.ShapeDtypeStruct((SPAN, tp_count, block, kv_cols), BF16),
            jax.ShapeDtypeStruct((rows, LANES), BF16),
            jax.ShapeDtypeStruct((block, model), F32),
            jax.ShapeDtypeStruct((block, LANES), BF16),
            jax.ShapeDtypeStruct((2,) + shard.shape, BF16),
            jax.ShapeDtypeStruct((tp_count, block, model), BF16),
            *[jax.ShapeDtypeStruct(w.shape, BF16) for w in weights],
            jax.ShapeDtypeStruct((ctx_count,) + grads.shape, BF16),
            jax.ShapeDtypeStruct((ctx_count,) + routes.shape, jnp.int32),
            jax.ShapeDtypeStruct((ctx_count, block, model), BF16),
        ],
        scratch_shapes=[
            pltpu.VMEM((2,) + shard.shape, BF16),
            pltpu.VMEM((heads, rows, LANES), BF16),
            pltpu.VMEM((pairs, SPAN * rows, LANES), BF16),
            pltpu.VMEM((pairs, SPAN * rows, LANES), BF16),
            pltpu.VMEM((tp_count * pairs, tall, LANES), F32),
            pltpu.VMEM((tp_count * pairs, tall, LANES), F32),
            pltpu.VMEM((tp_count,) + part, BF16),
            pltpu.VMEM((tp_count - 1,) + part, BF16),
            pltpu.VMEM((block, model), BF16),
            dma((2,)),
            dma((2, tp_count - 1)),
            dma((2, SPAN - 1)),
            dma((2, tp_count - 1)),
            dma((2, 3)),
            dma((2, ctx_count)),
            dma((2, ctx_count)),
            dma((2, chips)),
            dma((2, chips)),
            dma((3,)),
        ],
        compiler_params=pltpu.CompilerParams(
            vmem_limit_bytes=VMEM_LIMIT, collective_id=0, has_side_effects=True
        ),
        cost_estimate=pl.CostEstimate(
            flops=16 * SPAN * rows * rows * heads * LANES,
            bytes_accessed=32 * 1024 * 1024,
            transcendentals=0,
        ),
        name="forward",
    )(
        tokens, *gains, shard, first, second, o_first, o_second, cos, sin, codes, *weights,
        grads, routes,
    )


def joined(dk, dv, span):
    pairs = dk.shape[0]
    return jnp.concatenate(
        [dk[pair, span, :HEAD] for pair in range(pairs)]
        + [dv[pair, span, :HEAD] for pair in range(pairs)],
        axis=1,
    )


def backward_kernel(
    tokens, upstream_ref, routes, gain_one, gain_two, router, middle_ref, low_ref, weights,
    normed_all, lora, att, q_ref, kv_ref, first, second, o_first, o_second, cos, sin, back, mixed,
    output, input_grad, packed_out,
    k_aug, v_aug, up_aug, dk, dv, dq, branch_all, far_out, far_in, own_kv, parts, parts_in,
    second_acc, first_acc, o_in_acc, packed, ctx_in, tp_in, middle_grad,
    back_near, back_mine, back_pair, back_far, mixed_near, mixed_mine, mixed_pair, mixed_far,
    near_sem, mine_sem, far_sem, branch_sem, kv_sem, part_sem,
    ctx_sem, tp_sem, x_sem, tp_all_sem, ctx_all_sem,
    *, tp_count, ctx_count, experts, direct,
):
    tp, ctx, fsdp = (lax.axis_index(name) for name in ("tp", "ctx", "fsdp"))
    rank = lax.rem(ctx, SPAN)
    block, model = tokens.shape
    heads, rows_all, _ = q_ref.shape
    pairs = k_aug.shape[0]
    group = heads // pairs
    tall = group * block
    half = weights.shape[2]
    q_cols = heads * HEAD
    kv_cols = pairs * HEAD
    turn = cos.shape[1]
    partner = ctx + 1 - 2 * lax.rem(ctx, 2)
    cross = ring(ctx, 2, ctx_count)
    cross_partner = ring(partner, 2, ctx_count)
    other = {"fsdp": 1 - fsdp}

    barrier = pltpu.get_barrier_semaphore()
    pl.semaphore_signal(barrier, 1, device_id=other, device_id_type=pl.DeviceIdType.MESH)
    for k in range(1, tp_count):
        pl.semaphore_signal(
            barrier, 1, device_id={"tp": ring(tp, k, tp_count)},
            device_id_type=pl.DeviceIdType.MESH,
        )
    for k in range(1, ctx_count):
        pl.semaphore_signal(
            barrier, 1, device_id={"ctx": ring(ctx, k, ctx_count)},
            device_id_type=pl.DeviceIdType.MESH,
        )
    pl.semaphore_wait(barrier, tp_count + ctx_count - 1)

    sums = (
        (back, back_near, back_mine, back_pair, back_far),
        (mixed, mixed_near, mixed_mine, mixed_pair, mixed_far),
    )

    def near_copy(n, slot):
        source, near = sums[n][:2]
        return remote(
            source.at[(partner, cross_partner)[slot]], near.at[slot],
            near_sem.at[0, 2 * n + slot], near_sem.at[1, 2 * n + slot], {"ctx": partner},
        )

    def mine_copy(n, slot):
        return pltpu.make_async_copy(
            sums[n][0].at[(ctx, cross)[slot]], sums[n][2].at[slot], mine_sem.at[2 * n + slot]
        )

    def pair_copy(n):
        return remote(sums[n][3], sums[n][4], far_sem.at[0, n], far_sem.at[1, n], {"ctx": cross})

    def start_sum(n):
        for slot in (1, 0):
            near_copy(n, slot).start()
            mine_copy(n, slot).start()

    def pass_sum(n):
        near_copy(n, 1).wait_recv()
        mine_copy(n, 1).wait()
        _, near, mine, pair, _ = sums[n]
        pair[...] = (near[1].astype(F32) + mine[1].astype(F32)).astype(BF16)
        pair_copy(n).start()

    def end_sum(n):
        near_copy(n, 0).wait_recv()
        mine_copy(n, 0).wait()
        pair_copy(n).wait_recv()
        _, near, mine, _, far = sums[n]
        return near[0].astype(F32) + mine[0].astype(F32) + far[...].astype(F32)

    if direct:
        start_sum(0)
        start_sum(1)

    @pl.loop(0, rank + 1)
    def _(distance):
        @pl.loop(0, tp_count)
        def _(part):
            kv = kv_ref[distance, part]
            for pair in range(pairs):
                aug_keys(
                    kv, pair, pairs, (rank - distance) * SEGS_DEV + part * (block // SEG),
                    k_aug, v_aug, pl.multiple_of(distance * rows_all + part * block, block),
                )

    dk[...] = jnp.zeros(dk.shape, F32)
    dv[...] = jnp.zeros(dv.shape, F32)
    dq[...] = jnp.zeros(dq.shape, F32)
    second_acc[...] = jnp.zeros(second_acc.shape, F32)
    first_acc[...] = jnp.zeros(first_acc.shape, F32)
    o_in_acc[...] = jnp.zeros(o_in_acc.shape, F32)
    packed[...] = jnp.zeros(packed.shape, F32)

    middle = middle_ref[...]
    normed_two = rms_scale(middle, gain_two[...]).astype(BF16)
    logits = dot(normed_two, router[...])
    number = iota((block, LANES), 1)
    hit = jnp.zeros((block, LANES), F32)
    for k in range(routes.shape[1]):
        hit += (routes[:, k : k + 1] == number).astype(F32)
    kept = jnp.where(hit > 0.5, logits, MASKED)
    gates = jnp.exp(kept - jnp.max(kept, axis=1, keepdims=True)) * hit
    gates = gates / jnp.sum(gates, axis=1, keepdims=True)

    if direct:
        pass_sum(0)
        back_sum = end_sum(0)
    else:
        back_sum = back[...].astype(F32)
    table = back_sum[:, model:]
    slopes = table + pltpu.roll(table, LANES - experts, 1)
    logits_grad = gates * (slopes - jnp.sum(gates * slopes, axis=1, keepdims=True))
    high = logits_grad.astype(BF16)
    low = (logits_grad - high.astype(F32)).astype(BF16)
    normed_two_grad = back_sum[:, :model] + dot_nt(high, router[...]) + dot_nt(low, router[...])
    middle_grad[...] = upstream_ref[...].astype(F32) + rms_back(
        middle, gain_two[...], normed_two_grad
    )
    branch = (RESIDUAL_SCALE * middle_grad[...]).astype(BF16)
    branch_all[tp] = branch

    def branch_copy(k):
        return remote(
            branch_all.at[tp], branch_all.at[tp], branch_sem.at[0, k - 1], branch_sem.at[1, k - 1],
            {"tp": ring(tp, k, tp_count)},
        )

    for k in range(1, tp_count):
        branch_copy(k).start()
    packed[pl.ds(4 * RANK, RANK), :] = dot_tn(low_ref[...], branch)[:RANK]
    if direct:
        pass_sum(1)

    wide = heads * LANES
    r, c = iota((q_cols, wide), 0), iota((q_cols, wide), 1)
    same = r // HEAD == c // LANES
    place = (same & (r % HEAD == c % LANES)).astype(BF16)
    spread = (same & (c % LANES >= ONES) & (c % LANES < ONES + 2)).astype(BF16)

    def tile(part, pair, start, size, causal):
        index = part * pairs + pair
        rows = pl.ds(pl.multiple_of(part * block, block), block)
        queries = q_ref[pl.ds(pair * group, group), rows, :].reshape(tall, LANES)
        upstream = up_aug[pl.ds(pair * group, group), rows, :].reshape(tall, LANES)
        span = pl.ds(start, size)
        keys = k_aug[pair, span, :]
        probs = jnp.exp(dot_nt(keys, queries))
        if causal:
            q_row = iota(probs.shape, 1) % block
            probs = jnp.where(iota(probs.shape, 0) <= q_row, probs, 0.0)
        steep = (probs * dot_nt(v_aug[pair, span, :], upstream)).astype(BF16)
        dv[pair, span, :] += dot(probs.astype(BF16), upstream)
        dk[pair, span, :] += dot(steep, queries)
        dq[index] += dot_tn(steep, keys)

    @pl.loop(0, tp_count)
    def _(k):
        @pl.when(k > 0)
        def _():
            branch_copy(k).wait_recv()

        part = ring(tp, -k, tp_count)
        rows = pl.ds(pl.multiple_of(part * block, block), block)
        low_grad = dot_nt(branch_all[part], o_second[...]).astype(BF16)
        grads = dot_nt(low_grad, o_first[...])
        for side in range(2):
            grads += dot_nt(
                branch_all[part, :, side * half : (side + 1) * half],
                weights[side, pl.ds(half, q_cols), :],
            )
        grads = grads.astype(BF16)
        mixed_heads = att[rows, :]
        o_in_acc[...] += dot_tn(low_grad, mixed_heads)
        product = grads.astype(F32) * mixed_heads.astype(F32)
        minus = jnp.zeros((block, wide), F32)
        for _ in range(3):
            piece = product.astype(BF16)
            minus -= dot(piece, spread)
            product -= piece.astype(F32)
        top = minus.astype(BF16).astype(F32)
        lane = iota(minus.shape, 1) % LANES
        coded = dot(grads, place) + jnp.where(
            lane == ONES, top, jnp.where(lane == ONES + 1, minus - top, 0.0)
        )
        for head in range(heads):
            up_aug[head, rows, :] = coded[:, head * LANES : (head + 1) * LANES].astype(BF16)

        @pl.loop(0, pairs)
        def _(pair):
            tile(part, pair, pl.multiple_of(part * block, block), block, True)

            @pl.loop(0, part)
            def _(j):
                tile(part, pair, pl.multiple_of(j * block, block), block, False)

    def far_copy(distance):
        return remote(
            far_out.at[distance - 1], far_in.at[distance - 1],
            kv_sem.at[0, distance - 1], kv_sem.at[1, distance - 1],
            {"ctx": ring(ctx, -distance, ctx_count)},
        )

    size = min(rows_all, 512)

    @pl.loop(0, rank)
    def _(step):
        distance = rank - step
        start = distance * rows_all

        @pl.loop(0, tp_count * pairs * (rows_all // size))
        def _(n):
            index, piece = n // (rows_all // size), lax.rem(n, rows_all // size)
            tile(
                index // pairs, lax.rem(index, pairs),
                pl.multiple_of(start + piece * size, size), size, False,
            )

        @pl.loop(0, tp_count)
        def _(part):
            span = pl.ds(pl.multiple_of(start + part * block, block), block)
            far_out[distance - 1, pl.ds(pl.multiple_of(part * block, block), block), :] = joined(
                dk, dv, span
            ).astype(BF16)

        far_copy(distance).start()

    own_kv[...] = joined(dk, dv, pl.ds(0, rows_all))
    for distance in range(1, SPAN):

        @pl.when(rank + distance < SPAN)
        def _(distance=distance):
            far_copy(distance).wait_recv()
            own_kv[...] += far_in[distance - 1].astype(F32)

    def part_copy(k):
        return remote(
            parts.at[k], parts_in.at[k], part_sem.at[0, k], part_sem.at[1, k],
            {"tp": ring(tp, k + 1, tp_count)},
        )

    @pl.loop(0, tp_count)
    def _(k):
        part = ring(tp, k + 1, tp_count)
        rows = pl.ds(pl.multiple_of(part * block, block), block)
        pieces = []
        for pair in range(pairs):
            held = dq[part * pairs + pair]
            turned = SCORE_SCALE * jnp.concatenate(
                [held[member * block : (member + 1) * block, :HEAD] for member in range(group)],
                axis=1,
            )
            pieces.append(turned * cos[rows, :] - swap_halves(turned) * sin[rows, :])
        keys = own_kv[rows, :kv_cols]
        pieces.append(keys * cos[rows, :] - swap_halves(keys) * sin[rows, :])
        pieces.append(own_kv[rows, kv_cols:])
        grads = jnp.concatenate(pieces, axis=1).astype(BF16)
        for side in range(2):
            parts[k, :, side * half : (side + 1) * half] = dot_nt(
                grads, weights[side, pl.ds(0, half), :]
            ).astype(BF16)
        low_part = dot_nt(grads, second[...]).astype(BF16)
        parts[k, :, model:] = low_part

        @pl.when(k < tp_count - 1)
        def _():
            part_copy(k).start()

        second_acc[...] += dot_tn(lora[rows, :], grads)
        first_acc[...] += dot_tn(low_part, normed_all[part])

    packed[pl.ds(0, 3 * RANK), :] = first_acc[pl.ds(0, 3 * RANK), :]
    lanes = pl.ds(pl.multiple_of(tp * q_cols, q_cols), q_cols)
    packed[pl.ds(3 * RANK, RANK), lanes] = o_in_acc[pl.ds(0, RANK), :]
    packed[pl.ds(5 * RANK, RANK), lanes] = second_acc[pl.ds(0, RANK), :q_cols]
    lanes = pl.ds(pl.multiple_of(tp * kv_cols, kv_cols), kv_cols)
    packed[pl.ds(6 * RANK, RANK), lanes] = second_acc[pl.ds(RANK, RANK), q_cols : q_cols + kv_cols]
    lanes = pl.ds(pl.multiple_of(model // 2 + tp * kv_cols, kv_cols), kv_cols)
    packed[pl.ds(6 * RANK, RANK), lanes] = second_acc[pl.ds(2 * RANK, RANK), q_cols + kv_cols :]

    if direct:
        tall_rows, few_rows = packed.shape[0] // ctx_count, packed.shape[0] // (ctx_count * tp_count)

        def ctx_rows(index):
            return pl.ds(pl.multiple_of(index * tall_rows, tall_rows), tall_rows)

        def tp_rows(index):
            start = ctx * tall_rows + index * few_rows
            return pl.ds(pl.multiple_of(start, few_rows), few_rows)

        def ctx_copy(k):
            where = ring(ctx, k, ctx_count)
            return remote(
                packed.at[ctx_rows(where)], ctx_in.at[k - 1],
                ctx_sem.at[0, k - 1], ctx_sem.at[1, k - 1], {"ctx": where},
            )

        def tp_copy(k):
            where = ring(tp, k, tp_count)
            return remote(
                packed.at[tp_rows(where)], tp_in.at[k - 1],
                tp_sem.at[0, k - 1], tp_sem.at[1, k - 1], {"tp": where},
            )

        x_copy = remote(
            packed_out.at[fsdp, tp_rows(tp)], packed_out.at[fsdp, tp_rows(tp)],
            x_sem.at[0], x_sem.at[1], other,
        )

        def tp_all_copy(k):
            return remote(
                packed_out.at[:, tp_rows(tp)], packed_out.at[:, tp_rows(tp)],
                tp_all_sem.at[0, k - 1], tp_all_sem.at[1, k - 1], {"tp": ring(tp, k, tp_count)},
            )

        def ctx_all_copy(k):
            return remote(
                packed_out.at[:, ctx_rows(ctx)], packed_out.at[:, ctx_rows(ctx)],
                ctx_all_sem.at[0, k - 1], ctx_all_sem.at[1, k - 1],
                {"ctx": ring(ctx, k, ctx_count)},
            )

        for k in range(1, ctx_count):
            ctx_copy(k).start()
        for k in range(1, ctx_count):
            ctx_copy(k).wait()
        packed[ctx_rows(ctx), :] = packed[ctx_rows(ctx), :] + sum(
            ctx_in[k] for k in range(ctx_count - 1)
        )
        for k in range(1, tp_count):
            tp_copy(k).start()
        for k in range(1, tp_count):
            tp_copy(k).wait()
        packed_out[fsdp, tp_rows(tp), :] = packed[tp_rows(tp), :] + sum(
            tp_in[k] for k in range(tp_count - 1)
        )
        x_copy.start()
        x_copy.wait()
        for k in range(1, tp_count):
            tp_all_copy(k).start()
        for k in range(1, tp_count):
            tp_all_copy(k).wait()
        for k in range(1, ctx_count):
            ctx_all_copy(k).start()
    else:
        packed_out[0] = packed[...]

    summed = parts[tp_count - 1].astype(F32)
    for k in range(tp_count - 1):
        part_copy(k).wait_recv()
        summed += parts_in[k].astype(F32)
    normed_grad = summed[:, :model] + dot_nt(summed[:, model:].astype(BF16), first[...])
    inputs = tokens[...].astype(F32)
    input_grad[...] = (
        middle_grad[...] + rms_back(inputs, gain_one[...], normed_grad)
    ).astype(BF16)
    mixture = end_sum(1) if direct else mixed[...].astype(F32)
    output[...] = (middle_ref[...] + RESIDUAL_SCALE * mixture).astype(BF16)

    if direct:
        for k in range(1, ctx_count):
            ctx_all_copy(k).wait()
        for n in range(2):
            for slot in range(2):
                near_copy(n, slot).wait_send()
            pair_copy(n).wait_send()
    for k in range(1, tp_count):
        branch_copy(k).wait_send()
    for k in range(tp_count - 1):
        part_copy(k).wait_send()
    for distance in range(1, SPAN):

        @pl.when(distance <= rank)
        def _(distance=distance):
            far_copy(distance).wait_send()


def backward(
    tokens, upstream, routes, gains, router, middle, low, weights, normed, lora, att, queries, kv,
    first, second, o_first, o_second, cos, sin, back, mixed, tp_count, ctx_count, experts, direct,
):
    block, model = tokens.shape
    heads, rows, _ = queries.shape
    pairs = kv.shape[3] // (2 * HEAD)
    tall = heads // pairs * block
    cols = second.shape[1]
    kv_width = kv.shape[3]
    vmem = pl.BlockSpec(memory_space=pltpu.VMEM)
    hbm = pl.BlockSpec(memory_space=pl.ANY)
    dma = pltpu.SemaphoreType.DMA
    part = (block, model + LANES)
    packed = (8 * RANK, model)
    copies = 2 if direct else 1
    slim = (8, LANES)

    def buffers(width):
        shapes = [(2, block, width), (2, block, width), (block, width), (block, width)]
        return [pltpu.VMEM(shape if direct else slim, BF16) for shape in shapes]

    return pl.pallas_call(
        functools.partial(
            backward_kernel, tp_count=tp_count, ctx_count=ctx_count, experts=experts, direct=direct
        ),
        in_specs=[vmem] * 20 + [hbm if direct else vmem] * 2,
        out_specs=[vmem] * 3,
        out_shape=[
            jax.ShapeDtypeStruct((block, model), BF16),
            jax.ShapeDtypeStruct((block, model), BF16),
            jax.ShapeDtypeStruct((copies,) + packed, F32),
        ],
        scratch_shapes=[
            pltpu.VMEM((pairs, SPAN * rows, LANES), BF16),
            pltpu.VMEM((pairs, SPAN * rows, LANES), BF16),
            pltpu.VMEM((heads, rows, LANES), BF16),
            pltpu.VMEM((pairs, SPAN * rows, LANES), F32),
            pltpu.VMEM((pairs, SPAN * rows, LANES), F32),
            pltpu.VMEM((tp_count * pairs, tall, LANES), F32),
            pltpu.VMEM((tp_count, block, model), BF16),
            pltpu.VMEM((SPAN - 1, rows, kv_width), BF16),
            pltpu.VMEM((SPAN - 1, rows, kv_width), BF16),
            pltpu.VMEM((rows, kv_width), F32),
            pltpu.VMEM((tp_count,) + part, BF16),
            pltpu.VMEM((tp_count - 1,) + part, BF16),
            pltpu.VMEM((LANES, cols), F32),
            pltpu.VMEM((LANES, model), F32),
            pltpu.VMEM((LANES, heads * HEAD), F32),
            pltpu.VMEM(packed, F32),
            pltpu.VMEM((ctx_count - 1, packed[0] // ctx_count, model) if direct else slim, F32),
            pltpu.VMEM((tp_count - 1, 8, model) if direct else slim, F32),
            pltpu.VMEM((block, model), F32),
            *buffers(model + LANES),
            *buffers(model),
            dma((2, 4)),
            dma((4,)),
            dma((2, 2)),
            dma((2, tp_count - 1)),
            dma((2, SPAN - 1)),
            dma((2, tp_count - 1)),
            dma((2, ctx_count - 1)),
            dma((2, tp_count - 1)),
            dma((2,)),
            dma((2, tp_count - 1)),
            dma((2, ctx_count - 1)),
        ],
        compiler_params=pltpu.CompilerParams(
            vmem_limit_bytes=60 * 1024 * 1024, collective_id=1, has_side_effects=True
        ),
        cost_estimate=pl.CostEstimate(
            flops=32 * SPAN * rows * rows * heads * LANES,
            bytes_accessed=32 * 1024 * 1024,
            transcendentals=0,
        ),
        name="backward",
    )(
        tokens, upstream, routes, *gains, router, middle, low, weights, normed, lora, att, queries,
        kv, first, second, o_first, o_second, cos, sin, back, mixed,
    )


def columns_of(chosen):
    return iota((RANK, LANES), 1) == iota((RANK, LANES), 0) + chosen * RANK


def place_kernel(sets, packed, *outs):
    query_in, query_out, key_in, key_out, value_in, value_out, out_in, out_out = outs
    kv_cols = key_out.shape[1]
    exact = dict(precision=lax.Precision.HIGHEST, preferred_element_type=F32)

    def gathered(rows, lanes, turned):
        total = None
        for tree in range(packed.shape[0]):
            spots = columns_of(sets[tree]).astype(F32)
            piece = packed[tree, rows * RANK : (rows + 1) * RANK, lanes]
            pair = (piece, spots) if turned else (spots, piece)
            term = lax.dot_general(*pair, (((0,), (0,)), ((), ())), **exact)
            total = term if total is None else total + term
        return total

    whole = slice(None)
    query_in[...] = gathered(0, whole, True)
    key_in[...] = gathered(1, whole, True)
    value_in[...] = gathered(2, whole, True)
    out_in[...] = gathered(3, whole, True)
    out_out[...] = gathered(4, whole, False)
    query_out[...] = gathered(5, whole, False)
    key_out[...] = gathered(6, slice(0, kv_cols), False)
    value_out[...] = gathered(6, slice(kv_cols, 2 * kv_cols), False)


def place(sets, packed, outs):
    vmem = pl.BlockSpec(memory_space=pltpu.VMEM)
    return pl.pallas_call(
        place_kernel,
        in_specs=[pl.BlockSpec(memory_space=pltpu.SMEM), vmem],
        out_specs=[vmem] * len(outs),
        out_shape=[jax.ShapeDtypeStruct(o.shape, F32) for o in outs],
        compiler_params=pltpu.CompilerParams(vmem_limit_bytes=VMEM_LIMIT),
        name="place",
    )(sets, packed)


def place_experts_kernel(sets, part, gate_in, gate_out, up_in, up_out, down_in, down_out):
    hidden = gate_out.shape[2]

    def gathered(rows, lanes, turned):
        total = None
        for tree in range(part.shape[0]):
            spots = columns_of(sets[tree]).astype(BF16)
            piece = part[tree, 0, rows * RANK : (rows + 1) * RANK, lanes]
            term = dot_tn(piece, spots) if turned else dot_tn(spots, piece)
            total = term if total is None else total + term
        return total

    whole, left, right = slice(None), slice(0, hidden), slice(hidden, 2 * hidden)
    gate_in[0] = gathered(0, whole, True)
    up_in[0] = gathered(1, whole, True)
    gate_out[0] = gathered(2, left, False)
    up_out[0] = gathered(2, right, False)
    down_out[0] = gathered(3, whole, False)
    down_in[0] = gathered(4, left, True)


def place_experts(sets, part, outs):
    trees, local = part.shape[:2]
    return pl.pallas_call(
        place_experts_kernel,
        grid_spec=pltpu.PrefetchScalarGridSpec(
            num_scalar_prefetch=1,
            grid=(local,),
            in_specs=[pl.BlockSpec((trees, 1) + part.shape[2:], lambda e, s: (0, e, 0, 0))],
            out_specs=[pl.BlockSpec((1,) + o.shape[1:], lambda e, s: (e, 0, 0)) for o in outs],
        ),
        out_shape=[jax.ShapeDtypeStruct(o.shape, F32) for o in outs],
        compiler_params=pltpu.CompilerParams(vmem_limit_bytes=VMEM_LIMIT),
        name="place_experts",
    )(sets, part)


def expert_kernel(
    sets, base, x_ref, g_ref, routes, router,
    w_gate, w_up, w_down, w_gate_far, w_up_far, w_down_far, gate_in, up_in, gate_out, up_out, down_in, down_out,
    back_out, mixed_out, grad_out,
    rank_rows, gate_rows, slope_rows, mix, back, xs, firsts, tall_grad,
    gate_full, up_full, down_full,
    *, slots, sources,
):
    chunk, expert = pl.program_id(0), pl.program_id(1)
    experts = router.shape[0]
    tokens, model = x_ref.shape
    each = tokens // sources
    hidden = w_gate.shape[2]
    lanes = gate_in.shape[2]
    chosen = sets[chunk]

    @pl.when(expert == 0)
    def _():
        logits = dot_nt(router[...], x_ref[...])
        number = iota((experts, tokens), 0)
        hit = jnp.zeros((experts, tokens), F32)
        for k in range(routes.shape[0]):
            hit += (routes[k : k + 1, :] == number).astype(F32)
        kept = jnp.where(hit > 0.5, logits, MASKED)
        weights = jnp.exp(kept - jnp.max(kept, axis=0, keepdims=True)) * hit
        gate_rows[...] = weights / jnp.sum(weights, axis=0, keepdims=True)
        earlier = (iota((each, each), 0) < iota((each, each), 1)).astype(BF16)
        for s in range(sources):
            span = slice(s * each, (s + 1) * each)
            order = dot(hit[:, span].astype(BF16), earlier)
            rank_rows[:, span] = jnp.where(hit[:, span] > 0.5, order, -1.0)
        mix[...] = jnp.zeros(mix.shape, F32)
        back[...] = jnp.zeros(back.shape, F32)
        slope_rows[...] = jnp.zeros(slope_rows.shape, F32)

    row = base[0] + expert
    ranks = rank_rows[pl.ds(row, 1), :]
    gates = gate_rows[pl.ds(row, 1), :]
    slot_number = iota((slots, each), 0).astype(F32)
    picks, columns, upstreams = [], [], []
    for s in range(sources):
        span = slice(s * each, (s + 1) * each)
        pick = ranks[:, span] == slot_number
        columns.append(jnp.sum(jnp.where(pick, gates[:, span], 0.0), axis=1, keepdims=True))
        pick = pick.astype(BF16)
        picks.append(pick)
        xs[pl.ds(s * slots, slots), :] = dot(pick, x_ref[pl.ds(s * each, each), :]).astype(BF16)
        upstreams.append(dot(pick, g_ref[pl.ds(s * each, each), :]))
    gate_column = jnp.concatenate(columns, axis=0)
    upstream = RESIDUAL_SCALE * jnp.concatenate(upstreams, axis=0)

    firsts[:, :lanes] = gate_in[0]
    firsts[:, lanes:] = up_in[0]
    keep = (iota((1, 2 * lanes), 1) % lanes // RANK == chosen).astype(BF16)
    rows = xs[...]
    inner = dot(rows, firsts[...]).astype(BF16) * keep
    for full, near, far in (
        (gate_full, w_gate, w_gate_far),
        (up_full, w_up, w_up_far),
        (down_full, w_down, w_down_far),
    ):
        size = near.shape[1]
        full[pl.ds(pl.multiple_of(base[1] * size, size), size), :] = near[0]
        full[pl.ds(pl.multiple_of((1 - base[1]) * size, size), size), :] = far[0]
    gate_value = dot(rows, gate_full[...]) + dot(inner[:, :lanes], gate_out[0])
    up_value = dot(rows, up_full[...]) + dot(inner[:, lanes:], up_out[0])
    sigmoid = 1.0 / (1.0 + jnp.exp(-gate_value))
    silu = gate_value * sigmoid
    active = (silu * up_value).astype(BF16)
    down_inner = dot(active, down_in[0]).astype(BF16) * keep[:, :lanes]
    produced = (
        (dot(active, down_full[...]) + dot(down_inner, down_out[0])).astype(BF16).astype(F32)
    )
    slope = jnp.sum(upstream * produced, axis=1, keepdims=True)
    sent = (gate_column * produced).astype(BF16)
    slot_grad = (gate_column * upstream).astype(BF16)

    down_inner_grad = dot_nt(slot_grad, down_out[0]).astype(BF16) * keep[:, :lanes]
    active_grad = (
        (dot_nt(slot_grad, down_full[...]) + dot_nt(down_inner_grad, down_in[0]))
        .astype(BF16)
        .astype(F32)
    )
    gate_grad = (active_grad * up_value * (sigmoid + silu * (1.0 - sigmoid))).astype(BF16)
    up_grad = (active_grad * silu).astype(BF16)
    inner_grad = (
        jnp.concatenate([dot_nt(gate_grad, gate_out[0]), dot_nt(up_grad, up_out[0])], axis=1)
    ).astype(BF16) * keep
    row_grad = (
        dot_nt(gate_grad, gate_full[...])
        + dot_nt(up_grad, up_full[...])
        + dot_nt(inner_grad, firsts[...])
    ).astype(BF16)

    for s in range(sources):
        span = slice(s * slots, (s + 1) * slots)
        spot = pl.ds(s * each, each)
        mix[spot, :] += dot_tn(picks[s], sent[span, :])
        back[spot, :] += dot_tn(picks[s], row_grad[span, :])
        slope_rows[pl.ds(expert, 1), spot] = jnp.sum(
            jnp.where(picks[s] > 0.5, slope[span, :], 0.0), axis=0, keepdims=True
        )

    own = pl.multiple_of(chosen * RANK, RANK)
    tall_grad[...] = dot_tn(inner_grad, rows)
    grad_out[0, 0, pl.ds(0, RANK), :] = tall_grad[pl.ds(own, RANK), :].astype(BF16)
    grad_out[0, 0, pl.ds(RANK, RANK), :] = tall_grad[pl.ds(lanes + own, RANK), :].astype(BF16)
    tall_grad[pl.ds(0, lanes), :hidden] = dot_tn(inner[:, :lanes], gate_grad)
    tall_grad[pl.ds(0, lanes), hidden:] = dot_tn(inner[:, lanes:], up_grad)
    grad_out[0, 0, pl.ds(2 * RANK, RANK), :] = tall_grad[pl.ds(own, RANK), :].astype(BF16)
    tall_grad[pl.ds(0, lanes), :] = dot_tn(down_inner, slot_grad)
    grad_out[0, 0, pl.ds(3 * RANK, RANK), :] = tall_grad[pl.ds(own, RANK), :].astype(BF16)
    tall_grad[pl.ds(0, lanes), :hidden] = dot_tn(down_inner_grad, active)
    tall_grad[pl.ds(0, lanes), hidden:] = jnp.zeros((lanes, model - hidden), F32)
    grad_out[0, 0, pl.ds(4 * RANK, RANK), :] = tall_grad[pl.ds(own, RANK), :].astype(BF16)

    @pl.when(expert == pl.num_programs(1) - 1)
    def _():
        mixed_out[...] = mix[...].astype(BF16)
        back_out[:, :model] = back[...].astype(BF16)
        turned = slope_rows[...].T
        high = turned.astype(BF16)
        low = (turned - high.astype(F32)).astype(BF16)
        local, lane = iota((LANES, LANES), 0), iota((LANES, LANES), 1)
        inside = local < pl.num_programs(1)
        first = (inside & (lane == local + base[0])).astype(BF16)
        later = (inside & (lane == local + base[0] + experts)).astype(BF16)
        back_out[:, model:] = (dot(high, first) + dot(low, later)).astype(BF16)


def run_experts(
    sets, base, rows, upstream, routes, router, weights, adapters, slots, sources
):
    total, model = rows.shape
    experts = router.shape[0]
    local, half, hidden = weights[0].shape
    trees = sets.shape[0]
    tokens = total // trees
    lanes = adapters[0].shape[2]
    tall = sources * slots
    piece = lambda c, e, *_: (c, 0)
    fixed = lambda c, e, *_: (0, 0)
    expert = lambda c, e, *_: (e, 0, 0)
    return pl.pallas_call(
        functools.partial(expert_kernel, slots=slots, sources=sources),
        grid_spec=pltpu.PrefetchScalarGridSpec(
            num_scalar_prefetch=2,
            grid=(trees, local),
            in_specs=[
                pl.BlockSpec((tokens, model), piece),
                pl.BlockSpec((tokens, model), piece),
                pl.BlockSpec((routes.shape[0], tokens), lambda c, e, *_: (0, c)),
                pl.BlockSpec(router.shape, fixed),
                *[pl.BlockSpec((1,) + a.shape[1:], expert) for a in (*weights, *adapters)],
            ],
            out_specs=[
                pl.BlockSpec((tokens, model + LANES), piece),
                pl.BlockSpec((tokens, model), piece),
                pl.BlockSpec((1, 1, 5 * RANK, model), lambda c, e, *_: (c, e, 0, 0)),
            ],
            scratch_shapes=[
                pltpu.VMEM((experts, tokens), F32),
                pltpu.VMEM((experts, tokens), F32),
                pltpu.VMEM((LANES, tokens), F32),
                pltpu.VMEM((tokens, model), F32),
                pltpu.VMEM((tokens, model), F32),
                pltpu.VMEM((tall, model), BF16),
                pltpu.VMEM((model, 2 * lanes), BF16),
                pltpu.VMEM((2 * lanes, model), F32),
                pltpu.VMEM((2 * half, hidden), BF16),
                pltpu.VMEM((2 * half, hidden), BF16),
                pltpu.VMEM((hidden, model), BF16),
            ],
        ),
        out_shape=[
            jax.ShapeDtypeStruct((total, model + LANES), BF16),
            jax.ShapeDtypeStruct((total, model), BF16),
            jax.ShapeDtypeStruct((trees, local, 5 * RANK, model), BF16),
        ],
        compiler_params=pltpu.CompilerParams(vmem_limit_bytes=60 * 1024 * 1024),
        name="experts",
        cost_estimate=pl.CostEstimate(
            flops=2 * local * total * model * model * 2,
            bytes_accessed=8 * 1024 * 1024,
            transcendentals=0,
        ),
    )(sets, base, rows, upstream, routes, router, *weights, *adapters)


def take_set(table, chosen, axis):
    return lax.dynamic_slice_in_dim(table, chosen * RANK, RANK, axis)


def per_device(
    tokens,
    out_grad,
    routes,
    parents,
    adapter_set,
    gain_a,
    gain_b,
    w_query,
    key_projection_matrix,
    value_projection_matrix,
    w_output,
    w_router,
    w_gate,
    w_up,
    w_down,
    query_in,
    query_out,
    key_in,
    key_second_factor,
    value_in,
    value_second_factor,
    out_in,
    out_out,
    gate_in,
    gate_out,
    up_in,
    up_out,
    down_in,
    down_out,
):
    tp_rank = lax.axis_index("tp")
    ctx_rank = lax.axis_index("ctx")
    fsdp_rank = lax.axis_index("fsdp")
    ctx_count = lax.axis_size("ctx")
    tp_count = lax.axis_size("tp")
    fsdp_count = lax.axis_size("fsdp")
    tok_rows, model = tokens.shape
    q_cols = w_query.shape[1]
    kv_cols = key_projection_matrix.shape[1]
    heads, pairs = q_cols // HEAD, kv_cols // HEAD
    experts = w_router.shape[1]
    local_experts = w_gate.shape[0]
    sets = query_in.shape[1] // RANK
    slots = tok_rows * TOP * 3 // (2 * experts)
    trees = ctx_count // SPAN

    attention_shard = jnp.concatenate(
        [
            jnp.concatenate([w_query, key_projection_matrix, value_projection_matrix], axis=1),
            w_output,
        ],
        axis=0,
    )

    seg_start = (fsdp_rank * ctx_count + ctx_rank) * SEGS_DEV
    tree_index = seg_start // TREE_SEGS
    local_start = seg_start % TREE_SEGS
    rank = (local_start // SEGS_DEV).astype(jnp.int32).reshape(1)
    tree_parents = lax.dynamic_slice_in_dim(parents, tree_index * TREE_SEGS, TREE_SEGS, 0)
    reach, depth = tree_links(tree_parents)
    chosen = lax.dynamic_slice_in_dim(adapter_set, tree_index, 1, 0)[0]

    gain_one = gain_a.astype(F32)
    gain_two = gain_b.astype(F32)

    own_reach = lax.dynamic_slice_in_dim(reach, local_start, SEGS_DEV, 0)
    codes = jnp.pad(
        jnp.where(own_reach > 0.5, 0.0, MASKED), ((0, 0), (CODE, LANES - CODE - TREE_SEGS))
    )
    codes = jnp.repeat(codes.astype(BF16), SEG, axis=0)
    own_depth = lax.dynamic_slice_in_dim(depth, local_start, SEGS_DEV, 0)
    positions = (
        own_depth[:, None] * SEG + jnp.arange(SEG, dtype=jnp.int32).astype(F32)[None, :]
    ).reshape(-1)
    half_head = HEAD // 2
    freqs = ROPE_BASE ** (-(jnp.arange(half_head, dtype=jnp.int32).astype(F32) * 2.0) / HEAD)
    angles = positions[:, None] * jnp.tile(freqs, LANES // half_head)[None, :]
    cos, sin = jnp.cos(angles), jnp.sin(angles)

    first = jnp.pad(
        jnp.concatenate(
            [take_set(t, chosen, 1) for t in (query_in, key_in, value_in)], axis=1
        ),
        ((0, 0), (0, LANES - 3 * RANK)),
    )
    q_second = lax.dynamic_slice(query_out, (chosen * RANK, tp_rank * q_cols), (RANK, q_cols))
    k_second = lax.dynamic_slice(
        key_second_factor, (chosen * RANK, tp_rank * kv_cols), (RANK, kv_cols)
    )
    v_second = lax.dynamic_slice(
        value_second_factor, (chosen * RANK, tp_rank * kv_cols), (RANK, kv_cols)
    )
    second = jnp.concatenate(
        [
            jnp.pad(q_second, ((0, 0), (0, 2 * kv_cols))),
            jnp.pad(k_second, ((0, 0), (q_cols, kv_cols))),
            jnp.pad(v_second, ((0, 0), (q_cols + kv_cols, 0))),
            jnp.zeros((LANES - 3 * RANK, q_cols + 2 * kv_cols), BF16),
        ],
        axis=0,
    )
    o_first = jnp.pad(
        lax.dynamic_slice(out_in, (tp_rank * q_cols, chosen * RANK), (q_cols, RANK)),
        ((0, 0), (0, LANES - RANK)),
    )
    o_second = jnp.pad(take_set(out_out, chosen, 0), ((0, LANES - RANK), (0, 0)))

    (
        attended, queries, kv_parts, lora, middle, o_reduced, attention_weights,
        normed_all, *far_weights, upstream_all, routes_all, rows_all,
    ) = forward(
        tokens, (gain_one[None], gain_two[None]), attention_shard, first, second,
        o_first, o_second, cos, sin, codes, (w_gate, w_up, w_down), out_grad, routes.T,
        tp_count, ctx_count,
    )
    upstream_all = upstream_all.reshape(-1, model)
    rows_all = rows_all.reshape(-1, model)
    routes_all = routes_all.transpose(1, 0, 2).reshape(TOP, -1)

    tree_sets = lax.dynamic_slice_in_dim(adapter_set, fsdp_rank * trees, trees, 0)
    base = jnp.stack([ctx_rank * local_experts, fsdp_rank]).astype(jnp.int32)
    back, mixed, expert_part = run_experts(
        tree_sets,
        base,
        rows_all,
        upstream_all,
        routes_all,
        w_router.T,
        (w_gate, w_up, w_down, *far_weights),
        (gate_in, up_in, gate_out, up_out, down_in, down_out),
        slots,
        SPAN,
    )
    direct = ctx_count == SPAN
    if direct:
        back = back.reshape(ctx_count, tok_rows, -1)
        mixed = mixed.reshape(ctx_count, tok_rows, -1)
    else:
        back = lax.psum_scatter(back, "ctx", scatter_dimension=0, tiled=True)
        mixed = lax.psum_scatter(mixed, "ctx", scatter_dimension=0, tiled=True)
    output, input_grad, packed = backward(
        tokens, out_grad, routes, (gain_one[None], gain_two[None]),
        jnp.pad(w_router, ((0, 0), (0, LANES - experts))), middle, o_reduced, attention_weights,
        normed_all, lora, attended, queries, kv_parts, first, second, o_first, o_second,
        cos, sin, back, mixed, tp_count, ctx_count, experts, direct,
    )
    all_trees = fsdp_count * trees
    if not direct:
        mine = (jnp.arange(all_trees, dtype=jnp.int32) == tree_index)[:, None, None]
        packed = lax.psum(jnp.where(mine, packed, 0.0), ("fsdp", "ctx", "tp"))
    adapter_totals = place(
        adapter_set,
        packed,
        (
            query_in, query_out, key_in, key_second_factor, value_in, value_second_factor,
            out_in, out_out,
        ),
    )

    expert_part = lax.all_gather(lax.psum(expert_part, "tp"), "fsdp")
    expert_part = expert_part.reshape(all_trees, local_experts, 5 * RANK, model)
    expert_totals = place_experts(
        adapter_set, expert_part, (gate_in, gate_out, up_in, up_out, down_in, down_out)
    )
    return (output, input_grad, *adapter_totals, *expert_totals)


def solution(mesh):
    in_specs = (
        P(("fsdp", "ctx", "tp"), None),
        P(("fsdp", "ctx", "tp"), None),
        P(("fsdp", "ctx", "tp"), None),
        P(),
        P(),
        P(),
        P(),
        P("fsdp", "tp"),
        P("fsdp", "tp"),
        P("fsdp", "tp"),
        P("tp", "fsdp"),
        P(),
        P("ctx", "fsdp", None),
        P("ctx", "fsdp", None),
        P("ctx", "fsdp", None),
        P(),
        P(),
        P(),
        P(),
        P(),
        P(),
        P(),
        P(),
        P("ctx", None, None),
        P("ctx", None, None),
        P("ctx", None, None),
        P("ctx", None, None),
        P("ctx", None, None),
        P("ctx", None, None),
    )
    out_specs = (
        P(("fsdp", "ctx", "tp"), None),
        P(("fsdp", "ctx", "tp"), None),
        P(),
        P(),
        P(),
        P(),
        P(),
        P(),
        P(),
        P(),
        P("ctx", None, None),
        P("ctx", None, None),
        P("ctx", None, None),
        P("ctx", None, None),
        P("ctx", None, None),
        P("ctx", None, None),
    )
    return jax.shard_map(
        per_device, mesh=mesh, in_specs=in_specs, out_specs=out_specs, check_vma=False
    )
```

```python
import functools
import math

import jax
import jax.numpy as jnp
from jax import lax
from jax.experimental import pallas as pl
from jax.experimental.pallas import tpu as pltpu
from jax.sharding import PartitionSpec as P

HEAD = 64
TOP = 8
RANK = 16
SEG = 128
SEGS_DEV = 8
TREE_SEGS = 32
SPAN = TREE_SEGS // SEGS_DEV
LANES = 128

RESIDUAL_SCALE = 0.22
SCORE_SCALE = 0.015625
EPSILON = 1e-06
ROPE_BASE = 10000.0
MASKED = -1e30

F32 = jnp.float32
BF16 = jnp.bfloat16

CODE = HEAD
LSE = CODE + TREE_SEGS + 1
ONES = HEAD

VMEM_LIMIT = 56 * 1024 * 1024


def dot(a, b):
    return lax.dot_general(a, b, (((1,), (0,)), ((), ())), preferred_element_type=F32)


def dot_nt(a, b):
    return lax.dot_general(a, b, (((1,), (1,)), ((), ())), preferred_element_type=F32)


def dot_tn(a, b):
    return lax.dot_general(a, b, (((0,), (0,)), ((), ())), preferred_element_type=F32)


def iota(shape, dim):
    return lax.broadcasted_iota(jnp.int32, shape, dim)


def shifted(block, axis, distance):
    devices = range(lax.axis_size(axis))
    route = [(i - distance, i) for i in devices if i - distance in devices]
    return lax.ppermute(block, axis, route)


def rms_scale(values, gain_row):
    return (
        values * lax.rsqrt(jnp.mean(values * values, axis=-1, keepdims=True) + EPSILON) * gain_row
    )


def rms_back(values, gain_row, grad):
    inv = lax.rsqrt(jnp.mean(values * values, axis=-1, keepdims=True) + EPSILON)
    scaled = grad * gain_row
    inner = jnp.mean(scaled * values, axis=-1, keepdims=True)
    return inv * scaled - values * (inv * inv * inv * inner)


def tree_links(tree_parents):
    count = tree_parents.shape[0]
    columns = jnp.arange(count, dtype=jnp.int32)
    reach = (
        (tree_parents[:, None] == columns[None, :]) | (columns[:, None] == columns[None, :])
    ).astype(BF16)
    for _ in range(max(1, (count - 1).bit_length())):
        reach = jnp.minimum(dot(reach, reach), 1.0).astype(BF16)
    reach = reach.astype(F32)
    return reach, jnp.sum(reach, axis=1) - 1.0


def swap_halves(values):
    width = values.shape[-1]
    lane = iota(values.shape, 1) % HEAD
    ahead = pltpu.roll(values, width - HEAD // 2, 1)
    behind = pltpu.roll(values, HEAD // 2, 1)
    return jnp.where(lane < HEAD // 2, -ahead, behind)


def place_table(rows, source, target):
    r, c = iota((rows, LANES), 0), iota((rows, LANES), 1)
    return ((r - source == c - target) & (c >= target) & (c < target + HEAD)).astype(BF16)


def transfer_plan(local, tp_count):
    if local == 8 and tp_count % 2 == 0:
        return 5, 1, 1, 1
    return 0, local, 0, 0


def remote(src, dst, send, recv, where):
    return pltpu.make_async_remote_copy(
        src_ref=src,
        dst_ref=dst,
        send_sem=send,
        recv_sem=recv,
        device_id=where,
        device_id_type=pl.DeviceIdType.MESH,
    )


def far_moves(near, far, sems, pass_sems, shared, direct, first, land, other, tp):
    mate = {"tp": tp + 1 - 2 * lax.rem(tp, 2)}
    side = lax.rem(tp, 2)

    def piece(ref, rows, which):
        return ref.at[pl.ds(pl.multiple_of(which * rows, rows), rows)]

    def cross(n):
        moves = []
        for a, (source, target) in enumerate(zip(near, far)):
            src, dst = source.at[first + n], target.at[land + n]
            if n < shared:
                rows = src.shape[0] // 2
                src, dst = piece(src, rows, side), piece(dst, rows, side)
            moves.append(remote(src, dst, sems.at[0, n, a], sems.at[1, n, a], other))
        return moves

    def hand_on(n):
        moves = []
        for a, target in enumerate(far):
            dst = target.at[land + n]
            rows = dst.shape[0] // 2
            dst = piece(dst, rows, side)
            moves.append(remote(dst, dst, pass_sems.at[0, n, a], pass_sems.at[1, n, a], mate))
        return moves

    return cross, hand_on


def ring(me, step, count):
    return lax.rem(me + (step + count), count)


def aug_keys(kv, pair, pairs, first_seg, k_aug, v_aug, start):
    rows, width = kv.shape
    lane = iota((rows, LANES), 1)
    seg = first_seg + iota((rows, LANES), 0) // SEG
    key_code = ((lane - CODE == seg) | ((lane >= LSE) & (lane < LSE + 3))).astype(F32)
    one_code = ((lane == ONES) | (lane == ONES + 1)).astype(F32)
    span = pl.ds(start, rows)
    k_aug[pair, span, :] = (dot(kv, place_table(width, pair * HEAD, 0)) + key_code).astype(BF16)
    v_aug[pair, span, :] = (
        dot(kv, place_table(width, (pairs + pair) * HEAD, 0)) + one_code
    ).astype(BF16)


def forward_kernel(
    tokens, gain_one, gain_two, shard, first, second, o_first, o_second, cos, sin, codes,
    w_gate, w_up, w_down, grads, routes,
    att_out, q_out, kv_out, lora_out, middle_out, low_out, weights_out, normed_all,
    gate_far, up_far, down_far, grads_all, routes_all, rows_all,
    weights, q_aug, k_aug, v_aug, top, acc, parts, parts_in, rows_own,
    shard_sem, normed_sem, kv_sem, part_sem, far_sem, pass_far_sem, grads_sem, routes_sem, rows_sem,
    pass_sem, local_sem,
    *, tp_count, ctx_count, shared, straight,
):
    tp, ctx, fsdp = (lax.axis_index(name) for name in ("tp", "ctx", "fsdp"))
    rank = lax.rem(ctx, SPAN)
    block, model = tokens.shape
    heads = q_aug.shape[0]
    pairs = k_aug.shape[0]
    group = heads // pairs
    tall = group * block
    half = shard.shape[1]
    q_cols = heads * HEAD
    turn = cos.shape[1]
    chips = ctx_count // 2
    partner = ctx + 1 - 2 * lax.rem(ctx, 2)
    other = {"fsdp": 1 - fsdp}

    barrier = pltpu.get_barrier_semaphore()
    pl.semaphore_signal(barrier, 1, device_id=other, device_id_type=pl.DeviceIdType.MESH)
    for k in range(1, tp_count):
        pl.semaphore_signal(
            barrier, 1, device_id={"tp": ring(tp, k, tp_count)},
            device_id_type=pl.DeviceIdType.MESH,
        )
    for k in range(1, ctx_count):
        pl.semaphore_signal(
            barrier, 1, device_id={"ctx": ring(ctx, k, ctx_count)},
            device_id_type=pl.DeviceIdType.MESH,
        )
    pl.semaphore_wait(barrier, tp_count + ctx_count - 1)

    shard_copy = remote(shard, weights.at[fsdp], shard_sem.at[0], shard_sem.at[1], other)
    shard_copy.start()

    inputs = tokens[...].astype(F32)
    normed = rms_scale(inputs, gain_one[...]).astype(BF16)
    normed_all[tp] = normed

    def normed_copy(k):
        return remote(
            normed_all.at[tp], normed_all.at[tp], normed_sem.at[0, k - 1], normed_sem.at[1, k - 1],
            {"tp": ring(tp, k, tp_count)},
        )

    for k in range(1, tp_count):
        normed_copy(k).start()

    def side_copies(k):
        where = {"ctx": ring(ctx, k, ctx_count)}
        return (
            remote(grads, grads_all.at[ctx], grads_sem.at[0, k], grads_sem.at[1, k], where),
            remote(routes, routes_all.at[ctx], routes_sem.at[0, k], routes_sem.at[1, k], where),
        )

    own_copies = (
        pltpu.make_async_copy(grads, grads_all.at[ctx], local_sem.at[0]),
        pltpu.make_async_copy(routes, routes_all.at[ctx], local_sem.at[1]),
    )
    for copy in own_copies:
        copy.start()
    for k in range(1, ctx_count):
        for copy in side_copies(k):
            copy.start()

    weights[fsdp] = shard[...]
    shard_copy.wait()
    cross, hand_on = far_moves(
        (w_gate, w_up, w_down), (gate_far, up_far, down_far), far_sem, pass_far_sem,
        shared, straight, 0, 0, other, tp,
    )
    for n in range(shared + straight):
        for copy in cross(n):
            copy.start()

    def relay(n):
        if n < shared:
            for copy in cross(n):
                copy.wait_recv()
            for copy in hand_on(n):
                copy.start()

    weights_out[...] = weights[...]

    def kv_copy(distance, part):
        return remote(
            kv_out.at[0, part], kv_out.at[distance, part],
            kv_sem.at[0, distance - 1], kv_sem.at[1, distance - 1], {"ctx": ring(ctx, distance, ctx_count)},
        )

    @pl.loop(0, tp_count)
    def _(k):
        @pl.when(k > 0)
        def _():
            normed_copy(k).wait_recv()

        part = ring(tp, -k, tp_count)
        span = pl.ds(pl.multiple_of(part * block, block), block)
        rows = normed_all[part]
        lora = dot(rows, first[...]).astype(BF16)
        lora_out[span, :] = lora
        pre = (
            dot(rows[:, :half], weights[0, pl.ds(0, half), :])
            + dot(rows[:, half:], weights[1, pl.ds(0, half), :])
            + dot(lora, second[...])
        )
        turned = []
        for start in range(0, pre.shape[1] // 4 * 3, turn):
            piece = pre[:, start : start + turn]
            turned.append(piece * cos[span, :] + swap_halves(piece) * sin[span, :])
        queries = (
            jnp.concatenate(turned[: q_cols // turn], axis=1) * SCORE_SCALE
        ).astype(BF16)
        for head in range(heads):
            q_aug[head, span, :] = (
                dot(queries, place_table(q_cols, head * HEAD, 0)) + codes[span, :].astype(F32)
            ).astype(BF16)
        keys = jnp.concatenate(turned[q_cols // turn :], axis=1)
        kv = jnp.concatenate([keys, pre[:, q_cols + keys.shape[1] :]], axis=1).astype(BF16)
        kv_out[0, part] = kv
        for distance in range(1, SPAN):

            @pl.when(rank + distance < SPAN)
            def _(distance=distance):
                kv_copy(distance, part).start()

        for pair in range(pairs):
            aug_keys(
                kv, pair, pairs, rank * SEGS_DEV + part * (block // SEG), k_aug, v_aug,
                pl.multiple_of(part * block, block),
            )

    relay(0)

    def tile(part, pair, start, size, causal):
        index = part * pairs + pair
        rows = pl.ds(pl.multiple_of(part * block, block), block)
        queries = q_aug[pl.ds(pair * group, group), rows, :].reshape(tall, LANES)
        span = pl.ds(start, size)
        scores = dot_nt(queries, k_aug[pair, span, :])
        if causal:
            q_row = iota(scores.shape, 0) % block
            scores = jnp.where(iota(scores.shape, 1) <= q_row, scores, MASKED)
            now = jnp.broadcast_to(jnp.max(scores, axis=1, keepdims=True), (tall, LANES))
            probs = jnp.exp(scores - now[:, :1]).astype(BF16)
            acc[index] = dot(probs, v_aug[pair, span, :])
        else:
            before = top[index]
            now = jnp.maximum(before, jnp.max(scores, axis=1, keepdims=True))
            probs = jnp.exp(scores - now[:, :1]).astype(BF16)
            acc[index] = acc[index] * jnp.exp(before - now) + dot(probs, v_aug[pair, span, :])
        top[index] = now

    @pl.loop(0, tp_count * pairs)
    def _(index):
        part, pair = index // pairs, lax.rem(index, pairs)
        tile(part, pair, pl.multiple_of(part * block, block), block, True)

        @pl.loop(0, part)
        def _(j):
            tile(part, pair, pl.multiple_of(j * block, block), block, False)

    relay(1)
    group_rows = tp_count * block
    for distance in range(1, SPAN):

        @pl.when(distance <= rank)
        def _(distance=distance):
            remote(
                kv_out.at[0], kv_out.at[distance], kv_sem.at[0, distance - 1],
                kv_sem.at[1, distance - 1], {"ctx": ring(ctx, distance, ctx_count)},
            ).wait_recv()

            @pl.loop(0, tp_count)
            def _(part):
                kv = kv_out[distance, part]
                for pair in range(pairs):
                    aug_keys(
                        kv, pair, pairs,
                        (rank - distance) * SEGS_DEV + part * (block // SEG), k_aug, v_aug,
                        pl.multiple_of(distance * group_rows + part * block, block),
                    )

        @pl.when(distance > rank)
        def _(distance=distance):
            kv_out[distance] = jnp.zeros(kv_out.shape[1:], BF16)

    def part_copy(k):
        return remote(
            parts.at[k], parts_in.at[k], part_sem.at[0, k], part_sem.at[1, k],
            {"tp": ring(tp, k + 1, tp_count)},
        )

    @pl.loop(0, tp_count)
    def _(k):
        part = ring(tp, k + 1, tp_count)
        rows = pl.ds(pl.multiple_of(part * block, block), block)
        for pair in range(pairs):
            index = part * pairs + pair

            @pl.loop(1, rank + 1)
            def _(distance, pair=pair):
                tile(
                    part, pair, pl.multiple_of(distance * group_rows, group_rows), group_rows, False
                )

            summed = acc[index]
            total = summed[:, ONES : ONES + 1]
            result = (summed / total).astype(BF16)
            for member in range(group):
                head = pair * group + member
                att_out[rows, pl.ds(head * HEAD, HEAD)] = result[
                    member * block : (member + 1) * block, :HEAD
                ]
            minus = -(top[index] + jnp.log(total))
            high = minus.astype(BF16).astype(F32)
            middle = (minus - high).astype(BF16).astype(F32)
            lane = iota(minus.shape, 1)
            queries = q_aug[pl.ds(pair * group, group), rows, :].reshape(tall, LANES)
            coded = jnp.where(
                lane == LSE,
                high,
                jnp.where(
                    lane == LSE + 1,
                    middle,
                    jnp.where(lane == LSE + 2, minus - high - middle, queries.astype(F32)),
                ),
            )
            q_out[pl.ds(pair * group, group), rows, :] = coded.astype(BF16).reshape(
                group, block, LANES
            )
        mixed = att_out[rows, :]
        for side in range(2):
            parts[k, :, side * half : (side + 1) * half] = dot(
                mixed, weights[side, pl.ds(half, q_cols), :]
            ).astype(BF16)
        parts[k, :, model:] = dot(mixed, o_first[...]).astype(BF16)

        @pl.when(k < tp_count - 1)
        def _():
            part_copy(k).start()

        for n in range(2, shared):

            @pl.when(k == n - 1)
            def _(n=n):
                relay(n)

    summed = parts[tp_count - 1].astype(F32)
    for k in range(tp_count - 1):
        part_copy(k).wait_recv()
        summed += parts_in[k].astype(F32)
    low = summed[:, model:].astype(BF16)
    low_out[...] = low
    middle = inputs + RESIDUAL_SCALE * (summed[:, :model] + dot(low, o_second[...]))
    middle_out[...] = middle
    rows_own[...] = rms_scale(middle, gain_two[...]).astype(BF16)

    own_rows = pltpu.make_async_copy(rows_own, rows_all.at[ctx], local_sem.at[2])
    own_rows.start()
    to_partner = remote(
        rows_own, rows_all.at[ctx], rows_sem.at[0, 0], rows_sem.at[1, 0], {"ctx": partner}
    )
    to_partner.start()

    def rows_copy(k):
        return remote(
            rows_own, rows_all.at[ctx], rows_sem.at[0, k], rows_sem.at[1, k],
            {"ctx": ring(ctx, 2 * k, ctx_count)},
        )

    def pass_copy(k):
        source = ring(ctx, -2 * k, ctx_count)
        return remote(
            rows_all.at[source], rows_all.at[source], pass_sem.at[0, k], pass_sem.at[1, k],
            {"ctx": partner},
        )

    for k in range(1, chips):
        rows_copy(k).start()
    for k in range(1, chips):
        rows_copy(k).wait_recv()
        pass_copy(k).start()

    for k in range(1, tp_count):
        normed_copy(k).wait_send()
    for k in range(tp_count - 1):
        part_copy(k).wait_send()
    for distance in range(1, SPAN):

        @pl.when(rank + distance < SPAN)
        def _(distance=distance):
            remote(
                kv_out.at[0], kv_out.at[distance], kv_sem.at[0, distance - 1],
                kv_sem.at[1, distance - 1], {"ctx": ring(ctx, distance, ctx_count)},
            ).wait_send()

    for k in range(1, ctx_count):
        for copy in side_copies(k):
            copy.wait()
    for copy in own_copies:
        copy.wait()
    own_rows.wait()
    to_partner.wait()
    for k in range(1, chips):
        rows_copy(k).wait_send()
        pass_copy(k).wait()
    for n in range(shared + straight):
        for copy in cross(n):
            copy.wait_send()
            if n >= shared:
                copy.wait_recv()
    for n in range(shared):
        for copy in hand_on(n):
            copy.wait()


def forward(
    tokens, gains, shard, first, second, o_first, o_second, cos, sin, codes, weights, grads,
    routes, tp_count, ctx_count,
):
    block, model = tokens.shape
    rows = tp_count * block
    heads = o_first.shape[0] // HEAD
    cols = second.shape[1]
    kv_cols = cols - heads * HEAD
    pairs = kv_cols // (2 * HEAD)
    tall = heads // pairs * block
    chips = ctx_count // 2
    shared, straight, _, _ = transfer_plan(weights[0].shape[0], tp_count)
    vmem = pl.BlockSpec(memory_space=pltpu.VMEM)
    hbm = pl.BlockSpec(memory_space=pl.ANY)
    dma = pltpu.SemaphoreType.DMA
    part = (block, model + LANES)
    return pl.pallas_call(
        functools.partial(
            forward_kernel, tp_count=tp_count, ctx_count=ctx_count, shared=shared, straight=straight
        ),
        in_specs=[vmem] * 11 + [hbm] * 5,
        out_specs=[vmem] * 8 + [hbm] * 6,
        out_shape=[
            jax.ShapeDtypeStruct((rows, heads * HEAD), BF16),
            jax.ShapeDtypeStruct((heads, rows, LANES), BF16),
            jax.ShapeDtypeStruct((SPAN, tp_count, block, kv_cols), BF16),
            jax.ShapeDtypeStruct((rows, LANES), BF16),
            jax.ShapeDtypeStruct((block, model), F32),
            jax.ShapeDtypeStruct((block, LANES), BF16),
            jax.ShapeDtypeStruct((2,) + shard.shape, BF16),
            jax.ShapeDtypeStruct((tp_count, block, model), BF16),
            *[jax.ShapeDtypeStruct((shared + straight,) + w.shape[1:], BF16) for w in weights],
            jax.ShapeDtypeStruct((ctx_count,) + grads.shape, BF16),
            jax.ShapeDtypeStruct((ctx_count,) + routes.shape, jnp.int32),
            jax.ShapeDtypeStruct((ctx_count, block, model), BF16),
        ],
        scratch_shapes=[
            pltpu.VMEM((2,) + shard.shape, BF16),
            pltpu.VMEM((heads, rows, LANES), BF16),
            pltpu.VMEM((pairs, SPAN * rows, LANES), BF16),
            pltpu.VMEM((pairs, SPAN * rows, LANES), BF16),
            pltpu.VMEM((tp_count * pairs, tall, LANES), F32),
            pltpu.VMEM((tp_count * pairs, tall, LANES), F32),
            pltpu.VMEM((tp_count,) + part, BF16),
            pltpu.VMEM((tp_count - 1,) + part, BF16),
            pltpu.VMEM((block, model), BF16),
            dma((2,)),
            dma((2, tp_count - 1)),
            dma((2, SPAN - 1)),
            dma((2, tp_count - 1)),
            dma((2, shared + straight, 3)),
            dma((2, max(shared, 1), 3)),
            dma((2, ctx_count)),
            dma((2, ctx_count)),
            dma((2, chips)),
            dma((2, chips)),
            dma((3,)),
        ],
        compiler_params=pltpu.CompilerParams(
            vmem_limit_bytes=VMEM_LIMIT, collective_id=0, has_side_effects=True
        ),
        cost_estimate=pl.CostEstimate(
            flops=16 * SPAN * rows * rows * heads * LANES,
            bytes_accessed=32 * 1024 * 1024,
            transcendentals=0,
        ),
        name="forward",
    )(
        tokens, *gains, shard, first, second, o_first, o_second, cos, sin, codes, *weights,
        grads, routes,
    )


def joined(dk, dv, span):
    pairs = dk.shape[0]
    return jnp.concatenate(
        [dk[pair, span, :HEAD] for pair in range(pairs)]
        + [dv[pair, span, :HEAD] for pair in range(pairs)],
        axis=1,
    )


def backward_kernel(
    tokens, upstream_ref, routes, gain_one, gain_two, router, middle_ref, low_ref, weights,
    normed_all, lora, att, q_ref, kv_ref, first, second, o_first, o_second, cos, sin, back, mixed, shares,
    output, input_grad, packed_out, shares_out,
    k_aug, v_aug, up_aug, dk, dv, dq, branch_all, far_out, far_in, own_kv, parts, parts_in,
    second_acc, first_acc, o_in_acc, packed, ctx_in, tp_in, middle_grad,
    back_near, back_mine, back_pair, back_far, mixed_near, mixed_mine, mixed_pair, mixed_far,
    near_sem, mine_sem, far_sem, branch_sem, kv_sem, part_sem,
    ctx_sem, tp_sem, x_sem, tp_all_sem, ctx_all_sem, share_sem, swap_sem, own_sem,
    *, tp_count, ctx_count, experts, direct,
):
    tp, ctx, fsdp = (lax.axis_index(name) for name in ("tp", "ctx", "fsdp"))
    rank = lax.rem(ctx, SPAN)
    block, model = tokens.shape
    heads, rows_all, _ = q_ref.shape
    pairs = k_aug.shape[0]
    group = heads // pairs
    tall = group * block
    half = weights.shape[2]
    q_cols = heads * HEAD
    kv_cols = pairs * HEAD
    turn = cos.shape[1]
    partner = ctx + 1 - 2 * lax.rem(ctx, 2)
    cross = ring(ctx, 2, ctx_count)
    cross_partner = ring(partner, 2, ctx_count)
    other = {"fsdp": 1 - fsdp}

    barrier = pltpu.get_barrier_semaphore()
    pl.semaphore_signal(barrier, 1, device_id=other, device_id_type=pl.DeviceIdType.MESH)
    for k in range(1, tp_count):
        pl.semaphore_signal(
            barrier, 1, device_id={"tp": ring(tp, k, tp_count)},
            device_id_type=pl.DeviceIdType.MESH,
        )
    for k in range(1, ctx_count):
        pl.semaphore_signal(
            barrier, 1, device_id={"ctx": ring(ctx, k, ctx_count)},
            device_id_type=pl.DeviceIdType.MESH,
        )
    pl.semaphore_wait(barrier, tp_count + ctx_count - 1)

    sums = (
        (back, back_near, back_mine, back_pair, back_far),
        (mixed, mixed_near, mixed_mine, mixed_pair, mixed_far),
    )

    def near_copy(n, slot):
        source, near = sums[n][:2]
        return remote(
            source.at[(partner, cross_partner)[slot]], near.at[slot],
            near_sem.at[0, 2 * n + slot], near_sem.at[1, 2 * n + slot], {"ctx": partner},
        )

    def mine_copy(n, slot):
        return pltpu.make_async_copy(
            sums[n][0].at[(ctx, cross)[slot]], sums[n][2].at[slot], mine_sem.at[2 * n + slot]
        )

    def pair_copy(n):
        return remote(sums[n][3], sums[n][4], far_sem.at[0, n], far_sem.at[1, n], {"ctx": cross})

    def start_sum(n):
        for slot in (1, 0):
            near_copy(n, slot).start()
            mine_copy(n, slot).start()

    def pass_sum(n):
        near_copy(n, 1).wait_recv()
        mine_copy(n, 1).wait()
        _, near, mine, pair, _ = sums[n]
        pair[...] = (near[1].astype(F32) + mine[1].astype(F32)).astype(BF16)
        pair_copy(n).start()

    def end_sum(n):
        near_copy(n, 0).wait_recv()
        mine_copy(n, 0).wait()
        pair_copy(n).wait_recv()
        _, near, mine, _, far = sums[n]
        return near[0].astype(F32) + mine[0].astype(F32) + far[...].astype(F32)

    if direct:
        share = shares.shape[2]
        own_lanes = pl.ds(pl.multiple_of(tp * share, share), share)

        def share_copy(k):
            return remote(
                shares, shares_out.at[fsdp, :, :, own_lanes],
                share_sem.at[0, k - 1], share_sem.at[1, k - 1], {"tp": ring(tp, k, tp_count)},
            )

        share_own = pltpu.make_async_copy(shares, shares_out.at[fsdp, :, :, own_lanes], own_sem.at[0])
        swap = remote(
            shares_out.at[fsdp], shares_out.at[fsdp], swap_sem.at[0], swap_sem.at[1], other
        )

        start_sum(0)
        start_sum(1)
        share_own.start()
        for k in range(1, tp_count):
            share_copy(k).start()

    @pl.loop(0, rank + 1)
    def _(distance):
        @pl.loop(0, tp_count)
        def _(part):
            kv = kv_ref[distance, part]
            for pair in range(pairs):
                aug_keys(
                    kv, pair, pairs, (rank - distance) * SEGS_DEV + part * (block // SEG),
                    k_aug, v_aug, pl.multiple_of(distance * rows_all + part * block, block),
                )

    dk[...] = jnp.zeros(dk.shape, F32)
    dv[...] = jnp.zeros(dv.shape, F32)
    dq[...] = jnp.zeros(dq.shape, F32)
    second_acc[...] = jnp.zeros(second_acc.shape, F32)
    first_acc[...] = jnp.zeros(first_acc.shape, F32)
    o_in_acc[...] = jnp.zeros(o_in_acc.shape, F32)
    packed[...] = jnp.zeros(packed.shape, F32)

    middle = middle_ref[...]
    normed_two = rms_scale(middle, gain_two[...]).astype(BF16)
    logits = dot(normed_two, router[...])
    number = iota((block, LANES), 1)
    hit = jnp.zeros((block, LANES), F32)
    for k in range(routes.shape[1]):
        hit += (routes[:, k : k + 1] == number).astype(F32)
    kept = jnp.where(hit > 0.5, logits, MASKED)
    gates = jnp.exp(kept - jnp.max(kept, axis=1, keepdims=True)) * hit
    gates = gates / jnp.sum(gates, axis=1, keepdims=True)

    if direct:
        pass_sum(0)
        back_sum = end_sum(0)
    else:
        back_sum = back[...].astype(F32)
    table = back_sum[:, model:]
    slopes = table + pltpu.roll(table, LANES - experts, 1)
    logits_grad = gates * (slopes - jnp.sum(gates * slopes, axis=1, keepdims=True))
    high = logits_grad.astype(BF16)
    low = (logits_grad - high.astype(F32)).astype(BF16)
    normed_two_grad = back_sum[:, :model] + dot_nt(high, router[...]) + dot_nt(low, router[...])
    middle_grad[...] = upstream_ref[...].astype(F32) + rms_back(
        middle, gain_two[...], normed_two_grad
    )
    branch = (RESIDUAL_SCALE * middle_grad[...]).astype(BF16)
    branch_all[tp] = branch

    def branch_copy(k):
        return remote(
            branch_all.at[tp], branch_all.at[tp], branch_sem.at[0, k - 1], branch_sem.at[1, k - 1],
            {"tp": ring(tp, k, tp_count)},
        )

    for k in range(1, tp_count):
        branch_copy(k).start()
    packed[pl.ds(4 * RANK, RANK), :] = dot_tn(low_ref[...], branch)[:RANK]
    if direct:
        pass_sum(1)

    wide = heads * LANES
    r, c = iota((q_cols, wide), 0), iota((q_cols, wide), 1)
    same = r // HEAD == c // LANES
    place = (same & (r % HEAD == c % LANES)).astype(BF16)
    spread = (same & (c % LANES >= ONES) & (c % LANES < ONES + 2)).astype(BF16)

    def tile(part, pair, start, size, causal):
        index = part * pairs + pair
        rows = pl.ds(pl.multiple_of(part * block, block), block)
        queries = q_ref[pl.ds(pair * group, group), rows, :].reshape(tall, LANES)
        upstream = up_aug[pl.ds(pair * group, group), rows, :].reshape(tall, LANES)
        span = pl.ds(start, size)
        keys = k_aug[pair, span, :]
        probs = jnp.exp(dot_nt(keys, queries))
        if causal:
            q_row = iota(probs.shape, 1) % block
            probs = jnp.where(iota(probs.shape, 0) <= q_row, probs, 0.0)
        steep = (probs * dot_nt(v_aug[pair, span, :], upstream)).astype(BF16)
        dv[pair, span, :] += dot(probs.astype(BF16), upstream)
        dk[pair, span, :] += dot(steep, queries)
        dq[index] += dot_tn(steep, keys)

    @pl.loop(0, tp_count)
    def _(k):
        @pl.when(k > 0)
        def _():
            branch_copy(k).wait_recv()

        part = ring(tp, -k, tp_count)
        rows = pl.ds(pl.multiple_of(part * block, block), block)
        low_grad = dot_nt(branch_all[part], o_second[...]).astype(BF16)
        grads = dot_nt(low_grad, o_first[...])
        for side in range(2):
            grads += dot_nt(
                branch_all[part, :, side * half : (side + 1) * half],
                weights[side, pl.ds(half, q_cols), :],
            )
        grads = grads.astype(BF16)
        mixed_heads = att[rows, :]
        o_in_acc[...] += dot_tn(low_grad, mixed_heads)
        product = grads.astype(F32) * mixed_heads.astype(F32)
        minus = jnp.zeros((block, wide), F32)
        for _ in range(3):
            piece = product.astype(BF16)
            minus -= dot(piece, spread)
            product -= piece.astype(F32)
        top = minus.astype(BF16).astype(F32)
        lane = iota(minus.shape, 1) % LANES
        coded = dot(grads, place) + jnp.where(
            lane == ONES, top, jnp.where(lane == ONES + 1, minus - top, 0.0)
        )
        for head in range(heads):
            up_aug[head, rows, :] = coded[:, head * LANES : (head + 1) * LANES].astype(BF16)

        @pl.loop(0, pairs)
        def _(pair):
            tile(part, pair, pl.multiple_of(part * block, block), block, True)

            @pl.loop(0, part)
            def _(j):
                tile(part, pair, pl.multiple_of(j * block, block), block, False)

    def far_copy(distance):
        return remote(
            far_out.at[distance - 1], far_in.at[distance - 1],
            kv_sem.at[0, distance - 1], kv_sem.at[1, distance - 1],
            {"ctx": ring(ctx, -distance, ctx_count)},
        )

    size = min(rows_all, 512)

    @pl.loop(0, rank)
    def _(step):
        distance = rank - step
        start = distance * rows_all

        @pl.loop(0, tp_count * pairs * (rows_all // size))
        def _(n):
            index, piece = n // (rows_all // size), lax.rem(n, rows_all // size)
            tile(
                index // pairs, lax.rem(index, pairs),
                pl.multiple_of(start + piece * size, size), size, False,
            )

        @pl.loop(0, tp_count)
        def _(part):
            span = pl.ds(pl.multiple_of(start + part * block, block), block)
            far_out[distance - 1, pl.ds(pl.multiple_of(part * block, block), block), :] = joined(
                dk, dv, span
            ).astype(BF16)

        far_copy(distance).start()

    if direct:
        share_own.wait()
        for k in range(1, tp_count):
            share_copy(k).wait()
        swap.start()

    own_kv[...] = joined(dk, dv, pl.ds(0, rows_all))
    for distance in range(1, SPAN):

        @pl.when(rank + distance < SPAN)
        def _(distance=distance):
            far_copy(distance).wait_recv()
            own_kv[...] += far_in[distance - 1].astype(F32)

    def part_copy(k):
        return remote(
            parts.at[k], parts_in.at[k], part_sem.at[0, k], part_sem.at[1, k],
            {"tp": ring(tp, k + 1, tp_count)},
        )

    @pl.loop(0, tp_count)
    def _(k):
        part = ring(tp, k + 1, tp_count)
        rows = pl.ds(pl.multiple_of(part * block, block), block)
        pieces = []
        for pair in range(pairs):
            held = dq[part * pairs + pair]
            turned = SCORE_SCALE * jnp.concatenate(
                [held[member * block : (member + 1) * block, :HEAD] for member in range(group)],
                axis=1,
            )
            pieces.append(turned * cos[rows, :] - swap_halves(turned) * sin[rows, :])
        keys = own_kv[rows, :kv_cols]
        pieces.append(keys * cos[rows, :] - swap_halves(keys) * sin[rows, :])
        pieces.append(own_kv[rows, kv_cols:])
        grads = jnp.concatenate(pieces, axis=1).astype(BF16)
        for side in range(2):
            parts[k, :, side * half : (side + 1) * half] = dot_nt(
                grads, weights[side, pl.ds(0, half), :]
            ).astype(BF16)
        low_part = dot_nt(grads, second[...]).astype(BF16)
        parts[k, :, model:] = low_part

        @pl.when(k < tp_count - 1)
        def _():
            part_copy(k).start()

        second_acc[...] += dot_tn(lora[rows, :], grads)
        first_acc[...] += dot_tn(low_part, normed_all[part])

    packed[pl.ds(0, 3 * RANK), :] = first_acc[pl.ds(0, 3 * RANK), :]
    lanes = pl.ds(pl.multiple_of(tp * q_cols, q_cols), q_cols)
    packed[pl.ds(3 * RANK, RANK), lanes] = o_in_acc[pl.ds(0, RANK), :]
    packed[pl.ds(5 * RANK, RANK), lanes] = second_acc[pl.ds(0, RANK), :q_cols]
    lanes = pl.ds(pl.multiple_of(tp * kv_cols, kv_cols), kv_cols)
    packed[pl.ds(6 * RANK, RANK), lanes] = second_acc[pl.ds(RANK, RANK), q_cols : q_cols + kv_cols]
    lanes = pl.ds(pl.multiple_of(model // 2 + tp * kv_cols, kv_cols), kv_cols)
    packed[pl.ds(6 * RANK, RANK), lanes] = second_acc[pl.ds(2 * RANK, RANK), q_cols + kv_cols :]

    if direct:
        tall_rows, few_rows = packed.shape[0] // ctx_count, packed.shape[0] // (ctx_count * tp_count)

        def ctx_rows(index):
            return pl.ds(pl.multiple_of(index * tall_rows, tall_rows), tall_rows)

        def tp_rows(index):
            start = ctx * tall_rows + index * few_rows
            return pl.ds(pl.multiple_of(start, few_rows), few_rows)

        def ctx_copy(k):
            where = ring(ctx, k, ctx_count)
            return remote(
                packed.at[ctx_rows(where)], ctx_in.at[k - 1],
                ctx_sem.at[0, k - 1], ctx_sem.at[1, k - 1], {"ctx": where},
            )

        def tp_copy(k):
            where = ring(tp, k, tp_count)
            return remote(
                packed.at[tp_rows(where)], tp_in.at[k - 1],
                tp_sem.at[0, k - 1], tp_sem.at[1, k - 1], {"tp": where},
            )

        x_copy = remote(
            packed_out.at[fsdp, tp_rows(tp)], packed_out.at[fsdp, tp_rows(tp)],
            x_sem.at[0], x_sem.at[1], other,
        )

        def tp_all_copy(k):
            return remote(
                packed_out.at[:, tp_rows(tp)], packed_out.at[:, tp_rows(tp)],
                tp_all_sem.at[0, k - 1], tp_all_sem.at[1, k - 1], {"tp": ring(tp, k, tp_count)},
            )

        def ctx_all_copy(k):
            return remote(
                packed_out.at[:, ctx_rows(ctx)], packed_out.at[:, ctx_rows(ctx)],
                ctx_all_sem.at[0, k - 1], ctx_all_sem.at[1, k - 1],
                {"ctx": ring(ctx, k, ctx_count)},
            )

        for k in range(1, ctx_count):
            ctx_copy(k).start()
        for k in range(1, ctx_count):
            ctx_copy(k).wait()
        packed[ctx_rows(ctx), :] = packed[ctx_rows(ctx), :] + sum(
            ctx_in[k] for k in range(ctx_count - 1)
        )
        for k in range(1, tp_count):
            tp_copy(k).start()
        for k in range(1, tp_count):
            tp_copy(k).wait()
        packed_out[fsdp, tp_rows(tp), :] = packed[tp_rows(tp), :] + sum(
            tp_in[k] for k in range(tp_count - 1)
        )
        x_copy.start()
        x_copy.wait()
        for k in range(1, tp_count):
            tp_all_copy(k).start()
        for k in range(1, tp_count):
            tp_all_copy(k).wait()
        for k in range(1, ctx_count):
            ctx_all_copy(k).start()
    else:
        packed_out[0] = packed[...]

    summed = parts[tp_count - 1].astype(F32)
    for k in range(tp_count - 1):
        part_copy(k).wait_recv()
        summed += parts_in[k].astype(F32)
    normed_grad = summed[:, :model] + dot_nt(summed[:, model:].astype(BF16), first[...])
    inputs = tokens[...].astype(F32)
    input_grad[...] = (
        middle_grad[...] + rms_back(inputs, gain_one[...], normed_grad)
    ).astype(BF16)
    mixture = end_sum(1) if direct else mixed[...].astype(F32)
    output[...] = (middle_ref[...] + RESIDUAL_SCALE * mixture).astype(BF16)

    if direct:
        swap.wait()
        for k in range(1, ctx_count):
            ctx_all_copy(k).wait()
        for n in range(2):
            for slot in range(2):
                near_copy(n, slot).wait_send()
            pair_copy(n).wait_send()
    for k in range(1, tp_count):
        branch_copy(k).wait_send()
    for k in range(tp_count - 1):
        part_copy(k).wait_send()
    for distance in range(1, SPAN):

        @pl.when(distance <= rank)
        def _(distance=distance):
            far_copy(distance).wait_send()


def backward(
    tokens, upstream, routes, gains, router, middle, low, weights, normed, lora, att, queries, kv,
    first, second, o_first, o_second, cos, sin, back, mixed, shares, tp_count, ctx_count, experts, direct,
):
    block, model = tokens.shape
    heads, rows, _ = queries.shape
    pairs = kv.shape[3] // (2 * HEAD)
    tall = heads // pairs * block
    cols = second.shape[1]
    kv_width = kv.shape[3]
    vmem = pl.BlockSpec(memory_space=pltpu.VMEM)
    hbm = pl.BlockSpec(memory_space=pl.ANY)
    dma = pltpu.SemaphoreType.DMA
    part = (block, model + LANES)
    packed = (8 * RANK, model)
    copies = 2 if direct else 1
    slim = (8, LANES)

    def buffers(width):
        shapes = [(2, block, width), (2, block, width), (block, width), (block, width)]
        return [pltpu.VMEM(shape if direct else slim, BF16) for shape in shapes]

    return pl.pallas_call(
        functools.partial(
            backward_kernel, tp_count=tp_count, ctx_count=ctx_count, experts=experts, direct=direct
        ),
        in_specs=[vmem] * 20 + [hbm if direct else vmem] * 2 + [hbm],
        out_specs=[vmem] * 3 + [hbm],
        out_shape=[
            jax.ShapeDtypeStruct((block, model), BF16),
            jax.ShapeDtypeStruct((block, model), BF16),
            jax.ShapeDtypeStruct((copies,) + packed, F32),
            jax.ShapeDtypeStruct(
                (2,) + shares.shape[:2] + (tp_count * shares.shape[2],) if direct else slim, BF16
            ),
        ],
        scratch_shapes=[
            pltpu.VMEM((pairs, SPAN * rows, LANES), BF16),
            pltpu.VMEM((pairs, SPAN * rows, LANES), BF16),
            pltpu.VMEM((heads, rows, LANES), BF16),
            pltpu.VMEM((pairs, SPAN * rows, LANES), F32),
            pltpu.VMEM((pairs, SPAN * rows, LANES), F32),
            pltpu.VMEM((tp_count * pairs, tall, LANES), F32),
            pltpu.VMEM((tp_count, block, model), BF16),
            pltpu.VMEM((SPAN - 1, rows, kv_width), BF16),
            pltpu.VMEM((SPAN - 1, rows, kv_width), BF16),
            pltpu.VMEM((rows, kv_width), F32),
            pltpu.VMEM((tp_count,) + part, BF16),
            pltpu.VMEM((tp_count - 1,) + part, BF16),
            pltpu.VMEM((LANES, cols), F32),
            pltpu.VMEM((LANES, model), F32),
            pltpu.VMEM((LANES, heads * HEAD), F32),
            pltpu.VMEM(packed, F32),
            pltpu.VMEM((ctx_count - 1, packed[0] // ctx_count, model) if direct else slim, F32),
            pltpu.VMEM((tp_count - 1, 8, model) if direct else slim, F32),
            pltpu.VMEM((block, model), F32),
            *buffers(model + LANES),
            *buffers(model),
            dma((2, 4)),
            dma((4,)),
            dma((2, 2)),
            dma((2, tp_count - 1)),
            dma((2, SPAN - 1)),
            dma((2, tp_count - 1)),
            dma((2, ctx_count - 1)),
            dma((2, tp_count - 1)),
            dma((2,)),
            dma((2, tp_count - 1)),
            dma((2, ctx_count - 1)),
            dma((2, tp_count - 1)),
            dma((2,)),
            dma((1,)),
        ],
        compiler_params=pltpu.CompilerParams(
            vmem_limit_bytes=60 * 1024 * 1024, collective_id=1, has_side_effects=True
        ),
        cost_estimate=pl.CostEstimate(
            flops=32 * SPAN * rows * rows * heads * LANES,
            bytes_accessed=32 * 1024 * 1024,
            transcendentals=0,
        ),
        name="backward",
    )(
        tokens, upstream, routes, *gains, router, middle, low, weights, normed, lora, att, queries,
        kv, first, second, o_first, o_second, cos, sin, back, mixed, shares,
    )


def columns_of(chosen):
    return iota((RANK, LANES), 1) == iota((RANK, LANES), 0) + chosen * RANK


def place_kernel(sets, packed, *outs):
    query_in, query_out, key_in, key_out, value_in, value_out, out_in, out_out = outs
    kv_cols = key_out.shape[1]
    exact = dict(precision=lax.Precision.HIGHEST, preferred_element_type=F32)

    def gathered(rows, lanes, turned):
        total = None
        for tree in range(packed.shape[0]):
            spots = columns_of(sets[tree]).astype(F32)
            piece = packed[tree, rows * RANK : (rows + 1) * RANK, lanes]
            pair = (piece, spots) if turned else (spots, piece)
            term = lax.dot_general(*pair, (((0,), (0,)), ((), ())), **exact)
            total = term if total is None else total + term
        return total

    whole = slice(None)
    query_in[...] = gathered(0, whole, True)
    key_in[...] = gathered(1, whole, True)
    value_in[...] = gathered(2, whole, True)
    out_in[...] = gathered(3, whole, True)
    out_out[...] = gathered(4, whole, False)
    query_out[...] = gathered(5, whole, False)
    key_out[...] = gathered(6, slice(0, kv_cols), False)
    value_out[...] = gathered(6, slice(kv_cols, 2 * kv_cols), False)


def place(sets, packed, outs):
    vmem = pl.BlockSpec(memory_space=pltpu.VMEM)
    return pl.pallas_call(
        place_kernel,
        in_specs=[pl.BlockSpec(memory_space=pltpu.SMEM), vmem],
        out_specs=[vmem] * len(outs),
        out_shape=[jax.ShapeDtypeStruct(o.shape, F32) for o in outs],
        compiler_params=pltpu.CompilerParams(vmem_limit_bytes=VMEM_LIMIT),
        name="place",
    )(sets, packed)


def place_experts_kernel(sets, part, gate_in, gate_out, up_in, up_out, down_in, down_out):
    hidden = gate_out.shape[2]

    def gathered(rows, lanes, turned):
        total = None
        for tree in range(part.shape[0]):
            spots = columns_of(sets[tree]).astype(BF16)
            piece = part[tree, 0, rows * RANK : (rows + 1) * RANK, lanes]
            term = dot_tn(piece, spots) if turned else dot_tn(spots, piece)
            total = term if total is None else total + term
        return total

    whole, left, right = slice(None), slice(0, hidden), slice(hidden, 2 * hidden)
    gate_in[0] = gathered(0, whole, True)
    up_in[0] = gathered(1, whole, True)
    gate_out[0] = gathered(2, left, False)
    up_out[0] = gathered(2, right, False)
    down_out[0] = gathered(3, whole, False)
    down_in[0] = gathered(4, left, True)


def place_experts(sets, part, outs):
    trees, local = part.shape[:2]
    return pl.pallas_call(
        place_experts_kernel,
        grid_spec=pltpu.PrefetchScalarGridSpec(
            num_scalar_prefetch=1,
            grid=(local,),
            in_specs=[pl.BlockSpec((trees, 1) + part.shape[2:], lambda e, s: (0, e, 0, 0))],
            out_specs=[pl.BlockSpec((1,) + o.shape[1:], lambda e, s: (e, 0, 0)) for o in outs],
        ),
        out_shape=[jax.ShapeDtypeStruct(o.shape, F32) for o in outs],
        compiler_params=pltpu.CompilerParams(vmem_limit_bytes=VMEM_LIMIT),
        name="place_experts",
    )(sets, part)


def expert_kernel(
    sets, x_ref, g_ref, routes, router,
    w_gate, w_up, w_down, w_gate_far, w_up_far, w_down_far, all_gate, all_up, all_down, gate_in, up_in, gate_out, up_out, down_in, down_out,
    back_out, mixed_out, grad_out,
    rank_rows, gate_rows, slope_rows, mix, back, xs, firsts, tall_grad,
    gate_full, up_full, down_full, land_gate, land_up, land_down, grads, grads_in,
    far_sem, pass_far_sem, grads_sem, arrive_sem,
    *, slots, sources, early, shared, straight, tp_count,
):
    chunk, expert = pl.program_id(0), pl.program_id(1)
    tp, fsdp = lax.axis_index("tp"), lax.axis_index("fsdp")
    late = shared + straight
    gather = late > 0
    other = {"fsdp": 1 - fsdp}
    cross, hand_on = far_moves(
        (all_gate, all_up, all_down), (land_gate, land_up, land_down), far_sem, pass_far_sem,
        shared, straight, early, 0, other, tp,
    )

    if gather:

        @pl.when(expert == 0)
        def _():
            barrier = pltpu.get_barrier_semaphore()
            pl.semaphore_signal(
                barrier, 1, device_id=other, device_id_type=pl.DeviceIdType.MESH
            )
            for k in range(1, tp_count):
                pl.semaphore_signal(
                    barrier, 1, device_id={"tp": ring(tp, k, tp_count)},
                    device_id_type=pl.DeviceIdType.MESH,
                )
            pl.semaphore_wait(barrier, tp_count)
            for n in range(late):
                for copy in cross(n):
                    copy.start()

        for n in range(shared):

            @pl.when(expert == 2 + n)
            def _(n=n):
                for copy in cross(n):
                    copy.wait_recv()
                for copy in hand_on(n):
                    copy.start()

        for n in range(late):

            @pl.when(expert == early + n)
            def _(n=n):
                for copy in hand_on(n) if n < shared else cross(n):
                    copy.wait_recv()

    experts = router.shape[0]
    tokens, model = x_ref.shape
    each = tokens // sources
    hidden = w_gate.shape[2]
    lanes = gate_in.shape[2]
    chosen = sets[chunk]

    @pl.when(expert == 0)
    def _():
        logits = dot_nt(router[...], x_ref[...])
        number = iota((experts, tokens), 0)
        hit = jnp.zeros((experts, tokens), F32)
        for k in range(routes.shape[0]):
            hit += (routes[k : k + 1, :] == number).astype(F32)
        kept = jnp.where(hit > 0.5, logits, MASKED)
        weights = jnp.exp(kept - jnp.max(kept, axis=0, keepdims=True)) * hit
        gate_rows[...] = weights / jnp.sum(weights, axis=0, keepdims=True)
        earlier = (iota((each, each), 0) < iota((each, each), 1)).astype(BF16)
        for s in range(sources):
            span = slice(s * each, (s + 1) * each)
            order = dot(hit[:, span].astype(BF16), earlier)
            rank_rows[:, span] = jnp.where(hit[:, span] > 0.5, order, -1.0)
        mix[...] = jnp.zeros(mix.shape, F32)
        back[...] = jnp.zeros(back.shape, F32)
        slope_rows[...] = jnp.zeros(slope_rows.shape, F32)

    first_row = lax.axis_index("ctx") * pl.num_programs(1)
    row = first_row + expert
    ranks = rank_rows[pl.ds(row, 1), :]
    gates = gate_rows[pl.ds(row, 1), :]
    slot_number = iota((slots, each), 0).astype(F32)
    picks, columns, upstreams = [], [], []
    for s in range(sources):
        span = slice(s * each, (s + 1) * each)
        pick = ranks[:, span] == slot_number
        columns.append(jnp.sum(jnp.where(pick, gates[:, span], 0.0), axis=1, keepdims=True))
        pick = pick.astype(BF16)
        picks.append(pick)
        xs[pl.ds(s * slots, slots), :] = dot(pick, x_ref[pl.ds(s * each, each), :]).astype(BF16)
        upstreams.append(dot(pick, g_ref[pl.ds(s * each, each), :]))
    gate_column = jnp.concatenate(columns, axis=0)
    upstream = RESIDUAL_SCALE * jnp.concatenate(upstreams, axis=0)

    firsts[:, :lanes] = gate_in[0]
    firsts[:, lanes:] = up_in[0]
    keep = (iota((1, 2 * lanes), 1) % lanes // RANK == chosen).astype(BF16)
    rows = xs[...]
    inner = dot(rows, firsts[...]).astype(BF16) * keep
    for full, near, far, landed in (
        (gate_full, w_gate, w_gate_far, land_gate),
        (up_full, w_up, w_up_far, land_up),
        (down_full, w_down, w_down_far, land_down),
    ):
        size = near.shape[1]
        full[pl.ds(pl.multiple_of(fsdp * size, size), size), :] = near[0]
        spot = pl.ds(pl.multiple_of((1 - fsdp) * size, size), size)
        if not gather:
            full[spot, :] = far[0]
            continue

        @pl.when(expert < early)
        def _(full=full, far=far, spot=spot):
            full[spot, :] = far[0]

        @pl.when(expert >= early)
        def _(full=full, landed=landed, spot=spot):
            full[spot, :] = landed[jnp.maximum(expert - early, 0)]
    gate_value = dot(rows, gate_full[...]) + dot(inner[:, :lanes], gate_out[0])
    up_value = dot(rows, up_full[...]) + dot(inner[:, lanes:], up_out[0])
    sigmoid = 1.0 / (1.0 + jnp.exp(-gate_value))
    silu = gate_value * sigmoid
    active = (silu * up_value).astype(BF16)
    down_inner = dot(active, down_in[0]).astype(BF16) * keep[:, :lanes]
    produced = (
        (dot(active, down_full[...]) + dot(down_inner, down_out[0])).astype(BF16).astype(F32)
    )
    slope = jnp.sum(upstream * produced, axis=1, keepdims=True)
    sent = (gate_column * produced).astype(BF16)
    slot_grad = (gate_column * upstream).astype(BF16)

    down_inner_grad = dot_nt(slot_grad, down_out[0]).astype(BF16) * keep[:, :lanes]
    active_grad = (
        (dot_nt(slot_grad, down_full[...]) + dot_nt(down_inner_grad, down_in[0]))
        .astype(BF16)
        .astype(F32)
    )
    gate_grad = (active_grad * up_value * (sigmoid + silu * (1.0 - sigmoid))).astype(BF16)
    up_grad = (active_grad * silu).astype(BF16)
    inner_grad = (
        jnp.concatenate([dot_nt(gate_grad, gate_out[0]), dot_nt(up_grad, up_out[0])], axis=1)
    ).astype(BF16) * keep
    row_grad = (
        dot_nt(gate_grad, gate_full[...])
        + dot_nt(up_grad, up_full[...])
        + dot_nt(inner_grad, firsts[...])
    ).astype(BF16)

    for s in range(sources):
        span = slice(s * slots, (s + 1) * slots)
        spot = pl.ds(s * each, each)
        mix[spot, :] += dot_tn(picks[s], sent[span, :])
        back[spot, :] += dot_tn(picks[s], row_grad[span, :])
        slope_rows[pl.ds(expert, 1), spot] = jnp.sum(
            jnp.where(picks[s] > 0.5, slope[span, :], 0.0), axis=0, keepdims=True
        )

    keep_at = expert if gather else 0

    def folded(start, width):
        total = tall_grad[pl.ds(start, RANK), :width]
        for shift in range(RANK, lanes, RANK):
            total += tall_grad[pl.ds(start + shift, RANK), :width]
        return total.astype(BF16)

    tall_grad[...] = dot_tn(inner_grad, rows)
    grads[keep_at, pl.ds(0, RANK), :] = folded(0, model)
    grads[keep_at, pl.ds(RANK, RANK), :] = folded(lanes, model)
    tall_grad[pl.ds(0, lanes), :hidden] = dot_tn(inner[:, :lanes], gate_grad)
    tall_grad[pl.ds(0, lanes), hidden:] = dot_tn(inner[:, lanes:], up_grad)
    grads[keep_at, pl.ds(2 * RANK, RANK), :] = folded(0, model)
    tall_grad[pl.ds(0, lanes), :] = dot_tn(down_inner, slot_grad)
    grads[keep_at, pl.ds(3 * RANK, RANK), :] = folded(0, model)
    tall_grad[pl.ds(0, lanes), :hidden] = dot_tn(down_inner_grad, active)
    grads[keep_at, pl.ds(4 * RANK, RANK), :hidden] = folded(0, hidden)
    grads[keep_at, pl.ds(4 * RANK, RANK), hidden:] = jnp.zeros((RANK, model - hidden), BF16)

    share = tall_grad.shape[1] // tp_count

    def grads_copy(n, k):
        where = ring(tp, k, tp_count)
        lanes = pl.ds(pl.multiple_of(where * share, share), share)
        return remote(
            grads.at[n, :, lanes], grads_in.at[k - 1, n], grads_sem.at[k - 1, n],
            arrive_sem.at[k - 1, n], {"tp": where},
        )

    if gather:
        for k in range(1, tp_count):
            grads_copy(expert, k).start()
    else:
        grad_out[0, 0] = grads[0]

    if gather:

        @pl.when(expert == pl.num_programs(1) - 1)
        def _():
            for n in range(late):
                for copy in cross(n):
                    copy.wait_send()
            for n in range(shared):
                for copy in hand_on(n):
                    copy.wait_send()

            @pl.loop(0, pl.num_programs(1))
            def _(n):
                lanes = pl.ds(pl.multiple_of(tp * share, share), share)
                total = grads[n, :, lanes].astype(F32)
                for k in range(1, tp_count):
                    grads_copy(n, k).wait()
                    total += grads_in[k - 1, n].astype(F32)
                grad_out[n] = total.astype(BF16)

    @pl.when(expert == pl.num_programs(1) - 1)
    def _():
        mixed_out[...] = mix[...].astype(BF16)
        back_out[:, :model] = back[...].astype(BF16)
        turned = slope_rows[...].T
        high = turned.astype(BF16)
        low = (turned - high.astype(F32)).astype(BF16)
        local, lane = iota((LANES, LANES), 0), iota((LANES, LANES), 1)
        inside = local < pl.num_programs(1)
        first = (inside & (lane == local + first_row)).astype(BF16)
        later = (inside & (lane == local + first_row + experts)).astype(BF16)
        back_out[:, model:] = (dot(high, first) + dot(low, later)).astype(BF16)


def run_experts(
    sets, rows, upstream, routes, router, weights, far, adapters, slots, sources, tp_count
):
    total, model = rows.shape
    experts = router.shape[0]
    local, half, hidden = weights[0].shape
    trees = sets.shape[0]
    tokens = total // trees
    lanes = adapters[0].shape[2]
    tall = sources * slots
    piece = lambda c, e, *_: (c, 0)
    fixed = lambda c, e, *_: (0, 0)
    expert = lambda c, e, *_: (e, 0, 0)
    pairs, singles, shared, straight = transfer_plan(local, tp_count)
    early, late = pairs + singles, shared + straight
    arrived = lambda c, e, *_: (jnp.minimum(e, early - 1), 0, 0)
    hbm = pl.BlockSpec(memory_space=pl.ANY)
    dma = pltpu.SemaphoreType.DMA
    share = (local, 5 * RANK, model // tp_count)
    gradients = (
        (share, pl.BlockSpec(share, lambda c, e, *_: (0, 0, 0)))
        if late
        else (
            (trees, local, 5 * RANK, model),
            pl.BlockSpec((1, 1, 5 * RANK, model), lambda c, e, *_: (c, e, 0, 0)),
        )
    )
    return pl.pallas_call(
        functools.partial(
            expert_kernel, slots=slots, sources=sources, early=early, shared=shared,
            straight=straight, tp_count=tp_count,
        ),
        grid_spec=pltpu.PrefetchScalarGridSpec(
            num_scalar_prefetch=1,
            grid=(trees, local),
            in_specs=[
                pl.BlockSpec((tokens, model), piece),
                pl.BlockSpec((tokens, model), piece),
                pl.BlockSpec((routes.shape[0], tokens), lambda c, e, *_: (0, c)),
                pl.BlockSpec(router.shape, fixed),
                *[pl.BlockSpec((1,) + w.shape[1:], expert) for w in weights],
                *[pl.BlockSpec((1,) + w.shape[1:], arrived) for w in weights],
                *[hbm] * len(weights),
                *[pl.BlockSpec((1,) + a.shape[1:], expert) for a in adapters],
            ],
            out_specs=[
                pl.BlockSpec((tokens, model + LANES), piece),
                pl.BlockSpec((tokens, model), piece),
                gradients[1],
            ],
            scratch_shapes=[
                pltpu.VMEM((experts, tokens), F32),
                pltpu.VMEM((experts, tokens), F32),
                pltpu.VMEM((LANES, tokens), F32),
                pltpu.VMEM((tokens, model), F32),
                pltpu.VMEM((tokens, model), F32),
                pltpu.VMEM((tall, model), BF16),
                pltpu.VMEM((model, 2 * lanes), BF16),
                pltpu.VMEM((2 * lanes, model), F32),
                pltpu.VMEM((2 * half, hidden), BF16),
                pltpu.VMEM((2 * half, hidden), BF16),
                pltpu.VMEM((hidden, model), BF16),
                *[pltpu.VMEM((max(late, 1),) + w.shape[1:], BF16) for w in weights],
                pltpu.VMEM((local if late else 1, 5 * RANK, model), BF16),
                pltpu.VMEM((tp_count - 1,) + (share if late else (1, 16, LANES)), BF16),
                dma((2, max(late, 1), 3)),
                dma((2, max(shared, 1), 3)),
                dma((tp_count - 1, local)),
                dma((tp_count - 1, local)),
            ],
        ),
        out_shape=[
            jax.ShapeDtypeStruct((total, model + LANES), BF16),
            jax.ShapeDtypeStruct((total, model), BF16),
            jax.ShapeDtypeStruct(gradients[0], BF16),
        ],
        compiler_params=(
            pltpu.CompilerParams(
                vmem_limit_bytes=60 * 1024 * 1024, collective_id=2, has_side_effects=True
            )
            if late
            else pltpu.CompilerParams(vmem_limit_bytes=60 * 1024 * 1024)
        ),
        name="experts",
        cost_estimate=pl.CostEstimate(
            flops=2 * local * total * model * model * 2,
            bytes_accessed=8 * 1024 * 1024,
            transcendentals=0,
        ),
    )(sets, rows, upstream, routes, router, *weights, *far, *weights, *adapters)


def take_set(table, chosen, axis):
    return lax.dynamic_slice_in_dim(table, chosen * RANK, RANK, axis)


def per_device(
    tokens,
    out_grad,
    routes,
    parents,
    adapter_set,
    gain_a,
    gain_b,
    w_query,
    key_projection_matrix,
    value_projection_matrix,
    w_output,
    w_router,
    w_gate,
    w_up,
    w_down,
    query_in,
    query_out,
    key_in,
    key_second_factor,
    value_in,
    value_second_factor,
    out_in,
    out_out,
    gate_in,
    gate_out,
    up_in,
    up_out,
    down_in,
    down_out,
):
    tp_rank = lax.axis_index("tp")
    ctx_rank = lax.axis_index("ctx")
    fsdp_rank = lax.axis_index("fsdp")
    ctx_count = lax.axis_size("ctx")
    tp_count = lax.axis_size("tp")
    fsdp_count = lax.axis_size("fsdp")
    tok_rows, model = tokens.shape
    q_cols = w_query.shape[1]
    kv_cols = key_projection_matrix.shape[1]
    heads, pairs = q_cols // HEAD, kv_cols // HEAD
    experts = w_router.shape[1]
    local_experts = w_gate.shape[0]
    sets = query_in.shape[1] // RANK
    slots = tok_rows * TOP * 3 // (2 * experts)
    trees = ctx_count // SPAN

    attention_shard = jnp.concatenate(
        [
            jnp.concatenate([w_query, key_projection_matrix, value_projection_matrix], axis=1),
            w_output,
        ],
        axis=0,
    )

    seg_start = (fsdp_rank * ctx_count + ctx_rank) * SEGS_DEV
    tree_index = seg_start // TREE_SEGS
    local_start = seg_start % TREE_SEGS
    rank = (local_start // SEGS_DEV).astype(jnp.int32).reshape(1)
    tree_parents = lax.dynamic_slice_in_dim(parents, tree_index * TREE_SEGS, TREE_SEGS, 0)
    reach, depth = tree_links(tree_parents)
    chosen = lax.dynamic_slice_in_dim(adapter_set, tree_index, 1, 0)[0]

    gain_one = gain_a.astype(F32)
    gain_two = gain_b.astype(F32)

    own_reach = lax.dynamic_slice_in_dim(reach, local_start, SEGS_DEV, 0)
    codes = jnp.pad(
        jnp.where(own_reach > 0.5, 0.0, MASKED), ((0, 0), (CODE, LANES - CODE - TREE_SEGS))
    )
    codes = jnp.repeat(codes.astype(BF16), SEG, axis=0)
    own_depth = lax.dynamic_slice_in_dim(depth, local_start, SEGS_DEV, 0)
    positions = (
        own_depth[:, None] * SEG + jnp.arange(SEG, dtype=jnp.int32).astype(F32)[None, :]
    ).reshape(-1)
    half_head = HEAD // 2
    freqs = ROPE_BASE ** (-(jnp.arange(half_head, dtype=jnp.int32).astype(F32) * 2.0) / HEAD)
    angles = positions[:, None] * jnp.tile(freqs, LANES // half_head)[None, :]
    cos, sin = jnp.cos(angles), jnp.sin(angles)

    first = jnp.pad(
        jnp.concatenate(
            [take_set(t, chosen, 1) for t in (query_in, key_in, value_in)], axis=1
        ),
        ((0, 0), (0, LANES - 3 * RANK)),
    )
    q_second = lax.dynamic_slice(query_out, (chosen * RANK, tp_rank * q_cols), (RANK, q_cols))
    k_second = lax.dynamic_slice(
        key_second_factor, (chosen * RANK, tp_rank * kv_cols), (RANK, kv_cols)
    )
    v_second = lax.dynamic_slice(
        value_second_factor, (chosen * RANK, tp_rank * kv_cols), (RANK, kv_cols)
    )
    second = jnp.concatenate(
        [
            jnp.pad(q_second, ((0, 0), (0, 2 * kv_cols))),
            jnp.pad(k_second, ((0, 0), (q_cols, kv_cols))),
            jnp.pad(v_second, ((0, 0), (q_cols + kv_cols, 0))),
            jnp.zeros((LANES - 3 * RANK, q_cols + 2 * kv_cols), BF16),
        ],
        axis=0,
    )
    o_first = jnp.pad(
        lax.dynamic_slice(out_in, (tp_rank * q_cols, chosen * RANK), (q_cols, RANK)),
        ((0, 0), (0, LANES - RANK)),
    )
    o_second = jnp.pad(take_set(out_out, chosen, 0), ((0, LANES - RANK), (0, 0)))

    (
        attended, queries, kv_parts, lora, middle, o_reduced, attention_weights,
        normed_all, *far_weights, upstream_all, routes_all, rows_all,
    ) = forward(
        tokens, (gain_one[None], gain_two[None]), attention_shard, first, second,
        o_first, o_second, cos, sin, codes, (w_gate, w_up, w_down), out_grad, routes.T,
        tp_count, ctx_count,
    )
    upstream_all = upstream_all.reshape(-1, model)
    rows_all = rows_all.reshape(-1, model)
    routes_all = routes_all.transpose(1, 0, 2).reshape(TOP, -1)

    tree_sets = lax.dynamic_slice_in_dim(adapter_set, fsdp_rank * trees, trees, 0)
    back, mixed, expert_part = run_experts(
        tree_sets,
        rows_all,
        upstream_all,
        routes_all,
        w_router.T,
        (w_gate, w_up, w_down),
        far_weights,
        (gate_in, up_in, gate_out, up_out, down_in, down_out),
        slots,
        SPAN,
        tp_count,
    )
    direct = ctx_count == SPAN
    if direct:
        back = back.reshape(ctx_count, tok_rows, -1)
        mixed = mixed.reshape(ctx_count, tok_rows, -1)
    else:
        back = lax.psum_scatter(back, "ctx", scatter_dimension=0, tiled=True)
        mixed = lax.psum_scatter(mixed, "ctx", scatter_dimension=0, tiled=True)
    output, input_grad, packed, all_shares = backward(
        tokens, out_grad, routes, (gain_one[None], gain_two[None]),
        jnp.pad(w_router, ((0, 0), (0, LANES - experts))), middle, o_reduced, attention_weights,
        normed_all, lora, attended, queries, kv_parts, first, second, o_first, o_second,
        cos, sin, back, mixed, expert_part, tp_count, ctx_count, experts, direct,
    )
    all_trees = fsdp_count * trees
    if not direct:
        mine = (jnp.arange(all_trees, dtype=jnp.int32) == tree_index)[:, None, None]
        packed = lax.psum(jnp.where(mine, packed, 0.0), ("fsdp", "ctx", "tp"))
    adapter_totals = place(
        adapter_set,
        packed,
        (
            query_in, query_out, key_in, key_second_factor, value_in, value_second_factor,
            out_in, out_out,
        ),
    )

    if direct:
        expert_part = all_shares
    else:
        expert_part = lax.all_gather(lax.psum(expert_part, "tp"), "fsdp")
        expert_part = expert_part.reshape(all_trees, local_experts, 5 * RANK, model)
    expert_totals = place_experts(
        adapter_set, expert_part, (gate_in, gate_out, up_in, up_out, down_in, down_out)
    )
    return (output, input_grad, *adapter_totals, *expert_totals)


def solution(mesh):
    in_specs = (
        P(("fsdp", "ctx", "tp"), None),
        P(("fsdp", "ctx", "tp"), None),
        P(("fsdp", "ctx", "tp"), None),
        P(),
        P(),
        P(),
        P(),
        P("fsdp", "tp"),
        P("fsdp", "tp"),
        P("fsdp", "tp"),
        P("tp", "fsdp"),
        P(),
        P("ctx", "fsdp", None),
        P("ctx", "fsdp", None),
        P("ctx", "fsdp", None),
        P(),
        P(),
        P(),
        P(),
        P(),
        P(),
        P(),
        P(),
        P("ctx", None, None),
        P("ctx", None, None),
        P("ctx", None, None),
        P("ctx", None, None),
        P("ctx", None, None),
        P("ctx", None, None),
    )
    out_specs = (
        P(("fsdp", "ctx", "tp"), None),
        P(("fsdp", "ctx", "tp"), None),
        P(),
        P(),
        P(),
        P(),
        P(),
        P(),
        P(),
        P(),
        P("ctx", None, None),
        P("ctx", None, None),
        P("ctx", None, None),
        P("ctx", None, None),
        P("ctx", None, None),
        P("ctx", None, None),
    )
    return jax.shard_map(
        per_device, mesh=mesh, in_specs=in_specs, out_specs=out_specs, check_vma=False
    )
```

```python
import functools
import math

import jax
import jax.numpy as jnp
from jax import lax
from jax.experimental import pallas as pl
from jax.experimental.pallas import tpu as pltpu
from jax.sharding import PartitionSpec as P

HEAD = 64
TOP = 8
RANK = 16
SEG = 128
SEGS_DEV = 8
TREE_SEGS = 32
SPAN = TREE_SEGS // SEGS_DEV
LANES = 128

RESIDUAL_SCALE = 0.22
SCORE_SCALE = 0.015625
EPSILON = 1e-06
ROPE_BASE = 10000.0
MASKED = -1e30

F32 = jnp.float32
BF16 = jnp.bfloat16

CODE = HEAD
LSE = CODE + TREE_SEGS + 1
ONES = HEAD

VMEM_LIMIT = 56 * 1024 * 1024


def dot(a, b):
    return lax.dot_general(a, b, (((1,), (0,)), ((), ())), preferred_element_type=F32)


def dot_nt(a, b):
    return lax.dot_general(a, b, (((1,), (1,)), ((), ())), preferred_element_type=F32)


def dot_tn(a, b):
    return lax.dot_general(a, b, (((0,), (0,)), ((), ())), preferred_element_type=F32)


def iota(shape, dim):
    return lax.broadcasted_iota(jnp.int32, shape, dim)


def shifted(block, axis, distance):
    devices = range(lax.axis_size(axis))
    route = [(i - distance, i) for i in devices if i - distance in devices]
    return lax.ppermute(block, axis, route)


def rms_scale(values, gain_row):
    return (
        values * lax.rsqrt(jnp.mean(values * values, axis=-1, keepdims=True) + EPSILON) * gain_row
    )


def rms_back(values, gain_row, grad):
    inv = lax.rsqrt(jnp.mean(values * values, axis=-1, keepdims=True) + EPSILON)
    scaled = grad * gain_row
    inner = jnp.mean(scaled * values, axis=-1, keepdims=True)
    return inv * scaled - values * (inv * inv * inv * inner)


def tree_links(tree_parents):
    count = tree_parents.shape[0]
    columns = jnp.arange(count, dtype=jnp.int32)
    reach = (
        (tree_parents[:, None] == columns[None, :]) | (columns[:, None] == columns[None, :])
    ).astype(BF16)
    for _ in range(max(1, (count - 1).bit_length())):
        reach = jnp.minimum(dot(reach, reach), 1.0).astype(BF16)
    reach = reach.astype(F32)
    return reach, jnp.sum(reach, axis=1) - 1.0


def swap_halves(values):
    width = values.shape[-1]
    lane = iota(values.shape, 1) % HEAD
    ahead = pltpu.roll(values, width - HEAD // 2, 1)
    behind = pltpu.roll(values, HEAD // 2, 1)
    return jnp.where(lane < HEAD // 2, -ahead, behind)


def place_table(rows, source, target):
    r, c = iota((rows, LANES), 0), iota((rows, LANES), 1)
    return ((r - source == c - target) & (c >= target) & (c < target + HEAD)).astype(BF16)


def transfer_plan(local, tp_count):
    if local == 8 and tp_count % 2 == 0:
        return 3, 2, 2, 1
    return 0, local, 0, 0


BEGIN = {"start": (0, 1), "proj": (2,), "own": (3,), "k1": (4,), 0: (0,), 2: (1,), 4: (2,)}
RELAY = {"proj": (0,), "sum": (1, 2), 2: (0,), 4: (1,)}


def remote(src, dst, send, recv, where):
    return pltpu.make_async_remote_copy(
        src_ref=src,
        dst_ref=dst,
        send_sem=send,
        recv_sem=recv,
        device_id=where,
        device_id_type=pl.DeviceIdType.MESH,
    )


def far_moves(near, far, sems, pass_sems, shared, direct, first, land, other, tp):
    mate = {"tp": tp + 1 - 2 * lax.rem(tp, 2)}
    side = lax.rem(tp, 2)

    def piece(ref, rows, which):
        return ref.at[pl.ds(pl.multiple_of(which * rows, rows), rows)]

    def cross(n):
        moves = []
        for a, (source, target) in enumerate(zip(near, far)):
            src, dst = source.at[first + n], target.at[land + n]
            if n < shared:
                rows = src.shape[0] // 2
                src, dst = piece(src, rows, side), piece(dst, rows, side)
            moves.append(remote(src, dst, sems.at[0, n, a], sems.at[1, n, a], other))
        return moves

    def hand_on(n):
        moves = []
        for a, target in enumerate(far):
            dst = target.at[land + n]
            rows = dst.shape[0] // 2
            dst = piece(dst, rows, side)
            moves.append(remote(dst, dst, pass_sems.at[0, n, a], pass_sems.at[1, n, a], mate))
        return moves

    return cross, hand_on


class Line:
    def __init__(self, buffer, sems, me, count):
        self.buffer, self.sems, self.me, self.count = buffer, sems, me, count
        self.turns = 2 * count - 1

    def move(self, way, block):
        where = ring(self.me, 1 if way == 0 else -1, self.count)
        return remote(
            self.buffer.at[block], self.buffer.at[block],
            self.sems.at[way, 0, block], self.sems.at[way, 1, block], {"tp": where},
        )

    def goes(self, way):
        return self.me < self.count - 1 if way == 0 else self.me > 0

    def send(self, way, block):
        @pl.when(self.goes(way))
        def _():
            self.move(way, block).start()

    def start(self):
        self.send(0, self.me)
        self.send(1, self.me)

    def block(self, turn):
        step = (turn + 1) // 2
        block = jnp.where(lax.rem(turn, 2) == 1, self.me - step, self.me + step)
        valid = (block >= 0) & (block < self.count)
        return jnp.clip(block, 0, self.count - 1), valid

    def last(self):
        return jnp.maximum(2 * self.me - 1, 2 * (self.count - 1 - self.me))

    def arrive(self, turn, block):
        for way, odd in ((0, 1), (1, 0)):

            @pl.when((turn > 0) & (lax.rem(turn, 2) == odd))
            def _(way=way):
                self.move(way, block).wait_recv()
                self.send(way, block)

    def end(self):
        for block in range(self.count):
            for way, owned in ((0, block <= self.me), (1, block >= self.me)):

                @pl.when(owned & self.goes(way))
                def _(way=way):
                    self.move(way, block).wait_send()


def ring(me, step, count):
    return lax.rem(me + (step + count), count)


def aug_keys(kv, pair, pairs, first_seg, k_aug, v_aug, start):
    rows, width = kv.shape
    lane = iota((rows, LANES), 1)
    seg = first_seg + iota((rows, LANES), 0) // SEG
    key_code = ((lane - CODE == seg) | ((lane >= LSE) & (lane < LSE + 3))).astype(F32)
    one_code = ((lane == ONES) | (lane == ONES + 1)).astype(F32)
    span = pl.ds(start, rows)
    k_aug[pair, span, :] = (dot(kv, place_table(width, pair * HEAD, 0)) + key_code).astype(BF16)
    v_aug[pair, span, :] = (
        dot(kv, place_table(width, (pairs + pair) * HEAD, 0)) + one_code
    ).astype(BF16)


def forward_kernel(
    tokens, gain_one, gain_two, shard, first, second, o_first, o_second, cos, sin, codes,
    w_gate, w_up, w_down, grads, routes,
    att_out, q_out, kv_out, lora_out, middle_out, low_out, weights_out, normed_all,
    gate_far, up_far, down_far, grads_all, routes_all, rows_all,
    weights, q_aug, k_aug, v_aug, top, acc, parts, parts_in, rows_own,
    shard_sem, normed_sem, kv_sem, part_sem, far_sem, pass_far_sem, grads_sem, routes_sem, rows_sem,
    pass_sem, local_sem,
    *, tp_count, ctx_count, shared, straight,
):
    tp, ctx, fsdp = (lax.axis_index(name) for name in ("tp", "ctx", "fsdp"))
    rank = lax.rem(ctx, SPAN)
    block, model = tokens.shape
    heads = q_aug.shape[0]
    pairs = k_aug.shape[0]
    group = heads // pairs
    tall = group * block
    half = shard.shape[1]
    q_cols = heads * HEAD
    turn = cos.shape[1]
    chips = ctx_count // 2
    partner = ctx + 1 - 2 * lax.rem(ctx, 2)
    other = {"fsdp": 1 - fsdp}

    barrier = pltpu.get_barrier_semaphore()
    pl.semaphore_signal(barrier, 1, device_id=other, device_id_type=pl.DeviceIdType.MESH)
    for k in range(1, tp_count):
        pl.semaphore_signal(
            barrier, 1, device_id={"tp": ring(tp, k, tp_count)},
            device_id_type=pl.DeviceIdType.MESH,
        )
    for k in range(1, ctx_count):
        pl.semaphore_signal(
            barrier, 1, device_id={"ctx": ring(ctx, k, ctx_count)},
            device_id_type=pl.DeviceIdType.MESH,
        )
    pl.semaphore_wait(barrier, tp_count + ctx_count - 1)

    shard_copy = remote(shard, weights.at[fsdp], shard_sem.at[0], shard_sem.at[1], other)
    shard_copy.start()

    inputs = tokens[...].astype(F32)
    normed = rms_scale(inputs, gain_one[...]).astype(BF16)
    normed_all[tp] = normed

    line = Line(normed_all, normed_sem, tp, tp_count)
    line.start()

    def side_copies(k):
        where = {"ctx": ring(ctx, k, ctx_count)}
        return (
            remote(grads, grads_all.at[ctx], grads_sem.at[0, k], grads_sem.at[1, k], where),
            remote(routes, routes_all.at[ctx], routes_sem.at[0, k], routes_sem.at[1, k], where),
        )

    own_copies = (
        pltpu.make_async_copy(grads, grads_all.at[ctx], local_sem.at[0]),
        pltpu.make_async_copy(routes, routes_all.at[ctx], local_sem.at[1]),
    )
    for copy in own_copies:
        copy.start()
    for k in range(1, ctx_count):
        for copy in side_copies(k):
            copy.start()

    weights[fsdp] = shard[...]
    shard_copy.wait()
    cross, hand_on = far_moves(
        (w_gate, w_up, w_down), (gate_far, up_far, down_far), far_sem, pass_far_sem,
        shared, straight, 0, 0, other, tp,
    )

    def point(name):
        if not shared:
            if name == "start":
                for n in range(straight):
                    for copy in cross(n):
                        copy.start()
            return
        for n in RELAY.get(name, ()):
            for copy in cross(n):
                copy.wait_recv()
            for copy in hand_on(n):
                copy.start()
        for n in BEGIN.get(name, ()):
            for copy in cross(n):
                copy.start()

    point("start")
    weights_out[...] = weights[...]

    def kv_copy(distance, part):
        return remote(
            kv_out.at[0, part], kv_out.at[distance, part],
            kv_sem.at[0, distance - 1], kv_sem.at[1, distance - 1], {"ctx": ring(ctx, distance, ctx_count)},
        )

    def project(part):
        span = pl.ds(pl.multiple_of(part * block, block), block)
        rows = normed_all[part]
        lora = dot(rows, first[...]).astype(BF16)
        lora_out[span, :] = lora
        pre = (
            dot(rows[:, :half], weights[0, pl.ds(0, half), :])
            + dot(rows[:, half:], weights[1, pl.ds(0, half), :])
            + dot(lora, second[...])
        )
        turned = []
        for start in range(0, pre.shape[1] // 4 * 3, turn):
            piece = pre[:, start : start + turn]
            turned.append(piece * cos[span, :] + swap_halves(piece) * sin[span, :])
        queries = (
            jnp.concatenate(turned[: q_cols // turn], axis=1) * SCORE_SCALE
        ).astype(BF16)
        for head in range(heads):
            q_aug[head, span, :] = (
                dot(queries, place_table(q_cols, head * HEAD, 0)) + codes[span, :].astype(F32)
            ).astype(BF16)
        keys = jnp.concatenate(turned[q_cols // turn :], axis=1)
        kv = jnp.concatenate([keys, pre[:, q_cols + keys.shape[1] :]], axis=1).astype(BF16)
        kv_out[0, part] = kv
        for distance in range(1, SPAN):

            @pl.when(rank + distance < SPAN)
            def _(distance=distance):
                kv_copy(distance, part).start()

        for pair in range(pairs):
            aug_keys(
                kv, pair, pairs, rank * SEGS_DEV + part * (block // SEG), k_aug, v_aug,
                pl.multiple_of(part * block, block),
            )

    @pl.loop(0, line.turns)
    def _(turn):
        part, valid = line.block(turn)

        @pl.when(valid)
        def _():
            line.arrive(turn, part)
            project(part)

    point("proj")

    def tile(part, pair, start, size, causal):
        index = part * pairs + pair
        rows = pl.ds(pl.multiple_of(part * block, block), block)
        queries = q_aug[pl.ds(pair * group, group), rows, :].reshape(tall, LANES)
        span = pl.ds(start, size)
        scores = dot_nt(queries, k_aug[pair, span, :])
        if causal:
            q_row = iota(scores.shape, 0) % block
            scores = jnp.where(iota(scores.shape, 1) <= q_row, scores, MASKED)
            now = jnp.broadcast_to(jnp.max(scores, axis=1, keepdims=True), (tall, LANES))
            probs = jnp.exp(scores - now[:, :1]).astype(BF16)
            acc[index] = dot(probs, v_aug[pair, span, :])
        else:
            before = top[index]
            now = jnp.maximum(before, jnp.max(scores, axis=1, keepdims=True))
            probs = jnp.exp(scores - now[:, :1]).astype(BF16)
            acc[index] = acc[index] * jnp.exp(before - now) + dot(probs, v_aug[pair, span, :])
        top[index] = now

    @pl.loop(0, tp_count * pairs)
    def _(index):
        part, pair = index // pairs, lax.rem(index, pairs)
        tile(part, pair, pl.multiple_of(part * block, block), block, True)

        @pl.loop(0, part)
        def _(j):
            tile(part, pair, pl.multiple_of(j * block, block), block, False)

    point("own")
    group_rows = tp_count * block
    for distance in range(1, SPAN):

        @pl.when(distance <= rank)
        def _(distance=distance):
            remote(
                kv_out.at[0], kv_out.at[distance], kv_sem.at[0, distance - 1],
                kv_sem.at[1, distance - 1], {"ctx": ring(ctx, distance, ctx_count)},
            ).wait_recv()

            @pl.loop(0, tp_count)
            def _(part):
                kv = kv_out[distance, part]
                for pair in range(pairs):
                    aug_keys(
                        kv, pair, pairs,
                        (rank - distance) * SEGS_DEV + part * (block // SEG), k_aug, v_aug,
                        pl.multiple_of(distance * group_rows + part * block, block),
                    )

        @pl.when(distance > rank)
        def _(distance=distance):
            kv_out[distance] = jnp.zeros(kv_out.shape[1:], BF16)

    def part_copy(k):
        return remote(
            parts.at[k], parts_in.at[k], part_sem.at[0, k], part_sem.at[1, k],
            {"tp": ring(tp, k + 1, tp_count)},
        )

    @pl.loop(0, tp_count)
    def _(k):
        part = ring(tp, k + 1, tp_count)
        rows = pl.ds(pl.multiple_of(part * block, block), block)
        for pair in range(pairs):
            index = part * pairs + pair

            @pl.loop(1, rank + 1)
            def _(distance, pair=pair):
                tile(
                    part, pair, pl.multiple_of(distance * group_rows, group_rows), group_rows, False
                )

            summed = acc[index]
            total = summed[:, ONES : ONES + 1]
            result = (summed / total).astype(BF16)
            for member in range(group):
                head = pair * group + member
                att_out[rows, pl.ds(head * HEAD, HEAD)] = result[
                    member * block : (member + 1) * block, :HEAD
                ]
            minus = -(top[index] + jnp.log(total))
            high = minus.astype(BF16).astype(F32)
            middle = (minus - high).astype(BF16).astype(F32)
            lane = iota(minus.shape, 1)
            queries = q_aug[pl.ds(pair * group, group), rows, :].reshape(tall, LANES)
            coded = jnp.where(
                lane == LSE,
                high,
                jnp.where(
                    lane == LSE + 1,
                    middle,
                    jnp.where(lane == LSE + 2, minus - high - middle, queries.astype(F32)),
                ),
            )
            q_out[pl.ds(pair * group, group), rows, :] = coded.astype(BF16).reshape(
                group, block, LANES
            )
        mixed = att_out[rows, :]
        low = dot(mixed, o_first[...]).astype(BF16)
        low_out[rows, :] = low
        for side in range(2):
            columns = slice(side * half, (side + 1) * half)
            parts[k, :, columns] = (
                dot(mixed, weights[side, pl.ds(half, q_cols), :]) + dot(low, o_second[:, columns])
            ).astype(BF16)

        @pl.when(k < tp_count - 1)
        def _():
            part_copy(k).start()

        for n in range(tp_count):
            if f"k{n}" in BEGIN or f"k{n}" in RELAY:

                @pl.when(k == n)
                def _(n=n):
                    point(f"k{n}")

    summed = parts[tp_count - 1].astype(F32)
    for k in range(tp_count - 1):
        part_copy(k).wait_recv()
        summed += parts_in[k].astype(F32)
    point("sum")
    middle = inputs + RESIDUAL_SCALE * summed
    middle_out[...] = middle
    rows_own[...] = rms_scale(middle, gain_two[...]).astype(BF16)

    own_rows = pltpu.make_async_copy(rows_own, rows_all.at[ctx], local_sem.at[2])
    own_rows.start()
    to_partner = remote(
        rows_own, rows_all.at[ctx], rows_sem.at[0, 0], rows_sem.at[1, 0], {"ctx": partner}
    )
    to_partner.start()

    def rows_copy(k):
        return remote(
            rows_own, rows_all.at[ctx], rows_sem.at[0, k], rows_sem.at[1, k],
            {"ctx": ring(ctx, 2 * k, ctx_count)},
        )

    def pass_copy(k):
        source = ring(ctx, -2 * k, ctx_count)
        return remote(
            rows_all.at[source], rows_all.at[source], pass_sem.at[0, k], pass_sem.at[1, k],
            {"ctx": partner},
        )

    for k in range(1, chips):
        rows_copy(k).start()
    for k in range(1, chips):
        rows_copy(k).wait_recv()
        pass_copy(k).start()

    line.end()
    for k in range(tp_count - 1):
        part_copy(k).wait_send()
    for distance in range(1, SPAN):

        @pl.when(rank + distance < SPAN)
        def _(distance=distance):
            remote(
                kv_out.at[0], kv_out.at[distance], kv_sem.at[0, distance - 1],
                kv_sem.at[1, distance - 1], {"ctx": ring(ctx, distance, ctx_count)},
            ).wait_send()

    for k in range(1, ctx_count):
        for copy in side_copies(k):
            copy.wait()
    for copy in own_copies:
        copy.wait()
    own_rows.wait()
    to_partner.wait()
    for k in range(1, chips):
        rows_copy(k).wait_send()
        pass_copy(k).wait()
    for n in range(shared + straight):
        for copy in cross(n):
            copy.wait_send()
            if n >= shared:
                copy.wait_recv()
    for n in range(shared):
        for copy in hand_on(n):
            copy.wait()


def forward(
    tokens, gains, shard, first, second, o_first, o_second, cos, sin, codes, weights, grads,
    routes, tp_count, ctx_count,
):
    block, model = tokens.shape
    rows = tp_count * block
    heads = o_first.shape[0] // HEAD
    cols = second.shape[1]
    kv_cols = cols - heads * HEAD
    pairs = kv_cols // (2 * HEAD)
    tall = heads // pairs * block
    chips = ctx_count // 2
    shared, straight, _, _ = transfer_plan(weights[0].shape[0], tp_count)
    vmem = pl.BlockSpec(memory_space=pltpu.VMEM)
    hbm = pl.BlockSpec(memory_space=pl.ANY)
    dma = pltpu.SemaphoreType.DMA
    part = (block, model)
    return pl.pallas_call(
        functools.partial(
            forward_kernel, tp_count=tp_count, ctx_count=ctx_count, shared=shared, straight=straight
        ),
        in_specs=[vmem] * 11 + [hbm] * 5,
        out_specs=[vmem] * 8 + [hbm] * 6,
        out_shape=[
            jax.ShapeDtypeStruct((rows, heads * HEAD), BF16),
            jax.ShapeDtypeStruct((heads, rows, LANES), BF16),
            jax.ShapeDtypeStruct((SPAN, tp_count, block, kv_cols), BF16),
            jax.ShapeDtypeStruct((rows, LANES), BF16),
            jax.ShapeDtypeStruct((block, model), F32),
            jax.ShapeDtypeStruct((rows, LANES), BF16),
            jax.ShapeDtypeStruct((2,) + shard.shape, BF16),
            jax.ShapeDtypeStruct((tp_count, block, model), BF16),
            *[jax.ShapeDtypeStruct((shared + straight,) + w.shape[1:], BF16) for w in weights],
            jax.ShapeDtypeStruct((ctx_count,) + grads.shape, BF16),
            jax.ShapeDtypeStruct((ctx_count,) + routes.shape, jnp.int32),
            jax.ShapeDtypeStruct((ctx_count, block, model), BF16),
        ],
        scratch_shapes=[
            pltpu.VMEM((2,) + shard.shape, BF16),
            pltpu.VMEM((heads, rows, LANES), BF16),
            pltpu.VMEM((pairs, SPAN * rows, LANES), BF16),
            pltpu.VMEM((pairs, SPAN * rows, LANES), BF16),
            pltpu.VMEM((tp_count * pairs, tall, LANES), F32),
            pltpu.VMEM((tp_count * pairs, tall, LANES), F32),
            pltpu.VMEM((tp_count,) + part, BF16),
            pltpu.VMEM((tp_count - 1,) + part, BF16),
            pltpu.VMEM((block, model), BF16),
            dma((2,)),
            dma((2, 2, tp_count)),
            dma((2, SPAN - 1)),
            dma((2, tp_count - 1)),
            dma((2, shared + straight, 3)),
            dma((2, max(shared, 1), 3)),
            dma((2, ctx_count)),
            dma((2, ctx_count)),
            dma((2, chips)),
            dma((2, chips)),
            dma((3,)),
        ],
        compiler_params=pltpu.CompilerParams(
            vmem_limit_bytes=VMEM_LIMIT, collective_id=0, has_side_effects=True
        ),
        cost_estimate=pl.CostEstimate(
            flops=16 * SPAN * rows * rows * heads * LANES,
            bytes_accessed=32 * 1024 * 1024,
            transcendentals=0,
        ),
        name="forward",
    )(
        tokens, *gains, shard, first, second, o_first, o_second, cos, sin, codes, *weights,
        grads, routes,
    )


def joined(dk, dv, span):
    pairs = dk.shape[0]
    return jnp.concatenate(
        [dk[pair, span, :HEAD] for pair in range(pairs)]
        + [dv[pair, span, :HEAD] for pair in range(pairs)],
        axis=1,
    )


def backward_kernel(
    tokens, upstream_ref, routes, gain_one, gain_two, router, middle_ref, low_ref, weights,
    normed_all, lora, att, q_ref, kv_ref, first, second, o_first, o_second, cos, sin, back, mixed, shares,
    output, input_grad, packed_out, shares_out,
    k_aug, v_aug, up_aug, dk, dv, dq, branch_all, far_out, far_in, own_kv, parts, parts_in,
    second_acc, first_acc, o_in_acc, o_out_acc, packed, ctx_in, tp_in, middle_grad,
    back_near, back_mine, back_pair, back_far, mixed_near, mixed_mine, mixed_pair, mixed_far,
    near_sem, mine_sem, far_sem, branch_sem, kv_sem, part_sem,
    ctx_sem, tp_sem, x_sem, tp_all_sem, ctx_all_sem, share_sem, swap_sem, own_sem,
    *, tp_count, ctx_count, experts, direct,
):
    tp, ctx, fsdp = (lax.axis_index(name) for name in ("tp", "ctx", "fsdp"))
    rank = lax.rem(ctx, SPAN)
    block, model = tokens.shape
    heads, rows_all, _ = q_ref.shape
    pairs = k_aug.shape[0]
    group = heads // pairs
    tall = group * block
    half = weights.shape[2]
    q_cols = heads * HEAD
    kv_cols = pairs * HEAD
    turn = cos.shape[1]
    partner = ctx + 1 - 2 * lax.rem(ctx, 2)
    cross = ring(ctx, 2, ctx_count)
    cross_partner = ring(partner, 2, ctx_count)
    other = {"fsdp": 1 - fsdp}

    barrier = pltpu.get_barrier_semaphore()
    pl.semaphore_signal(barrier, 1, device_id=other, device_id_type=pl.DeviceIdType.MESH)
    for k in range(1, tp_count):
        pl.semaphore_signal(
            barrier, 1, device_id={"tp": ring(tp, k, tp_count)},
            device_id_type=pl.DeviceIdType.MESH,
        )
    for k in range(1, ctx_count):
        pl.semaphore_signal(
            barrier, 1, device_id={"ctx": ring(ctx, k, ctx_count)},
            device_id_type=pl.DeviceIdType.MESH,
        )
    pl.semaphore_wait(barrier, tp_count + ctx_count - 1)

    sums = (
        (back, back_near, back_mine, back_pair, back_far),
        (mixed, mixed_near, mixed_mine, mixed_pair, mixed_far),
    )

    def near_copy(n, slot):
        source, near = sums[n][:2]
        return remote(
            source.at[(partner, cross_partner)[slot]], near.at[slot],
            near_sem.at[0, 2 * n + slot], near_sem.at[1, 2 * n + slot], {"ctx": partner},
        )

    def mine_copy(n, slot):
        return pltpu.make_async_copy(
            sums[n][0].at[(ctx, cross)[slot]], sums[n][2].at[slot], mine_sem.at[2 * n + slot]
        )

    def pair_copy(n):
        return remote(sums[n][3], sums[n][4], far_sem.at[0, n], far_sem.at[1, n], {"ctx": cross})

    def start_sum(n):
        for slot in (1, 0):
            near_copy(n, slot).start()
            mine_copy(n, slot).start()

    def pass_sum(n):
        near_copy(n, 1).wait_recv()
        mine_copy(n, 1).wait()
        _, near, mine, pair, _ = sums[n]
        pair[...] = (near[1].astype(F32) + mine[1].astype(F32)).astype(BF16)
        pair_copy(n).start()

    def end_sum(n):
        near_copy(n, 0).wait_recv()
        mine_copy(n, 0).wait()
        pair_copy(n).wait_recv()
        _, near, mine, _, far = sums[n]
        return near[0].astype(F32) + mine[0].astype(F32) + far[...].astype(F32)

    if direct:
        share = shares.shape[2]
        own_lanes = pl.ds(pl.multiple_of(tp * share, share), share)

        def share_copy(k):
            return remote(
                shares, shares_out.at[fsdp, :, :, own_lanes],
                share_sem.at[0, k - 1], share_sem.at[1, k - 1], {"tp": ring(tp, k, tp_count)},
            )

        share_own = pltpu.make_async_copy(shares, shares_out.at[fsdp, :, :, own_lanes], own_sem.at[0])
        swap = remote(
            shares_out.at[fsdp], shares_out.at[fsdp], swap_sem.at[0], swap_sem.at[1], other
        )

        start_sum(0)
        start_sum(1)
        share_own.start()
        for k in range(1, tp_count):
            share_copy(k).start()

    @pl.loop(0, rank + 1)
    def _(distance):
        @pl.loop(0, tp_count)
        def _(part):
            kv = kv_ref[distance, part]
            for pair in range(pairs):
                aug_keys(
                    kv, pair, pairs, (rank - distance) * SEGS_DEV + part * (block // SEG),
                    k_aug, v_aug, pl.multiple_of(distance * rows_all + part * block, block),
                )

    dk[...] = jnp.zeros(dk.shape, F32)
    dv[...] = jnp.zeros(dv.shape, F32)
    dq[...] = jnp.zeros(dq.shape, F32)
    second_acc[...] = jnp.zeros(second_acc.shape, F32)
    first_acc[...] = jnp.zeros(first_acc.shape, F32)
    o_in_acc[...] = jnp.zeros(o_in_acc.shape, F32)
    o_out_acc[...] = jnp.zeros(o_out_acc.shape, F32)
    packed[...] = jnp.zeros(packed.shape, F32)

    middle = middle_ref[...]
    normed_two = rms_scale(middle, gain_two[...]).astype(BF16)
    logits = dot(normed_two, router[...])
    number = iota((block, LANES), 1)
    hit = jnp.zeros((block, LANES), F32)
    for k in range(routes.shape[1]):
        hit += (routes[:, k : k + 1] == number).astype(F32)
    kept = jnp.where(hit > 0.5, logits, MASKED)
    gates = jnp.exp(kept - jnp.max(kept, axis=1, keepdims=True)) * hit
    gates = gates / jnp.sum(gates, axis=1, keepdims=True)

    if direct:
        pass_sum(0)
        back_sum = end_sum(0)
    else:
        back_sum = back[...].astype(F32)
    table = back_sum[:, model:]
    slopes = table + pltpu.roll(table, LANES - experts, 1)
    logits_grad = gates * (slopes - jnp.sum(gates * slopes, axis=1, keepdims=True))
    high = logits_grad.astype(BF16)
    low = (logits_grad - high.astype(F32)).astype(BF16)
    normed_two_grad = back_sum[:, :model] + dot_nt(high, router[...]) + dot_nt(low, router[...])
    middle_grad[...] = upstream_ref[...].astype(F32) + rms_back(
        middle, gain_two[...], normed_two_grad
    )
    branch = (RESIDUAL_SCALE * middle_grad[...]).astype(BF16)
    branch_all[tp] = branch

    line = Line(branch_all, branch_sem, tp, tp_count)
    line.start()
    if direct:
        pass_sum(1)

    wide = heads * LANES
    r, c = iota((q_cols, wide), 0), iota((q_cols, wide), 1)
    same = r // HEAD == c // LANES
    place = (same & (r % HEAD == c % LANES)).astype(BF16)
    spread = (same & (c % LANES >= ONES) & (c % LANES < ONES + 2)).astype(BF16)

    def tile(part, pair, start, size, causal):
        index = part * pairs + pair
        rows = pl.ds(pl.multiple_of(part * block, block), block)
        queries = q_ref[pl.ds(pair * group, group), rows, :].reshape(tall, LANES)
        upstream = up_aug[pl.ds(pair * group, group), rows, :].reshape(tall, LANES)
        span = pl.ds(start, size)
        keys = k_aug[pair, span, :]
        probs = jnp.exp(dot_nt(keys, queries))
        if causal:
            q_row = iota(probs.shape, 1) % block
            probs = jnp.where(iota(probs.shape, 0) <= q_row, probs, 0.0)
        steep = (probs * dot_nt(v_aug[pair, span, :], upstream)).astype(BF16)
        dv[pair, span, :] += dot(probs.astype(BF16), upstream)
        dk[pair, span, :] += dot(steep, queries)
        dq[index] += dot_tn(steep, keys)

    def far_copy(distance):
        return remote(
            far_out.at[distance - 1], far_in.at[distance - 1],
            kv_sem.at[0, distance - 1], kv_sem.at[1, distance - 1],
            {"ctx": ring(ctx, -distance, ctx_count)},
        )

    size = min(rows_all, 512)

    def take_block(part):
        rows = pl.ds(pl.multiple_of(part * block, block), block)
        low_grad = dot_nt(branch_all[part], o_second[...]).astype(BF16)
        grads = dot_nt(low_grad, o_first[...])
        for side in range(2):
            grads += dot_nt(
                branch_all[part, :, side * half : (side + 1) * half],
                weights[side, pl.ds(half, q_cols), :],
            )
        grads = grads.astype(BF16)
        mixed_heads = att[rows, :]
        o_in_acc[...] += dot_tn(low_grad, mixed_heads)
        o_out_acc[...] += dot_tn(low_ref[rows, :], branch_all[part])
        product = grads.astype(F32) * mixed_heads.astype(F32)
        minus = jnp.zeros((block, wide), F32)
        for _ in range(3):
            piece = product.astype(BF16)
            minus -= dot(piece, spread)
            product -= piece.astype(F32)
        top = minus.astype(BF16).astype(F32)
        lane = iota(minus.shape, 1) % LANES
        coded = dot(grads, place) + jnp.where(
            lane == ONES, top, jnp.where(lane == ONES + 1, minus - top, 0.0)
        )
        for head in range(heads):
            up_aug[head, rows, :] = coded[:, head * LANES : (head + 1) * LANES].astype(BF16)

    @pl.loop(0, line.turns)
    def _(turn):
        part, valid = line.block(turn)

        @pl.when(valid)
        def _():
            line.arrive(turn, part)
            take_block(part)

            @pl.loop(0, rank)
            def _(step):
                distance = rank - step
                start = distance * rows_all

                @pl.loop(0, pairs * (rows_all // size))
                def _(n):
                    pair, piece = n // (rows_all // size), lax.rem(n, rows_all // size)
                    tile(part, pair, pl.multiple_of(start + piece * size, size), size, False)

                @pl.when(turn == line.last())
                def _():
                    @pl.loop(0, tp_count)
                    def _(spot):
                        span = pl.ds(pl.multiple_of(start + spot * block, block), block)
                        rows = pl.ds(pl.multiple_of(spot * block, block), block)
                        far_out[distance - 1, rows, :] = joined(dk, dv, span).astype(BF16)

                    far_copy(distance).start()

            @pl.loop(0, pairs)
            def _(pair):
                tile(part, pair, pl.multiple_of(part * block, block), block, True)

                @pl.loop(0, part)
                def _(j):
                    tile(part, pair, pl.multiple_of(j * block, block), block, False)

    if direct:
        share_own.wait()
        for k in range(1, tp_count):
            share_copy(k).wait()
        swap.start()

    own_kv[...] = joined(dk, dv, pl.ds(0, rows_all))
    for distance in range(1, SPAN):

        @pl.when(rank + distance < SPAN)
        def _(distance=distance):
            far_copy(distance).wait_recv()
            own_kv[...] += far_in[distance - 1].astype(F32)

    def part_copy(k):
        return remote(
            parts.at[k], parts_in.at[k], part_sem.at[0, k], part_sem.at[1, k],
            {"tp": ring(tp, k + 1, tp_count)},
        )

    @pl.loop(0, tp_count)
    def _(k):
        part = ring(tp, k + 1, tp_count)
        rows = pl.ds(pl.multiple_of(part * block, block), block)
        pieces = []
        for pair in range(pairs):
            held = dq[part * pairs + pair]
            turned = SCORE_SCALE * jnp.concatenate(
                [held[member * block : (member + 1) * block, :HEAD] for member in range(group)],
                axis=1,
            )
            pieces.append(turned * cos[rows, :] - swap_halves(turned) * sin[rows, :])
        keys = own_kv[rows, :kv_cols]
        pieces.append(keys * cos[rows, :] - swap_halves(keys) * sin[rows, :])
        pieces.append(own_kv[rows, kv_cols:])
        grads = jnp.concatenate(pieces, axis=1).astype(BF16)
        low_part = dot_nt(grads, second[...]).astype(BF16)
        for side in range(2):
            columns = slice(side * half, (side + 1) * half)
            parts[k, :, columns] = (
                dot_nt(grads, weights[side, pl.ds(0, half), :])
                + dot_nt(low_part, first[columns, :])
            ).astype(BF16)

        @pl.when(k < tp_count - 1)
        def _():
            part_copy(k).start()

        second_acc[...] += dot_tn(lora[rows, :], grads)
        first_acc[...] += dot_tn(low_part, normed_all[part])

    packed[pl.ds(0, 3 * RANK), :] = first_acc[pl.ds(0, 3 * RANK), :]
    packed[pl.ds(4 * RANK, RANK), :] = o_out_acc[pl.ds(0, RANK), :]
    lanes = pl.ds(pl.multiple_of(tp * q_cols, q_cols), q_cols)
    packed[pl.ds(3 * RANK, RANK), lanes] = o_in_acc[pl.ds(0, RANK), :]
    packed[pl.ds(5 * RANK, RANK), lanes] = second_acc[pl.ds(0, RANK), :q_cols]
    lanes = pl.ds(pl.multiple_of(tp * kv_cols, kv_cols), kv_cols)
    packed[pl.ds(6 * RANK, RANK), lanes] = second_acc[pl.ds(RANK, RANK), q_cols : q_cols + kv_cols]
    lanes = pl.ds(pl.multiple_of(model // 2 + tp * kv_cols, kv_cols), kv_cols)
    packed[pl.ds(6 * RANK, RANK), lanes] = second_acc[pl.ds(2 * RANK, RANK), q_cols + kv_cols :]

    if direct:
        tall_rows, few_rows = packed.shape[0] // ctx_count, packed.shape[0] // (ctx_count * tp_count)

        def ctx_rows(index):
            return pl.ds(pl.multiple_of(index * tall_rows, tall_rows), tall_rows)

        def tp_rows(index):
            start = ctx * tall_rows + index * few_rows
            return pl.ds(pl.multiple_of(start, few_rows), few_rows)

        def ctx_copy(k):
            where = ring(ctx, k, ctx_count)
            return remote(
                packed.at[ctx_rows(where)], ctx_in.at[k - 1],
                ctx_sem.at[0, k - 1], ctx_sem.at[1, k - 1], {"ctx": where},
            )

        def tp_copy(k):
            where = ring(tp, k, tp_count)
            return remote(
                packed.at[tp_rows(where)], tp_in.at[k - 1],
                tp_sem.at[0, k - 1], tp_sem.at[1, k - 1], {"tp": where},
            )

        x_copy = remote(
            packed_out.at[fsdp, tp_rows(tp)], packed_out.at[fsdp, tp_rows(tp)],
            x_sem.at[0], x_sem.at[1], other,
        )

        def tp_all_copy(k):
            return remote(
                packed_out.at[:, tp_rows(tp)], packed_out.at[:, tp_rows(tp)],
                tp_all_sem.at[0, k - 1], tp_all_sem.at[1, k - 1], {"tp": ring(tp, k, tp_count)},
            )

        def ctx_all_copy(k):
            return remote(
                packed_out.at[:, ctx_rows(ctx)], packed_out.at[:, ctx_rows(ctx)],
                ctx_all_sem.at[0, k - 1], ctx_all_sem.at[1, k - 1],
                {"ctx": ring(ctx, k, ctx_count)},
            )

        for k in range(1, ctx_count):
            ctx_copy(k).start()
        for k in range(1, ctx_count):
            ctx_copy(k).wait()
        packed[ctx_rows(ctx), :] = packed[ctx_rows(ctx), :] + sum(
            ctx_in[k] for k in range(ctx_count - 1)
        )
        for k in range(1, tp_count):
            tp_copy(k).start()
        for k in range(1, tp_count):
            tp_copy(k).wait()
        packed_out[fsdp, tp_rows(tp), :] = packed[tp_rows(tp), :] + sum(
            tp_in[k] for k in range(tp_count - 1)
        )
        x_copy.start()
        x_copy.wait()
        for k in range(1, tp_count):
            tp_all_copy(k).start()
        for k in range(1, tp_count):
            tp_all_copy(k).wait()
        for k in range(1, ctx_count):
            ctx_all_copy(k).start()
    else:
        packed_out[0] = packed[...]

    summed = parts[tp_count - 1].astype(F32)
    for k in range(tp_count - 1):
        part_copy(k).wait_recv()
        summed += parts_in[k].astype(F32)
    inputs = tokens[...].astype(F32)
    input_grad[...] = (middle_grad[...] + rms_back(inputs, gain_one[...], summed)).astype(BF16)
    mixture = end_sum(1) if direct else mixed[...].astype(F32)
    output[...] = (middle_ref[...] + RESIDUAL_SCALE * mixture).astype(BF16)

    if direct:
        swap.wait()
        for k in range(1, ctx_count):
            ctx_all_copy(k).wait()
        for n in range(2):
            for slot in range(2):
                near_copy(n, slot).wait_send()
            pair_copy(n).wait_send()
    line.end()
    for k in range(tp_count - 1):
        part_copy(k).wait_send()
    for distance in range(1, SPAN):

        @pl.when(distance <= rank)
        def _(distance=distance):
            far_copy(distance).wait_send()


def backward(
    tokens, upstream, routes, gains, router, middle, low, weights, normed, lora, att, queries, kv,
    first, second, o_first, o_second, cos, sin, back, mixed, shares, tp_count, ctx_count, experts, direct,
):
    block, model = tokens.shape
    heads, rows, _ = queries.shape
    pairs = kv.shape[3] // (2 * HEAD)
    tall = heads // pairs * block
    cols = second.shape[1]
    kv_width = kv.shape[3]
    vmem = pl.BlockSpec(memory_space=pltpu.VMEM)
    hbm = pl.BlockSpec(memory_space=pl.ANY)
    dma = pltpu.SemaphoreType.DMA
    part = (block, model)
    packed = (8 * RANK, model)
    copies = 2 if direct else 1
    slim = (8, LANES)

    def buffers(width):
        shapes = [(2, block, width), (2, block, width), (block, width), (block, width)]
        return [pltpu.VMEM(shape if direct else slim, BF16) for shape in shapes]

    return pl.pallas_call(
        functools.partial(
            backward_kernel, tp_count=tp_count, ctx_count=ctx_count, experts=experts, direct=direct
        ),
        in_specs=[vmem] * 20 + [hbm if direct else vmem] * 2 + [hbm],
        out_specs=[vmem] * 3 + [hbm],
        out_shape=[
            jax.ShapeDtypeStruct((block, model), BF16),
            jax.ShapeDtypeStruct((block, model), BF16),
            jax.ShapeDtypeStruct((copies,) + packed, F32),
            jax.ShapeDtypeStruct(
                (2,) + shares.shape[:2] + (tp_count * shares.shape[2],) if direct else slim, BF16
            ),
        ],
        scratch_shapes=[
            pltpu.VMEM((pairs, SPAN * rows, LANES), BF16),
            pltpu.VMEM((pairs, SPAN * rows, LANES), BF16),
            pltpu.VMEM((heads, rows, LANES), BF16),
            pltpu.VMEM((pairs, SPAN * rows, LANES), F32),
            pltpu.VMEM((pairs, SPAN * rows, LANES), F32),
            pltpu.VMEM((tp_count * pairs, tall, LANES), F32),
            pltpu.VMEM((tp_count, block, model), BF16),
            pltpu.VMEM((SPAN - 1, rows, kv_width), BF16),
            pltpu.VMEM((SPAN - 1, rows, kv_width), BF16),
            pltpu.VMEM((rows, kv_width), F32),
            pltpu.VMEM((tp_count,) + part, BF16),
            pltpu.VMEM((tp_count - 1,) + part, BF16),
            pltpu.VMEM((LANES, cols), F32),
            pltpu.VMEM((LANES, model), F32),
            pltpu.VMEM((LANES, heads * HEAD), F32),
            pltpu.VMEM((LANES, model), F32),
            pltpu.VMEM(packed, F32),
            pltpu.VMEM((ctx_count - 1, packed[0] // ctx_count, model) if direct else slim, F32),
            pltpu.VMEM((tp_count - 1, 8, model) if direct else slim, F32),
            pltpu.VMEM((block, model), F32),
            *buffers(model + LANES),
            *buffers(model),
            dma((2, 4)),
            dma((4,)),
            dma((2, 2)),
            dma((2, 2, tp_count)),
            dma((2, SPAN - 1)),
            dma((2, tp_count - 1)),
            dma((2, ctx_count - 1)),
            dma((2, tp_count - 1)),
            dma((2,)),
            dma((2, tp_count - 1)),
            dma((2, ctx_count - 1)),
            dma((2, tp_count - 1)),
            dma((2,)),
            dma((1,)),
        ],
        compiler_params=pltpu.CompilerParams(
            vmem_limit_bytes=60 * 1024 * 1024, collective_id=1, has_side_effects=True
        ),
        cost_estimate=pl.CostEstimate(
            flops=32 * SPAN * rows * rows * heads * LANES,
            bytes_accessed=32 * 1024 * 1024,
            transcendentals=0,
        ),
        name="backward",
    )(
        tokens, upstream, routes, *gains, router, middle, low, weights, normed, lora, att, queries,
        kv, first, second, o_first, o_second, cos, sin, back, mixed, shares,
    )


def columns_of(chosen):
    return iota((RANK, LANES), 1) == iota((RANK, LANES), 0) + chosen * RANK


def place_kernel(sets, packed, *outs):
    query_in, query_out, key_in, key_out, value_in, value_out, out_in, out_out = outs
    kv_cols = key_out.shape[1]
    exact = dict(precision=lax.Precision.HIGHEST, preferred_element_type=F32)

    def gathered(rows, lanes, turned):
        total = None
        for tree in range(packed.shape[0]):
            spots = columns_of(sets[tree]).astype(F32)
            piece = packed[tree, rows * RANK : (rows + 1) * RANK, lanes]
            pair = (piece, spots) if turned else (spots, piece)
            term = lax.dot_general(*pair, (((0,), (0,)), ((), ())), **exact)
            total = term if total is None else total + term
        return total

    whole = slice(None)
    query_in[...] = gathered(0, whole, True)
    key_in[...] = gathered(1, whole, True)
    value_in[...] = gathered(2, whole, True)
    out_in[...] = gathered(3, whole, True)
    out_out[...] = gathered(4, whole, False)
    query_out[...] = gathered(5, whole, False)
    key_out[...] = gathered(6, slice(0, kv_cols), False)
    value_out[...] = gathered(6, slice(kv_cols, 2 * kv_cols), False)


def place(sets, packed, outs):
    vmem = pl.BlockSpec(memory_space=pltpu.VMEM)
    return pl.pallas_call(
        place_kernel,
        in_specs=[pl.BlockSpec(memory_space=pltpu.SMEM), vmem],
        out_specs=[vmem] * len(outs),
        out_shape=[jax.ShapeDtypeStruct(o.shape, F32) for o in outs],
        compiler_params=pltpu.CompilerParams(vmem_limit_bytes=VMEM_LIMIT),
        name="place",
    )(sets, packed)


def place_experts_kernel(sets, part, gate_in, gate_out, up_in, up_out, down_in, down_out):
    hidden = gate_out.shape[2]

    def gathered(rows, lanes, turned):
        total = None
        for tree in range(part.shape[0]):
            spots = columns_of(sets[tree]).astype(BF16)
            piece = part[tree, 0, rows * RANK : (rows + 1) * RANK, lanes]
            term = dot_tn(piece, spots) if turned else dot_tn(spots, piece)
            total = term if total is None else total + term
        return total

    whole, left, right = slice(None), slice(0, hidden), slice(hidden, 2 * hidden)
    gate_in[0] = gathered(0, whole, True)
    up_in[0] = gathered(1, whole, True)
    gate_out[0] = gathered(2, left, False)
    up_out[0] = gathered(2, right, False)
    down_out[0] = gathered(3, whole, False)
    down_in[0] = gathered(4, left, True)


def place_experts(sets, part, outs):
    trees, local = part.shape[:2]
    return pl.pallas_call(
        place_experts_kernel,
        grid_spec=pltpu.PrefetchScalarGridSpec(
            num_scalar_prefetch=1,
            grid=(local,),
            in_specs=[pl.BlockSpec((trees, 1) + part.shape[2:], lambda e, s: (0, e, 0, 0))],
            out_specs=[pl.BlockSpec((1,) + o.shape[1:], lambda e, s: (e, 0, 0)) for o in outs],
        ),
        out_shape=[jax.ShapeDtypeStruct(o.shape, F32) for o in outs],
        compiler_params=pltpu.CompilerParams(vmem_limit_bytes=VMEM_LIMIT),
        name="place_experts",
    )(sets, part)


def expert_kernel(
    sets, x_ref, g_ref, routes, router,
    w_gate, w_up, w_down, w_gate_far, w_up_far, w_down_far, all_gate, all_up, all_down, gate_in, up_in, gate_out, up_out, down_in, down_out,
    back_out, mixed_out, grad_out,
    rank_rows, gate_rows, slope_rows, mix, back, xs, firsts, tall_grad,
    gate_full, up_full, down_full, land_gate, land_up, land_down, grads, grads_in,
    far_sem, pass_far_sem, grads_sem, arrive_sem,
    *, slots, sources, early, shared, straight, tp_count,
):
    chunk, expert = pl.program_id(0), pl.program_id(1)
    tp, fsdp = lax.axis_index("tp"), lax.axis_index("fsdp")
    late = shared + straight
    gather = late > 0
    other = {"fsdp": 1 - fsdp}
    cross, hand_on = far_moves(
        (all_gate, all_up, all_down), (land_gate, land_up, land_down), far_sem, pass_far_sem,
        shared, straight, early, 0, other, tp,
    )

    if gather:

        @pl.when(expert == 0)
        def _():
            barrier = pltpu.get_barrier_semaphore()
            pl.semaphore_signal(
                barrier, 1, device_id=other, device_id_type=pl.DeviceIdType.MESH
            )
            for k in range(1, tp_count):
                pl.semaphore_signal(
                    barrier, 1, device_id={"tp": ring(tp, k, tp_count)},
                    device_id_type=pl.DeviceIdType.MESH,
                )
            pl.semaphore_wait(barrier, tp_count)
            for n in BEGIN[0]:
                for copy in cross(n):
                    copy.start()

        for step in range(1, early + late):
            if step in BEGIN or step in RELAY:

                @pl.when(expert == step)
                def _(step=step):
                    for n in RELAY.get(step, ()):
                        for copy in cross(n):
                            copy.wait_recv()
                        for copy in hand_on(n):
                            copy.start()
                    for n in BEGIN.get(step, ()):
                        for copy in cross(n):
                            copy.start()

        for n in range(late):

            @pl.when(expert == early + n)
            def _(n=n):
                for copy in hand_on(n) if n < shared else cross(n):
                    copy.wait_recv()

    experts = router.shape[0]
    tokens, model = x_ref.shape
    each = tokens // sources
    hidden = w_gate.shape[2]
    lanes = gate_in.shape[2]
    chosen = sets[chunk]

    @pl.when(expert == 0)
    def _():
        logits = dot_nt(router[...], x_ref[...])
        number = iota((experts, tokens), 0)
        hit = jnp.zeros((experts, tokens), F32)
        for k in range(routes.shape[0]):
            hit += (routes[k : k + 1, :] == number).astype(F32)
        kept = jnp.where(hit > 0.5, logits, MASKED)
        weights = jnp.exp(kept - jnp.max(kept, axis=0, keepdims=True)) * hit
        gate_rows[...] = weights / jnp.sum(weights, axis=0, keepdims=True)
        earlier = (iota((each, each), 0) < iota((each, each), 1)).astype(BF16)
        for s in range(sources):
            span = slice(s * each, (s + 1) * each)
            order = dot(hit[:, span].astype(BF16), earlier)
            rank_rows[:, span] = jnp.where(hit[:, span] > 0.5, order, -1.0)
        mix[...] = jnp.zeros(mix.shape, F32)
        back[...] = jnp.zeros(back.shape, F32)
        slope_rows[...] = jnp.zeros(slope_rows.shape, F32)

    first_row = lax.axis_index("ctx") * pl.num_programs(1)
    row = first_row + expert
    ranks = rank_rows[pl.ds(row, 1), :]
    gates = gate_rows[pl.ds(row, 1), :]
    slot_number = iota((slots, each), 0).astype(F32)
    picks, columns, upstreams = [], [], []
    for s in range(sources):
        span = slice(s * each, (s + 1) * each)
        pick = ranks[:, span] == slot_number
        columns.append(jnp.sum(jnp.where(pick, gates[:, span], 0.0), axis=1, keepdims=True))
        pick = pick.astype(BF16)
        picks.append(pick)
        xs[pl.ds(s * slots, slots), :] = dot(pick, x_ref[pl.ds(s * each, each), :]).astype(BF16)
        upstreams.append(dot(pick, g_ref[pl.ds(s * each, each), :]))
    gate_column = jnp.concatenate(columns, axis=0)
    upstream = RESIDUAL_SCALE * jnp.concatenate(upstreams, axis=0)

    firsts[:, :lanes] = gate_in[0]
    firsts[:, lanes:] = up_in[0]
    keep = (iota((1, 2 * lanes), 1) % lanes // RANK == chosen).astype(BF16)
    rows = xs[...]
    inner = dot(rows, firsts[...]).astype(BF16) * keep
    for full, near, far, landed in (
        (gate_full, w_gate, w_gate_far, land_gate),
        (up_full, w_up, w_up_far, land_up),
        (down_full, w_down, w_down_far, land_down),
    ):
        size = near.shape[1]
        full[pl.ds(pl.multiple_of(fsdp * size, size), size), :] = near[0]
        spot = pl.ds(pl.multiple_of((1 - fsdp) * size, size), size)
        if not gather:
            full[spot, :] = far[0]
            continue

        @pl.when(expert < early)
        def _(full=full, far=far, spot=spot):
            full[spot, :] = far[0]

        @pl.when(expert >= early)
        def _(full=full, landed=landed, spot=spot):
            full[spot, :] = landed[jnp.maximum(expert - early, 0)]
    gate_value = dot(rows, gate_full[...]) + dot(inner[:, :lanes], gate_out[0])
    up_value = dot(rows, up_full[...]) + dot(inner[:, lanes:], up_out[0])
    sigmoid = 1.0 / (1.0 + jnp.exp(-gate_value))
    silu = gate_value * sigmoid
    active = (silu * up_value).astype(BF16)
    down_inner = dot(active, down_in[0]).astype(BF16) * keep[:, :lanes]
    produced = (
        (dot(active, down_full[...]) + dot(down_inner, down_out[0])).astype(BF16).astype(F32)
    )
    slope = jnp.sum(upstream * produced, axis=1, keepdims=True)
    sent = (gate_column * produced).astype(BF16)
    slot_grad = (gate_column * upstream).astype(BF16)

    down_inner_grad = dot_nt(slot_grad, down_out[0]).astype(BF16) * keep[:, :lanes]
    active_grad = (
        (dot_nt(slot_grad, down_full[...]) + dot_nt(down_inner_grad, down_in[0]))
        .astype(BF16)
        .astype(F32)
    )
    gate_grad = (active_grad * up_value * (sigmoid + silu * (1.0 - sigmoid))).astype(BF16)
    up_grad = (active_grad * silu).astype(BF16)
    inner_grad = (
        jnp.concatenate([dot_nt(gate_grad, gate_out[0]), dot_nt(up_grad, up_out[0])], axis=1)
    ).astype(BF16) * keep
    row_grad = (
        dot_nt(gate_grad, gate_full[...])
        + dot_nt(up_grad, up_full[...])
        + dot_nt(inner_grad, firsts[...])
    ).astype(BF16)

    for s in range(sources):
        span = slice(s * slots, (s + 1) * slots)
        spot = pl.ds(s * each, each)
        mix[spot, :] += dot_tn(picks[s], sent[span, :])
        back[spot, :] += dot_tn(picks[s], row_grad[span, :])
        slope_rows[pl.ds(expert, 1), spot] = jnp.sum(
            jnp.where(picks[s] > 0.5, slope[span, :], 0.0), axis=0, keepdims=True
        )

    keep_at = expert if gather else 0

    def folded(start, width):
        total = tall_grad[pl.ds(start, RANK), :width]
        for shift in range(RANK, lanes, RANK):
            total += tall_grad[pl.ds(start + shift, RANK), :width]
        return total.astype(BF16)

    tall_grad[...] = dot_tn(inner_grad, rows)
    grads[keep_at, pl.ds(0, RANK), :] = folded(0, model)
    grads[keep_at, pl.ds(RANK, RANK), :] = folded(lanes, model)
    tall_grad[pl.ds(0, lanes), :hidden] = dot_tn(inner[:, :lanes], gate_grad)
    tall_grad[pl.ds(0, lanes), hidden:] = dot_tn(inner[:, lanes:], up_grad)
    grads[keep_at, pl.ds(2 * RANK, RANK), :] = folded(0, model)
    tall_grad[pl.ds(0, lanes), :] = dot_tn(down_inner, slot_grad)
    grads[keep_at, pl.ds(3 * RANK, RANK), :] = folded(0, model)
    tall_grad[pl.ds(0, lanes), :hidden] = dot_tn(down_inner_grad, active)
    grads[keep_at, pl.ds(4 * RANK, RANK), :hidden] = folded(0, hidden)
    grads[keep_at, pl.ds(4 * RANK, RANK), hidden:] = jnp.zeros((RANK, model - hidden), BF16)

    share = tall_grad.shape[1] // tp_count

    def grads_copy(n, k):
        where = ring(tp, k, tp_count)
        lanes = pl.ds(pl.multiple_of(where * share, share), share)
        return remote(
            grads.at[n, :, lanes], grads_in.at[k - 1, n], grads_sem.at[k - 1, n],
            arrive_sem.at[k - 1, n], {"tp": where},
        )

    if gather:
        for k in range(1, tp_count):
            grads_copy(expert, k).start()
    else:
        grad_out[0, 0] = grads[0]

    if gather:

        @pl.when(expert == pl.num_programs(1) - 1)
        def _():
            for n in range(late):
                for copy in cross(n):
                    copy.wait_send()
            for n in range(shared):
                for copy in hand_on(n):
                    copy.wait_send()

            @pl.loop(0, pl.num_programs(1))
            def _(n):
                lanes = pl.ds(pl.multiple_of(tp * share, share), share)
                total = grads[n, :, lanes].astype(F32)
                for k in range(1, tp_count):
                    grads_copy(n, k).wait()
                    total += grads_in[k - 1, n].astype(F32)
                grad_out[n] = total.astype(BF16)

    @pl.when(expert == pl.num_programs(1) - 1)
    def _():
        mixed_out[...] = mix[...].astype(BF16)
        back_out[:, :model] = back[...].astype(BF16)
        turned = slope_rows[...].T
        high = turned.astype(BF16)
        low = (turned - high.astype(F32)).astype(BF16)
        local, lane = iota((LANES, LANES), 0), iota((LANES, LANES), 1)
        inside = local < pl.num_programs(1)
        first = (inside & (lane == local + first_row)).astype(BF16)
        later = (inside & (lane == local + first_row + experts)).astype(BF16)
        back_out[:, model:] = (dot(high, first) + dot(low, later)).astype(BF16)


def run_experts(
    sets, rows, upstream, routes, router, weights, far, adapters, slots, sources, tp_count
):
    total, model = rows.shape
    experts = router.shape[0]
    local, half, hidden = weights[0].shape
    trees = sets.shape[0]
    tokens = total // trees
    lanes = adapters[0].shape[2]
    tall = sources * slots
    piece = lambda c, e, *_: (c, 0)
    fixed = lambda c, e, *_: (0, 0)
    expert = lambda c, e, *_: (e, 0, 0)
    pairs, singles, shared, straight = transfer_plan(local, tp_count)
    early, late = pairs + singles, shared + straight
    arrived = lambda c, e, *_: (jnp.minimum(e, early - 1), 0, 0)
    hbm = pl.BlockSpec(memory_space=pl.ANY)
    dma = pltpu.SemaphoreType.DMA
    share = (local, 5 * RANK, model // tp_count)
    gradients = (
        (share, pl.BlockSpec(share, lambda c, e, *_: (0, 0, 0)))
        if late
        else (
            (trees, local, 5 * RANK, model),
            pl.BlockSpec((1, 1, 5 * RANK, model), lambda c, e, *_: (c, e, 0, 0)),
        )
    )
    return pl.pallas_call(
        functools.partial(
            expert_kernel, slots=slots, sources=sources, early=early, shared=shared,
            straight=straight, tp_count=tp_count,
        ),
        grid_spec=pltpu.PrefetchScalarGridSpec(
            num_scalar_prefetch=1,
            grid=(trees, local),
            in_specs=[
                pl.BlockSpec((tokens, model), piece),
                pl.BlockSpec((tokens, model), piece),
                pl.BlockSpec((routes.shape[0], tokens), lambda c, e, *_: (0, c)),
                pl.BlockSpec(router.shape, fixed),
                *[pl.BlockSpec((1,) + w.shape[1:], expert) for w in weights],
                *[pl.BlockSpec((1,) + w.shape[1:], arrived) for w in weights],
                *[hbm] * len(weights),
                *[pl.BlockSpec((1,) + a.shape[1:], expert) for a in adapters],
            ],
            out_specs=[
                pl.BlockSpec((tokens, model + LANES), piece),
                pl.BlockSpec((tokens, model), piece),
                gradients[1],
            ],
            scratch_shapes=[
                pltpu.VMEM((experts, tokens), F32),
                pltpu.VMEM((experts, tokens), F32),
                pltpu.VMEM((LANES, tokens), F32),
                pltpu.VMEM((tokens, model), F32),
                pltpu.VMEM((tokens, model), F32),
                pltpu.VMEM((tall, model), BF16),
                pltpu.VMEM((model, 2 * lanes), BF16),
                pltpu.VMEM((2 * lanes, model), F32),
                pltpu.VMEM((2 * half, hidden), BF16),
                pltpu.VMEM((2 * half, hidden), BF16),
                pltpu.VMEM((hidden, model), BF16),
                *[pltpu.VMEM((max(late, 1),) + w.shape[1:], BF16) for w in weights],
                pltpu.VMEM((local if late else 1, 5 * RANK, model), BF16),
                pltpu.VMEM((tp_count - 1,) + (share if late else (1, 16, LANES)), BF16),
                dma((2, max(late, 1), 3)),
                dma((2, max(shared, 1), 3)),
                dma((tp_count - 1, local)),
                dma((tp_count - 1, local)),
            ],
        ),
        out_shape=[
            jax.ShapeDtypeStruct((total, model + LANES), BF16),
            jax.ShapeDtypeStruct((total, model), BF16),
            jax.ShapeDtypeStruct(gradients[0], BF16),
        ],
        compiler_params=(
            pltpu.CompilerParams(
                vmem_limit_bytes=60 * 1024 * 1024, collective_id=2, has_side_effects=True
            )
            if late
            else pltpu.CompilerParams(vmem_limit_bytes=60 * 1024 * 1024)
        ),
        name="experts",
        cost_estimate=pl.CostEstimate(
            flops=2 * local * total * model * model * 2,
            bytes_accessed=8 * 1024 * 1024,
            transcendentals=0,
        ),
    )(sets, rows, upstream, routes, router, *weights, *far, *weights, *adapters)


def take_set(table, chosen, axis):
    return lax.dynamic_slice_in_dim(table, chosen * RANK, RANK, axis)


def per_device(
    tokens,
    out_grad,
    routes,
    parents,
    adapter_set,
    gain_a,
    gain_b,
    w_query,
    key_projection_matrix,
    value_projection_matrix,
    w_output,
    w_router,
    w_gate,
    w_up,
    w_down,
    query_in,
    query_out,
    key_in,
    key_second_factor,
    value_in,
    value_second_factor,
    out_in,
    out_out,
    gate_in,
    gate_out,
    up_in,
    up_out,
    down_in,
    down_out,
):
    tp_rank = lax.axis_index("tp")
    ctx_rank = lax.axis_index("ctx")
    fsdp_rank = lax.axis_index("fsdp")
    ctx_count = lax.axis_size("ctx")
    tp_count = lax.axis_size("tp")
    fsdp_count = lax.axis_size("fsdp")
    tok_rows, model = tokens.shape
    q_cols = w_query.shape[1]
    kv_cols = key_projection_matrix.shape[1]
    heads, pairs = q_cols // HEAD, kv_cols // HEAD
    experts = w_router.shape[1]
    local_experts = w_gate.shape[0]
    sets = query_in.shape[1] // RANK
    slots = tok_rows * TOP * 3 // (2 * experts)
    trees = ctx_count // SPAN

    attention_shard = jnp.concatenate(
        [
            jnp.concatenate([w_query, key_projection_matrix, value_projection_matrix], axis=1),
            w_output,
        ],
        axis=0,
    )

    seg_start = (fsdp_rank * ctx_count + ctx_rank) * SEGS_DEV
    tree_index = seg_start // TREE_SEGS
    local_start = seg_start % TREE_SEGS
    rank = (local_start // SEGS_DEV).astype(jnp.int32).reshape(1)
    tree_parents = lax.dynamic_slice_in_dim(parents, tree_index * TREE_SEGS, TREE_SEGS, 0)
    reach, depth = tree_links(tree_parents)
    chosen = lax.dynamic_slice_in_dim(adapter_set, tree_index, 1, 0)[0]

    gain_one = gain_a.astype(F32)
    gain_two = gain_b.astype(F32)

    own_reach = lax.dynamic_slice_in_dim(reach, local_start, SEGS_DEV, 0)
    codes = jnp.pad(
        jnp.where(own_reach > 0.5, 0.0, MASKED), ((0, 0), (CODE, LANES - CODE - TREE_SEGS))
    )
    codes = jnp.repeat(codes.astype(BF16), SEG, axis=0)
    own_depth = lax.dynamic_slice_in_dim(depth, local_start, SEGS_DEV, 0)
    positions = (
        own_depth[:, None] * SEG + jnp.arange(SEG, dtype=jnp.int32).astype(F32)[None, :]
    ).reshape(-1)
    half_head = HEAD // 2
    freqs = ROPE_BASE ** (-(jnp.arange(half_head, dtype=jnp.int32).astype(F32) * 2.0) / HEAD)
    angles = positions[:, None] * jnp.tile(freqs, LANES // half_head)[None, :]
    cos, sin = jnp.cos(angles), jnp.sin(angles)

    first = jnp.pad(
        jnp.concatenate(
            [take_set(t, chosen, 1) for t in (query_in, key_in, value_in)], axis=1
        ),
        ((0, 0), (0, LANES - 3 * RANK)),
    )
    q_second = lax.dynamic_slice(query_out, (chosen * RANK, tp_rank * q_cols), (RANK, q_cols))
    k_second = lax.dynamic_slice(
        key_second_factor, (chosen * RANK, tp_rank * kv_cols), (RANK, kv_cols)
    )
    v_second = lax.dynamic_slice(
        value_second_factor, (chosen * RANK, tp_rank * kv_cols), (RANK, kv_cols)
    )
    second = jnp.concatenate(
        [
            jnp.pad(q_second, ((0, 0), (0, 2 * kv_cols))),
            jnp.pad(k_second, ((0, 0), (q_cols, kv_cols))),
            jnp.pad(v_second, ((0, 0), (q_cols + kv_cols, 0))),
            jnp.zeros((LANES - 3 * RANK, q_cols + 2 * kv_cols), BF16),
        ],
        axis=0,
    )
    o_first = jnp.pad(
        lax.dynamic_slice(out_in, (tp_rank * q_cols, chosen * RANK), (q_cols, RANK)),
        ((0, 0), (0, LANES - RANK)),
    )
    o_second = jnp.pad(take_set(out_out, chosen, 0), ((0, LANES - RANK), (0, 0)))

    (
        attended, queries, kv_parts, lora, middle, o_reduced, attention_weights,
        normed_all, *far_weights, upstream_all, routes_all, rows_all,
    ) = forward(
        tokens, (gain_one[None], gain_two[None]), attention_shard, first, second,
        o_first, o_second, cos, sin, codes, (w_gate, w_up, w_down), out_grad, routes.T,
        tp_count, ctx_count,
    )
    upstream_all = upstream_all.reshape(-1, model)
    rows_all = rows_all.reshape(-1, model)
    routes_all = routes_all.transpose(1, 0, 2).reshape(TOP, -1)

    tree_sets = lax.dynamic_slice_in_dim(adapter_set, fsdp_rank * trees, trees, 0)
    back, mixed, expert_part = run_experts(
        tree_sets,
        rows_all,
        upstream_all,
        routes_all,
        w_router.T,
        (w_gate, w_up, w_down),
        far_weights,
        (gate_in, up_in, gate_out, up_out, down_in, down_out),
        slots,
        SPAN,
        tp_count,
    )
    direct = ctx_count == SPAN
    if direct:
        back = back.reshape(ctx_count, tok_rows, -1)
        mixed = mixed.reshape(ctx_count, tok_rows, -1)
    else:
        back = lax.psum_scatter(back, "ctx", scatter_dimension=0, tiled=True)
        mixed = lax.psum_scatter(mixed, "ctx", scatter_dimension=0, tiled=True)
    output, input_grad, packed, all_shares = backward(
        tokens, out_grad, routes, (gain_one[None], gain_two[None]),
        jnp.pad(w_router, ((0, 0), (0, LANES - experts))), middle, o_reduced, attention_weights,
        normed_all, lora, attended, queries, kv_parts, first, second, o_first, o_second,
        cos, sin, back, mixed, expert_part, tp_count, ctx_count, experts, direct,
    )
    all_trees = fsdp_count * trees
    if not direct:
        mine = (jnp.arange(all_trees, dtype=jnp.int32) == tree_index)[:, None, None]
        packed = lax.psum(jnp.where(mine, packed, 0.0), ("fsdp", "ctx", "tp"))
    adapter_totals = place(
        adapter_set,
        packed,
        (
            query_in, query_out, key_in, key_second_factor, value_in, value_second_factor,
            out_in, out_out,
        ),
    )

    if direct:
        expert_part = all_shares
    else:
        expert_part = lax.all_gather(lax.psum(expert_part, "tp"), "fsdp")
        expert_part = expert_part.reshape(all_trees, local_experts, 5 * RANK, model)
    expert_totals = place_experts(
        adapter_set, expert_part, (gate_in, gate_out, up_in, up_out, down_in, down_out)
    )
    return (output, input_grad, *adapter_totals, *expert_totals)


def solution(mesh):
    in_specs = (
        P(("fsdp", "ctx", "tp"), None),
        P(("fsdp", "ctx", "tp"), None),
        P(("fsdp", "ctx", "tp"), None),
        P(),
        P(),
        P(),
        P(),
        P("fsdp", "tp"),
        P("fsdp", "tp"),
        P("fsdp", "tp"),
        P("tp", "fsdp"),
        P(),
        P("ctx", "fsdp", None),
        P("ctx", "fsdp", None),
        P("ctx", "fsdp", None),
        P(),
        P(),
        P(),
        P(),
        P(),
        P(),
        P(),
        P(),
        P("ctx", None, None),
        P("ctx", None, None),
        P("ctx", None, None),
        P("ctx", None, None),
        P("ctx", None, None),
        P("ctx", None, None),
    )
    out_specs = (
        P(("fsdp", "ctx", "tp"), None),
        P(("fsdp", "ctx", "tp"), None),
        P(),
        P(),
        P(),
        P(),
        P(),
        P(),
        P(),
        P(),
        P("ctx", None, None),
        P("ctx", None, None),
        P("ctx", None, None),
        P("ctx", None, None),
        P("ctx", None, None),
        P("ctx", None, None),
    )
    return jax.shard_map(
        per_device, mesh=mesh, in_specs=in_specs, out_specs=out_specs, check_vma=False
    )
```

```python
import functools

import jax
import jax.numpy as jnp
import numpy as np
from jax import lax
from jax.experimental import pallas as pl
from jax.experimental.pallas import tpu as pltpu
from jax.sharding import PartitionSpec as P

HEAD = 64
TOP = 8
RANK = 16
SEG = 128
SEGS_DEV = 8
TREE_SEGS = 32
SPAN = TREE_SEGS // SEGS_DEV
LANES = 128

RESIDUAL_SCALE = 0.22
SCORE_SCALE = 0.015625
EPSILON = 1e-06
ROPE_BASE = 10000.0
MASKED = -1e30

F32 = jnp.float32
BF16 = jnp.bfloat16

CODE = HEAD
LSE = CODE + TREE_SEGS + 1
ONES = HEAD

VMEM_LIMIT = 56 * 1024 * 1024


def dot(a, b):
    return lax.dot_general(a, b, (((1,), (0,)), ((), ())), preferred_element_type=F32)


def dot_nt(a, b):
    return lax.dot_general(a, b, (((1,), (1,)), ((), ())), preferred_element_type=F32)


def dot_tn(a, b):
    return lax.dot_general(a, b, (((0,), (0,)), ((), ())), preferred_element_type=F32)


def iota(shape, dim):
    return lax.broadcasted_iota(jnp.int32, shape, dim)


def rms_scale(values, gain_row):
    return (
        values * lax.rsqrt(jnp.mean(values * values, axis=-1, keepdims=True) + EPSILON) * gain_row
    )


def rms_back(values, gain_row, grad):
    inv = lax.rsqrt(jnp.mean(values * values, axis=-1, keepdims=True) + EPSILON)
    scaled = grad * gain_row
    inner = jnp.mean(scaled * values, axis=-1, keepdims=True)
    return inv * scaled - values * (inv * inv * inv * inner)


def swap_halves(values):
    width = values.shape[-1]
    lane = iota(values.shape, 1) % HEAD
    ahead = pltpu.roll(values, width - HEAD // 2, 1)
    behind = pltpu.roll(values, HEAD // 2, 1)
    return jnp.where(lane < HEAD // 2, -ahead, behind)


def place_table(rows, source, target):
    r, c = iota((rows, LANES), 0), iota((rows, LANES), 1)
    return ((r - source == c - target) & (c >= target) & (c < target + HEAD)).astype(BF16)


def transfer_plan(local, tp_count):
    if local == 8 and tp_count % 2 == 0:
        return 3, 2, 2, 1
    return 0, local, 0, 0


BEGIN = {"start": (0, 1), "proj": (2,), "own": (3,), "k1": (4,), 0: (0,), 2: (1,), 4: (2,)}
RELAY = {"proj": (0,), "sum": (1, 2), 2: (0,), 4: (1,)}


def remote(src, dst, send, recv, where):
    return pltpu.make_async_remote_copy(
        src_ref=src,
        dst_ref=dst,
        send_sem=send,
        recv_sem=recv,
        device_id=where,
        device_id_type=pl.DeviceIdType.MESH,
    )


def far_moves(near, far, sems, pass_sems, shared, direct, first, land, other, tp):
    mate = {"tp": tp + 1 - 2 * lax.rem(tp, 2)}
    side = lax.rem(tp, 2)

    def piece(ref, rows, which):
        return ref.at[pl.ds(pl.multiple_of(which * rows, rows), rows)]

    def cross(n):
        moves = []
        for a, (source, target) in enumerate(zip(near, far)):
            src, dst = source.at[first + n], target.at[land + n]
            if n < shared:
                rows = src.shape[0] // 2
                src, dst = piece(src, rows, side), piece(dst, rows, side)
            moves.append(remote(src, dst, sems.at[0, n, a], sems.at[1, n, a], other))
        return moves

    def hand_on(n):
        moves = []
        for a, target in enumerate(far):
            dst = target.at[land + n]
            rows = dst.shape[0] // 2
            dst = piece(dst, rows, side)
            moves.append(remote(dst, dst, pass_sems.at[0, n, a], pass_sems.at[1, n, a], mate))
        return moves

    return cross, hand_on


class Line:
    def __init__(self, buffer, sems, me, count):
        self.buffer, self.sems, self.me, self.count = buffer, sems, me, count
        self.turns = 2 * count - 1

    def move(self, way, block):
        where = ring(self.me, 1 if way == 0 else -1, self.count)
        return remote(
            self.buffer.at[block], self.buffer.at[block],
            self.sems.at[way, 0, block], self.sems.at[way, 1, block], {"tp": where},
        )

    def goes(self, way):
        return self.me < self.count - 1 if way == 0 else self.me > 0

    def send(self, way, block):
        @pl.when(self.goes(way))
        def _():
            self.move(way, block).start()

    def start(self):
        self.send(0, self.me)
        self.send(1, self.me)

    def block(self, turn):
        step = (turn + 1) // 2
        block = jnp.where(lax.rem(turn, 2) == 1, self.me - step, self.me + step)
        valid = (block >= 0) & (block < self.count)
        return jnp.clip(block, 0, self.count - 1), valid

    def last(self):
        return jnp.maximum(2 * self.me - 1, 2 * (self.count - 1 - self.me))

    def arrive(self, turn, block):
        for way, odd in ((0, 1), (1, 0)):

            @pl.when((turn > 0) & (lax.rem(turn, 2) == odd))
            def _(way=way):
                self.move(way, block).wait_recv()
                self.send(way, block)

    def end(self):
        for block in range(self.count):
            for way, owned in ((0, block <= self.me), (1, block >= self.me)):

                @pl.when(owned & self.goes(way))
                def _(way=way):
                    self.move(way, block).wait_send()


def ring(me, step, count):
    return lax.rem(me + (step + count), count)


def aug_keys(kv, pair, pairs, first_seg, k_aug, v_aug, start):
    rows, width = kv.shape
    lane = iota((rows, LANES), 1)
    seg = first_seg + iota((rows, LANES), 0) // SEG
    key_code = ((lane - CODE == seg) | ((lane >= LSE) & (lane < LSE + 3))).astype(F32)
    one_code = ((lane == ONES) | (lane == ONES + 1)).astype(F32)
    span = pl.ds(start, rows)
    k_aug[pair, span, :] = (dot(kv, place_table(width, pair * HEAD, 0)) + key_code).astype(BF16)
    v_aug[pair, span, :] = (
        dot(kv, place_table(width, (pairs + pair) * HEAD, 0)) + one_code
    ).astype(BF16)


def forward_kernel(
    parents, adapter_set, tokens, gain_one, gain_two, freqs, w_query, w_key, w_value, w_output,
    query_in, query_out, key_in, key_out, value_in, value_out, out_in, out_out,
    w_gate, w_up, w_down, grads, routes,
    att_out, q_out, kv_out, lora_out, middle_out, low_out, weights, normed_all,
    first, second, o_first, o_second, cos, sin,
    gate_far, up_far, down_far, grads_all, routes_all, rows_all,
    q_aug, k_aug, v_aug, top, acc, parts, parts_in, rows_own, code_table, depth_table,
    shard_sem, normed_sem, kv_sem, part_sem, far_sem, pass_far_sem, grads_sem, routes_sem, rows_sem,
    pass_sem, local_sem,
    *, tp_count, ctx_count, shared, straight,
):
    tp, ctx, fsdp = (lax.axis_index(name) for name in ("tp", "ctx", "fsdp"))
    rank = lax.rem(ctx, SPAN)
    block, model = tokens.shape
    heads = q_aug.shape[0]
    pairs = k_aug.shape[0]
    group = heads // pairs
    tall = group * block
    half = model // 2
    q_cols = heads * HEAD
    kv_cols = pairs * HEAD
    turn = cos.shape[1]
    chips = ctx_count // 2
    partner = ctx + 1 - 2 * lax.rem(ctx, 2)
    other = {"fsdp": 1 - fsdp}

    barrier = pltpu.get_barrier_semaphore()
    pl.semaphore_signal(barrier, 1, device_id=other, device_id_type=pl.DeviceIdType.MESH)
    for k in range(1, tp_count):
        pl.semaphore_signal(
            barrier, 1, device_id={"tp": ring(tp, k, tp_count)},
            device_id_type=pl.DeviceIdType.MESH,
        )
    for k in range(1, ctx_count):
        pl.semaphore_signal(
            barrier, 1, device_id={"ctx": ring(ctx, k, ctx_count)},
            device_id_type=pl.DeviceIdType.MESH,
        )
    pl.semaphore_wait(barrier, tp_count + ctx_count - 1)

    corners = (
        (w_query, 0, 0),
        (w_key, 0, q_cols),
        (w_value, 0, q_cols + kv_cols),
        (w_output, half, 0),
    )
    shard_copies = []
    for n, (source, row, column) in enumerate(corners):
        spot = weights.at[fsdp, pl.ds(row, source.shape[0]), pl.ds(column, source.shape[1])]
        shard_copies.append(remote(source, spot, shard_sem.at[0, n], shard_sem.at[1, n], other))
    for copy in shard_copies:
        copy.start()

    inputs = tokens[...].astype(F32)
    normed = rms_scale(inputs, gain_one[...].astype(F32).reshape(1, model)).astype(BF16)
    normed_all[tp] = normed

    line = Line(normed_all, normed_sem, tp, tp_count)
    line.start()

    def side_copies(k):
        where = {"ctx": ring(ctx, k, ctx_count)}
        return (
            remote(grads, grads_all.at[ctx], grads_sem.at[0, k], grads_sem.at[1, k], where),
            remote(routes, routes_all.at[ctx], routes_sem.at[0, k], routes_sem.at[1, k], where),
        )

    own_copies = (
        pltpu.make_async_copy(grads, grads_all.at[ctx], local_sem.at[0]),
        pltpu.make_async_copy(routes, routes_all.at[ctx], local_sem.at[1]),
    )
    for copy in own_copies:
        copy.start()
    for k in range(1, ctx_count):
        for copy in side_copies(k):
            copy.start()

    for source, row, column in corners:
        weights[fsdp, pl.ds(row, source.shape[0]), pl.ds(column, source.shape[1])] = source[...]

    tree = (fsdp * ctx_count + ctx) // SPAN
    spot_row, spot_lane = iota((LANES, LANES), 0), iota((LANES, LANES), 1)
    linked = (spot_row == spot_lane) & (spot_row < TREE_SEGS)
    for n in range(TREE_SEGS):
        linked |= (spot_row == n) & (spot_lane == parents[tree * TREE_SEGS + n])
    reach = linked.astype(F32)
    for _ in range((TREE_SEGS - 1).bit_length()):
        reach = jnp.minimum(dot(reach.astype(BF16), reach.astype(BF16)), 1.0)
    depth_table[...] = jnp.broadcast_to(
        jnp.sum(reach, axis=1, keepdims=True) - 1.0, (LANES, LANES)
    ).astype(BF16)
    coded = (spot_lane >= CODE) & (spot_lane < CODE + TREE_SEGS)
    code_table[...] = jnp.where(
        coded & (pltpu.roll(reach, CODE, 1) < 0.5), MASKED, 0.0
    ).astype(BF16)

    chosen = adapter_set[tree]

    def pick(n):
        inside = (spot_lane >= n * RANK) & (spot_lane < (n + 1) * RANK)
        return (inside & (spot_row == spot_lane - n * RANK + chosen * RANK)).astype(BF16)

    first[...] = (
        dot(query_in[...], pick(0)) + dot(key_in[...], pick(1)) + dot(value_in[...], pick(2))
    ).astype(BF16)
    for n, (source, column, width) in enumerate(
        ((query_out, 0, q_cols), (key_out, q_cols, kv_cols), (value_out, q_cols + kv_cols, kv_cols))
    ):
        lanes = pl.ds(pl.multiple_of(tp * width, width), width)
        second[:, column : column + width] = dot_tn(pick(n), source[:, lanes]).astype(BF16)
    own = pl.ds(pl.multiple_of(tp * q_cols, q_cols), q_cols)
    o_first[...] = dot(out_in[own, :], pick(0)).astype(BF16)
    o_second[...] = dot_tn(pick(0), out_out[...]).astype(BF16)

    for copy in shard_copies:
        copy.wait()
    cross, hand_on = far_moves(
        (w_gate, w_up, w_down), (gate_far, up_far, down_far), far_sem, pass_far_sem,
        shared, straight, 0, 0, other, tp,
    )

    def point(name):
        if not shared:
            if name == "start":
                for n in range(straight):
                    for copy in cross(n):
                        copy.start()
            return
        for n in RELAY.get(name, ()):
            for copy in cross(n):
                copy.wait_recv()
            for copy in hand_on(n):
                copy.start()
        for n in BEGIN.get(name, ()):
            for copy in cross(n):
                copy.start()

    point("start")

    def kv_copy(distance, part):
        return remote(
            kv_out.at[0, part], kv_out.at[distance, part],
            kv_sem.at[0, distance - 1], kv_sem.at[1, distance - 1], {"ctx": ring(ctx, distance, ctx_count)},
        )

    def project(part):
        span = pl.ds(pl.multiple_of(part * block, block), block)
        rows = normed_all[part]
        seg = rank * SEGS_DEV + (part * block + iota((block, LANES), 0)) // SEG
        at_seg = (seg == iota((block, LANES), 1)).astype(BF16)
        offset = lax.rem(iota((block, LANES), 0), SEG).astype(F32)
        angles = (dot(at_seg, depth_table[...]) * SEG + offset) * freqs[...]
        cos[span, :] = jnp.cos(angles)
        sin[span, :] = jnp.sin(angles)
        codes = dot(at_seg, code_table[...])
        lora = dot(rows, first[...]).astype(BF16)
        lora_out[span, :] = lora
        pre = (
            dot(rows[:, :half], weights[0, pl.ds(0, half), :])
            + dot(rows[:, half:], weights[1, pl.ds(0, half), :])
            + dot(lora, second[...])
        )
        turned = []
        for start in range(0, pre.shape[1] // 4 * 3, turn):
            piece = pre[:, start : start + turn]
            turned.append(piece * cos[span, :] + swap_halves(piece) * sin[span, :])
        queries = (
            jnp.concatenate(turned[: q_cols // turn], axis=1) * SCORE_SCALE
        ).astype(BF16)
        for head in range(heads):
            q_aug[head, span, :] = (
                dot(queries, place_table(q_cols, head * HEAD, 0)) + codes
            ).astype(BF16)
        keys = jnp.concatenate(turned[q_cols // turn :], axis=1)
        kv = jnp.concatenate([keys, pre[:, q_cols + keys.shape[1] :]], axis=1).astype(BF16)
        kv_out[0, part] = kv
        for distance in range(1, SPAN):

            @pl.when(rank + distance < SPAN)
            def _(distance=distance):
                kv_copy(distance, part).start()

        for pair in range(pairs):
            aug_keys(
                kv, pair, pairs, rank * SEGS_DEV + part * (block // SEG), k_aug, v_aug,
                pl.multiple_of(part * block, block),
            )

    @pl.loop(0, line.turns)
    def _(turn):
        part, valid = line.block(turn)

        @pl.when(valid)
        def _():
            line.arrive(turn, part)
            project(part)

    point("proj")

    def tile(part, pair, start, size, causal):
        index = part * pairs + pair
        rows = pl.ds(pl.multiple_of(part * block, block), block)
        queries = q_aug[pl.ds(pair * group, group), rows, :].reshape(tall, LANES)
        span = pl.ds(start, size)
        scores = dot_nt(queries, k_aug[pair, span, :])
        if causal:
            q_row = iota(scores.shape, 0) % block
            scores = jnp.where(iota(scores.shape, 1) <= q_row, scores, MASKED)
            now = jnp.broadcast_to(jnp.max(scores, axis=1, keepdims=True), (tall, LANES))
            probs = jnp.exp(scores - now[:, :1]).astype(BF16)
            acc[index] = dot(probs, v_aug[pair, span, :])
        else:
            before = top[index]
            now = jnp.maximum(before, jnp.max(scores, axis=1, keepdims=True))
            probs = jnp.exp(scores - now[:, :1]).astype(BF16)
            acc[index] = acc[index] * jnp.exp(before - now) + dot(probs, v_aug[pair, span, :])
        top[index] = now

    @pl.loop(0, tp_count * pairs)
    def _(index):
        part, pair = index // pairs, lax.rem(index, pairs)
        tile(part, pair, pl.multiple_of(part * block, block), block, True)

        @pl.loop(0, part)
        def _(j):
            tile(part, pair, pl.multiple_of(j * block, block), block, False)

    point("own")
    group_rows = tp_count * block
    for distance in range(1, SPAN):

        @pl.when(distance <= rank)
        def _(distance=distance):
            remote(
                kv_out.at[0], kv_out.at[distance], kv_sem.at[0, distance - 1],
                kv_sem.at[1, distance - 1], {"ctx": ring(ctx, distance, ctx_count)},
            ).wait_recv()

            @pl.loop(0, tp_count)
            def _(part):
                kv = kv_out[distance, part]
                for pair in range(pairs):
                    aug_keys(
                        kv, pair, pairs,
                        (rank - distance) * SEGS_DEV + part * (block // SEG), k_aug, v_aug,
                        pl.multiple_of(distance * group_rows + part * block, block),
                    )

        @pl.when(distance > rank)
        def _(distance=distance):
            kv_out[distance] = jnp.zeros(kv_out.shape[1:], BF16)

    def part_copy(k):
        return remote(
            parts.at[k], parts_in.at[k], part_sem.at[0, k], part_sem.at[1, k],
            {"tp": ring(tp, k + 1, tp_count)},
        )

    @pl.loop(0, tp_count)
    def _(k):
        part = ring(tp, k + 1, tp_count)
        rows = pl.ds(pl.multiple_of(part * block, block), block)
        for pair in range(pairs):
            index = part * pairs + pair

            @pl.loop(1, rank + 1)
            def _(distance, pair=pair):
                tile(
                    part, pair, pl.multiple_of(distance * group_rows, group_rows), group_rows, False
                )

            summed = acc[index]
            total = summed[:, ONES : ONES + 1]
            result = (summed / total).astype(BF16)
            for member in range(group):
                head = pair * group + member
                att_out[rows, pl.ds(head * HEAD, HEAD)] = result[
                    member * block : (member + 1) * block, :HEAD
                ]
            minus = -(top[index] + jnp.log(total))
            high = minus.astype(BF16).astype(F32)
            middle = (minus - high).astype(BF16).astype(F32)
            lane = iota(minus.shape, 1)
            queries = q_aug[pl.ds(pair * group, group), rows, :].reshape(tall, LANES)
            coded = jnp.where(
                lane == LSE,
                high,
                jnp.where(
                    lane == LSE + 1,
                    middle,
                    jnp.where(lane == LSE + 2, minus - high - middle, queries.astype(F32)),
                ),
            )
            q_out[pl.ds(pair * group, group), rows, :] = coded.astype(BF16).reshape(
                group, block, LANES
            )
        mixed = att_out[rows, :]
        low = dot(mixed, o_first[...]).astype(BF16)
        low_out[rows, :] = low
        for side in range(2):
            columns = slice(side * half, (side + 1) * half)
            parts[k, :, columns] = (
                dot(mixed, weights[side, pl.ds(half, q_cols), :]) + dot(low, o_second[:, columns])
            ).astype(BF16)

        @pl.when(k < tp_count - 1)
        def _():
            part_copy(k).start()

        for n in range(tp_count):
            if f"k{n}" in BEGIN or f"k{n}" in RELAY:

                @pl.when(k == n)
                def _(n=n):
                    point(f"k{n}")

    summed = parts[tp_count - 1].astype(F32)
    for k in range(tp_count - 1):
        part_copy(k).wait_recv()
        summed += parts_in[k].astype(F32)
    point("sum")
    middle = inputs + RESIDUAL_SCALE * summed
    middle_out[...] = middle
    rows_own[...] = rms_scale(middle, gain_two[...].astype(F32).reshape(1, model)).astype(BF16)

    own_rows = pltpu.make_async_copy(rows_own, rows_all.at[ctx], local_sem.at[2])
    own_rows.start()
    to_partner = remote(
        rows_own, rows_all.at[ctx], rows_sem.at[0, 0], rows_sem.at[1, 0], {"ctx": partner}
    )
    to_partner.start()

    def rows_copy(k):
        return remote(
            rows_own, rows_all.at[ctx], rows_sem.at[0, k], rows_sem.at[1, k],
            {"ctx": ring(ctx, 2 * k, ctx_count)},
        )

    def pass_copy(k):
        source = ring(ctx, -2 * k, ctx_count)
        return remote(
            rows_all.at[source], rows_all.at[source], pass_sem.at[0, k], pass_sem.at[1, k],
            {"ctx": partner},
        )

    for k in range(1, chips):
        rows_copy(k).start()
    for k in range(1, chips):
        rows_copy(k).wait_recv()
        pass_copy(k).start()

    line.end()
    for k in range(tp_count - 1):
        part_copy(k).wait_send()
    for distance in range(1, SPAN):

        @pl.when(rank + distance < SPAN)
        def _(distance=distance):
            remote(
                kv_out.at[0], kv_out.at[distance], kv_sem.at[0, distance - 1],
                kv_sem.at[1, distance - 1], {"ctx": ring(ctx, distance, ctx_count)},
            ).wait_send()

    for k in range(1, ctx_count):
        for copy in side_copies(k):
            copy.wait()
    for copy in own_copies:
        copy.wait()
    own_rows.wait()
    to_partner.wait()
    for k in range(1, chips):
        rows_copy(k).wait_send()
        pass_copy(k).wait()
    for n in range(shared + straight):
        for copy in cross(n):
            copy.wait_send()
            if n >= shared:
                copy.wait_recv()
    for n in range(shared):
        for copy in hand_on(n):
            copy.wait()


def forward(
    parents, adapter_set, tokens, gains, attention, adapters, weights, grads, routes,
    tp_count, ctx_count,
):
    block, model = tokens.shape
    rows = tp_count * block
    q_cols, kv_cols = attention[0].shape[1], attention[1].shape[1]
    heads, pairs = q_cols // HEAD, kv_cols // HEAD
    cols = q_cols + 2 * kv_cols
    tall = heads // pairs * block
    chips = ctx_count // 2
    shared, straight, _, _ = transfer_plan(weights[0].shape[0], tp_count)
    vmem = pl.BlockSpec(memory_space=pltpu.VMEM)
    smem = pl.BlockSpec(memory_space=pltpu.SMEM)
    hbm = pl.BlockSpec(memory_space=pl.ANY)
    dma = pltpu.SemaphoreType.DMA
    part = (block, model)
    half_head = HEAD // 2
    freqs = np.float32(ROPE_BASE) ** (-(np.arange(half_head, dtype=np.float32) * 2) / HEAD)
    freqs = jnp.asarray(np.tile(freqs.astype(np.float32), LANES // half_head)[None])
    return pl.pallas_call(
        functools.partial(
            forward_kernel, tp_count=tp_count, ctx_count=ctx_count, shared=shared, straight=straight
        ),
        in_specs=[smem] * 2 + [vmem] * 16 + [hbm] * 5,
        out_specs=[vmem] * 14 + [hbm] * 6,
        out_shape=[
            jax.ShapeDtypeStruct((rows, q_cols), BF16),
            jax.ShapeDtypeStruct((heads, rows, LANES), BF16),
            jax.ShapeDtypeStruct((SPAN, tp_count, block, 2 * kv_cols), BF16),
            jax.ShapeDtypeStruct((rows, LANES), BF16),
            jax.ShapeDtypeStruct((block, model), F32),
            jax.ShapeDtypeStruct((rows, LANES), BF16),
            jax.ShapeDtypeStruct((2, model // 2 + q_cols, model // 2), BF16),
            jax.ShapeDtypeStruct((tp_count, block, model), BF16),
            jax.ShapeDtypeStruct((model, LANES), BF16),
            jax.ShapeDtypeStruct((LANES, cols), BF16),
            jax.ShapeDtypeStruct((q_cols, LANES), BF16),
            jax.ShapeDtypeStruct((LANES, model), BF16),
            jax.ShapeDtypeStruct((rows, LANES), F32),
            jax.ShapeDtypeStruct((rows, LANES), F32),
            *[jax.ShapeDtypeStruct((shared + straight,) + w.shape[1:], BF16) for w in weights],
            jax.ShapeDtypeStruct((ctx_count,) + grads.shape, BF16),
            jax.ShapeDtypeStruct((ctx_count,) + routes.shape, jnp.int32),
            jax.ShapeDtypeStruct((ctx_count, block, model), BF16),
        ],
        scratch_shapes=[
            pltpu.VMEM((heads, rows, LANES), BF16),
            pltpu.VMEM((pairs, SPAN * rows, LANES), BF16),
            pltpu.VMEM((pairs, SPAN * rows, LANES), BF16),
            pltpu.VMEM((tp_count * pairs, tall, LANES), F32),
            pltpu.VMEM((tp_count * pairs, tall, LANES), F32),
            pltpu.VMEM((tp_count,) + part, BF16),
            pltpu.VMEM((tp_count - 1,) + part, BF16),
            pltpu.VMEM((block, model), BF16),
            pltpu.VMEM((LANES, LANES), BF16),
            pltpu.VMEM((LANES, LANES), BF16),
            dma((2, 4)),
            dma((2, 2, tp_count)),
            dma((2, SPAN - 1)),
            dma((2, tp_count - 1)),
            dma((2, shared + straight, 3)),
            dma((2, max(shared, 1), 3)),
            dma((2, ctx_count)),
            dma((2, ctx_count)),
            dma((2, chips)),
            dma((2, chips)),
            dma((3,)),
        ],
        compiler_params=pltpu.CompilerParams(
            vmem_limit_bytes=VMEM_LIMIT, collective_id=0, has_side_effects=True
        ),
        cost_estimate=pl.CostEstimate(
            flops=16 * SPAN * rows * rows * heads * LANES,
            bytes_accessed=32 * 1024 * 1024,
            transcendentals=0,
        ),
        name="forward",
    )(
        parents, adapter_set, tokens, *gains, freqs, *attention, *adapters, *weights, grads, routes,
    )


def joined(dk, dv, span):
    pairs = dk.shape[0]
    return jnp.concatenate(
        [dk[pair, span, :HEAD] for pair in range(pairs)]
        + [dv[pair, span, :HEAD] for pair in range(pairs)],
        axis=1,
    )


def backward_kernel(
    tokens, upstream_ref, routes, gain_one, gain_two, w_router, middle_ref, low_ref, weights,
    normed_all, lora, att, q_ref, kv_ref, first, second, o_first, o_second, cos, sin, back, mixed, shares,
    output, input_grad, packed_out, shares_out,
    k_aug, v_aug, up_aug, dk, dv, dq, branch_all, far_out, far_in, own_kv, row_grads, low_grads, parts, parts_in,
    second_acc, first_acc, o_in_acc, o_out_acc, packed, ctx_in, tp_in, middle_grad, router,
    back_near, back_mine, back_pair, back_far, mixed_near, mixed_mine, mixed_pair, mixed_far,
    near_sem, mine_sem, far_sem, branch_sem, kv_sem, part_sem,
    ctx_sem, tp_sem, x_sem, ctx_all_sem, share_sem, swap_sem, own_sem,
    *, tp_count, ctx_count, experts, direct,
):
    tp, ctx, fsdp = (lax.axis_index(name) for name in ("tp", "ctx", "fsdp"))
    rank = lax.rem(ctx, SPAN)
    block, model = tokens.shape
    heads, rows_all, _ = q_ref.shape
    pairs = k_aug.shape[0]
    group = heads // pairs
    tall = group * block
    half = weights.shape[2]
    q_cols = heads * HEAD
    kv_cols = pairs * HEAD
    turn = cos.shape[1]
    partner = ctx + 1 - 2 * lax.rem(ctx, 2)
    cross = ring(ctx, 2, ctx_count)
    cross_partner = ring(partner, 2, ctx_count)
    other = {"fsdp": 1 - fsdp}

    barrier = pltpu.get_barrier_semaphore()
    pl.semaphore_signal(barrier, 1, device_id=other, device_id_type=pl.DeviceIdType.MESH)
    for k in range(1, tp_count):
        pl.semaphore_signal(
            barrier, 1, device_id={"tp": ring(tp, k, tp_count)},
            device_id_type=pl.DeviceIdType.MESH,
        )
    for k in range(1, ctx_count):
        pl.semaphore_signal(
            barrier, 1, device_id={"ctx": ring(ctx, k, ctx_count)},
            device_id_type=pl.DeviceIdType.MESH,
        )
    pl.semaphore_wait(barrier, tp_count + ctx_count - 1)

    sums = (
        (back, back_near, back_mine, back_pair, back_far),
        (mixed, mixed_near, mixed_mine, mixed_pair, mixed_far),
    )

    def near_copy(n, slot):
        source, near = sums[n][:2]
        return remote(
            source.at[(partner, cross_partner)[slot]], near.at[slot],
            near_sem.at[0, 2 * n + slot], near_sem.at[1, 2 * n + slot], {"ctx": partner},
        )

    def mine_copy(n, slot):
        return pltpu.make_async_copy(
            sums[n][0].at[(ctx, cross)[slot]], sums[n][2].at[slot], mine_sem.at[2 * n + slot]
        )

    def pair_copy(n):
        return remote(sums[n][3], sums[n][4], far_sem.at[0, n], far_sem.at[1, n], {"ctx": cross})

    def start_sum(n):
        for slot in (1, 0):
            near_copy(n, slot).start()
            mine_copy(n, slot).start()

    def pass_sum(n):
        near_copy(n, 1).wait_recv()
        mine_copy(n, 1).wait()
        _, near, mine, pair, _ = sums[n]
        pair[...] = (near[1].astype(F32) + mine[1].astype(F32)).astype(BF16)
        pair_copy(n).start()

    def end_sum(n):
        near_copy(n, 0).wait_recv()
        mine_copy(n, 0).wait()
        pair_copy(n).wait_recv()
        _, near, mine, _, far = sums[n]
        return near[0].astype(F32) + mine[0].astype(F32) + far[...].astype(F32)

    if direct:
        share = shares.shape[2]
        own_lanes = pl.ds(pl.multiple_of(tp * share, share), share)

        def share_copy(k):
            return remote(
                shares, shares_out.at[fsdp, :, :, own_lanes],
                share_sem.at[0, k - 1], share_sem.at[1, k - 1], {"tp": ring(tp, k, tp_count)},
            )

        share_own = pltpu.make_async_copy(shares, shares_out.at[fsdp, :, :, own_lanes], own_sem.at[0])
        swap = remote(
            shares_out.at[fsdp], shares_out.at[fsdp], swap_sem.at[0], swap_sem.at[1], other
        )

        start_sum(0)
        start_sum(1)
        share_own.start()

    @pl.loop(0, rank + 1)
    def _(distance):
        @pl.loop(0, tp_count)
        def _(part):
            kv = kv_ref[distance, part]
            for pair in range(pairs):
                aug_keys(
                    kv, pair, pairs, (rank - distance) * SEGS_DEV + part * (block // SEG),
                    k_aug, v_aug, pl.multiple_of(distance * rows_all + part * block, block),
                )

    dk[...] = jnp.zeros(dk.shape, F32)
    dv[...] = jnp.zeros(dv.shape, F32)
    dq[...] = jnp.zeros(dq.shape, F32)
    second_acc[...] = jnp.zeros(second_acc.shape, F32)
    first_acc[...] = jnp.zeros(first_acc.shape, F32)
    o_in_acc[...] = jnp.zeros(o_in_acc.shape, F32)
    o_out_acc[...] = jnp.zeros(o_out_acc.shape, F32)
    packed[...] = jnp.zeros(packed.shape, F32)

    middle = middle_ref[...]
    scale_one = gain_one[...].astype(F32).reshape(1, model)
    scale_two = gain_two[...].astype(F32).reshape(1, model)
    normed_two = rms_scale(middle, scale_two).astype(BF16)
    router[...] = jnp.zeros(router.shape, BF16)
    router[pl.ds(0, experts), :] = w_router[...]
    logits = dot_nt(normed_two, router[...])
    number = iota((LANES, block), 0)
    hit = jnp.zeros((LANES, block), F32)
    for k in range(routes.shape[0]):
        hit += (routes[k : k + 1, :] == number).astype(F32)
    hit = hit.T
    kept = jnp.where(hit > 0.5, logits, MASKED)
    gates = jnp.exp(kept - jnp.max(kept, axis=1, keepdims=True)) * hit
    gates = gates / jnp.sum(gates, axis=1, keepdims=True)

    if direct:
        pass_sum(0)
        back_sum = end_sum(0)
    else:
        back_sum = back[...].astype(F32)
    table = back_sum[:, model:]
    slopes = table + pltpu.roll(table, LANES - experts, 1)
    logits_grad = gates * (slopes - jnp.sum(gates * slopes, axis=1, keepdims=True))
    high = logits_grad.astype(BF16)
    low = (logits_grad - high.astype(F32)).astype(BF16)
    normed_two_grad = back_sum[:, :model] + dot(high, router[...]) + dot(low, router[...])
    middle_grad[...] = upstream_ref[...].astype(F32) + rms_back(
        middle, scale_two, normed_two_grad
    )
    branch = (RESIDUAL_SCALE * middle_grad[...]).astype(BF16)
    branch_all[tp] = branch

    line = Line(branch_all, branch_sem, tp, tp_count)
    line.start()
    if direct:
        pass_sum(1)

    wide = heads * LANES
    r, c = iota((q_cols, wide), 0), iota((q_cols, wide), 1)
    same = r // HEAD == c // LANES
    place = (same & (r % HEAD == c % LANES)).astype(BF16)
    spread = (same & (c % LANES >= ONES) & (c % LANES < ONES + 2)).astype(BF16)

    def tile(part, pair, start, size, causal):
        index = part * pairs + pair
        rows = pl.ds(pl.multiple_of(part * block, block), block)
        queries = q_ref[pl.ds(pair * group, group), rows, :].reshape(tall, LANES)
        upstream = up_aug[pl.ds(pair * group, group), rows, :].reshape(tall, LANES)
        span = pl.ds(start, size)
        keys = k_aug[pair, span, :]
        probs = jnp.exp(dot_nt(keys, queries))
        if causal:
            q_row = iota(probs.shape, 1) % block
            probs = jnp.where(iota(probs.shape, 0) <= q_row, probs, 0.0)
        steep = (probs * dot_nt(v_aug[pair, span, :], upstream)).astype(BF16)
        dv[pair, span, :] += dot(probs.astype(BF16), upstream)
        dk[pair, span, :] += dot(steep, queries)
        dq[index] += dot_tn(steep, keys)

    def far_copy(distance):
        return remote(
            far_out.at[distance - 1], far_in.at[distance - 1],
            kv_sem.at[0, distance - 1], kv_sem.at[1, distance - 1],
            {"ctx": ring(ctx, -distance, ctx_count)},
        )

    size = min(rows_all, 512)

    def take_block(part):
        rows = pl.ds(pl.multiple_of(part * block, block), block)
        low_grad = dot_nt(branch_all[part], o_second[...]).astype(BF16)
        grads = dot_nt(low_grad, o_first[...])
        for side in range(2):
            grads += dot_nt(
                branch_all[part, :, side * half : (side + 1) * half],
                weights[side, pl.ds(half, q_cols), :],
            )
        grads = grads.astype(BF16)
        mixed_heads = att[rows, :]
        o_in_acc[...] += dot_tn(low_grad, mixed_heads)
        o_out_acc[...] += dot_tn(low_ref[rows, :], branch_all[part])
        product = grads.astype(F32) * mixed_heads.astype(F32)
        minus = jnp.zeros((block, wide), F32)
        for _ in range(3):
            piece = product.astype(BF16)
            minus -= dot(piece, spread)
            product -= piece.astype(F32)
        top = minus.astype(BF16).astype(F32)
        lane = iota(minus.shape, 1) % LANES
        coded = dot(grads, place) + jnp.where(
            lane == ONES, top, jnp.where(lane == ONES + 1, minus - top, 0.0)
        )
        for head in range(heads):
            up_aug[head, rows, :] = coded[:, head * LANES : (head + 1) * LANES].astype(BF16)

    @pl.loop(0, line.turns)
    def _(turn):
        part, valid = line.block(turn)

        @pl.when(valid)
        def _():
            line.arrive(turn, part)
            take_block(part)

            @pl.loop(0, rank)
            def _(step):
                distance = rank - step
                start = distance * rows_all

                @pl.loop(0, pairs * (rows_all // size))
                def _(n):
                    pair, piece = n // (rows_all // size), lax.rem(n, rows_all // size)
                    tile(part, pair, pl.multiple_of(start + piece * size, size), size, False)

                @pl.when(turn == line.last())
                def _():
                    @pl.loop(0, tp_count)
                    def _(spot):
                        span = pl.ds(pl.multiple_of(start + spot * block, block), block)
                        rows = pl.ds(pl.multiple_of(spot * block, block), block)
                        far_out[distance - 1, rows, :] = joined(dk, dv, span).astype(BF16)

                    far_copy(distance).start()

            if direct:

                @pl.when(turn == line.last())
                def _():
                    for k in range(1, tp_count):
                        share_copy(k).start()

            @pl.loop(0, pairs)
            def _(pair):
                tile(part, pair, pl.multiple_of(part * block, block), block, True)

                @pl.loop(0, part)
                def _(j):
                    tile(part, pair, pl.multiple_of(j * block, block), block, False)

    own_kv[...] = joined(dk, dv, pl.ds(0, rows_all))
    for distance in range(1, SPAN):

        @pl.when(rank + distance < SPAN)
        def _(distance=distance):
            far_copy(distance).wait_recv()
            own_kv[...] += far_in[distance - 1].astype(F32)

    def part_copy(k):
        return remote(
            parts.at[k], parts_in.at[k], part_sem.at[0, k], part_sem.at[1, k],
            {"tp": ring(tp, k + 1, tp_count)},
        )

    @pl.loop(0, tp_count)
    def _(part):
        rows = pl.ds(pl.multiple_of(part * block, block), block)
        pieces = []
        for pair in range(pairs):
            held = dq[part * pairs + pair]
            turned = SCORE_SCALE * jnp.concatenate(
                [held[member * block : (member + 1) * block, :HEAD] for member in range(group)],
                axis=1,
            )
            pieces.append(turned * cos[rows, :] - swap_halves(turned) * sin[rows, :])
        keys = own_kv[rows, :kv_cols]
        pieces.append(keys * cos[rows, :] - swap_halves(keys) * sin[rows, :])
        pieces.append(own_kv[rows, kv_cols:])
        grads = jnp.concatenate(pieces, axis=1).astype(BF16)
        row_grads[rows, :] = grads
        low_part = dot_nt(grads, second[...]).astype(BF16)
        low_grads[rows, :] = low_part
        second_acc[...] += dot_tn(lora[rows, :], grads)
        first_acc[...] += dot_tn(low_part, normed_all[part])

    packed[pl.ds(0, 3 * RANK), :] = first_acc[pl.ds(0, 3 * RANK), :]
    packed[pl.ds(4 * RANK, RANK), :] = o_out_acc[pl.ds(0, RANK), :]
    lanes = pl.ds(pl.multiple_of(tp * q_cols, q_cols), q_cols)
    packed[pl.ds(3 * RANK, RANK), lanes] = o_in_acc[pl.ds(0, RANK), :]
    packed[pl.ds(5 * RANK, RANK), lanes] = second_acc[pl.ds(0, RANK), :q_cols]
    lanes = pl.ds(pl.multiple_of(tp * kv_cols, kv_cols), kv_cols)
    packed[pl.ds(6 * RANK, RANK), lanes] = second_acc[pl.ds(RANK, RANK), q_cols : q_cols + kv_cols]
    lanes = pl.ds(pl.multiple_of(model // 2 + tp * kv_cols, kv_cols), kv_cols)
    packed[pl.ds(6 * RANK, RANK), lanes] = second_acc[pl.ds(2 * RANK, RANK), q_cols + kv_cols :]

    def make_parts():
        @pl.loop(0, tp_count)
        def _(k):
            part = ring(tp, k + 1, tp_count)
            rows = pl.ds(pl.multiple_of(part * block, block), block)
            grads = row_grads[rows, :]
            for side in range(2):
                columns = slice(side * half, (side + 1) * half)
                parts[k, :, columns] = (
                    dot_nt(grads, weights[side, pl.ds(0, half), :])
                    + dot_nt(low_grads[rows, :], first[columns, :])
                ).astype(BF16)

    def send_parts():
        for k in range(tp_count - 1):
            part_copy(k).start()

    if direct:
        tall_rows = packed.shape[0] // ctx_count

        def ctx_rows(index):
            return pl.ds(pl.multiple_of(index * tall_rows, tall_rows), tall_rows)

        def ctx_copy(k):
            where = ring(ctx, k, ctx_count)
            return remote(
                packed.at[ctx_rows(where)], ctx_in.at[k - 1],
                ctx_sem.at[0, k - 1], ctx_sem.at[1, k - 1], {"ctx": where},
            )

        def tp_copy(k):
            return remote(
                tp_in.at[tp], tp_in.at[tp], tp_sem.at[0, k - 1], tp_sem.at[1, k - 1],
                {"tp": ring(tp, k, tp_count)},
            )

        x_copy = remote(
            packed_out.at[fsdp, ctx_rows(ctx)], packed_out.at[fsdp, ctx_rows(ctx)],
            x_sem.at[0], x_sem.at[1], other,
        )

        def ctx_all_copy(k):
            return remote(
                packed_out.at[:, ctx_rows(ctx)], packed_out.at[:, ctx_rows(ctx)],
                ctx_all_sem.at[0, k - 1], ctx_all_sem.at[1, k - 1],
                {"ctx": ring(ctx, k, ctx_count)},
            )

        for k in range(1, ctx_count):
            ctx_copy(k).start()
        make_parts()
        for k in range(1, ctx_count):
            ctx_copy(k).wait()
        tp_in[tp] = (packed[ctx_rows(ctx), :] + sum(ctx_in[k] for k in range(ctx_count - 1))).astype(
            BF16
        )
        for k in range(1, tp_count):
            tp_copy(k).start()
        send_parts()
        for k in range(1, tp_count):
            tp_copy(k).wait()
        packed_out[fsdp, ctx_rows(ctx), :] = sum(tp_in[k].astype(F32) for k in range(tp_count))
        x_copy.start()
        x_copy.wait()
        for k in range(1, ctx_count):
            ctx_all_copy(k).start()
        share_own.wait()
        for k in range(1, tp_count):
            share_copy(k).wait()
        swap.start()
    else:
        packed_out[0] = packed[...]
        make_parts()
        send_parts()

    summed = parts[tp_count - 1].astype(F32)
    for k in range(tp_count - 1):
        part_copy(k).wait_recv()
        summed += parts_in[k].astype(F32)
    inputs = tokens[...].astype(F32)
    input_grad[...] = (middle_grad[...] + rms_back(inputs, scale_one, summed)).astype(BF16)
    mixture = end_sum(1) if direct else mixed[...].astype(F32)
    output[...] = (middle_ref[...] + RESIDUAL_SCALE * mixture).astype(BF16)

    if direct:
        swap.wait()
        for k in range(1, ctx_count):
            ctx_all_copy(k).wait()
        for n in range(2):
            for slot in range(2):
                near_copy(n, slot).wait_send()
            pair_copy(n).wait_send()
    line.end()
    for k in range(tp_count - 1):
        part_copy(k).wait_send()
    for distance in range(1, SPAN):

        @pl.when(distance <= rank)
        def _(distance=distance):
            far_copy(distance).wait_send()


def backward(
    tokens, upstream, routes, gains, router, middle, low, weights, normed, lora, att, queries, kv,
    first, second, o_first, o_second, cos, sin, back, mixed, shares, tp_count, ctx_count, experts, direct,
):
    block, model = tokens.shape
    heads, rows, _ = queries.shape
    pairs = kv.shape[3] // (2 * HEAD)
    tall = heads // pairs * block
    cols = second.shape[1]
    kv_width = kv.shape[3]
    vmem = pl.BlockSpec(memory_space=pltpu.VMEM)
    hbm = pl.BlockSpec(memory_space=pl.ANY)
    dma = pltpu.SemaphoreType.DMA
    part = (block, model)
    packed = (8 * RANK, model)
    copies = 2 if direct else 1
    slim = (8, LANES)

    def buffers(width):
        shapes = [(2, block, width), (2, block, width), (block, width), (block, width)]
        return [pltpu.VMEM(shape if direct else slim, BF16) for shape in shapes]

    return pl.pallas_call(
        functools.partial(
            backward_kernel, tp_count=tp_count, ctx_count=ctx_count, experts=experts, direct=direct
        ),
        in_specs=[vmem] * 20 + [hbm if direct else vmem] * 2 + [hbm],
        out_specs=[vmem] * 3 + [hbm],
        out_shape=[
            jax.ShapeDtypeStruct((block, model), BF16),
            jax.ShapeDtypeStruct((block, model), BF16),
            jax.ShapeDtypeStruct((copies,) + packed, F32),
            jax.ShapeDtypeStruct(
                (2,) + shares.shape[:2] + (tp_count * shares.shape[2],) if direct else slim, BF16
            ),
        ],
        scratch_shapes=[
            pltpu.VMEM((pairs, SPAN * rows, LANES), BF16),
            pltpu.VMEM((pairs, SPAN * rows, LANES), BF16),
            pltpu.VMEM((heads, rows, LANES), BF16),
            pltpu.VMEM((pairs, SPAN * rows, LANES), F32),
            pltpu.VMEM((pairs, SPAN * rows, LANES), F32),
            pltpu.VMEM((tp_count * pairs, tall, LANES), F32),
            pltpu.VMEM((tp_count, block, model), BF16),
            pltpu.VMEM((SPAN - 1, rows, kv_width), BF16),
            pltpu.VMEM((SPAN - 1, rows, kv_width), BF16),
            pltpu.VMEM((rows, kv_width), F32),
            pltpu.VMEM((rows, cols), BF16),
            pltpu.VMEM((rows, LANES), BF16),
            pltpu.VMEM((tp_count,) + part, BF16),
            pltpu.VMEM((tp_count - 1,) + part, BF16),
            pltpu.VMEM((LANES, cols), F32),
            pltpu.VMEM((LANES, model), F32),
            pltpu.VMEM((LANES, heads * HEAD), F32),
            pltpu.VMEM((LANES, model), F32),
            pltpu.VMEM(packed, F32),
            pltpu.VMEM((ctx_count - 1, packed[0] // ctx_count, model) if direct else slim, F32),
            pltpu.VMEM((tp_count, packed[0] // ctx_count, model) if direct else slim, BF16),
            pltpu.VMEM((block, model), F32),
            pltpu.VMEM((LANES, model), BF16),
            *buffers(model + LANES),
            *buffers(model),
            dma((2, 4)),
            dma((4,)),
            dma((2, 2)),
            dma((2, 2, tp_count)),
            dma((2, SPAN - 1)),
            dma((2, tp_count - 1)),
            dma((2, ctx_count - 1)),
            dma((2, tp_count - 1)),
            dma((2,)),
            dma((2, ctx_count - 1)),
            dma((2, tp_count - 1)),
            dma((2,)),
            dma((1,)),
        ],
        compiler_params=pltpu.CompilerParams(
            vmem_limit_bytes=60 * 1024 * 1024, collective_id=1, has_side_effects=True
        ),
        cost_estimate=pl.CostEstimate(
            flops=32 * SPAN * rows * rows * heads * LANES,
            bytes_accessed=32 * 1024 * 1024,
            transcendentals=0,
        ),
        name="backward",
    )(
        tokens, upstream, routes, *gains, router, middle, low, weights, normed, lora, att, queries,
        kv, first, second, o_first, o_second, cos, sin, back, mixed, shares,
    )


def place_kernel(sets, packed, part, *outs):
    query_in, query_out, key_in, key_out, value_in, value_out, out_in, out_out = outs[:8]
    gate_in, gate_out, up_in, up_out, down_in, down_out = outs[8:]
    kv_cols, hidden = key_out.shape[1], gate_out.shape[2]
    trees = part.shape[0]
    spots = jnp.concatenate(
        [
            (iota((RANK, LANES), 1) == iota((RANK, LANES), 0) + sets[tree] * RANK).astype(BF16)
            for tree in range(trees)
        ],
        axis=0,
    )
    spots_twice = jnp.concatenate([spots, spots], axis=0)

    def block(rows):
        return slice(rows * RANK, (rows + 1) * RANK)

    @pl.when(pl.program_id(0) == 0)
    def _():
        def gathered(rows, lanes, turned):
            pieces = jnp.concatenate(
                [packed[tree, block(rows), lanes] for tree in range(trees)], axis=0
            )
            high = pieces.astype(BF16)
            both = jnp.concatenate([high, (pieces - high.astype(F32)).astype(BF16)], axis=0)
            return dot_tn(both, spots_twice) if turned else dot_tn(spots_twice, both)

        whole = slice(None)
        query_in[...] = gathered(0, whole, True)
        key_in[...] = gathered(1, whole, True)
        value_in[...] = gathered(2, whole, True)
        out_in[...] = gathered(3, whole, True)
        out_out[...] = gathered(4, whole, False)
        query_out[...] = gathered(5, whole, False)
        key_out[...] = gathered(6, slice(0, kv_cols), False)
        value_out[...] = gathered(6, slice(kv_cols, 2 * kv_cols), False)

    def pieces(rows, lanes):
        return jnp.concatenate([part[tree, 0, block(rows), lanes] for tree in range(trees)], axis=0)

    whole, left, right = slice(None), slice(0, hidden), slice(hidden, 2 * hidden)
    gate_in[0] = dot_tn(pieces(0, whole), spots)
    up_in[0] = dot_tn(pieces(1, whole), spots)
    gate_out[0] = dot_tn(spots, pieces(2, left))
    up_out[0] = dot_tn(spots, pieces(2, right))
    down_out[0] = dot_tn(spots, pieces(3, whole))
    down_in[0] = dot_tn(pieces(4, left), spots)


def place(sets, packed, part, once, each):
    trees, local = part.shape[:2]
    return pl.pallas_call(
        place_kernel,
        grid_spec=pltpu.PrefetchScalarGridSpec(
            num_scalar_prefetch=1,
            grid=(local,),
            in_specs=[
                pl.BlockSpec(packed.shape, lambda e, s: (0, 0, 0)),
                pl.BlockSpec((trees, 1) + part.shape[2:], lambda e, s: (0, e, 0, 0)),
            ],
            out_specs=[
                *[pl.BlockSpec(o.shape, lambda e, s: (0, 0)) for o in once],
                *[pl.BlockSpec((1,) + o.shape[1:], lambda e, s: (e, 0, 0)) for o in each],
            ],
        ),
        out_shape=[jax.ShapeDtypeStruct(o.shape, F32) for o in (*once, *each)],
        compiler_params=pltpu.CompilerParams(vmem_limit_bytes=VMEM_LIMIT),
        name="place",
    )(sets, packed, part)


def expert_kernel(
    sets, x_ref, g_ref, routes, router,
    w_gate, w_up, w_down, w_gate_far, w_up_far, w_down_far, all_gate, all_up, all_down, gate_in, up_in, gate_out, up_out, down_in, down_out,
    back_out, mixed_out, grad_out,
    rank_rows, gate_rows, slope_rows, mix, back, xs, firsts, tall_grad,
    gate_full, up_full, down_full, land_gate, land_up, land_down, grads, grads_in,
    far_sem, pass_far_sem, grads_sem, arrive_sem,
    *, slots, sources, early, shared, straight, tp_count,
):
    chunk, expert = pl.program_id(0), pl.program_id(1)
    tp, fsdp = lax.axis_index("tp"), lax.axis_index("fsdp")
    late = shared + straight
    gather = late > 0
    other = {"fsdp": 1 - fsdp}
    cross, hand_on = far_moves(
        (all_gate, all_up, all_down), (land_gate, land_up, land_down), far_sem, pass_far_sem,
        shared, straight, early, 0, other, tp,
    )

    if gather:

        @pl.when(expert == 0)
        def _():
            barrier = pltpu.get_barrier_semaphore()
            pl.semaphore_signal(
                barrier, 1, device_id=other, device_id_type=pl.DeviceIdType.MESH
            )
            for k in range(1, tp_count):
                pl.semaphore_signal(
                    barrier, 1, device_id={"tp": ring(tp, k, tp_count)},
                    device_id_type=pl.DeviceIdType.MESH,
                )
            pl.semaphore_wait(barrier, tp_count)
            for n in BEGIN[0]:
                for copy in cross(n):
                    copy.start()

        for step in range(1, early + late):
            if step in BEGIN or step in RELAY:

                @pl.when(expert == step)
                def _(step=step):
                    for n in RELAY.get(step, ()):
                        for copy in cross(n):
                            copy.wait_recv()
                        for copy in hand_on(n):
                            copy.start()
                    for n in BEGIN.get(step, ()):
                        for copy in cross(n):
                            copy.start()

        for n in range(late):

            @pl.when(expert == early + n)
            def _(n=n):
                for copy in hand_on(n) if n < shared else cross(n):
                    copy.wait_recv()

    experts = router.shape[0]
    tokens, model = x_ref.shape
    each = tokens // sources
    hidden = w_gate.shape[2]
    lanes = gate_in.shape[2]
    chosen = sets[fsdp * pl.num_programs(0) + chunk]

    @pl.when(expert == 0)
    def _():
        logits = dot_nt(router[...], x_ref[...])
        number = iota((experts, tokens), 0)
        hit = jnp.zeros((experts, tokens), F32)
        for k in range(routes.shape[0]):
            hit += (routes[k : k + 1, :] == number).astype(F32)
        kept = jnp.where(hit > 0.5, logits, MASKED)
        weights = jnp.exp(kept - jnp.max(kept, axis=0, keepdims=True)) * hit
        gate_rows[...] = weights / jnp.sum(weights, axis=0, keepdims=True)
        earlier = (iota((each, each), 0) < iota((each, each), 1)).astype(BF16)
        for s in range(sources):
            span = slice(s * each, (s + 1) * each)
            order = dot(hit[:, span].astype(BF16), earlier)
            rank_rows[:, span] = jnp.where(hit[:, span] > 0.5, order, -1.0)
        mix[...] = jnp.zeros(mix.shape, F32)
        back[...] = jnp.zeros(back.shape, F32)
        slope_rows[...] = jnp.zeros(slope_rows.shape, F32)

    first_row = lax.axis_index("ctx") * pl.num_programs(1)
    row = first_row + expert
    ranks = rank_rows[pl.ds(row, 1), :]
    gates = gate_rows[pl.ds(row, 1), :]
    slot_number = iota((slots, each), 0).astype(F32)
    picks, columns, upstreams = [], [], []
    for s in range(sources):
        span = slice(s * each, (s + 1) * each)
        pick = ranks[:, span] == slot_number
        columns.append(jnp.sum(jnp.where(pick, gates[:, span], 0.0), axis=1, keepdims=True))
        pick = pick.astype(BF16)
        picks.append(pick)
        xs[pl.ds(s * slots, slots), :] = dot(pick, x_ref[pl.ds(s * each, each), :]).astype(BF16)
        upstreams.append(dot(pick, g_ref[pl.ds(s * each, each), :]))
    gate_column = jnp.concatenate(columns, axis=0)
    upstream = RESIDUAL_SCALE * jnp.concatenate(upstreams, axis=0)

    firsts[:, :lanes] = gate_in[0]
    firsts[:, lanes:] = up_in[0]
    keep = (iota((1, 2 * lanes), 1) % lanes // RANK == chosen).astype(BF16)
    rows = xs[...]
    inner = dot(rows, firsts[...]).astype(BF16) * keep
    for full, near, far, landed in (
        (gate_full, w_gate, w_gate_far, land_gate),
        (up_full, w_up, w_up_far, land_up),
        (down_full, w_down, w_down_far, land_down),
    ):
        size = near.shape[1]
        full[pl.ds(pl.multiple_of(fsdp * size, size), size), :] = near[0]
        spot = pl.ds(pl.multiple_of((1 - fsdp) * size, size), size)
        if not gather:
            full[spot, :] = far[0]
            continue

        @pl.when(expert < early)
        def _(full=full, far=far, spot=spot):
            full[spot, :] = far[0]

        @pl.when(expert >= early)
        def _(full=full, landed=landed, spot=spot):
            full[spot, :] = landed[jnp.maximum(expert - early, 0)]
    gate_value = dot(rows, gate_full[...]) + dot(inner[:, :lanes], gate_out[0])
    up_value = dot(rows, up_full[...]) + dot(inner[:, lanes:], up_out[0])
    sigmoid = 1.0 / (1.0 + jnp.exp(-gate_value))
    silu = gate_value * sigmoid
    active = (silu * up_value).astype(BF16)
    down_inner = dot(active, down_in[0]).astype(BF16) * keep[:, :lanes]
    produced = (
        (dot(active, down_full[...]) + dot(down_inner, down_out[0])).astype(BF16).astype(F32)
    )
    slope = jnp.sum(upstream * produced, axis=1, keepdims=True)
    sent = (gate_column * produced).astype(BF16)
    slot_grad = (gate_column * upstream).astype(BF16)

    down_inner_grad = dot_nt(slot_grad, down_out[0]).astype(BF16) * keep[:, :lanes]
    active_grad = (
        (dot_nt(slot_grad, down_full[...]) + dot_nt(down_inner_grad, down_in[0]))
        .astype(BF16)
        .astype(F32)
    )
    gate_grad = (active_grad * up_value * (sigmoid + silu * (1.0 - sigmoid))).astype(BF16)
    up_grad = (active_grad * silu).astype(BF16)
    inner_grad = (
        jnp.concatenate([dot_nt(gate_grad, gate_out[0]), dot_nt(up_grad, up_out[0])], axis=1)
    ).astype(BF16) * keep
    row_grad = (
        dot_nt(gate_grad, gate_full[...])
        + dot_nt(up_grad, up_full[...])
        + dot_nt(inner_grad, firsts[...])
    ).astype(BF16)

    for s in range(sources):
        span = slice(s * slots, (s + 1) * slots)
        spot = pl.ds(s * each, each)
        mix[spot, :] += dot_tn(picks[s], sent[span, :])
        back[spot, :] += dot_tn(picks[s], row_grad[span, :])
        slope_rows[pl.ds(expert, 1), spot] = jnp.sum(
            jnp.where(picks[s] > 0.5, slope[span, :], 0.0), axis=0, keepdims=True
        )

    keep_at = expert if gather else 0

    def folded(start, width):
        total = tall_grad[pl.ds(start, RANK), :width]
        for shift in range(RANK, lanes, RANK):
            total += tall_grad[pl.ds(start + shift, RANK), :width]
        return total.astype(BF16)

    tall_grad[...] = dot_tn(inner_grad, rows)
    grads[keep_at, pl.ds(0, RANK), :] = folded(0, model)
    grads[keep_at, pl.ds(RANK, RANK), :] = folded(lanes, model)
    tall_grad[pl.ds(0, lanes), :hidden] = dot_tn(inner[:, :lanes], gate_grad)
    tall_grad[pl.ds(0, lanes), hidden:] = dot_tn(inner[:, lanes:], up_grad)
    grads[keep_at, pl.ds(2 * RANK, RANK), :] = folded(0, model)
    tall_grad[pl.ds(0, lanes), :] = dot_tn(down_inner, slot_grad)
    grads[keep_at, pl.ds(3 * RANK, RANK), :] = folded(0, model)
    tall_grad[pl.ds(0, lanes), :hidden] = dot_tn(down_inner_grad, active)
    grads[keep_at, pl.ds(4 * RANK, RANK), :hidden] = folded(0, hidden)
    grads[keep_at, pl.ds(4 * RANK, RANK), hidden:] = jnp.zeros((RANK, model - hidden), BF16)

    share = tall_grad.shape[1] // tp_count

    def grads_copy(n, k):
        where = ring(tp, k, tp_count)
        lanes = pl.ds(pl.multiple_of(where * share, share), share)
        return remote(
            grads.at[n, :, lanes], grads_in.at[k - 1, n], grads_sem.at[k - 1, n],
            arrive_sem.at[k - 1, n], {"tp": where},
        )

    if gather:
        for k in range(1, tp_count):
            grads_copy(expert, k).start()
    else:
        grad_out[0, 0] = grads[0]

    if gather:

        @pl.when(expert == pl.num_programs(1) - 1)
        def _():
            for n in range(late):
                for copy in cross(n):
                    copy.wait_send()
            for n in range(shared):
                for copy in hand_on(n):
                    copy.wait_send()

            @pl.loop(0, pl.num_programs(1))
            def _(n):
                lanes = pl.ds(pl.multiple_of(tp * share, share), share)
                total = grads[n, :, lanes].astype(F32)
                for k in range(1, tp_count):
                    grads_copy(n, k).wait()
                    total += grads_in[k - 1, n].astype(F32)
                grad_out[n] = total.astype(BF16)

    @pl.when(expert == pl.num_programs(1) - 1)
    def _():
        mixed_out[...] = mix[...].astype(BF16)
        back_out[:, :model] = back[...].astype(BF16)
        turned = slope_rows[...].T
        high = turned.astype(BF16)
        low = (turned - high.astype(F32)).astype(BF16)
        local, lane = iota((LANES, LANES), 0), iota((LANES, LANES), 1)
        inside = local < pl.num_programs(1)
        first = (inside & (lane == local + first_row)).astype(BF16)
        later = (inside & (lane == local + first_row + experts)).astype(BF16)
        back_out[:, model:] = (dot(high, first) + dot(low, later)).astype(BF16)


def run_experts(
    sets, rows, upstream, routes, router, weights, far, adapters, slots, sources, tp_count
):
    total, model = rows.shape
    experts = router.shape[0]
    local, half, hidden = weights[0].shape
    trees = sets.shape[0] // 2
    tokens = total // trees
    lanes = adapters[0].shape[2]
    tall = sources * slots
    piece = lambda c, e, *_: (c, 0)
    fixed = lambda c, e, *_: (0, 0)
    expert = lambda c, e, *_: (e, 0, 0)
    pairs, singles, shared, straight = transfer_plan(local, tp_count)
    early, late = pairs + singles, shared + straight
    arrived = lambda c, e, *_: (jnp.minimum(e, early - 1), 0, 0)
    hbm = pl.BlockSpec(memory_space=pl.ANY)
    dma = pltpu.SemaphoreType.DMA
    share = (local, 5 * RANK, model // tp_count)
    gradients = (
        (share, pl.BlockSpec(share, lambda c, e, *_: (0, 0, 0)))
        if late
        else (
            (trees, local, 5 * RANK, model),
            pl.BlockSpec((1, 1, 5 * RANK, model), lambda c, e, *_: (c, e, 0, 0)),
        )
    )
    return pl.pallas_call(
        functools.partial(
            expert_kernel, slots=slots, sources=sources, early=early, shared=shared,
            straight=straight, tp_count=tp_count,
        ),
        grid_spec=pltpu.PrefetchScalarGridSpec(
            num_scalar_prefetch=1,
            grid=(trees, local),
            in_specs=[
                pl.BlockSpec((tokens, model), piece),
                pl.BlockSpec((tokens, model), piece),
                pl.BlockSpec((routes.shape[0], tokens), lambda c, e, *_: (0, c)),
                pl.BlockSpec(router.shape, fixed),
                *[pl.BlockSpec((1,) + w.shape[1:], expert) for w in weights],
                *[pl.BlockSpec((1,) + w.shape[1:], arrived) for w in weights],
                *[hbm] * len(weights),
                *[pl.BlockSpec((1,) + a.shape[1:], expert) for a in adapters],
            ],
            out_specs=[
                pl.BlockSpec((tokens, model + LANES), piece),
                pl.BlockSpec((tokens, model), piece),
                gradients[1],
            ],
            scratch_shapes=[
                pltpu.VMEM((experts, tokens), F32),
                pltpu.VMEM((experts, tokens), F32),
                pltpu.VMEM((LANES, tokens), F32),
                pltpu.VMEM((tokens, model), F32),
                pltpu.VMEM((tokens, model), F32),
                pltpu.VMEM((tall, model), BF16),
                pltpu.VMEM((model, 2 * lanes), BF16),
                pltpu.VMEM((2 * lanes, model), F32),
                pltpu.VMEM((2 * half, hidden), BF16),
                pltpu.VMEM((2 * half, hidden), BF16),
                pltpu.VMEM((hidden, model), BF16),
                *[pltpu.VMEM((max(late, 1),) + w.shape[1:], BF16) for w in weights],
                pltpu.VMEM((local if late else 1, 5 * RANK, model), BF16),
                pltpu.VMEM((tp_count - 1,) + (share if late else (1, 16, LANES)), BF16),
                dma((2, max(late, 1), 3)),
                dma((2, max(shared, 1), 3)),
                dma((tp_count - 1, local)),
                dma((tp_count - 1, local)),
            ],
        ),
        out_shape=[
            jax.ShapeDtypeStruct((total, model + LANES), BF16),
            jax.ShapeDtypeStruct((total, model), BF16),
            jax.ShapeDtypeStruct(gradients[0], BF16),
        ],
        compiler_params=(
            pltpu.CompilerParams(
                vmem_limit_bytes=60 * 1024 * 1024, collective_id=2, has_side_effects=True
            )
            if late
            else pltpu.CompilerParams(vmem_limit_bytes=60 * 1024 * 1024)
        ),
        name="experts",
        cost_estimate=pl.CostEstimate(
            flops=2 * local * total * model * model * 2,
            bytes_accessed=8 * 1024 * 1024,
            transcendentals=0,
        ),
    )(sets, rows, upstream, routes, router, *weights, *far, *weights, *adapters)


def per_device(
    tokens,
    out_grad,
    routes,
    parents,
    adapter_set,
    gain_a,
    gain_b,
    w_query,
    key_projection_matrix,
    value_projection_matrix,
    w_output,
    w_router,
    w_gate,
    w_up,
    w_down,
    query_in,
    query_out,
    key_in,
    key_second_factor,
    value_in,
    value_second_factor,
    out_in,
    out_out,
    gate_in,
    gate_out,
    up_in,
    up_out,
    down_in,
    down_out,
):
    ctx_rank = lax.axis_index("ctx")
    fsdp_rank = lax.axis_index("fsdp")
    ctx_count = lax.axis_size("ctx")
    tp_count = lax.axis_size("tp")
    fsdp_count = lax.axis_size("fsdp")
    tok_rows, model = tokens.shape
    experts = w_router.shape[1]
    local_experts = w_gate.shape[0]
    slots = tok_rows * TOP * 3 // (2 * experts)
    trees = ctx_count // SPAN
    tree_index = (fsdp_rank * ctx_count + ctx_rank) // SPAN

    (
        attended, queries, kv_parts, lora, middle, o_reduced, attention_weights, normed_all,
        first, second, o_first, o_second, cos, sin,
        *far_weights, upstream_all, routes_all, rows_all,
    ) = forward(
        parents, adapter_set, tokens, (gain_a, gain_b),
        (w_query, key_projection_matrix, value_projection_matrix, w_output),
        (
            query_in, query_out, key_in, key_second_factor, value_in, value_second_factor,
            out_in, out_out,
        ),
        (w_gate, w_up, w_down), out_grad, routes.T, tp_count, ctx_count,
    )
    upstream_all = upstream_all.reshape(-1, model)
    rows_all = rows_all.reshape(-1, model)
    routes_all = routes_all.transpose(1, 0, 2).reshape(TOP, -1)

    back, mixed, expert_part = run_experts(
        adapter_set,
        rows_all,
        upstream_all,
        routes_all,
        w_router.T,
        (w_gate, w_up, w_down),
        far_weights,
        (gate_in, up_in, gate_out, up_out, down_in, down_out),
        slots,
        SPAN,
        tp_count,
    )
    direct = ctx_count == SPAN
    if direct:
        back = back.reshape(ctx_count, tok_rows, -1)
        mixed = mixed.reshape(ctx_count, tok_rows, -1)
    else:
        back = lax.psum_scatter(back, "ctx", scatter_dimension=0, tiled=True)
        mixed = lax.psum_scatter(mixed, "ctx", scatter_dimension=0, tiled=True)
    output, input_grad, packed, all_shares = backward(
        tokens, out_grad, routes.T, (gain_a, gain_b), w_router.T, middle, o_reduced, attention_weights,
        normed_all, lora, attended, queries, kv_parts, first, second, o_first, o_second,
        cos, sin, back, mixed, expert_part, tp_count, ctx_count, experts, direct,
    )
    all_trees = fsdp_count * trees
    if not direct:
        mine = (jnp.arange(all_trees, dtype=jnp.int32) == tree_index)[:, None, None]
        packed = lax.psum(jnp.where(mine, packed, 0.0), ("fsdp", "ctx", "tp"))
    if direct:
        expert_part = all_shares
    else:
        expert_part = lax.all_gather(lax.psum(expert_part, "tp"), "fsdp")
        expert_part = expert_part.reshape(all_trees, local_experts, 5 * RANK, model)
    adapter_grads = place(
        adapter_set, packed, expert_part,
        (
            query_in, query_out, key_in, key_second_factor, value_in, value_second_factor,
            out_in, out_out,
        ),
        (gate_in, gate_out, up_in, up_out, down_in, down_out),
    )
    return (output, input_grad, *adapter_grads)


def solution(mesh):
    in_specs = (
        P(("fsdp", "ctx", "tp"), None),
        P(("fsdp", "ctx", "tp"), None),
        P(("fsdp", "ctx", "tp"), None),
        P(),
        P(),
        P(),
        P(),
        P("fsdp", "tp"),
        P("fsdp", "tp"),
        P("fsdp", "tp"),
        P("tp", "fsdp"),
        P(),
        P("ctx", "fsdp", None),
        P("ctx", "fsdp", None),
        P("ctx", "fsdp", None),
        P(),
        P(),
        P(),
        P(),
        P(),
        P(),
        P(),
        P(),
        P("ctx", None, None),
        P("ctx", None, None),
        P("ctx", None, None),
        P("ctx", None, None),
        P("ctx", None, None),
        P("ctx", None, None),
    )
    out_specs = (
        P(("fsdp", "ctx", "tp"), None),
        P(("fsdp", "ctx", "tp"), None),
        P(),
        P(),
        P(),
        P(),
        P(),
        P(),
        P(),
        P(),
        P("ctx", None, None),
        P("ctx", None, None),
        P("ctx", None, None),
        P("ctx", None, None),
        P("ctx", None, None),
        P("ctx", None, None),
    )
    return jax.shard_map(
        per_device, mesh=mesh, in_specs=in_specs, out_specs=out_specs, check_vma=False
    )
```

```python
import functools

import jax
import jax.numpy as jnp
import numpy as np
from jax import lax
from jax.experimental import pallas as pl
from jax.experimental.pallas import tpu as pltpu
from jax.sharding import PartitionSpec as P

HEAD = 64
TOP = 8
RANK = 16
SEG = 128
SEGS_DEV = 8
TREE_SEGS = 32
SPAN = TREE_SEGS // SEGS_DEV
LANES = 128

RESIDUAL_SCALE = 0.22
SCORE_SCALE = 0.015625
EPSILON = 1e-06
ROPE_BASE = 10000.0
MASKED = -1e30

F32 = jnp.float32
BF16 = jnp.bfloat16

CODE = HEAD
LSE = CODE + TREE_SEGS + 1
ONES = HEAD

VMEM_LIMIT = 56 * 1024 * 1024


def dot(a, b):
    return lax.dot_general(a, b, (((1,), (0,)), ((), ())), preferred_element_type=F32)


def dot_nt(a, b):
    return lax.dot_general(a, b, (((1,), (1,)), ((), ())), preferred_element_type=F32)


def dot_tn(a, b):
    return lax.dot_general(a, b, (((0,), (0,)), ((), ())), preferred_element_type=F32)


def iota(shape, dim):
    return lax.broadcasted_iota(jnp.int32, shape, dim)


def rms_scale(values, gain_row):
    return (
        values * lax.rsqrt(jnp.mean(values * values, axis=-1, keepdims=True) + EPSILON) * gain_row
    )


def rms_back(values, gain_row, grad):
    inv = lax.rsqrt(jnp.mean(values * values, axis=-1, keepdims=True) + EPSILON)
    scaled = grad * gain_row
    inner = jnp.mean(scaled * values, axis=-1, keepdims=True)
    return inv * scaled - values * (inv * inv * inv * inner)


def swap_halves(values):
    width = values.shape[-1]
    lane = iota(values.shape, 1) % HEAD
    ahead = pltpu.roll(values, width - HEAD // 2, 1)
    behind = pltpu.roll(values, HEAD // 2, 1)
    return jnp.where(lane < HEAD // 2, -ahead, behind)


def place_table(rows, source, target):
    r, c = iota((rows, LANES), 0), iota((rows, LANES), 1)
    return ((r - source == c - target) & (c >= target) & (c < target + HEAD)).astype(BF16)


def transfer_plan(local, tp_count):
    if local == 8 and tp_count % 2 == 0:
        return 3, 2, 2, 1
    return 0, local, 0, 0


BEGIN = {'start': (0, 1), 'proj': (2,), 'own': (3,), 'k1': (4,), 0: (0,), 2: (1,), 3: (2,)}
RELAY = {'k0': (0, 1), 'k3': (2,), 2: (0,), 4: (1,)}


def remote(src, dst, send, recv, where):
    return pltpu.make_async_remote_copy(
        src_ref=src,
        dst_ref=dst,
        send_sem=send,
        recv_sem=recv,
        device_id=where,
        device_id_type=pl.DeviceIdType.MESH,
    )


def far_moves(near, far, sems, pass_sems, shared, direct, first, land, other, tp):
    mate = {"tp": tp + 1 - 2 * lax.rem(tp, 2)}
    side = lax.rem(tp, 2)

    def piece(ref, rows, which):
        return ref.at[pl.ds(pl.multiple_of(which * rows, rows), rows)]

    def cross(n):
        moves = []
        for a, (source, target) in enumerate(zip(near, far)):
            src, dst = source.at[first + n], target.at[land + n]
            if n < shared:
                rows = src.shape[0] // 2
                src, dst = piece(src, rows, side), piece(dst, rows, side)
            moves.append(remote(src, dst, sems.at[0, n, a], sems.at[1, n, a], other))
        return moves

    def hand_on(n):
        moves = []
        for a, target in enumerate(far):
            dst = target.at[land + n]
            rows = dst.shape[0] // 2
            dst = piece(dst, rows, side)
            moves.append(remote(dst, dst, pass_sems.at[0, n, a], pass_sems.at[1, n, a], mate))
        return moves

    return cross, hand_on


class Line:
    def __init__(self, buffer, sems, me, count):
        self.buffer, self.sems, self.me, self.count = buffer, sems, me, count
        self.turns = 2 * count - 1

    def move(self, way, block):
        where = ring(self.me, 1 if way == 0 else -1, self.count)
        return remote(
            self.buffer.at[block], self.buffer.at[block],
            self.sems.at[way, 0, block], self.sems.at[way, 1, block], {"tp": where},
        )

    def goes(self, way):
        return self.me < self.count - 1 if way == 0 else self.me > 0

    def send(self, way, block):
        @pl.when(self.goes(way))
        def _():
            self.move(way, block).start()

    def start(self):
        self.send(0, self.me)
        self.send(1, self.me)

    def block(self, turn):
        step = (turn + 1) // 2
        block = jnp.where(lax.rem(turn, 2) == 1, self.me - step, self.me + step)
        valid = (block >= 0) & (block < self.count)
        return jnp.clip(block, 0, self.count - 1), valid

    def last(self):
        return jnp.maximum(2 * self.me - 1, 2 * (self.count - 1 - self.me))

    def arrive(self, turn, block):
        for way, odd in ((0, 1), (1, 0)):

            @pl.when((turn > 0) & (lax.rem(turn, 2) == odd))
            def _(way=way):
                self.move(way, block).wait_recv()
                self.send(way, block)

    def end(self):
        for block in range(self.count):
            for way, owned in ((0, block <= self.me), (1, block >= self.me)):

                @pl.when(owned & self.goes(way))
                def _(way=way):
                    self.move(way, block).wait_send()


def ring(me, step, count):
    return lax.rem(me + (step + count), count)


def aug_keys(kv, pair, pairs, first_seg, k_aug, v_aug, start):
    rows, width = kv.shape
    lane = iota((rows, LANES), 1)
    seg = first_seg + iota((rows, LANES), 0) // SEG
    key_code = ((lane - CODE == seg) | ((lane >= LSE) & (lane < LSE + 3))).astype(F32)
    one_code = ((lane == ONES) | (lane == ONES + 1)).astype(F32)
    span = pl.ds(start, rows)
    k_aug[pair, span, :] = (dot(kv, place_table(width, pair * HEAD, 0)) + key_code).astype(BF16)
    v_aug[pair, span, :] = (
        dot(kv, place_table(width, (pairs + pair) * HEAD, 0)) + one_code
    ).astype(BF16)


def forward_kernel(
    parents, adapter_set, tokens, gain_one, gain_two, freqs, w_query, w_key, w_value, w_output,
    query_in, query_out, key_in, key_out, value_in, value_out, out_in, out_out,
    w_gate, w_up, w_down, grads, routes,
    att_out, q_out, kv_out, lora_out, middle_out, low_out, weights, normed_all,
    first, second, o_first, o_second, cos, sin, w_rows, att_rows,
    gate_far, up_far, down_far, grads_all, routes_all, rows_all,
    q_aug, k_aug, v_aug, top, acc, rows_own, code_table, depth_table,
    shard_sem, normed_sem, kv_sem, part_sem, w_rows_sem, far_sem, pass_far_sem, grads_sem, routes_sem, rows_sem,
    pass_sem, local_sem,
    *, tp_count, ctx_count, shared, straight,
):
    tp, ctx, fsdp = (lax.axis_index(name) for name in ("tp", "ctx", "fsdp"))
    rank = lax.rem(ctx, SPAN)
    block, model = tokens.shape
    heads = q_aug.shape[0]
    pairs = k_aug.shape[0]
    group = heads // pairs
    tall = group * block
    half = model // 2
    q_cols = heads * HEAD
    kv_cols = pairs * HEAD
    turn = cos.shape[1]
    chips = ctx_count // 2
    partner = ctx + 1 - 2 * lax.rem(ctx, 2)
    other = {"fsdp": 1 - fsdp}

    barrier = pltpu.get_barrier_semaphore()
    pl.semaphore_signal(barrier, 1, device_id=other, device_id_type=pl.DeviceIdType.MESH)
    for k in range(1, tp_count):
        pl.semaphore_signal(
            barrier, 1, device_id={"tp": ring(tp, k, tp_count)},
            device_id_type=pl.DeviceIdType.MESH,
        )
    for k in range(1, ctx_count):
        pl.semaphore_signal(
            barrier, 1, device_id={"ctx": ring(ctx, k, ctx_count)},
            device_id_type=pl.DeviceIdType.MESH,
        )
    pl.semaphore_wait(barrier, tp_count + ctx_count - 1)

    corners = (
        (w_query, 0, 0),
        (w_key, 0, q_cols),
        (w_value, 0, q_cols + kv_cols),
        (w_output, half, 0),
    )
    shard_copies = []
    for n, (source, row, column) in enumerate(corners):
        spot = weights.at[fsdp, pl.ds(row, source.shape[0]), pl.ds(column, source.shape[1])]
        shard_copies.append(remote(source, spot, shard_sem.at[0, n], shard_sem.at[1, n], other))
    for copy in shard_copies:
        copy.start()

    inputs = tokens[...].astype(F32)
    normed = rms_scale(inputs, gain_one[...].astype(F32).reshape(1, model)).astype(BF16)
    normed_all[tp] = normed

    line = Line(normed_all, normed_sem, tp, tp_count)
    line.start()

    def side_copies(k):
        where = {"ctx": ring(ctx, k, ctx_count)}
        return (
            remote(grads, grads_all.at[ctx], grads_sem.at[0, k], grads_sem.at[1, k], where),
            remote(routes, routes_all.at[ctx], routes_sem.at[0, k], routes_sem.at[1, k], where),
        )

    own_copies = (
        pltpu.make_async_copy(grads, grads_all.at[ctx], local_sem.at[0]),
        pltpu.make_async_copy(routes, routes_all.at[ctx], local_sem.at[1]),
    )
    for copy in own_copies:
        copy.start()
    for k in range(1, ctx_count):
        for copy in side_copies(k):
            copy.start()

    for source, row, column in corners:
        weights[fsdp, pl.ds(row, source.shape[0]), pl.ds(column, source.shape[1])] = source[...]

    tree = (fsdp * ctx_count + ctx) // SPAN
    spot_row, spot_lane = iota((LANES, LANES), 0), iota((LANES, LANES), 1)
    linked = (spot_row == spot_lane) & (spot_row < TREE_SEGS)
    for n in range(TREE_SEGS):
        linked |= (spot_row == n) & (spot_lane == parents[tree * TREE_SEGS + n])
    reach = linked.astype(F32)
    for _ in range((TREE_SEGS - 1).bit_length()):
        reach = jnp.minimum(dot(reach.astype(BF16), reach.astype(BF16)), 1.0)
    depth_table[...] = jnp.broadcast_to(
        jnp.sum(reach, axis=1, keepdims=True) - 1.0, (LANES, LANES)
    ).astype(BF16)
    coded = (spot_lane >= CODE) & (spot_lane < CODE + TREE_SEGS)
    code_table[...] = jnp.where(
        coded & (pltpu.roll(reach, CODE, 1) < 0.5), MASKED, 0.0
    ).astype(BF16)

    chosen = adapter_set[tree]

    def pick(n):
        inside = (spot_lane >= n * RANK) & (spot_lane < (n + 1) * RANK)
        return (inside & (spot_row == spot_lane - n * RANK + chosen * RANK)).astype(BF16)

    first[...] = (
        dot(query_in[...], pick(0)) + dot(key_in[...], pick(1)) + dot(value_in[...], pick(2))
    ).astype(BF16)
    for n, (source, column, width) in enumerate(
        ((query_out, 0, q_cols), (key_out, q_cols, kv_cols), (value_out, q_cols + kv_cols, kv_cols))
    ):
        lanes = pl.ds(pl.multiple_of(tp * width, width), width)
        second[:, column : column + width] = dot_tn(pick(n), source[:, lanes]).astype(BF16)
    o_first[...] = dot(out_in[...], pick(0)).astype(BF16)
    o_second[...] = dot_tn(pick(0), out_out[...]).astype(BF16)

    for copy in shard_copies:
        copy.wait()
    cross, hand_on = far_moves(
        (w_gate, w_up, w_down), (gate_far, up_far, down_far), far_sem, pass_far_sem,
        shared, straight, 0, 0, other, tp,
    )

    def point(name):
        if not shared:
            if name == "start":
                for n in range(straight):
                    for copy in cross(n):
                        copy.start()
            return
        for n in RELAY.get(name, ()):
            for copy in cross(n):
                copy.wait_recv()
            for copy in hand_on(n):
                copy.start()
        for n in BEGIN.get(name, ()):
            for copy in cross(n):
                copy.start()

    point("start")

    def kv_copy(distance, part):
        return remote(
            kv_out.at[0, part], kv_out.at[distance, part],
            kv_sem.at[0, distance - 1], kv_sem.at[1, distance - 1], {"ctx": ring(ctx, distance, ctx_count)},
        )

    def project(part):
        span = pl.ds(pl.multiple_of(part * block, block), block)
        rows = normed_all[part]
        seg = rank * SEGS_DEV + (part * block + iota((block, LANES), 0)) // SEG
        at_seg = (seg == iota((block, LANES), 1)).astype(BF16)
        offset = lax.rem(iota((block, LANES), 0), SEG).astype(F32)
        angles = (dot(at_seg, depth_table[...]) * SEG + offset) * freqs[...]
        cos[span, :] = jnp.cos(angles)
        sin[span, :] = jnp.sin(angles)
        codes = dot(at_seg, code_table[...])
        lora = dot(rows, first[...]).astype(BF16)
        lora_out[span, :] = lora
        pre = (
            dot(rows[:, :half], weights[0, pl.ds(0, half), :])
            + dot(rows[:, half:], weights[1, pl.ds(0, half), :])
            + dot(lora, second[...])
        )
        turned = []
        for start in range(0, pre.shape[1] // 4 * 3, turn):
            piece = pre[:, start : start + turn]
            turned.append(piece * cos[span, :] + swap_halves(piece) * sin[span, :])
        queries = (
            jnp.concatenate(turned[: q_cols // turn], axis=1) * SCORE_SCALE
        ).astype(BF16)
        for head in range(heads):
            q_aug[head, span, :] = (
                dot(queries, place_table(q_cols, head * HEAD, 0)) + codes
            ).astype(BF16)
        keys = jnp.concatenate(turned[q_cols // turn :], axis=1)
        kv = jnp.concatenate([keys, pre[:, q_cols + keys.shape[1] :]], axis=1).astype(BF16)
        kv_out[0, part] = kv
        for distance in range(1, SPAN):

            @pl.when(rank + distance < SPAN)
            def _(distance=distance):
                kv_copy(distance, part).start()

        for pair in range(pairs):
            aug_keys(
                kv, pair, pairs, rank * SEGS_DEV + part * (block // SEG), k_aug, v_aug,
                pl.multiple_of(part * block, block),
            )

    @pl.loop(0, line.turns)
    def _(turn):
        part, valid = line.block(turn)

        @pl.when(valid)
        def _():
            line.arrive(turn, part)
            project(part)

    w_line = Line(w_rows, w_rows_sem, tp, tp_count)
    for side in range(2):
        w_rows[tp, side] = weights[side, pl.ds(half, q_cols), :]
    w_line.start()
    point("proj")

    def advance(step):
        @pl.loop(2 * step - 1, 2 * step + 1)
        def _(turn):
            shard, valid = w_line.block(turn)

            @pl.when(valid)
            def _():
                w_line.arrive(turn, shard)

    def tile(part, pair, start, size, causal):
        index = part * pairs + pair
        rows = pl.ds(pl.multiple_of(part * block, block), block)
        queries = q_aug[pl.ds(pair * group, group), rows, :].reshape(tall, LANES)
        span = pl.ds(start, size)
        scores = dot_nt(queries, k_aug[pair, span, :])
        if causal:
            q_row = iota(scores.shape, 0) % block
            scores = jnp.where(iota(scores.shape, 1) <= q_row, scores, MASKED)
            now = jnp.broadcast_to(jnp.max(scores, axis=1, keepdims=True), (tall, LANES))
            probs = jnp.exp(scores - now[:, :1]).astype(BF16)
            acc[index] = dot(probs, v_aug[pair, span, :])
        else:
            before = top[index]
            now = jnp.maximum(before, jnp.max(scores, axis=1, keepdims=True))
            probs = jnp.exp(scores - now[:, :1]).astype(BF16)
            acc[index] = acc[index] * jnp.exp(before - now) + dot(probs, v_aug[pair, span, :])
        top[index] = now

    @pl.loop(0, tp_count * pairs)
    def _(index):
        part, pair = index // pairs, lax.rem(index, pairs)
        tile(part, pair, pl.multiple_of(part * block, block), block, True)

        @pl.loop(0, part)
        def _(j):
            tile(part, pair, pl.multiple_of(j * block, block), block, False)

    advance(1)
    point("own")
    group_rows = tp_count * block
    for distance in range(1, SPAN):

        @pl.when(distance <= rank)
        def _(distance=distance):
            remote(
                kv_out.at[0], kv_out.at[distance], kv_sem.at[0, distance - 1],
                kv_sem.at[1, distance - 1], {"ctx": ring(ctx, distance, ctx_count)},
            ).wait_recv()

            @pl.loop(0, tp_count)
            def _(part):
                kv = kv_out[distance, part]
                for pair in range(pairs):
                    aug_keys(
                        kv, pair, pairs,
                        (rank - distance) * SEGS_DEV + part * (block // SEG), k_aug, v_aug,
                        pl.multiple_of(distance * group_rows + part * block, block),
                    )

        @pl.when(distance > rank)
        def _(distance=distance):
            kv_out[distance] = jnp.zeros(kv_out.shape[1:], BF16)

    def part_copy(k):
        part = ring(tp, k + 1, tp_count)
        rows = pl.ds(pl.multiple_of(part * block, block), block)
        return remote(
            att_out.at[rows], att_rows.at[tp], part_sem.at[0, k], part_sem.at[1, k], {"tp": part}
        )

    @pl.loop(0, tp_count)
    def _(k):
        part = ring(tp, k + 1, tp_count)
        rows = pl.ds(pl.multiple_of(part * block, block), block)
        for pair in range(pairs):
            index = part * pairs + pair

            @pl.loop(1, rank + 1)
            def _(distance, pair=pair):
                tile(
                    part, pair, pl.multiple_of(distance * group_rows, group_rows), group_rows, False
                )

            summed = acc[index]
            total = summed[:, ONES : ONES + 1]
            result = (summed / total).astype(BF16)
            for member in range(group):
                head = pair * group + member
                att_out[rows, pl.ds(head * HEAD, HEAD)] = result[
                    member * block : (member + 1) * block, :HEAD
                ]
            minus = -(top[index] + jnp.log(total))
            high = minus.astype(BF16).astype(F32)
            middle = (minus - high).astype(BF16).astype(F32)
            lane = iota(minus.shape, 1)
            queries = q_aug[pl.ds(pair * group, group), rows, :].reshape(tall, LANES)
            coded = jnp.where(
                lane == LSE,
                high,
                jnp.where(
                    lane == LSE + 1,
                    middle,
                    jnp.where(lane == LSE + 2, minus - high - middle, queries.astype(F32)),
                ),
            )
            q_out[pl.ds(pair * group, group), rows, :] = coded.astype(BF16).reshape(
                group, block, LANES
            )

        @pl.when(k < tp_count - 1)
        def _():
            part_copy(k).start()

        @pl.when(k == tp_count - 1)
        def _():
            att_rows[tp] = att_out[rows, :]

        for step in range(2, tp_count):

            @pl.when(k == step - 2)
            def _(step=step):
                advance(step)

        for n in range(tp_count):
            if f"k{n}" in BEGIN or f"k{n}" in RELAY:

                @pl.when(k == n)
                def _(n=n):
                    point(f"k{n}")

    for k in range(tp_count - 1):
        part_copy(k).wait_recv()
    point("sum")
    low = sum(
        dot(att_rows[t], o_first[pl.ds(t * q_cols, q_cols), :]) for t in range(tp_count)
    ).astype(BF16)
    low_out[...] = low
    branch = dot(low, o_second[...]) + jnp.concatenate(
        [sum(dot(att_rows[t], w_rows[t, side]) for t in range(tp_count)) for side in range(2)],
        axis=1,
    )
    middle = inputs + RESIDUAL_SCALE * branch
    middle_out[...] = middle
    rows_own[...] = rms_scale(middle, gain_two[...].astype(F32).reshape(1, model)).astype(BF16)

    own_rows = pltpu.make_async_copy(rows_own, rows_all.at[ctx], local_sem.at[2])
    own_rows.start()
    to_partner = remote(
        rows_own, rows_all.at[ctx], rows_sem.at[0, 0], rows_sem.at[1, 0], {"ctx": partner}
    )
    to_partner.start()

    def rows_copy(k):
        return remote(
            rows_own, rows_all.at[ctx], rows_sem.at[0, k], rows_sem.at[1, k],
            {"ctx": ring(ctx, 2 * k, ctx_count)},
        )

    def pass_copy(k):
        source = ring(ctx, -2 * k, ctx_count)
        return remote(
            rows_all.at[source], rows_all.at[source], pass_sem.at[0, k], pass_sem.at[1, k],
            {"ctx": partner},
        )

    for k in range(1, chips):
        rows_copy(k).start()
    for k in range(1, chips):
        rows_copy(k).wait_recv()
        pass_copy(k).start()

    line.end()
    w_line.end()
    for k in range(tp_count - 1):
        part_copy(k).wait_send()
    for distance in range(1, SPAN):

        @pl.when(rank + distance < SPAN)
        def _(distance=distance):
            remote(
                kv_out.at[0], kv_out.at[distance], kv_sem.at[0, distance - 1],
                kv_sem.at[1, distance - 1], {"ctx": ring(ctx, distance, ctx_count)},
            ).wait_send()

    for k in range(1, ctx_count):
        for copy in side_copies(k):
            copy.wait()
    for copy in own_copies:
        copy.wait()
    own_rows.wait()
    to_partner.wait()
    for k in range(1, chips):
        rows_copy(k).wait_send()
        pass_copy(k).wait()
    for n in range(shared + straight):
        for copy in cross(n):
            copy.wait_send()
            if n >= shared:
                copy.wait_recv()
    for n in range(shared):
        for copy in hand_on(n):
            copy.wait()


def forward(
    parents, adapter_set, tokens, gains, attention, adapters, weights, grads, routes,
    tp_count, ctx_count,
):
    block, model = tokens.shape
    rows = tp_count * block
    q_cols, kv_cols = attention[0].shape[1], attention[1].shape[1]
    heads, pairs = q_cols // HEAD, kv_cols // HEAD
    cols = q_cols + 2 * kv_cols
    tall = heads // pairs * block
    chips = ctx_count // 2
    shared, straight, _, _ = transfer_plan(weights[0].shape[0], tp_count)
    vmem = pl.BlockSpec(memory_space=pltpu.VMEM)
    smem = pl.BlockSpec(memory_space=pltpu.SMEM)
    hbm = pl.BlockSpec(memory_space=pl.ANY)
    dma = pltpu.SemaphoreType.DMA
    half_head = HEAD // 2
    freqs = np.float32(ROPE_BASE) ** (-(np.arange(half_head, dtype=np.float32) * 2) / HEAD)
    freqs = jnp.asarray(np.tile(freqs.astype(np.float32), LANES // half_head)[None])
    return pl.pallas_call(
        functools.partial(
            forward_kernel, tp_count=tp_count, ctx_count=ctx_count, shared=shared, straight=straight
        ),
        in_specs=[smem] * 2 + [vmem] * 16 + [hbm] * 5,
        out_specs=[vmem] * 16 + [hbm] * 6,
        out_shape=[
            jax.ShapeDtypeStruct((rows, q_cols), BF16),
            jax.ShapeDtypeStruct((heads, rows, LANES), BF16),
            jax.ShapeDtypeStruct((SPAN, tp_count, block, 2 * kv_cols), BF16),
            jax.ShapeDtypeStruct((rows, LANES), BF16),
            jax.ShapeDtypeStruct((block, model), F32),
            jax.ShapeDtypeStruct((block, LANES), BF16),
            jax.ShapeDtypeStruct((2, model // 2 + q_cols, model // 2), BF16),
            jax.ShapeDtypeStruct((tp_count, block, model), BF16),
            jax.ShapeDtypeStruct((model, LANES), BF16),
            jax.ShapeDtypeStruct((LANES, cols), BF16),
            jax.ShapeDtypeStruct((tp_count * q_cols, LANES), BF16),
            jax.ShapeDtypeStruct((LANES, model), BF16),
            jax.ShapeDtypeStruct((rows, LANES), F32),
            jax.ShapeDtypeStruct((rows, LANES), F32),
            jax.ShapeDtypeStruct((tp_count, 2, q_cols, model // 2), BF16),
            jax.ShapeDtypeStruct((tp_count, block, q_cols), BF16),
            *[jax.ShapeDtypeStruct((shared + straight,) + w.shape[1:], BF16) for w in weights],
            jax.ShapeDtypeStruct((ctx_count,) + grads.shape, BF16),
            jax.ShapeDtypeStruct((ctx_count,) + routes.shape, jnp.int32),
            jax.ShapeDtypeStruct((ctx_count, block, model), BF16),
        ],
        scratch_shapes=[
            pltpu.VMEM((heads, rows, LANES), BF16),
            pltpu.VMEM((pairs, SPAN * rows, LANES), BF16),
            pltpu.VMEM((pairs, SPAN * rows, LANES), BF16),
            pltpu.VMEM((tp_count * pairs, tall, LANES), F32),
            pltpu.VMEM((tp_count * pairs, tall, LANES), F32),
            pltpu.VMEM((block, model), BF16),
            pltpu.VMEM((LANES, LANES), BF16),
            pltpu.VMEM((LANES, LANES), BF16),
            dma((2, 4)),
            dma((2, 2, tp_count)),
            dma((2, SPAN - 1)),
            dma((2, tp_count - 1)),
            dma((2, 2, tp_count)),
            dma((2, shared + straight, 3)),
            dma((2, max(shared, 1), 3)),
            dma((2, ctx_count)),
            dma((2, ctx_count)),
            dma((2, chips)),
            dma((2, chips)),
            dma((3,)),
        ],
        compiler_params=pltpu.CompilerParams(
            vmem_limit_bytes=VMEM_LIMIT, collective_id=0, has_side_effects=True
        ),
        cost_estimate=pl.CostEstimate(
            flops=16 * SPAN * rows * rows * heads * LANES,
            bytes_accessed=32 * 1024 * 1024,
            transcendentals=0,
        ),
        name="forward",
    )(
        parents, adapter_set, tokens, *gains, freqs, *attention, *adapters, *weights, grads, routes,
    )


def joined(dk, dv, span):
    pairs = dk.shape[0]
    return jnp.concatenate(
        [dk[pair, span, :HEAD] for pair in range(pairs)]
        + [dv[pair, span, :HEAD] for pair in range(pairs)],
        axis=1,
    )


def backward_kernel(
    tokens, upstream_ref, routes, gain_one, gain_two, w_router, middle_ref, low_ref, weights,
    normed_all, lora, att, q_ref, kv_ref, first, second, o_first, o_second, cos, sin, w_rows, att_rows, back, mixed, shares,
    output, input_grad, packed_out, shares_out,
    k_aug, v_aug, up_aug, dk, dv, dq, do_out, do_all, far_out, far_in, own_kv, row_grads, low_grads, parts, parts_in,
    second_acc, first_acc, packed, ctx_in, tp_in, middle_grad, router,
    back_near, back_mine, back_pair, back_far, mixed_near, mixed_mine, mixed_pair, mixed_far,
    near_sem, mine_sem, far_sem, branch_sem, kv_sem, part_sem,
    ctx_sem, tp_sem, x_sem, ctx_all_sem, share_sem, swap_sem, own_sem,
    *, tp_count, ctx_count, experts, direct,
):
    tp, ctx, fsdp = (lax.axis_index(name) for name in ("tp", "ctx", "fsdp"))
    rank = lax.rem(ctx, SPAN)
    block, model = tokens.shape
    heads, rows_all, _ = q_ref.shape
    pairs = k_aug.shape[0]
    group = heads // pairs
    tall = group * block
    half = weights.shape[2]
    q_cols = heads * HEAD
    kv_cols = pairs * HEAD
    turn = cos.shape[1]
    partner = ctx + 1 - 2 * lax.rem(ctx, 2)
    cross = ring(ctx, 2, ctx_count)
    cross_partner = ring(partner, 2, ctx_count)
    other = {"fsdp": 1 - fsdp}

    barrier = pltpu.get_barrier_semaphore()
    pl.semaphore_signal(barrier, 1, device_id=other, device_id_type=pl.DeviceIdType.MESH)
    for k in range(1, tp_count):
        pl.semaphore_signal(
            barrier, 1, device_id={"tp": ring(tp, k, tp_count)},
            device_id_type=pl.DeviceIdType.MESH,
        )
    for k in range(1, ctx_count):
        pl.semaphore_signal(
            barrier, 1, device_id={"ctx": ring(ctx, k, ctx_count)},
            device_id_type=pl.DeviceIdType.MESH,
        )
    pl.semaphore_wait(barrier, tp_count + ctx_count - 1)

    sums = (
        (back, back_near, back_mine, back_pair, back_far),
        (mixed, mixed_near, mixed_mine, mixed_pair, mixed_far),
    )

    def near_copy(n, slot):
        source, near = sums[n][:2]
        return remote(
            source.at[(partner, cross_partner)[slot]], near.at[slot],
            near_sem.at[0, 2 * n + slot], near_sem.at[1, 2 * n + slot], {"ctx": partner},
        )

    def mine_copy(n, slot):
        return pltpu.make_async_copy(
            sums[n][0].at[(ctx, cross)[slot]], sums[n][2].at[slot], mine_sem.at[2 * n + slot]
        )

    def pair_copy(n):
        return remote(sums[n][3], sums[n][4], far_sem.at[0, n], far_sem.at[1, n], {"ctx": cross})

    def start_sum(n):
        for slot in (1, 0):
            near_copy(n, slot).start()
            mine_copy(n, slot).start()

    def pass_sum(n):
        near_copy(n, 1).wait_recv()
        mine_copy(n, 1).wait()
        _, near, mine, pair, _ = sums[n]
        pair[...] = (near[1].astype(F32) + mine[1].astype(F32)).astype(BF16)
        pair_copy(n).start()

    def end_sum(n):
        near_copy(n, 0).wait_recv()
        mine_copy(n, 0).wait()
        pair_copy(n).wait_recv()
        _, near, mine, _, far = sums[n]
        return near[0].astype(F32) + mine[0].astype(F32) + far[...].astype(F32)

    if direct:
        share = shares.shape[2]
        own_lanes = pl.ds(pl.multiple_of(tp * share, share), share)

        def share_copy(k):
            return remote(
                shares, shares_out.at[fsdp, :, :, own_lanes],
                share_sem.at[0, k - 1], share_sem.at[1, k - 1], {"tp": ring(tp, k, tp_count)},
            )

        share_own = pltpu.make_async_copy(shares, shares_out.at[fsdp, :, :, own_lanes], own_sem.at[0])
        swap = remote(
            shares_out.at[fsdp], shares_out.at[fsdp], swap_sem.at[0], swap_sem.at[1], other
        )

        start_sum(0)
        start_sum(1)
        share_own.start()

    @pl.loop(0, rank + 1)
    def _(distance):
        @pl.loop(0, tp_count)
        def _(part):
            kv = kv_ref[distance, part]
            for pair in range(pairs):
                aug_keys(
                    kv, pair, pairs, (rank - distance) * SEGS_DEV + part * (block // SEG),
                    k_aug, v_aug, pl.multiple_of(distance * rows_all + part * block, block),
                )

    dk[...] = jnp.zeros(dk.shape, F32)
    dv[...] = jnp.zeros(dv.shape, F32)
    dq[...] = jnp.zeros(dq.shape, F32)
    second_acc[...] = jnp.zeros(second_acc.shape, F32)
    first_acc[...] = jnp.zeros(first_acc.shape, F32)
    packed[...] = jnp.zeros(packed.shape, F32)

    middle = middle_ref[...]
    scale_one = gain_one[...].astype(F32).reshape(1, model)
    scale_two = gain_two[...].astype(F32).reshape(1, model)
    normed_two = rms_scale(middle, scale_two).astype(BF16)
    router[...] = jnp.zeros(router.shape, BF16)
    router[pl.ds(0, experts), :] = w_router[...]
    logits = dot_nt(normed_two, router[...])
    number = iota((LANES, block), 0)
    hit = jnp.zeros((LANES, block), F32)
    for k in range(routes.shape[0]):
        hit += (routes[k : k + 1, :] == number).astype(F32)
    hit = hit.T
    kept = jnp.where(hit > 0.5, logits, MASKED)
    gates = jnp.exp(kept - jnp.max(kept, axis=1, keepdims=True)) * hit
    gates = gates / jnp.sum(gates, axis=1, keepdims=True)

    if direct:
        pass_sum(0)
        back_sum = end_sum(0)
    else:
        back_sum = back[...].astype(F32)
    table = back_sum[:, model:]
    slopes = table + pltpu.roll(table, LANES - experts, 1)
    logits_grad = gates * (slopes - jnp.sum(gates * slopes, axis=1, keepdims=True))
    high = logits_grad.astype(BF16)
    low = (logits_grad - high.astype(F32)).astype(BF16)
    normed_two_grad = back_sum[:, :model] + dot(high, router[...]) + dot(low, router[...])
    middle_grad[...] = upstream_ref[...].astype(F32) + rms_back(
        middle, scale_two, normed_two_grad
    )
    branch = (RESIDUAL_SCALE * middle_grad[...]).astype(BF16)
    low_grad = dot_nt(branch, o_second[...]).astype(BF16)

    def do_copy(k):
        where = ring(tp, k, tp_count)
        return remote(
            do_out.at[where], do_all.at[tp], branch_sem.at[0, k - 1], branch_sem.at[1, k - 1],
            {"tp": where},
        )

    for t in range(tp_count):
        do_out[t] = (
            dot_nt(branch[:, :half], w_rows[t, 0])
            + dot_nt(branch[:, half:], w_rows[t, 1])
            + dot_nt(low_grad, o_first[pl.ds(t * q_cols, q_cols), :])
        ).astype(BF16)
    for k in range(1, tp_count):
        do_copy(k).start()
    do_all[tp] = do_out[tp]
    for t in range(tp_count):
        packed[pl.ds(3 * RANK, RANK), t * q_cols : (t + 1) * q_cols] = dot_tn(
            low_grad, att_rows[t]
        )[:RANK]
    packed[pl.ds(4 * RANK, RANK), :] = dot_tn(low_ref[...], branch)[:RANK]
    if direct:
        pass_sum(1)

    wide = heads * LANES
    r, c = iota((q_cols, wide), 0), iota((q_cols, wide), 1)
    same = r // HEAD == c // LANES
    place = (same & (r % HEAD == c % LANES)).astype(BF16)
    spread = (same & (c % LANES >= ONES) & (c % LANES < ONES + 2)).astype(BF16)

    def tile(part, pair, start, size, causal):
        index = part * pairs + pair
        rows = pl.ds(pl.multiple_of(part * block, block), block)
        queries = q_ref[pl.ds(pair * group, group), rows, :].reshape(tall, LANES)
        upstream = up_aug[pl.ds(pair * group, group), rows, :].reshape(tall, LANES)
        span = pl.ds(start, size)
        keys = k_aug[pair, span, :]
        probs = jnp.exp(dot_nt(keys, queries))
        if causal:
            q_row = iota(probs.shape, 1) % block
            probs = jnp.where(iota(probs.shape, 0) <= q_row, probs, 0.0)
        steep = (probs * dot_nt(v_aug[pair, span, :], upstream)).astype(BF16)
        dv[pair, span, :] += dot(probs.astype(BF16), upstream)
        dk[pair, span, :] += dot(steep, queries)
        dq[index] += dot_tn(steep, keys)

    def far_copy(distance):
        return remote(
            far_out.at[distance - 1], far_in.at[distance - 1],
            kv_sem.at[0, distance - 1], kv_sem.at[1, distance - 1],
            {"ctx": ring(ctx, -distance, ctx_count)},
        )

    size = min(rows_all, 1024)

    def take_block(part):
        rows = pl.ds(pl.multiple_of(part * block, block), block)
        grads = do_all[part]
        mixed_heads = att[rows, :]
        product = grads.astype(F32) * mixed_heads.astype(F32)
        minus = jnp.zeros((block, wide), F32)
        for _ in range(3):
            piece = product.astype(BF16)
            minus -= dot(piece, spread)
            product -= piece.astype(F32)
        top = minus.astype(BF16).astype(F32)
        lane = iota(minus.shape, 1) % LANES
        coded = dot(grads, place) + jnp.where(
            lane == ONES, top, jnp.where(lane == ONES + 1, minus - top, 0.0)
        )
        for head in range(heads):
            up_aug[head, rows, :] = coded[:, head * LANES : (head + 1) * LANES].astype(BF16)

    @pl.loop(0, tp_count)
    def _(turn):
        part = ring(tp, -turn, tp_count)

        @pl.when(turn > 0)
        def _():
            do_copy(turn).wait_recv()

        @pl.when(turn >= 0)
        def _():
            take_block(part)

            @pl.loop(0, rank)
            def _(step):
                distance = rank - step
                start = distance * rows_all

                @pl.loop(0, pairs * (rows_all // size))
                def _(n):
                    pair, piece = n // (rows_all // size), lax.rem(n, rows_all // size)
                    tile(part, pair, pl.multiple_of(start + piece * size, size), size, False)

                @pl.when(turn == tp_count - 1)
                def _():
                    @pl.loop(0, tp_count)
                    def _(spot):
                        span = pl.ds(pl.multiple_of(start + spot * block, block), block)
                        rows = pl.ds(pl.multiple_of(spot * block, block), block)
                        far_out[distance - 1, rows, :] = joined(dk, dv, span).astype(BF16)

                    far_copy(distance).start()

            if direct:

                @pl.when(turn == tp_count - 1)
                def _():
                    for k in range(1, tp_count):
                        share_copy(k).start()

            @pl.loop(0, pairs)
            def _(pair):
                tile(part, pair, pl.multiple_of(part * block, block), block, True)

                @pl.loop(0, part)
                def _(j):
                    tile(part, pair, pl.multiple_of(j * block, block), block, False)

    own_kv[...] = joined(dk, dv, pl.ds(0, rows_all))
    for distance in range(1, SPAN):

        @pl.when(rank + distance < SPAN)
        def _(distance=distance):
            far_copy(distance).wait_recv()
            own_kv[...] += far_in[distance - 1].astype(F32)

    def part_copy(k):
        return remote(
            parts.at[k], parts_in.at[k], part_sem.at[0, k], part_sem.at[1, k],
            {"tp": ring(tp, k + 1, tp_count)},
        )

    @pl.loop(0, tp_count)
    def _(part):
        rows = pl.ds(pl.multiple_of(part * block, block), block)
        pieces = []
        for pair in range(pairs):
            held = dq[part * pairs + pair]
            turned = SCORE_SCALE * jnp.concatenate(
                [held[member * block : (member + 1) * block, :HEAD] for member in range(group)],
                axis=1,
            )
            pieces.append(turned * cos[rows, :] - swap_halves(turned) * sin[rows, :])
        keys = own_kv[rows, :kv_cols]
        pieces.append(keys * cos[rows, :] - swap_halves(keys) * sin[rows, :])
        pieces.append(own_kv[rows, kv_cols:])
        grads = jnp.concatenate(pieces, axis=1).astype(BF16)
        row_grads[rows, :] = grads
        low_part = dot_nt(grads, second[...]).astype(BF16)
        low_grads[rows, :] = low_part
        second_acc[...] += dot_tn(lora[rows, :], grads)
        first_acc[...] += dot_tn(low_part, normed_all[part])

    packed[pl.ds(0, 3 * RANK), :] = first_acc[pl.ds(0, 3 * RANK), :]
    lanes = pl.ds(pl.multiple_of(tp * q_cols, q_cols), q_cols)
    packed[pl.ds(5 * RANK, RANK), lanes] = second_acc[pl.ds(0, RANK), :q_cols]
    lanes = pl.ds(pl.multiple_of(tp * kv_cols, kv_cols), kv_cols)
    packed[pl.ds(6 * RANK, RANK), lanes] = second_acc[pl.ds(RANK, RANK), q_cols : q_cols + kv_cols]
    lanes = pl.ds(pl.multiple_of(model // 2 + tp * kv_cols, kv_cols), kv_cols)
    packed[pl.ds(6 * RANK, RANK), lanes] = second_acc[pl.ds(2 * RANK, RANK), q_cols + kv_cols :]

    def make_parts():
        @pl.loop(0, tp_count)
        def _(k):
            part = ring(tp, k + 1, tp_count)
            rows = pl.ds(pl.multiple_of(part * block, block), block)
            grads = row_grads[rows, :]
            for side in range(2):
                columns = slice(side * half, (side + 1) * half)
                parts[k, :, columns] = (
                    dot_nt(grads, weights[side, pl.ds(0, half), :])
                    + dot_nt(low_grads[rows, :], first[columns, :])
                ).astype(BF16)

    def send_parts():
        for k in range(tp_count - 1):
            part_copy(k).start()

    if direct:
        tall_rows = packed.shape[0] // ctx_count

        def ctx_rows(index):
            return pl.ds(pl.multiple_of(index * tall_rows, tall_rows), tall_rows)

        def ctx_copy(k):
            where = ring(ctx, k, ctx_count)
            return remote(
                packed.at[ctx_rows(where)], ctx_in.at[k - 1],
                ctx_sem.at[0, k - 1], ctx_sem.at[1, k - 1], {"ctx": where},
            )

        def tp_copy(k):
            return remote(
                tp_in.at[tp], tp_in.at[tp], tp_sem.at[0, k - 1], tp_sem.at[1, k - 1],
                {"tp": ring(tp, k, tp_count)},
            )

        x_copy = remote(
            packed_out.at[fsdp, ctx_rows(ctx)], packed_out.at[fsdp, ctx_rows(ctx)],
            x_sem.at[0], x_sem.at[1], other,
        )

        def ctx_all_copy(k):
            return remote(
                packed_out.at[:, ctx_rows(ctx)], packed_out.at[:, ctx_rows(ctx)],
                ctx_all_sem.at[0, k - 1], ctx_all_sem.at[1, k - 1],
                {"ctx": ring(ctx, k, ctx_count)},
            )

        for k in range(1, ctx_count):
            ctx_copy(k).start()
        make_parts()
        for k in range(1, ctx_count):
            ctx_copy(k).wait()
        tp_in[tp] = (packed[ctx_rows(ctx), :] + sum(ctx_in[k] for k in range(ctx_count - 1))).astype(
            BF16
        )
        for k in range(1, tp_count):
            tp_copy(k).start()
        send_parts()
        for k in range(1, tp_count):
            tp_copy(k).wait()
        packed_out[fsdp, ctx_rows(ctx), :] = sum(tp_in[k].astype(F32) for k in range(tp_count))
        x_copy.start()
        x_copy.wait()
        for k in range(1, ctx_count):
            ctx_all_copy(k).start()
        share_own.wait()
        for k in range(1, tp_count):
            share_copy(k).wait()
        swap.start()
    else:
        packed_out[0] = packed[...]
        make_parts()
        send_parts()

    summed = parts[tp_count - 1].astype(F32)
    for k in range(tp_count - 1):
        part_copy(k).wait_recv()
        summed += parts_in[k].astype(F32)
    inputs = tokens[...].astype(F32)
    input_grad[...] = (middle_grad[...] + rms_back(inputs, scale_one, summed)).astype(BF16)
    mixture = end_sum(1) if direct else mixed[...].astype(F32)
    output[...] = (middle_ref[...] + RESIDUAL_SCALE * mixture).astype(BF16)

    if direct:
        swap.wait()
        for k in range(1, ctx_count):
            ctx_all_copy(k).wait()
        for n in range(2):
            for slot in range(2):
                near_copy(n, slot).wait_send()
            pair_copy(n).wait_send()
    for k in range(1, tp_count):
        do_copy(k).wait_send()
    for k in range(tp_count - 1):
        part_copy(k).wait_send()
    for distance in range(1, SPAN):

        @pl.when(distance <= rank)
        def _(distance=distance):
            far_copy(distance).wait_send()


def backward(
    tokens, upstream, routes, gains, router, middle, low, weights, normed, lora, att, queries, kv,
    first, second, o_first, o_second, cos, sin, w_rows, att_rows, back, mixed, shares,
    tp_count, ctx_count, experts, direct,
):
    block, model = tokens.shape
    heads, rows, _ = queries.shape
    pairs = kv.shape[3] // (2 * HEAD)
    tall = heads // pairs * block
    cols = second.shape[1]
    kv_width = kv.shape[3]
    vmem = pl.BlockSpec(memory_space=pltpu.VMEM)
    hbm = pl.BlockSpec(memory_space=pl.ANY)
    dma = pltpu.SemaphoreType.DMA
    part = (block, model)
    packed = (8 * RANK, model)
    copies = 2 if direct else 1
    slim = (8, LANES)

    def buffers(width):
        shapes = [(2, block, width), (2, block, width), (block, width), (block, width)]
        return [pltpu.VMEM(shape if direct else slim, BF16) for shape in shapes]

    return pl.pallas_call(
        functools.partial(
            backward_kernel, tp_count=tp_count, ctx_count=ctx_count, experts=experts, direct=direct
        ),
        in_specs=[vmem] * 22 + [hbm if direct else vmem] * 2 + [hbm],
        out_specs=[vmem] * 3 + [hbm],
        out_shape=[
            jax.ShapeDtypeStruct((block, model), BF16),
            jax.ShapeDtypeStruct((block, model), BF16),
            jax.ShapeDtypeStruct((copies,) + packed, F32),
            jax.ShapeDtypeStruct(
                (2,) + shares.shape[:2] + (tp_count * shares.shape[2],) if direct else slim, BF16
            ),
        ],
        scratch_shapes=[
            pltpu.VMEM((pairs, SPAN * rows, LANES), BF16),
            pltpu.VMEM((pairs, SPAN * rows, LANES), BF16),
            pltpu.VMEM((heads, rows, LANES), BF16),
            pltpu.VMEM((pairs, SPAN * rows, LANES), F32),
            pltpu.VMEM((pairs, SPAN * rows, LANES), F32),
            pltpu.VMEM((tp_count * pairs, tall, LANES), F32),
            pltpu.VMEM((tp_count, block, heads * HEAD), BF16),
            pltpu.VMEM((tp_count, block, heads * HEAD), BF16),
            pltpu.VMEM((SPAN - 1, rows, kv_width), BF16),
            pltpu.VMEM((SPAN - 1, rows, kv_width), BF16),
            pltpu.VMEM((rows, kv_width), F32),
            pltpu.VMEM((rows, cols), BF16),
            pltpu.VMEM((rows, LANES), BF16),
            pltpu.VMEM((tp_count,) + part, BF16),
            pltpu.VMEM((tp_count - 1,) + part, BF16),
            pltpu.VMEM((LANES, cols), F32),
            pltpu.VMEM((LANES, model), F32),
            pltpu.VMEM(packed, F32),
            pltpu.VMEM((ctx_count - 1, packed[0] // ctx_count, model) if direct else slim, F32),
            pltpu.VMEM((tp_count, packed[0] // ctx_count, model) if direct else slim, BF16),
            pltpu.VMEM((block, model), F32),
            pltpu.VMEM((LANES, model), BF16),
            *buffers(model + LANES),
            *buffers(model),
            dma((2, 4)),
            dma((4,)),
            dma((2, 2)),
            dma((2, tp_count - 1)),
            dma((2, SPAN - 1)),
            dma((2, tp_count - 1)),
            dma((2, ctx_count - 1)),
            dma((2, tp_count - 1)),
            dma((2,)),
            dma((2, ctx_count - 1)),
            dma((2, tp_count - 1)),
            dma((2,)),
            dma((1,)),
        ],
        compiler_params=pltpu.CompilerParams(
            vmem_limit_bytes=60 * 1024 * 1024, collective_id=1, has_side_effects=True
        ),
        cost_estimate=pl.CostEstimate(
            flops=32 * SPAN * rows * rows * heads * LANES,
            bytes_accessed=32 * 1024 * 1024,
            transcendentals=0,
        ),
        name="backward",
    )(
        tokens, upstream, routes, *gains, router, middle, low, weights, normed, lora, att, queries,
        kv, first, second, o_first, o_second, cos, sin, w_rows, att_rows, back, mixed, shares,
    )


def place_kernel(sets, packed, part, *outs):
    query_in, query_out, key_in, key_out, value_in, value_out, out_in, out_out = outs[:8]
    gate_in, gate_out, up_in, up_out, down_in, down_out = outs[8:]
    kv_cols, hidden = key_out.shape[1], gate_out.shape[2]
    trees = part.shape[0]
    spots = jnp.concatenate(
        [
            (iota((RANK, LANES), 1) == iota((RANK, LANES), 0) + sets[tree] * RANK).astype(BF16)
            for tree in range(trees)
        ],
        axis=0,
    )
    spots_twice = jnp.concatenate([spots, spots], axis=0)

    def block(rows):
        return slice(rows * RANK, (rows + 1) * RANK)

    @pl.when(pl.program_id(0) == 0)
    def _():
        def gathered(rows, lanes, turned):
            pieces = jnp.concatenate(
                [packed[tree, block(rows), lanes] for tree in range(trees)], axis=0
            )
            high = pieces.astype(BF16)
            both = jnp.concatenate([high, (pieces - high.astype(F32)).astype(BF16)], axis=0)
            return dot_tn(both, spots_twice) if turned else dot_tn(spots_twice, both)

        whole = slice(None)
        query_in[...] = gathered(0, whole, True)
        key_in[...] = gathered(1, whole, True)
        value_in[...] = gathered(2, whole, True)
        out_in[...] = gathered(3, whole, True)
        out_out[...] = gathered(4, whole, False)
        query_out[...] = gathered(5, whole, False)
        key_out[...] = gathered(6, slice(0, kv_cols), False)
        value_out[...] = gathered(6, slice(kv_cols, 2 * kv_cols), False)

    def pieces(rows, lanes):
        return jnp.concatenate([part[tree, 0, block(rows), lanes] for tree in range(trees)], axis=0)

    whole, left, right = slice(None), slice(0, hidden), slice(hidden, 2 * hidden)
    gate_in[0] = dot_tn(pieces(0, whole), spots)
    up_in[0] = dot_tn(pieces(1, whole), spots)
    gate_out[0] = dot_tn(spots, pieces(2, left))
    up_out[0] = dot_tn(spots, pieces(2, right))
    down_out[0] = dot_tn(spots, pieces(3, whole))
    down_in[0] = dot_tn(pieces(4, left), spots)


def place(sets, packed, part, once, each):
    trees, local = part.shape[:2]
    return pl.pallas_call(
        place_kernel,
        grid_spec=pltpu.PrefetchScalarGridSpec(
            num_scalar_prefetch=1,
            grid=(local,),
            in_specs=[
                pl.BlockSpec(packed.shape, lambda e, s: (0, 0, 0)),
                pl.BlockSpec((trees, 1) + part.shape[2:], lambda e, s: (0, e, 0, 0)),
            ],
            out_specs=[
                *[pl.BlockSpec(o.shape, lambda e, s: (0, 0)) for o in once],
                *[pl.BlockSpec((1,) + o.shape[1:], lambda e, s: (e, 0, 0)) for o in each],
            ],
        ),
        out_shape=[jax.ShapeDtypeStruct(o.shape, F32) for o in (*once, *each)],
        compiler_params=pltpu.CompilerParams(vmem_limit_bytes=VMEM_LIMIT),
        name="place",
    )(sets, packed, part)


def expert_kernel(
    sets, x_ref, g_ref, routes, router,
    w_gate, w_up, w_down, w_gate_far, w_up_far, w_down_far, all_gate, all_up, all_down, gate_in, up_in, gate_out, up_out, down_in, down_out,
    back_out, mixed_out, grad_out,
    rank_rows, gate_rows, slope_rows, mix, back, xs, firsts, tall_grad,
    gate_full, up_full, down_full, land_gate, land_up, land_down, grads, grads_in,
    far_sem, pass_far_sem, grads_sem, arrive_sem,
    *, slots, sources, early, shared, straight, tp_count,
):
    chunk, expert = pl.program_id(0), pl.program_id(1)
    tp, fsdp = lax.axis_index("tp"), lax.axis_index("fsdp")
    late = shared + straight
    gather = late > 0
    other = {"fsdp": 1 - fsdp}
    cross, hand_on = far_moves(
        (all_gate, all_up, all_down), (land_gate, land_up, land_down), far_sem, pass_far_sem,
        shared, straight, early, 0, other, tp,
    )

    if gather:

        @pl.when(expert == 0)
        def _():
            barrier = pltpu.get_barrier_semaphore()
            pl.semaphore_signal(
                barrier, 1, device_id=other, device_id_type=pl.DeviceIdType.MESH
            )
            for k in range(1, tp_count):
                pl.semaphore_signal(
                    barrier, 1, device_id={"tp": ring(tp, k, tp_count)},
                    device_id_type=pl.DeviceIdType.MESH,
                )
            pl.semaphore_wait(barrier, tp_count)
            for n in BEGIN[0]:
                for copy in cross(n):
                    copy.start()

        for step in range(1, early + late):
            if step in BEGIN or step in RELAY:

                @pl.when(expert == step)
                def _(step=step):
                    for n in RELAY.get(step, ()):
                        for copy in cross(n):
                            copy.wait_recv()
                        for copy in hand_on(n):
                            copy.start()
                    for n in BEGIN.get(step, ()):
                        for copy in cross(n):
                            copy.start()

        for n in range(late):

            @pl.when(expert == early + n)
            def _(n=n):
                for copy in hand_on(n) if n < shared else cross(n):
                    copy.wait_recv()

    experts = router.shape[0]
    tokens, model = x_ref.shape
    each = tokens // sources
    hidden = w_gate.shape[2]
    lanes = gate_in.shape[2]
    chosen = sets[fsdp * pl.num_programs(0) + chunk]

    @pl.when(expert == 0)
    def _():
        logits = dot_nt(router[...], x_ref[...])
        number = iota((experts, tokens), 0)
        hit = jnp.zeros((experts, tokens), F32)
        for k in range(routes.shape[0]):
            hit += (routes[k : k + 1, :] == number).astype(F32)
        kept = jnp.where(hit > 0.5, logits, MASKED)
        weights = jnp.exp(kept - jnp.max(kept, axis=0, keepdims=True)) * hit
        gate_rows[...] = weights / jnp.sum(weights, axis=0, keepdims=True)
        earlier = (iota((each, each), 0) < iota((each, each), 1)).astype(BF16)
        for s in range(sources):
            span = slice(s * each, (s + 1) * each)
            order = dot(hit[:, span].astype(BF16), earlier)
            rank_rows[:, span] = jnp.where(hit[:, span] > 0.5, order, -1.0)
        mix[...] = jnp.zeros(mix.shape, F32)
        back[...] = jnp.zeros(back.shape, F32)
        slope_rows[...] = jnp.zeros(slope_rows.shape, F32)

    first_row = lax.axis_index("ctx") * pl.num_programs(1)
    row = first_row + expert
    ranks = rank_rows[pl.ds(row, 1), :]
    gates = gate_rows[pl.ds(row, 1), :]
    slot_number = iota((slots, each), 0).astype(F32)
    picks, columns, upstreams = [], [], []
    for s in range(sources):
        span = slice(s * each, (s + 1) * each)
        pick = ranks[:, span] == slot_number
        columns.append(jnp.sum(jnp.where(pick, gates[:, span], 0.0), axis=1, keepdims=True))
        pick = pick.astype(BF16)
        picks.append(pick)
        xs[pl.ds(s * slots, slots), :] = dot(pick, x_ref[pl.ds(s * each, each), :]).astype(BF16)
        upstreams.append(dot(pick, g_ref[pl.ds(s * each, each), :]))
    gate_column = jnp.concatenate(columns, axis=0)
    upstream = RESIDUAL_SCALE * jnp.concatenate(upstreams, axis=0)

    firsts[:, :lanes] = gate_in[0]
    firsts[:, lanes:] = up_in[0]
    keep = (iota((1, 2 * lanes), 1) % lanes // RANK == chosen).astype(BF16)
    rows = xs[...]
    inner = dot(rows, firsts[...]).astype(BF16) * keep
    for full, near, far, landed in (
        (gate_full, w_gate, w_gate_far, land_gate),
        (up_full, w_up, w_up_far, land_up),
        (down_full, w_down, w_down_far, land_down),
    ):
        size = near.shape[1]
        full[pl.ds(pl.multiple_of(fsdp * size, size), size), :] = near[0]
        spot = pl.ds(pl.multiple_of((1 - fsdp) * size, size), size)
        if not gather:
            full[spot, :] = far[0]
            continue

        @pl.when(expert < early)
        def _(full=full, far=far, spot=spot):
            full[spot, :] = far[0]

        @pl.when(expert >= early)
        def _(full=full, landed=landed, spot=spot):
            full[spot, :] = landed[jnp.maximum(expert - early, 0)]
    gate_value = dot(rows, gate_full[...]) + dot(inner[:, :lanes], gate_out[0])
    up_value = dot(rows, up_full[...]) + dot(inner[:, lanes:], up_out[0])
    sigmoid = 1.0 / (1.0 + jnp.exp(-gate_value))
    silu = gate_value * sigmoid
    active = (silu * up_value).astype(BF16)
    down_inner = dot(active, down_in[0]).astype(BF16) * keep[:, :lanes]
    produced = (
        (dot(active, down_full[...]) + dot(down_inner, down_out[0])).astype(BF16).astype(F32)
    )
    slope = jnp.sum(upstream * produced, axis=1, keepdims=True)
    sent = (gate_column * produced).astype(BF16)
    slot_grad = (gate_column * upstream).astype(BF16)

    down_inner_grad = dot_nt(slot_grad, down_out[0]).astype(BF16) * keep[:, :lanes]
    active_grad = (
        (dot_nt(slot_grad, down_full[...]) + dot_nt(down_inner_grad, down_in[0]))
        .astype(BF16)
        .astype(F32)
    )
    gate_grad = (active_grad * up_value * (sigmoid + silu * (1.0 - sigmoid))).astype(BF16)
    up_grad = (active_grad * silu).astype(BF16)
    inner_grad = (
        jnp.concatenate([dot_nt(gate_grad, gate_out[0]), dot_nt(up_grad, up_out[0])], axis=1)
    ).astype(BF16) * keep
    row_grad = (
        dot_nt(gate_grad, gate_full[...])
        + dot_nt(up_grad, up_full[...])
        + dot_nt(inner_grad, firsts[...])
    ).astype(BF16)

    for s in range(sources):
        span = slice(s * slots, (s + 1) * slots)
        spot = pl.ds(s * each, each)
        mix[spot, :] += dot_tn(picks[s], sent[span, :])
        back[spot, :] += dot_tn(picks[s], row_grad[span, :])
        slope_rows[pl.ds(expert, 1), spot] = jnp.sum(
            jnp.where(picks[s] > 0.5, slope[span, :], 0.0), axis=0, keepdims=True
        )

    keep_at = expert if gather else 0

    def folded(start, width):
        total = tall_grad[pl.ds(start, RANK), :width]
        for shift in range(RANK, lanes, RANK):
            total += tall_grad[pl.ds(start + shift, RANK), :width]
        return total.astype(BF16)

    tall_grad[...] = dot_tn(inner_grad, rows)
    grads[keep_at, pl.ds(0, RANK), :] = folded(0, model)
    grads[keep_at, pl.ds(RANK, RANK), :] = folded(lanes, model)
    tall_grad[pl.ds(0, lanes), :hidden] = dot_tn(inner[:, :lanes], gate_grad)
    tall_grad[pl.ds(0, lanes), hidden:] = dot_tn(inner[:, lanes:], up_grad)
    grads[keep_at, pl.ds(2 * RANK, RANK), :] = folded(0, model)
    tall_grad[pl.ds(0, lanes), :] = dot_tn(down_inner, slot_grad)
    grads[keep_at, pl.ds(3 * RANK, RANK), :] = folded(0, model)
    tall_grad[pl.ds(0, lanes), :hidden] = dot_tn(down_inner_grad, active)
    grads[keep_at, pl.ds(4 * RANK, RANK), :hidden] = folded(0, hidden)
    grads[keep_at, pl.ds(4 * RANK, RANK), hidden:] = jnp.zeros((RANK, model - hidden), BF16)

    share = tall_grad.shape[1] // tp_count

    def grads_copy(n, k):
        where = ring(tp, k, tp_count)
        lanes = pl.ds(pl.multiple_of(where * share, share), share)
        return remote(
            grads.at[n, :, lanes], grads_in.at[k - 1, n], grads_sem.at[k - 1, n],
            arrive_sem.at[k - 1, n], {"tp": where},
        )

    if gather:
        for k in range(1, tp_count):
            grads_copy(expert, k).start()
    else:
        grad_out[0, 0] = grads[0]

    if gather:

        @pl.when(expert == pl.num_programs(1) - 1)
        def _():
            for n in range(late):
                for copy in cross(n):
                    copy.wait_send()
            for n in range(shared):
                for copy in hand_on(n):
                    copy.wait_send()

            @pl.loop(0, pl.num_programs(1))
            def _(n):
                lanes = pl.ds(pl.multiple_of(tp * share, share), share)
                total = grads[n, :, lanes].astype(F32)
                for k in range(1, tp_count):
                    grads_copy(n, k).wait()
                    total += grads_in[k - 1, n].astype(F32)
                grad_out[n] = total.astype(BF16)

    @pl.when(expert == pl.num_programs(1) - 1)
    def _():
        mixed_out[...] = mix[...].astype(BF16)
        back_out[:, :model] = back[...].astype(BF16)
        turned = slope_rows[...].T
        high = turned.astype(BF16)
        low = (turned - high.astype(F32)).astype(BF16)
        local, lane = iota((LANES, LANES), 0), iota((LANES, LANES), 1)
        inside = local < pl.num_programs(1)
        first = (inside & (lane == local + first_row)).astype(BF16)
        later = (inside & (lane == local + first_row + experts)).astype(BF16)
        back_out[:, model:] = (dot(high, first) + dot(low, later)).astype(BF16)


def run_experts(
    sets, rows, upstream, routes, router, weights, far, adapters, slots, sources, tp_count
):
    total, model = rows.shape
    experts = router.shape[0]
    local, half, hidden = weights[0].shape
    trees = sets.shape[0] // 2
    tokens = total // trees
    lanes = adapters[0].shape[2]
    tall = sources * slots
    piece = lambda c, e, *_: (c, 0)
    fixed = lambda c, e, *_: (0, 0)
    expert = lambda c, e, *_: (e, 0, 0)
    pairs, singles, shared, straight = transfer_plan(local, tp_count)
    early, late = pairs + singles, shared + straight
    arrived = lambda c, e, *_: (jnp.minimum(e, early - 1), 0, 0)
    hbm = pl.BlockSpec(memory_space=pl.ANY)
    dma = pltpu.SemaphoreType.DMA
    share = (local, 5 * RANK, model // tp_count)
    gradients = (
        (share, pl.BlockSpec(share, lambda c, e, *_: (0, 0, 0)))
        if late
        else (
            (trees, local, 5 * RANK, model),
            pl.BlockSpec((1, 1, 5 * RANK, model), lambda c, e, *_: (c, e, 0, 0)),
        )
    )
    return pl.pallas_call(
        functools.partial(
            expert_kernel, slots=slots, sources=sources, early=early, shared=shared,
            straight=straight, tp_count=tp_count,
        ),
        grid_spec=pltpu.PrefetchScalarGridSpec(
            num_scalar_prefetch=1,
            grid=(trees, local),
            in_specs=[
                pl.BlockSpec((tokens, model), piece),
                pl.BlockSpec((tokens, model), piece),
                pl.BlockSpec((routes.shape[0], tokens), lambda c, e, *_: (0, c)),
                pl.BlockSpec(router.shape, fixed),
                *[pl.BlockSpec((1,) + w.shape[1:], expert) for w in weights],
                *[pl.BlockSpec((1,) + w.shape[1:], arrived) for w in weights],
                *[hbm] * len(weights),
                *[pl.BlockSpec((1,) + a.shape[1:], expert) for a in adapters],
            ],
            out_specs=[
                pl.BlockSpec((tokens, model + LANES), piece),
                pl.BlockSpec((tokens, model), piece),
                gradients[1],
            ],
            scratch_shapes=[
                pltpu.VMEM((experts, tokens), F32),
                pltpu.VMEM((experts, tokens), F32),
                pltpu.VMEM((LANES, tokens), F32),
                pltpu.VMEM((tokens, model), F32),
                pltpu.VMEM((tokens, model), F32),
                pltpu.VMEM((tall, model), BF16),
                pltpu.VMEM((model, 2 * lanes), BF16),
                pltpu.VMEM((2 * lanes, model), F32),
                pltpu.VMEM((2 * half, hidden), BF16),
                pltpu.VMEM((2 * half, hidden), BF16),
                pltpu.VMEM((hidden, model), BF16),
                *[pltpu.VMEM((max(late, 1),) + w.shape[1:], BF16) for w in weights],
                pltpu.VMEM((local if late else 1, 5 * RANK, model), BF16),
                pltpu.VMEM((tp_count - 1,) + (share if late else (1, 16, LANES)), BF16),
                dma((2, max(late, 1), 3)),
                dma((2, max(shared, 1), 3)),
                dma((tp_count - 1, local)),
                dma((tp_count - 1, local)),
            ],
        ),
        out_shape=[
            jax.ShapeDtypeStruct((total, model + LANES), BF16),
            jax.ShapeDtypeStruct((total, model), BF16),
            jax.ShapeDtypeStruct(gradients[0], BF16),
        ],
        compiler_params=(
            pltpu.CompilerParams(
                vmem_limit_bytes=60 * 1024 * 1024, collective_id=2, has_side_effects=True
            )
            if late
            else pltpu.CompilerParams(vmem_limit_bytes=60 * 1024 * 1024)
        ),
        name="experts",
        cost_estimate=pl.CostEstimate(
            flops=2 * local * total * model * model * 2,
            bytes_accessed=8 * 1024 * 1024,
            transcendentals=0,
        ),
    )(sets, rows, upstream, routes, router, *weights, *far, *weights, *adapters)


def per_device(
    tokens,
    out_grad,
    routes,
    parents,
    adapter_set,
    gain_a,
    gain_b,
    w_query,
    key_projection_matrix,
    value_projection_matrix,
    w_output,
    w_router,
    w_gate,
    w_up,
    w_down,
    query_in,
    query_out,
    key_in,
    key_second_factor,
    value_in,
    value_second_factor,
    out_in,
    out_out,
    gate_in,
    gate_out,
    up_in,
    up_out,
    down_in,
    down_out,
):
    ctx_rank = lax.axis_index("ctx")
    fsdp_rank = lax.axis_index("fsdp")
    ctx_count = lax.axis_size("ctx")
    tp_count = lax.axis_size("tp")
    fsdp_count = lax.axis_size("fsdp")
    tok_rows, model = tokens.shape
    experts = w_router.shape[1]
    local_experts = w_gate.shape[0]
    slots = tok_rows * TOP * 3 // (2 * experts)
    trees = ctx_count // SPAN
    tree_index = (fsdp_rank * ctx_count + ctx_rank) // SPAN

    (
        attended, queries, kv_parts, lora, middle, o_reduced, attention_weights, normed_all,
        first, second, o_first, o_second, cos, sin, w_rows, att_rows,
        *far_weights, upstream_all, routes_all, rows_all,
    ) = forward(
        parents, adapter_set, tokens, (gain_a, gain_b),
        (w_query, key_projection_matrix, value_projection_matrix, w_output),
        (
            query_in, query_out, key_in, key_second_factor, value_in, value_second_factor,
            out_in, out_out,
        ),
        (w_gate, w_up, w_down), out_grad, routes.T, tp_count, ctx_count,
    )
    upstream_all = upstream_all.reshape(-1, model)
    rows_all = rows_all.reshape(-1, model)
    routes_all = routes_all.transpose(1, 0, 2).reshape(TOP, -1)

    back, mixed, expert_part = run_experts(
        adapter_set,
        rows_all,
        upstream_all,
        routes_all,
        w_router.T,
        (w_gate, w_up, w_down),
        far_weights,
        (gate_in, up_in, gate_out, up_out, down_in, down_out),
        slots,
        SPAN,
        tp_count,
    )
    direct = ctx_count == SPAN
    if direct:
        back = back.reshape(ctx_count, tok_rows, -1)
        mixed = mixed.reshape(ctx_count, tok_rows, -1)
    else:
        back = lax.psum_scatter(back, "ctx", scatter_dimension=0, tiled=True)
        mixed = lax.psum_scatter(mixed, "ctx", scatter_dimension=0, tiled=True)
    output, input_grad, packed, all_shares = backward(
        tokens, out_grad, routes.T, (gain_a, gain_b), w_router.T, middle, o_reduced, attention_weights,
        normed_all, lora, attended, queries, kv_parts, first, second, o_first, o_second,
        cos, sin, w_rows, att_rows, back, mixed, expert_part, tp_count, ctx_count, experts, direct,
    )
    all_trees = fsdp_count * trees
    if not direct:
        mine = (jnp.arange(all_trees, dtype=jnp.int32) == tree_index)[:, None, None]
        packed = lax.psum(jnp.where(mine, packed, 0.0), ("fsdp", "ctx", "tp"))
    if direct:
        expert_part = all_shares
    else:
        expert_part = lax.all_gather(lax.psum(expert_part, "tp"), "fsdp")
        expert_part = expert_part.reshape(all_trees, local_experts, 5 * RANK, model)
    adapter_grads = place(
        adapter_set, packed, expert_part,
        (
            query_in, query_out, key_in, key_second_factor, value_in, value_second_factor,
            out_in, out_out,
        ),
        (gate_in, gate_out, up_in, up_out, down_in, down_out),
    )
    return (output, input_grad, *adapter_grads)


def solution(mesh):
    in_specs = (
        P(("fsdp", "ctx", "tp"), None),
        P(("fsdp", "ctx", "tp"), None),
        P(("fsdp", "ctx", "tp"), None),
        P(),
        P(),
        P(),
        P(),
        P("fsdp", "tp"),
        P("fsdp", "tp"),
        P("fsdp", "tp"),
        P("tp", "fsdp"),
        P(),
        P("ctx", "fsdp", None),
        P("ctx", "fsdp", None),
        P("ctx", "fsdp", None),
        P(),
        P(),
        P(),
        P(),
        P(),
        P(),
        P(),
        P(),
        P("ctx", None, None),
        P("ctx", None, None),
        P("ctx", None, None),
        P("ctx", None, None),
        P("ctx", None, None),
        P("ctx", None, None),
    )
    out_specs = (
        P(("fsdp", "ctx", "tp"), None),
        P(("fsdp", "ctx", "tp"), None),
        P(),
        P(),
        P(),
        P(),
        P(),
        P(),
        P(),
        P(),
        P("ctx", None, None),
        P("ctx", None, None),
        P("ctx", None, None),
        P("ctx", None, None),
        P("ctx", None, None),
        P("ctx", None, None),
    )
    return jax.shard_map(
        per_device, mesh=mesh, in_specs=in_specs, out_specs=out_specs, check_vma=False
    )
```

```python
import functools

import jax
import jax.numpy as jnp
import numpy as np
from jax import lax
from jax.experimental import pallas as pl
from jax.experimental.pallas import tpu as pltpu
from jax.sharding import PartitionSpec as P

HEAD = 64
TOP = 8
RANK = 16
SEG = 128
SEGS_DEV = 8
TREE_SEGS = 32
SPAN = TREE_SEGS // SEGS_DEV
LANES = 128

RESIDUAL_SCALE = 0.22
SCORE_SCALE = 0.015625
EPSILON = 1e-06
ROPE_BASE = 10000.0
MASKED = -1e30

F32 = jnp.float32
BF16 = jnp.bfloat16

CODE = HEAD
LSE = CODE + TREE_SEGS + 1
ONES = HEAD

VMEM_LIMIT = 56 * 1024 * 1024


def dot(a, b):
    return lax.dot_general(a, b, (((1,), (0,)), ((), ())), preferred_element_type=F32)


def dot_nt(a, b):
    return lax.dot_general(a, b, (((1,), (1,)), ((), ())), preferred_element_type=F32)


def dot_tn(a, b):
    return lax.dot_general(a, b, (((0,), (0,)), ((), ())), preferred_element_type=F32)


def iota(shape, dim):
    return lax.broadcasted_iota(jnp.int32, shape, dim)


def rms_scale(values, gain_row):
    return (
        values * lax.rsqrt(jnp.mean(values * values, axis=-1, keepdims=True) + EPSILON) * gain_row
    )


def rms_back(values, gain_row, grad):
    inv = lax.rsqrt(jnp.mean(values * values, axis=-1, keepdims=True) + EPSILON)
    scaled = grad * gain_row
    inner = jnp.mean(scaled * values, axis=-1, keepdims=True)
    return inv * scaled - values * (inv * inv * inv * inner)


def swap_halves(values):
    width = values.shape[-1]
    lane = iota(values.shape, 1) % HEAD
    ahead = pltpu.roll(values, width - HEAD // 2, 1)
    behind = pltpu.roll(values, HEAD // 2, 1)
    return jnp.where(lane < HEAD // 2, -ahead, behind)


def place_table(rows, source, target):
    r, c = iota((rows, LANES), 0), iota((rows, LANES), 1)
    return ((r - source == c - target) & (c >= target) & (c < target + HEAD)).astype(BF16)


def transfer_plan(local, tp_count):
    if local == 8 and tp_count % 2 == 0:
        return 3, 2, 2, 1
    return 0, local, 0, 0


BEGIN = {'start': (0, 1), 'proj': (2,), 'own': (3,), 'k1': (4,), 0: (0,), 2: (1,), 3: (2,)}
RELAY = {'k0': (0, 1), 'k3': (2,), 2: (0,), 4: (1,)}


def remote(src, dst, send, recv, where):
    return pltpu.make_async_remote_copy(
        src_ref=src,
        dst_ref=dst,
        send_sem=send,
        recv_sem=recv,
        device_id=where,
        device_id_type=pl.DeviceIdType.MESH,
    )


def far_moves(near, far, sems, pass_sems, shared, direct, first, land, other, tp):
    mate = {"tp": tp + 1 - 2 * lax.rem(tp, 2)}
    side = lax.rem(tp, 2)

    def piece(ref, rows, which):
        return ref.at[pl.ds(pl.multiple_of(which * rows, rows), rows)]

    def cross(n):
        moves = []
        for a, (source, target) in enumerate(zip(near, far)):
            src, dst = source.at[first + n], target.at[land + n]
            if n < shared:
                rows = src.shape[0] // 2
                src, dst = piece(src, rows, side), piece(dst, rows, side)
            moves.append(remote(src, dst, sems.at[0, n, a], sems.at[1, n, a], other))
        return moves

    def hand_on(n):
        moves = []
        for a, target in enumerate(far):
            dst = target.at[land + n]
            rows = dst.shape[0] // 2
            dst = piece(dst, rows, side)
            moves.append(remote(dst, dst, pass_sems.at[0, n, a], pass_sems.at[1, n, a], mate))
        return moves

    return cross, hand_on


class Line:
    def __init__(self, buffer, sems, me, count):
        self.buffer, self.sems, self.me, self.count = buffer, sems, me, count
        self.turns = 2 * count - 1

    def move(self, way, block):
        where = ring(self.me, 1 if way == 0 else -1, self.count)
        return remote(
            self.buffer.at[block], self.buffer.at[block],
            self.sems.at[way, 0, block], self.sems.at[way, 1, block], {"tp": where},
        )

    def goes(self, way):
        return self.me < self.count - 1 if way == 0 else self.me > 0

    def send(self, way, block):
        @pl.when(self.goes(way))
        def _():
            self.move(way, block).start()

    def start(self):
        self.send(0, self.me)
        self.send(1, self.me)

    def block(self, turn):
        step = (turn + 1) // 2
        block = jnp.where(lax.rem(turn, 2) == 1, self.me - step, self.me + step)
        valid = (block >= 0) & (block < self.count)
        return jnp.clip(block, 0, self.count - 1), valid

    def last(self):
        return jnp.maximum(2 * self.me - 1, 2 * (self.count - 1 - self.me))

    def arrive(self, turn, block):
        for way, odd in ((0, 1), (1, 0)):

            @pl.when((turn > 0) & (lax.rem(turn, 2) == odd))
            def _(way=way):
                self.move(way, block).wait_recv()
                self.send(way, block)

    def end(self):
        for block in range(self.count):
            for way, owned in ((0, block <= self.me), (1, block >= self.me)):

                @pl.when(owned & self.goes(way))
                def _(way=way):
                    self.move(way, block).wait_send()


def ring(me, step, count):
    return lax.rem(me + (step + count), count)


def aug_keys(kv, pair, pairs, first_seg, k_aug, v_aug, start):
    rows, width = kv.shape
    lane = iota((rows, LANES), 1)
    seg = first_seg + iota((rows, LANES), 0) // SEG
    key_code = ((lane - CODE == seg) | ((lane >= LSE) & (lane < LSE + 3))).astype(F32)
    one_code = ((lane == ONES) | (lane == ONES + 1)).astype(F32)
    span = pl.ds(start, rows)
    k_aug[pair, span, :] = (dot(kv, place_table(width, pair * HEAD, 0)) + key_code).astype(BF16)
    v_aug[pair, span, :] = (
        dot(kv, place_table(width, (pairs + pair) * HEAD, 0)) + one_code
    ).astype(BF16)


def forward_kernel(
    parents, adapter_set, tokens, gain_one, gain_two, freqs, w_query, w_key, w_value, w_output,
    query_in, query_out, key_in, key_out, value_in, value_out, out_in, out_out,
    w_gate, w_up, w_down, grads, routes,
    att_out, q_out, kv_out, lora_out, middle_out, low_out, weights, normed_all,
    first, second, o_first, o_second, cos, sin, w_rows, att_rows,
    gate_far, up_far, down_far, grads_all, routes_all, rows_all,
    q_aug, k_aug, v_aug, top, acc, rows_own, code_table, depth_table,
    shard_sem, normed_sem, kv_sem, part_sem, w_rows_sem, far_sem, pass_far_sem, grads_sem, routes_sem, rows_sem,
    pass_sem, local_sem,
    *, tp_count, ctx_count, shared, straight,
):
    tp, ctx, fsdp = (lax.axis_index(name) for name in ("tp", "ctx", "fsdp"))
    rank = lax.rem(ctx, SPAN)
    block, model = tokens.shape
    heads = q_aug.shape[0]
    pairs = k_aug.shape[0]
    group = heads // pairs
    tall = group * block
    half = model // 2
    q_cols = heads * HEAD
    kv_cols = pairs * HEAD
    turn = cos.shape[1]
    chips = ctx_count // 2
    partner = ctx + 1 - 2 * lax.rem(ctx, 2)
    other = {"fsdp": 1 - fsdp}

    barrier = pltpu.get_barrier_semaphore()
    pl.semaphore_signal(barrier, 1, device_id=other, device_id_type=pl.DeviceIdType.MESH)
    for k in range(1, tp_count):
        pl.semaphore_signal(
            barrier, 1, device_id={"tp": ring(tp, k, tp_count)},
            device_id_type=pl.DeviceIdType.MESH,
        )
    for k in range(1, ctx_count):
        pl.semaphore_signal(
            barrier, 1, device_id={"ctx": ring(ctx, k, ctx_count)},
            device_id_type=pl.DeviceIdType.MESH,
        )
    pl.semaphore_wait(barrier, tp_count + ctx_count - 1)

    corners = (
        (w_query, 0, 0),
        (w_key, 0, q_cols),
        (w_value, 0, q_cols + kv_cols),
        (w_output, half, 0),
    )
    shard_copies = []
    for n, (source, row, column) in enumerate(corners):
        spot = weights.at[fsdp, pl.ds(row, source.shape[0]), pl.ds(column, source.shape[1])]
        shard_copies.append(remote(source, spot, shard_sem.at[0, n], shard_sem.at[1, n], other))
    for copy in shard_copies:
        copy.start()

    inputs = tokens[...].astype(F32)
    normed = rms_scale(inputs, gain_one[...].astype(F32).reshape(1, model)).astype(BF16)
    normed_all[tp] = normed

    line = Line(normed_all, normed_sem, tp, tp_count)
    line.start()

    def side_copies(k):
        where = {"ctx": ring(ctx, k, ctx_count)}
        return (
            remote(grads, grads_all.at[ctx], grads_sem.at[0, k], grads_sem.at[1, k], where),
            remote(routes, routes_all.at[ctx], routes_sem.at[0, k], routes_sem.at[1, k], where),
        )

    own_copies = (
        pltpu.make_async_copy(grads, grads_all.at[ctx], local_sem.at[0]),
        pltpu.make_async_copy(routes, routes_all.at[ctx], local_sem.at[1]),
    )
    for copy in own_copies:
        copy.start()
    for k in range(1, ctx_count):
        for copy in side_copies(k):
            copy.start()

    for source, row, column in corners:
        weights[fsdp, pl.ds(row, source.shape[0]), pl.ds(column, source.shape[1])] = source[...]

    tree = (fsdp * ctx_count + ctx) // SPAN
    spot_row, spot_lane = iota((LANES, LANES), 0), iota((LANES, LANES), 1)
    linked = (spot_row == spot_lane) & (spot_row < TREE_SEGS)
    for n in range(TREE_SEGS):
        linked |= (spot_row == n) & (spot_lane == parents[tree * TREE_SEGS + n])
    reach = linked.astype(F32)
    for _ in range((TREE_SEGS - 1).bit_length()):
        reach = jnp.minimum(dot(reach.astype(BF16), reach.astype(BF16)), 1.0)
    depth_table[...] = jnp.broadcast_to(
        jnp.sum(reach, axis=1, keepdims=True) - 1.0, (LANES, LANES)
    ).astype(BF16)
    coded = (spot_lane >= CODE) & (spot_lane < CODE + TREE_SEGS)
    code_table[...] = jnp.where(
        coded & (pltpu.roll(reach, CODE, 1) < 0.5), MASKED, 0.0
    ).astype(BF16)

    chosen = adapter_set[tree]

    def pick(n):
        inside = (spot_lane >= n * RANK) & (spot_lane < (n + 1) * RANK)
        return (inside & (spot_row == spot_lane - n * RANK + chosen * RANK)).astype(BF16)

    first[...] = (
        dot(query_in[...], pick(0)) + dot(key_in[...], pick(1)) + dot(value_in[...], pick(2))
    ).astype(BF16)
    for n, (source, column, width) in enumerate(
        ((query_out, 0, q_cols), (key_out, q_cols, kv_cols), (value_out, q_cols + kv_cols, kv_cols))
    ):
        lanes = pl.ds(pl.multiple_of(tp * width, width), width)
        second[:, column : column + width] = dot_tn(pick(n), source[:, lanes]).astype(BF16)
    o_first[...] = dot(out_in[...], pick(0)).astype(BF16)
    o_second[...] = dot_tn(pick(0), out_out[...]).astype(BF16)

    for copy in shard_copies:
        copy.wait()
    cross, hand_on = far_moves(
        (w_gate, w_up, w_down), (gate_far, up_far, down_far), far_sem, pass_far_sem,
        shared, straight, 0, 0, other, tp,
    )

    def point(name):
        if not shared:
            if name == "start":
                for n in range(straight):
                    for copy in cross(n):
                        copy.start()
            return
        for n in RELAY.get(name, ()):
            for copy in cross(n):
                copy.wait_recv()
            for copy in hand_on(n):
                copy.start()
        for n in BEGIN.get(name, ()):
            for copy in cross(n):
                copy.start()

    point("start")

    def kv_copy(distance, part):
        return remote(
            kv_out.at[0, part], kv_out.at[distance, part],
            kv_sem.at[0, distance - 1], kv_sem.at[1, distance - 1], {"ctx": ring(ctx, distance, ctx_count)},
        )

    def project(part):
        span = pl.ds(pl.multiple_of(part * block, block), block)
        rows = normed_all[part]
        seg = rank * SEGS_DEV + (part * block + iota((block, LANES), 0)) // SEG
        at_seg = (seg == iota((block, LANES), 1)).astype(BF16)
        offset = lax.rem(iota((block, LANES), 0), SEG).astype(F32)
        angles = (dot(at_seg, depth_table[...]) * SEG + offset) * freqs[...]
        cos[span, :] = jnp.cos(angles)
        sin[span, :] = jnp.sin(angles)
        codes = dot(at_seg, code_table[...])
        lora = dot(rows, first[...]).astype(BF16)
        lora_out[span, :] = lora
        pre = (
            dot(rows[:, :half], weights[0, pl.ds(0, half), :])
            + dot(rows[:, half:], weights[1, pl.ds(0, half), :])
            + dot(lora, second[...])
        )
        turned = []
        for start in range(0, pre.shape[1] // 4 * 3, turn):
            piece = pre[:, start : start + turn]
            turned.append(piece * cos[span, :] + swap_halves(piece) * sin[span, :])
        queries = (
            jnp.concatenate(turned[: q_cols // turn], axis=1) * SCORE_SCALE
        ).astype(BF16)
        for head in range(heads):
            q_aug[head, span, :] = (
                dot(queries, place_table(q_cols, head * HEAD, 0)) + codes
            ).astype(BF16)
        keys = jnp.concatenate(turned[q_cols // turn :], axis=1)
        kv = jnp.concatenate([keys, pre[:, q_cols + keys.shape[1] :]], axis=1).astype(BF16)
        kv_out[0, part] = kv
        for distance in range(1, SPAN):

            @pl.when(rank + distance < SPAN)
            def _(distance=distance):
                kv_copy(distance, part).start()

        for pair in range(pairs):
            aug_keys(
                kv, pair, pairs, rank * SEGS_DEV + part * (block // SEG), k_aug, v_aug,
                pl.multiple_of(part * block, block),
            )

    @pl.loop(0, line.turns)
    def _(turn):
        part, valid = line.block(turn)

        @pl.when(valid)
        def _():
            line.arrive(turn, part)
            project(part)

    w_line = Line(w_rows, w_rows_sem, tp, tp_count)
    for side in range(2):
        w_rows[tp, side] = weights[side, pl.ds(half, q_cols), :]
    w_line.start()
    point("proj")

    def advance(step):
        @pl.loop(2 * step - 1, 2 * step + 1)
        def _(turn):
            shard, valid = w_line.block(turn)

            @pl.when(valid)
            def _():
                w_line.arrive(turn, shard)

    def tile(part, pair, start, size, causal):
        index = part * pairs + pair
        rows = pl.ds(pl.multiple_of(part * block, block), block)
        queries = q_aug[pl.ds(pair * group, group), rows, :].reshape(tall, LANES)
        span = pl.ds(start, size)
        scores = dot_nt(queries, k_aug[pair, span, :])
        if causal:
            q_row = iota(scores.shape, 0) % block
            scores = jnp.where(iota(scores.shape, 1) <= q_row, scores, MASKED)
            now = jnp.broadcast_to(jnp.max(scores, axis=1, keepdims=True), (tall, LANES))
            probs = jnp.exp(scores - now[:, :1]).astype(BF16)
            acc[index] = dot(probs, v_aug[pair, span, :])
        else:
            before = top[index]
            now = jnp.maximum(before, jnp.max(scores, axis=1, keepdims=True))
            probs = jnp.exp(scores - now[:, :1]).astype(BF16)
            acc[index] = acc[index] * jnp.exp(before - now) + dot(probs, v_aug[pair, span, :])
        top[index] = now

    @pl.loop(0, tp_count * pairs)
    def _(index):
        part, pair = index // pairs, lax.rem(index, pairs)
        tile(part, pair, pl.multiple_of(part * block, block), block, True)

        @pl.loop(0, part)
        def _(j):
            tile(part, pair, pl.multiple_of(j * block, block), block, False)

    advance(1)
    point("own")
    group_rows = tp_count * block
    for distance in range(1, SPAN):

        @pl.when(distance <= rank)
        def _(distance=distance):
            remote(
                kv_out.at[0], kv_out.at[distance], kv_sem.at[0, distance - 1],
                kv_sem.at[1, distance - 1], {"ctx": ring(ctx, distance, ctx_count)},
            ).wait_recv()

            @pl.loop(0, tp_count)
            def _(part):
                kv = kv_out[distance, part]
                for pair in range(pairs):
                    aug_keys(
                        kv, pair, pairs,
                        (rank - distance) * SEGS_DEV + part * (block // SEG), k_aug, v_aug,
                        pl.multiple_of(distance * group_rows + part * block, block),
                    )

        @pl.when(distance > rank)
        def _(distance=distance):
            kv_out[distance] = jnp.zeros(kv_out.shape[1:], BF16)

    def part_copy(k):
        part = ring(tp, k + 1, tp_count)
        rows = pl.ds(pl.multiple_of(part * block, block), block)
        return remote(
            att_out.at[rows], att_rows.at[tp], part_sem.at[0, k], part_sem.at[1, k], {"tp": part}
        )

    @pl.loop(0, tp_count)
    def _(k):
        part = ring(tp, k + 1, tp_count)
        rows = pl.ds(pl.multiple_of(part * block, block), block)
        for pair in range(pairs):
            index = part * pairs + pair

            @pl.loop(1, rank + 1)
            def _(distance, pair=pair):
                tile(
                    part, pair, pl.multiple_of(distance * group_rows, group_rows), group_rows, False
                )

            summed = acc[index]
            total = summed[:, ONES : ONES + 1]
            result = (summed / total).astype(BF16)
            for member in range(group):
                head = pair * group + member
                att_out[rows, pl.ds(head * HEAD, HEAD)] = result[
                    member * block : (member + 1) * block, :HEAD
                ]
            minus = -(top[index] + jnp.log(total))
            high = minus.astype(BF16).astype(F32)
            middle = (minus - high).astype(BF16).astype(F32)
            lane = iota(minus.shape, 1)
            queries = q_aug[pl.ds(pair * group, group), rows, :].reshape(tall, LANES)
            coded = jnp.where(
                lane == LSE,
                high,
                jnp.where(
                    lane == LSE + 1,
                    middle,
                    jnp.where(lane == LSE + 2, minus - high - middle, queries.astype(F32)),
                ),
            )
            q_out[pl.ds(pair * group, group), rows, :] = coded.astype(BF16).reshape(
                group, block, LANES
            )

        @pl.when(k < tp_count - 1)
        def _():
            part_copy(k).start()

        @pl.when(k == tp_count - 1)
        def _():
            att_rows[tp] = att_out[rows, :]

        for step in range(2, tp_count):

            @pl.when(k == step - 2)
            def _(step=step):
                advance(step)

        for n in range(tp_count):
            if f"k{n}" in BEGIN or f"k{n}" in RELAY:

                @pl.when(k == n)
                def _(n=n):
                    point(f"k{n}")

    for k in range(tp_count - 1):
        part_copy(k).wait_recv()
    point("sum")
    low = sum(
        dot(att_rows[t], o_first[pl.ds(t * q_cols, q_cols), :]) for t in range(tp_count)
    ).astype(BF16)
    low_out[...] = low
    branch = dot(low, o_second[...]) + jnp.concatenate(
        [sum(dot(att_rows[t], w_rows[t, side]) for t in range(tp_count)) for side in range(2)],
        axis=1,
    )
    middle = inputs + RESIDUAL_SCALE * branch
    middle_out[...] = middle
    rows_own[...] = rms_scale(middle, gain_two[...].astype(F32).reshape(1, model)).astype(BF16)

    own_rows = pltpu.make_async_copy(rows_own, rows_all.at[ctx], local_sem.at[2])
    own_rows.start()
    to_partner = remote(
        rows_own, rows_all.at[ctx], rows_sem.at[0, 0], rows_sem.at[1, 0], {"ctx": partner}
    )
    to_partner.start()

    def rows_copy(k):
        return remote(
            rows_own, rows_all.at[ctx], rows_sem.at[0, k], rows_sem.at[1, k],
            {"ctx": ring(ctx, 2 * k, ctx_count)},
        )

    def pass_copy(k):
        source = ring(ctx, -2 * k, ctx_count)
        return remote(
            rows_all.at[source], rows_all.at[source], pass_sem.at[0, k], pass_sem.at[1, k],
            {"ctx": partner},
        )

    for k in range(1, chips):
        rows_copy(k).start()
    for k in range(1, chips):
        rows_copy(k).wait_recv()
        pass_copy(k).start()

    line.end()
    w_line.end()
    for k in range(tp_count - 1):
        part_copy(k).wait_send()
    for distance in range(1, SPAN):

        @pl.when(rank + distance < SPAN)
        def _(distance=distance):
            remote(
                kv_out.at[0], kv_out.at[distance], kv_sem.at[0, distance - 1],
                kv_sem.at[1, distance - 1], {"ctx": ring(ctx, distance, ctx_count)},
            ).wait_send()

    for k in range(1, ctx_count):
        for copy in side_copies(k):
            copy.wait()
    for copy in own_copies:
        copy.wait()
    own_rows.wait()
    to_partner.wait()
    for k in range(1, chips):
        rows_copy(k).wait_send()
        pass_copy(k).wait()
    for n in range(shared + straight):
        for copy in cross(n):
            copy.wait_send()
            if n >= shared:
                copy.wait_recv()
    for n in range(shared):
        for copy in hand_on(n):
            copy.wait()


def forward(
    parents, adapter_set, tokens, gains, attention, adapters, weights, grads, routes,
    tp_count, ctx_count,
):
    block, model = tokens.shape
    rows = tp_count * block
    q_cols, kv_cols = attention[0].shape[1], attention[1].shape[1]
    heads, pairs = q_cols // HEAD, kv_cols // HEAD
    cols = q_cols + 2 * kv_cols
    tall = heads // pairs * block
    chips = ctx_count // 2
    shared, straight, _, _ = transfer_plan(weights[0].shape[0], tp_count)
    vmem = pl.BlockSpec(memory_space=pltpu.VMEM)
    smem = pl.BlockSpec(memory_space=pltpu.SMEM)
    hbm = pl.BlockSpec(memory_space=pl.ANY)
    dma = pltpu.SemaphoreType.DMA
    half_head = HEAD // 2
    freqs = np.float32(ROPE_BASE) ** (-(np.arange(half_head, dtype=np.float32) * 2) / HEAD)
    freqs = jnp.asarray(np.tile(freqs.astype(np.float32), LANES // half_head)[None])
    return pl.pallas_call(
        functools.partial(
            forward_kernel, tp_count=tp_count, ctx_count=ctx_count, shared=shared, straight=straight
        ),
        in_specs=[smem] * 2 + [vmem] * 16 + [hbm] * 5,
        out_specs=[vmem] * 16 + [hbm] * 6,
        out_shape=[
            jax.ShapeDtypeStruct((rows, q_cols), BF16),
            jax.ShapeDtypeStruct((heads, rows, LANES), BF16),
            jax.ShapeDtypeStruct((SPAN, tp_count, block, 2 * kv_cols), BF16),
            jax.ShapeDtypeStruct((rows, LANES), BF16),
            jax.ShapeDtypeStruct((block, model), F32),
            jax.ShapeDtypeStruct((block, LANES), BF16),
            jax.ShapeDtypeStruct((2, model // 2 + q_cols, model // 2), BF16),
            jax.ShapeDtypeStruct((tp_count, block, model), BF16),
            jax.ShapeDtypeStruct((model, LANES), BF16),
            jax.ShapeDtypeStruct((LANES, cols), BF16),
            jax.ShapeDtypeStruct((tp_count * q_cols, LANES), BF16),
            jax.ShapeDtypeStruct((LANES, model), BF16),
            jax.ShapeDtypeStruct((rows, LANES), F32),
            jax.ShapeDtypeStruct((rows, LANES), F32),
            jax.ShapeDtypeStruct((tp_count, 2, q_cols, model // 2), BF16),
            jax.ShapeDtypeStruct((tp_count, block, q_cols), BF16),
            *[jax.ShapeDtypeStruct((shared + straight,) + w.shape[1:], BF16) for w in weights],
            jax.ShapeDtypeStruct((ctx_count,) + grads.shape, BF16),
            jax.ShapeDtypeStruct((ctx_count,) + routes.shape, jnp.int32),
            jax.ShapeDtypeStruct((ctx_count, block, model), BF16),
        ],
        scratch_shapes=[
            pltpu.VMEM((heads, rows, LANES), BF16),
            pltpu.VMEM((pairs, SPAN * rows, LANES), BF16),
            pltpu.VMEM((pairs, SPAN * rows, LANES), BF16),
            pltpu.VMEM((tp_count * pairs, tall, LANES), F32),
            pltpu.VMEM((tp_count * pairs, tall, LANES), F32),
            pltpu.VMEM((block, model), BF16),
            pltpu.VMEM((LANES, LANES), BF16),
            pltpu.VMEM((LANES, LANES), BF16),
            dma((2, 4)),
            dma((2, 2, tp_count)),
            dma((2, SPAN - 1)),
            dma((2, tp_count - 1)),
            dma((2, 2, tp_count)),
            dma((2, shared + straight, 3)),
            dma((2, max(shared, 1), 3)),
            dma((2, ctx_count)),
            dma((2, ctx_count)),
            dma((2, chips)),
            dma((2, chips)),
            dma((3,)),
        ],
        compiler_params=pltpu.CompilerParams(
            vmem_limit_bytes=VMEM_LIMIT, collective_id=0, has_side_effects=True
        ),
        cost_estimate=pl.CostEstimate(
            flops=16 * SPAN * rows * rows * heads * LANES,
            bytes_accessed=32 * 1024 * 1024,
            transcendentals=0,
        ),
        name="forward",
    )(
        parents, adapter_set, tokens, *gains, freqs, *attention, *adapters, *weights, grads, routes,
    )


def joined(dk, dv, span):
    pairs = dk.shape[0]
    return jnp.concatenate(
        [dk[pair, span, :HEAD] for pair in range(pairs)]
        + [dv[pair, span, :HEAD] for pair in range(pairs)],
        axis=1,
    )


def backward_kernel(
    tokens, upstream_ref, routes, gain_one, gain_two, w_router, middle_ref, low_ref, weights,
    normed_all, lora, att, q_ref, kv_ref, first, second, o_first, o_second, cos, sin, w_rows, att_rows, back, mixed, shares, help_q,
    output, input_grad, packed_out, shares_out,
    k_aug, v_aug, up_aug, dk, dv, dq, help_up, help_dq, help_sum, do_out, do_all, far_out, far_in, own_kv, row_grads, low_grads, parts, parts_in,
    second_acc, first_acc, packed, ctx_in, tp_in, middle_grad, router,
    back_near, back_mine, back_pair, back_far, mixed_near, mixed_mine, mixed_pair, mixed_far,
    near_sem, mine_sem, far_sem, branch_sem, kv_sem, part_sem,
    ctx_sem, tp_sem, x_sem, ctx_all_sem, share_sem, swap_sem, own_sem,
    up_sem, sum_sem,
    *, tp_count, ctx_count, experts, direct,
):
    tp, ctx, fsdp = (lax.axis_index(name) for name in ("tp", "ctx", "fsdp"))
    rank = lax.rem(ctx, SPAN)
    block, model = tokens.shape
    heads, rows_all, _ = q_ref.shape
    pairs = k_aug.shape[0]
    group = heads // pairs
    tall = group * block
    half = weights.shape[2]
    q_cols = heads * HEAD
    kv_cols = pairs * HEAD
    turn = cos.shape[1]
    partner = ctx + 1 - 2 * lax.rem(ctx, 2)
    cross = ring(ctx, 2, ctx_count)
    cross_partner = ring(partner, 2, ctx_count)
    other = {"fsdp": 1 - fsdp}

    barrier = pltpu.get_barrier_semaphore()
    pl.semaphore_signal(barrier, 1, device_id=other, device_id_type=pl.DeviceIdType.MESH)
    for k in range(1, tp_count):
        pl.semaphore_signal(
            barrier, 1, device_id={"tp": ring(tp, k, tp_count)},
            device_id_type=pl.DeviceIdType.MESH,
        )
    for k in range(1, ctx_count):
        pl.semaphore_signal(
            barrier, 1, device_id={"ctx": ring(ctx, k, ctx_count)},
            device_id_type=pl.DeviceIdType.MESH,
        )
    pl.semaphore_wait(barrier, tp_count + ctx_count - 1)

    sums = (
        (back, back_near, back_mine, back_pair, back_far),
        (mixed, mixed_near, mixed_mine, mixed_pair, mixed_far),
    )

    def near_copy(n, slot):
        source, near = sums[n][:2]
        return remote(
            source.at[(partner, cross_partner)[slot]], near.at[slot],
            near_sem.at[0, 2 * n + slot], near_sem.at[1, 2 * n + slot], {"ctx": partner},
        )

    def mine_copy(n, slot):
        return pltpu.make_async_copy(
            sums[n][0].at[(ctx, cross)[slot]], sums[n][2].at[slot], mine_sem.at[2 * n + slot]
        )

    def pair_copy(n):
        return remote(sums[n][3], sums[n][4], far_sem.at[0, n], far_sem.at[1, n], {"ctx": cross})

    def start_sum(n):
        for slot in (1, 0):
            near_copy(n, slot).start()
            mine_copy(n, slot).start()

    def pass_sum(n):
        near_copy(n, 1).wait_recv()
        mine_copy(n, 1).wait()
        _, near, mine, pair, _ = sums[n]
        pair[...] = (near[1].astype(F32) + mine[1].astype(F32)).astype(BF16)
        pair_copy(n).start()

    def end_sum(n):
        near_copy(n, 0).wait_recv()
        mine_copy(n, 0).wait()
        pair_copy(n).wait_recv()
        _, near, mine, _, far = sums[n]
        return near[0].astype(F32) + mine[0].astype(F32) + far[...].astype(F32)

    if direct:
        share = shares.shape[2]
        own_lanes = pl.ds(pl.multiple_of(tp * share, share), share)

        def share_copy(k):
            return remote(
                shares, shares_out.at[fsdp, :, :, own_lanes],
                share_sem.at[0, k - 1], share_sem.at[1, k - 1], {"tp": ring(tp, k, tp_count)},
            )

        share_own = pltpu.make_async_copy(shares, shares_out.at[fsdp, :, :, own_lanes], own_sem.at[0])
        swap = remote(
            shares_out.at[fsdp], shares_out.at[fsdp], swap_sem.at[0], swap_sem.at[1], other
        )

        near_copy(0, 1).start()
        for slot in (1, 0):
            mine_copy(0, slot).start()
        pass_sum(0)
        near_copy(0, 0).start()
        start_sum(1)
        share_own.start()

    last_rank, first_rank = rank == SPAN - 1, rank == 0
    mirror = {"ctx": ctx + SPAN - 1 - 2 * rank}
    far_count = jnp.where(last_rank, rank - 1, rank) if direct else rank

    @pl.loop(0, far_count + 1)
    def _(distance):
        @pl.loop(0, tp_count)
        def _(part):
            kv = kv_ref[distance, part]
            for pair in range(pairs):
                aug_keys(
                    kv, pair, pairs, (rank - distance) * SEGS_DEV + part * (block // SEG),
                    k_aug, v_aug, pl.multiple_of(distance * rows_all + part * block, block),
                )

    dk[...] = jnp.zeros(dk.shape, F32)
    dv[...] = jnp.zeros(dv.shape, F32)
    dq[...] = jnp.zeros(dq.shape, F32)
    second_acc[...] = jnp.zeros(second_acc.shape, F32)
    first_acc[...] = jnp.zeros(first_acc.shape, F32)
    packed[...] = jnp.zeros(packed.shape, F32)

    middle = middle_ref[...]
    scale_one = gain_one[...].astype(F32).reshape(1, model)
    scale_two = gain_two[...].astype(F32).reshape(1, model)
    normed_two = rms_scale(middle, scale_two).astype(BF16)
    router[...] = jnp.zeros(router.shape, BF16)
    router[pl.ds(0, experts), :] = w_router[...]
    logits = dot_nt(normed_two, router[...])
    number = iota((LANES, block), 0)
    hit = jnp.zeros((LANES, block), F32)
    for k in range(routes.shape[0]):
        hit += (routes[k : k + 1, :] == number).astype(F32)
    hit = hit.T
    kept = jnp.where(hit > 0.5, logits, MASKED)
    gates = jnp.exp(kept - jnp.max(kept, axis=1, keepdims=True)) * hit
    gates = gates / jnp.sum(gates, axis=1, keepdims=True)

    if direct:
        back_sum = end_sum(0)
    else:
        back_sum = back[...].astype(F32)
    table = back_sum[:, model:]
    slopes = table + pltpu.roll(table, LANES - experts, 1)
    logits_grad = gates * (slopes - jnp.sum(gates * slopes, axis=1, keepdims=True))
    high = logits_grad.astype(BF16)
    low = (logits_grad - high.astype(F32)).astype(BF16)
    normed_two_grad = back_sum[:, :model] + dot(high, router[...]) + dot(low, router[...])
    middle_grad[...] = upstream_ref[...].astype(F32) + rms_back(
        middle, scale_two, normed_two_grad
    )
    branch = (RESIDUAL_SCALE * middle_grad[...]).astype(BF16)
    low_grad = dot_nt(branch, o_second[...]).astype(BF16)

    def do_copy(k):
        where = ring(tp, k, tp_count)
        return remote(
            do_out.at[where], do_all.at[tp], branch_sem.at[0, k - 1], branch_sem.at[1, k - 1],
            {"tp": where},
        )

    for t in range(tp_count):
        do_out[t] = (
            dot_nt(branch[:, :half], w_rows[t, 0])
            + dot_nt(branch[:, half:], w_rows[t, 1])
            + dot_nt(low_grad, o_first[pl.ds(t * q_cols, q_cols), :])
        ).astype(BF16)
    for k in range(1, tp_count):
        do_copy(k).start()
    do_all[tp] = do_out[tp]
    for t in range(tp_count):
        packed[pl.ds(3 * RANK, RANK), t * q_cols : (t + 1) * q_cols] = dot_tn(
            low_grad, att_rows[t]
        )[:RANK]
    packed[pl.ds(4 * RANK, RANK), :] = dot_tn(low_ref[...], branch)[:RANK]
    if direct:
        pass_sum(1)

    wide = heads * LANES
    r, c = iota((q_cols, wide), 0), iota((q_cols, wide), 1)
    same = r // HEAD == c // LANES
    place = (same & (r % HEAD == c % LANES)).astype(BF16)
    spread = (same & (c % LANES >= ONES) & (c % LANES < ONES + 2)).astype(BF16)

    def tile(part, pair, start, size, causal, from_q=q_ref, from_up=up_aug, into=dq):
        index = part * pairs + pair
        rows = pl.ds(pl.multiple_of(part * block, block), block)
        queries = from_q[pl.ds(pair * group, group), rows, :].reshape(tall, LANES)
        upstream = from_up[pl.ds(pair * group, group), rows, :].reshape(tall, LANES)
        span = pl.ds(start, size)
        keys = k_aug[pair, span, :]
        probs = jnp.exp(dot_nt(keys, queries))
        if causal:
            q_row = iota(probs.shape, 1) % block
            probs = jnp.where(iota(probs.shape, 0) <= q_row, probs, 0.0)
        steep = (probs * dot_nt(v_aug[pair, span, :], upstream)).astype(BF16)
        dv[pair, span, :] += dot(probs.astype(BF16), upstream)
        dk[pair, span, :] += dot(steep, queries)
        into[pair if into is help_dq else index] += dot_tn(steep, keys)

    def far_copy(distance):
        return remote(
            far_out.at[distance - 1], far_in.at[distance - 1],
            kv_sem.at[0, distance - 1], kv_sem.at[1, distance - 1],
            {"ctx": ring(ctx, -distance, ctx_count)},
        )

    size = min(rows_all, 1024)

    def take_block(part):
        rows = pl.ds(pl.multiple_of(part * block, block), block)
        grads = do_all[part]
        mixed_heads = att[rows, :]
        product = grads.astype(F32) * mixed_heads.astype(F32)
        minus = jnp.zeros((block, wide), F32)
        for _ in range(3):
            piece = product.astype(BF16)
            minus -= dot(piece, spread)
            product -= piece.astype(F32)
        top = minus.astype(BF16).astype(F32)
        lane = iota(minus.shape, 1) % LANES
        coded = dot(grads, place) + jnp.where(
            lane == ONES, top, jnp.where(lane == ONES + 1, minus - top, 0.0)
        )
        for head in range(heads):
            up_aug[head, rows, :] = coded[:, head * LANES : (head + 1) * LANES].astype(BF16)

    def up_copy(part):
        rows = pl.ds(pl.multiple_of(part * block, block), block)
        return remote(
            up_aug.at[:, rows], help_up.at[:, rows], up_sem.at[0, part], up_sem.at[1, part], mirror
        )

    def sum_copy(part):
        spot = pl.ds(part * pairs, pairs)
        return remote(
            help_sum.at[spot], help_sum.at[spot], sum_sem.at[0, part], sum_sem.at[1, part], mirror
        )

    @pl.loop(0, tp_count)
    def _(turn):
        part = ring(tp, -turn, tp_count)

        @pl.when(turn > 0)
        def _():
            do_copy(turn).wait_recv()

        @pl.when(turn >= 0)
        def _():
            take_block(part)
            if direct:

                @pl.when(last_rank)
                def _():
                    up_copy(part).start()

            @pl.loop(0, far_count)
            def _(step):
                distance = far_count - step
                start = distance * rows_all

                @pl.loop(0, pairs * (rows_all // size))
                def _(n):
                    pair, piece = n // (rows_all // size), lax.rem(n, rows_all // size)
                    tile(part, pair, pl.multiple_of(start + piece * size, size), size, False)

                @pl.when(turn == tp_count - 1)
                def _():
                    @pl.loop(0, tp_count)
                    def _(spot):
                        span = pl.ds(pl.multiple_of(start + spot * block, block), block)
                        rows = pl.ds(pl.multiple_of(spot * block, block), block)
                        far_out[distance - 1, rows, :] = joined(dk, dv, span).astype(BF16)

                    far_copy(distance).start()

            if direct:

                @pl.when(turn == 1)
                def _():
                    for k in range(1, tp_count):
                        share_copy(k).start()

            @pl.loop(0, pairs)
            def _(pair):
                tile(part, pair, pl.multiple_of(part * block, block), block, True)

                @pl.loop(0, part)
                def _(j):
                    tile(part, pair, pl.multiple_of(j * block, block), block, False)

            if direct:

                @pl.when(first_rank)
                def _():
                    up_copy(part).wait_recv()
                    help_dq[...] = jnp.zeros(help_dq.shape, F32)

                    @pl.loop(0, pairs)
                    def _(pair):
                        tile(part, pair, 0, rows_all, False, help_q, help_up, help_dq)

                    spot = pl.ds(part * pairs, pairs)
                    help_sum[spot] = help_dq[...].astype(BF16)
                    sum_copy(part).start()

    if direct:

        @pl.when(last_rank)
        def _():
            @pl.loop(0, tp_count)
            def _(part):
                sum_copy(part).wait_recv()
                spot = pl.ds(part * pairs, pairs)
                dq[spot] += help_sum[spot].astype(F32)

    own_kv[...] = joined(dk, dv, pl.ds(0, rows_all))
    far_steps = far_out.shape[0] + 1
    for distance in range(1, far_steps):

        @pl.when(rank + distance < SPAN)
        def _(distance=distance):
            far_copy(distance).wait_recv()
            own_kv[...] += far_in[distance - 1].astype(F32)

    def part_copy(k):
        return remote(
            parts.at[k], parts_in.at[k], part_sem.at[0, k], part_sem.at[1, k],
            {"tp": ring(tp, k + 1, tp_count)},
        )

    @pl.loop(0, tp_count)
    def _(part):
        rows = pl.ds(pl.multiple_of(part * block, block), block)
        pieces = []
        for pair in range(pairs):
            held = dq[part * pairs + pair]
            turned = SCORE_SCALE * jnp.concatenate(
                [held[member * block : (member + 1) * block, :HEAD] for member in range(group)],
                axis=1,
            )
            pieces.append(turned * cos[rows, :] - swap_halves(turned) * sin[rows, :])
        keys = own_kv[rows, :kv_cols]
        pieces.append(keys * cos[rows, :] - swap_halves(keys) * sin[rows, :])
        pieces.append(own_kv[rows, kv_cols:])
        grads = jnp.concatenate(pieces, axis=1).astype(BF16)
        row_grads[rows, :] = grads
        low_part = dot_nt(grads, second[...]).astype(BF16)
        low_grads[rows, :] = low_part
        second_acc[...] += dot_tn(lora[rows, :], grads)
        first_acc[...] += dot_tn(low_part, normed_all[part])

    packed[pl.ds(0, 3 * RANK), :] = first_acc[pl.ds(0, 3 * RANK), :]
    lanes = pl.ds(pl.multiple_of(tp * q_cols, q_cols), q_cols)
    packed[pl.ds(5 * RANK, RANK), lanes] = second_acc[pl.ds(0, RANK), :q_cols]
    lanes = pl.ds(pl.multiple_of(tp * kv_cols, kv_cols), kv_cols)
    packed[pl.ds(6 * RANK, RANK), lanes] = second_acc[pl.ds(RANK, RANK), q_cols : q_cols + kv_cols]
    lanes = pl.ds(pl.multiple_of(model // 2 + tp * kv_cols, kv_cols), kv_cols)
    packed[pl.ds(6 * RANK, RANK), lanes] = second_acc[pl.ds(2 * RANK, RANK), q_cols + kv_cols :]

    def make_parts():
        @pl.loop(0, tp_count)
        def _(k):
            part = ring(tp, k + 1, tp_count)
            rows = pl.ds(pl.multiple_of(part * block, block), block)
            grads = row_grads[rows, :]
            for side in range(2):
                columns = slice(side * half, (side + 1) * half)
                parts[k, :, columns] = (
                    dot_nt(grads, weights[side, pl.ds(0, half), :])
                    + dot_nt(low_grads[rows, :], first[columns, :])
                ).astype(BF16)

    def send_parts():
        for k in range(tp_count - 1):
            part_copy(k).start()

    if direct:
        tall_rows = packed.shape[0] // ctx_count

        def ctx_rows(index):
            return pl.ds(pl.multiple_of(index * tall_rows, tall_rows), tall_rows)

        def ctx_copy(k):
            where = ring(ctx, k, ctx_count)
            return remote(
                packed.at[ctx_rows(where)], ctx_in.at[k - 1],
                ctx_sem.at[0, k - 1], ctx_sem.at[1, k - 1], {"ctx": where},
            )

        def tp_copy(k):
            return remote(
                tp_in.at[tp], tp_in.at[tp], tp_sem.at[0, k - 1], tp_sem.at[1, k - 1],
                {"tp": ring(tp, k, tp_count)},
            )

        x_copy = remote(
            packed_out.at[fsdp, ctx_rows(ctx)], packed_out.at[fsdp, ctx_rows(ctx)],
            x_sem.at[0], x_sem.at[1], other,
        )

        def ctx_all_copy(k):
            return remote(
                packed_out.at[:, ctx_rows(ctx)], packed_out.at[:, ctx_rows(ctx)],
                ctx_all_sem.at[0, k - 1], ctx_all_sem.at[1, k - 1],
                {"ctx": ring(ctx, k, ctx_count)},
            )

        for k in range(1, ctx_count):
            ctx_copy(k).start()
        make_parts()
        for k in range(1, ctx_count):
            ctx_copy(k).wait()
        tp_in[tp] = (packed[ctx_rows(ctx), :] + sum(ctx_in[k] for k in range(ctx_count - 1))).astype(
            BF16
        )
        for k in range(1, tp_count):
            tp_copy(k).start()
        send_parts()
        for k in range(1, tp_count):
            tp_copy(k).wait()
        packed_out[fsdp, ctx_rows(ctx), :] = sum(tp_in[k].astype(F32) for k in range(tp_count))
        x_copy.start()
        x_copy.wait()
        for k in range(1, ctx_count):
            ctx_all_copy(k).start()
        share_own.wait()
        for k in range(1, tp_count):
            share_copy(k).wait()
        swap.start()
    else:
        packed_out[0] = packed[...]
        make_parts()
        send_parts()

    summed = parts[tp_count - 1].astype(F32)
    for k in range(tp_count - 1):
        part_copy(k).wait_recv()
        summed += parts_in[k].astype(F32)
    inputs = tokens[...].astype(F32)
    input_grad[...] = (middle_grad[...] + rms_back(inputs, scale_one, summed)).astype(BF16)
    mixture = end_sum(1) if direct else mixed[...].astype(F32)
    output[...] = (middle_ref[...] + RESIDUAL_SCALE * mixture).astype(BF16)

    if direct:
        swap.wait()
        for k in range(1, ctx_count):
            ctx_all_copy(k).wait()
        for n in range(2):
            for slot in range(2):
                near_copy(n, slot).wait_send()
            pair_copy(n).wait_send()
    for k in range(1, tp_count):
        do_copy(k).wait_send()
    if direct:
        for part in range(tp_count):

            @pl.when(last_rank)
            def _(part=part):
                up_copy(part).wait_send()

            @pl.when(first_rank)
            def _(part=part):
                sum_copy(part).wait_send()

    for k in range(tp_count - 1):
        part_copy(k).wait_send()
    for distance in range(1, far_steps):

        @pl.when(distance <= far_count)
        def _(distance=distance):
            far_copy(distance).wait_send()


def backward(
    tokens, upstream, routes, gains, router, middle, low, weights, normed, lora, att, queries, kv,
    first, second, o_first, o_second, cos, sin, w_rows, att_rows, back, mixed, shares, help_q,
    tp_count, ctx_count, experts, direct,
):
    block, model = tokens.shape
    heads, rows, _ = queries.shape
    pairs = kv.shape[3] // (2 * HEAD)
    tall = heads // pairs * block
    cols = second.shape[1]
    kv_width = kv.shape[3]
    vmem = pl.BlockSpec(memory_space=pltpu.VMEM)
    hbm = pl.BlockSpec(memory_space=pl.ANY)
    dma = pltpu.SemaphoreType.DMA
    part = (block, model)
    packed = (8 * RANK, model)
    copies = 2 if direct else 1
    slim = (8, LANES)

    def buffers(width):
        shapes = [(2, block, width), (2, block, width), (block, width), (block, width)]
        return [pltpu.VMEM(shape if direct else slim, BF16) for shape in shapes]

    return pl.pallas_call(
        functools.partial(
            backward_kernel, tp_count=tp_count, ctx_count=ctx_count, experts=experts, direct=direct
        ),
        in_specs=[vmem] * 22 + [hbm if direct else vmem] * 2 + [hbm, vmem if direct else hbm],
        out_specs=[vmem] * 3 + [hbm],
        out_shape=[
            jax.ShapeDtypeStruct((block, model), BF16),
            jax.ShapeDtypeStruct((block, model), BF16),
            jax.ShapeDtypeStruct((copies,) + packed, F32),
            jax.ShapeDtypeStruct(
                (2,) + shares.shape[:2] + (tp_count * shares.shape[2],) if direct else slim, BF16
            ),
        ],
        scratch_shapes=[
            pltpu.VMEM((pairs, SPAN * rows, LANES), BF16),
            pltpu.VMEM((pairs, SPAN * rows, LANES), BF16),
            pltpu.VMEM((heads, rows, LANES), BF16),
            pltpu.VMEM((pairs, SPAN * rows, LANES), F32),
            pltpu.VMEM((pairs, SPAN * rows, LANES), F32),
            pltpu.VMEM((tp_count * pairs, tall, LANES), F32),
            pltpu.VMEM((heads, rows, LANES) if direct else slim, BF16),
            pltpu.VMEM((pairs, tall, LANES) if direct else slim, F32),
            pltpu.VMEM((tp_count * pairs, tall, LANES) if direct else slim, BF16),
            pltpu.VMEM((tp_count, block, heads * HEAD), BF16),
            pltpu.VMEM((tp_count, block, heads * HEAD), BF16),
            pltpu.VMEM((SPAN - 2 if direct else SPAN - 1, rows, kv_width), BF16),
            pltpu.VMEM((SPAN - 2 if direct else SPAN - 1, rows, kv_width), BF16),
            pltpu.VMEM((rows, kv_width), F32),
            pltpu.VMEM((rows, cols), BF16),
            pltpu.VMEM((rows, LANES), BF16),
            pltpu.VMEM((tp_count,) + part, BF16),
            pltpu.VMEM((tp_count - 1,) + part, BF16),
            pltpu.VMEM((LANES, cols), F32),
            pltpu.VMEM((LANES, model), F32),
            pltpu.VMEM(packed, F32),
            pltpu.VMEM((ctx_count - 1, packed[0] // ctx_count, model) if direct else slim, F32),
            pltpu.VMEM((tp_count, packed[0] // ctx_count, model) if direct else slim, BF16),
            pltpu.VMEM((block, model), F32),
            pltpu.VMEM((LANES, model), BF16),
            *buffers(model + LANES),
            *buffers(model),
            dma((2, 4)),
            dma((4,)),
            dma((2, 2)),
            dma((2, tp_count - 1)),
            dma((2, SPAN - 1)),
            dma((2, tp_count - 1)),
            dma((2, ctx_count - 1)),
            dma((2, tp_count - 1)),
            dma((2,)),
            dma((2, ctx_count - 1)),
            dma((2, tp_count - 1)),
            dma((2,)),
            dma((1,)),
            dma((2, tp_count)),
            dma((2, tp_count)),
        ],
        compiler_params=pltpu.CompilerParams(
            vmem_limit_bytes=60 * 1024 * 1024, collective_id=1, has_side_effects=True
        ),
        cost_estimate=pl.CostEstimate(
            flops=32 * SPAN * rows * rows * heads * LANES,
            bytes_accessed=32 * 1024 * 1024,
            transcendentals=0,
        ),
        name="backward",
    )(
        tokens, upstream, routes, *gains, router, middle, low, weights, normed, lora, att, queries,
        kv, first, second, o_first, o_second, cos, sin, w_rows, att_rows, back, mixed, shares, help_q,
    )


def place_kernel(sets, packed, part, *outs):
    query_in, query_out, key_in, key_out, value_in, value_out, out_in, out_out = outs[:8]
    gate_in, gate_out, up_in, up_out, down_in, down_out = outs[8:]
    kv_cols, hidden = key_out.shape[1], gate_out.shape[2]
    trees = part.shape[0]
    spots = jnp.concatenate(
        [
            (iota((RANK, LANES), 1) == iota((RANK, LANES), 0) + sets[tree] * RANK).astype(BF16)
            for tree in range(trees)
        ],
        axis=0,
    )
    spots_twice = jnp.concatenate([spots, spots], axis=0)

    def block(rows):
        return slice(rows * RANK, (rows + 1) * RANK)

    @pl.when(pl.program_id(0) == 0)
    def _():
        def gathered(rows, lanes, turned):
            pieces = jnp.concatenate(
                [packed[tree, block(rows), lanes] for tree in range(trees)], axis=0
            )
            high = pieces.astype(BF16)
            both = jnp.concatenate([high, (pieces - high.astype(F32)).astype(BF16)], axis=0)
            return dot_tn(both, spots_twice) if turned else dot_tn(spots_twice, both)

        whole = slice(None)
        query_in[...] = gathered(0, whole, True)
        key_in[...] = gathered(1, whole, True)
        value_in[...] = gathered(2, whole, True)
        out_in[...] = gathered(3, whole, True)
        out_out[...] = gathered(4, whole, False)
        query_out[...] = gathered(5, whole, False)
        key_out[...] = gathered(6, slice(0, kv_cols), False)
        value_out[...] = gathered(6, slice(kv_cols, 2 * kv_cols), False)

    whole, left, right = slice(None), slice(0, hidden), slice(hidden, 2 * hidden)
    for n in range(part.shape[1]):

        def pieces(rows, lanes, n=n):
            return jnp.concatenate(
                [part[tree, n, block(rows), lanes] for tree in range(trees)], axis=0
            )

        gate_in[n] = dot_tn(pieces(0, whole), spots)
        up_in[n] = dot_tn(pieces(1, whole), spots)
        gate_out[n] = dot_tn(spots, pieces(2, left))
        up_out[n] = dot_tn(spots, pieces(2, right))
        down_out[n] = dot_tn(spots, pieces(3, whole))
        down_in[n] = dot_tn(pieces(4, left), spots)


def place(sets, packed, part, once, each):
    trees, local = part.shape[:2]
    batch = 2 if local % 2 == 0 else 1
    return pl.pallas_call(
        place_kernel,
        grid_spec=pltpu.PrefetchScalarGridSpec(
            num_scalar_prefetch=1,
            grid=(local // batch,),
            in_specs=[
                pl.BlockSpec(packed.shape, lambda e, s: (0, 0, 0)),
                pl.BlockSpec((trees, batch) + part.shape[2:], lambda e, s: (0, e, 0, 0)),
            ],
            out_specs=[
                *[pl.BlockSpec(o.shape, lambda e, s: (0, 0)) for o in once],
                *[pl.BlockSpec((batch,) + o.shape[1:], lambda e, s: (e, 0, 0)) for o in each],
            ],
        ),
        out_shape=[jax.ShapeDtypeStruct(o.shape, F32) for o in (*once, *each)],
        compiler_params=pltpu.CompilerParams(vmem_limit_bytes=VMEM_LIMIT),
        name="place",
    )(sets, packed, part)


def expert_kernel(
    sets, x_ref, g_ref, routes, router,
    w_gate, w_up, w_down, w_gate_far, w_up_far, w_down_far, all_gate, all_up, all_down, queries, gate_in, up_in, gate_out, up_out, down_in, down_out,
    back_out, mixed_out, grad_out, help_queries,
    rank_rows, gate_rows, slope_rows, mix, back, xs, firsts, tall_grad,
    gate_full, up_full, down_full, land_gate, land_up, land_down, grads, grads_in,
    far_sem, pass_far_sem, grads_sem, arrive_sem, query_sem,
    *, slots, sources, early, shared, straight, tp_count,
):
    chunk, expert = pl.program_id(0), pl.program_id(1)
    tp, fsdp = lax.axis_index("tp"), lax.axis_index("fsdp")
    late = shared + straight
    gather = late > 0
    other = {"fsdp": 1 - fsdp}
    cross, hand_on = far_moves(
        (all_gate, all_up, all_down), (land_gate, land_up, land_down), far_sem, pass_far_sem,
        shared, straight, early, 0, other, tp,
    )

    ctx = lax.axis_index("ctx")
    rank = lax.rem(ctx, SPAN)
    mirror = {"ctx": ctx + SPAN - 1 - 2 * rank}

    def query_copy():
        return remote(queries, help_queries, query_sem.at[0], query_sem.at[1], mirror)

    if gather:

        @pl.when(expert == 0)
        def _():
            barrier = pltpu.get_barrier_semaphore()
            for where in (other, mirror):
                pl.semaphore_signal(
                    barrier, 1, device_id=where, device_id_type=pl.DeviceIdType.MESH
                )
            for k in range(1, tp_count):
                pl.semaphore_signal(
                    barrier, 1, device_id={"tp": ring(tp, k, tp_count)},
                    device_id_type=pl.DeviceIdType.MESH,
                )
            pl.semaphore_wait(barrier, tp_count + 1)

            @pl.when(rank == SPAN - 1)
            def _():
                query_copy().start()

            for n in BEGIN[0]:
                for copy in cross(n):
                    copy.start()

        for step in range(1, early + late):
            if step in BEGIN or step in RELAY:

                @pl.when(expert == step)
                def _(step=step):
                    for n in RELAY.get(step, ()):
                        for copy in cross(n):
                            copy.wait_recv()
                        for copy in hand_on(n):
                            copy.start()
                    for n in BEGIN.get(step, ()):
                        for copy in cross(n):
                            copy.start()

        for n in range(late):

            @pl.when(expert == early + n)
            def _(n=n):
                for copy in hand_on(n) if n < shared else cross(n):
                    copy.wait_recv()

    experts = router.shape[0]
    tokens, model = x_ref.shape
    each = tokens // sources
    hidden = w_gate.shape[2]
    lanes = gate_in.shape[2]
    chosen = sets[fsdp * pl.num_programs(0) + chunk]

    @pl.when(expert == 0)
    def _():
        logits = dot_nt(router[...], x_ref[...])
        number = iota((experts, tokens), 0)
        hit = jnp.zeros((experts, tokens), F32)
        for k in range(routes.shape[0]):
            hit += (routes[k : k + 1, :] == number).astype(F32)
        kept = jnp.where(hit > 0.5, logits, MASKED)
        weights = jnp.exp(kept - jnp.max(kept, axis=0, keepdims=True)) * hit
        gate_rows[...] = weights / jnp.sum(weights, axis=0, keepdims=True)
        earlier = (iota((each, each), 0) < iota((each, each), 1)).astype(BF16)
        for s in range(sources):
            span = slice(s * each, (s + 1) * each)
            order = dot(hit[:, span].astype(BF16), earlier)
            rank_rows[:, span] = jnp.where(hit[:, span] > 0.5, order, -1.0)
        mix[...] = jnp.zeros(mix.shape, F32)
        back[...] = jnp.zeros(back.shape, F32)
        slope_rows[...] = jnp.zeros(slope_rows.shape, F32)

    first_row = lax.axis_index("ctx") * pl.num_programs(1)
    row = first_row + expert
    ranks = rank_rows[pl.ds(row, 1), :]
    gates = gate_rows[pl.ds(row, 1), :]
    slot_number = iota((slots, each), 0).astype(F32)
    picks, columns, upstreams = [], [], []
    for s in range(sources):
        span = slice(s * each, (s + 1) * each)
        pick = ranks[:, span] == slot_number
        columns.append(jnp.sum(jnp.where(pick, gates[:, span], 0.0), axis=1, keepdims=True))
        pick = pick.astype(BF16)
        picks.append(pick)
        xs[pl.ds(s * slots, slots), :] = dot(pick, x_ref[pl.ds(s * each, each), :]).astype(BF16)
        upstreams.append(dot(pick, g_ref[pl.ds(s * each, each), :]))
    gate_column = jnp.concatenate(columns, axis=0)
    upstream = RESIDUAL_SCALE * jnp.concatenate(upstreams, axis=0)

    firsts[:, :lanes] = gate_in[0]
    firsts[:, lanes:] = up_in[0]
    keep = (iota((1, 2 * lanes), 1) % lanes // RANK == chosen).astype(BF16)
    rows = xs[...]
    inner = dot(rows, firsts[...]).astype(BF16) * keep
    for full, near, far, landed in (
        (gate_full, w_gate, w_gate_far, land_gate),
        (up_full, w_up, w_up_far, land_up),
        (down_full, w_down, w_down_far, land_down),
    ):
        size = near.shape[1]
        full[pl.ds(pl.multiple_of(fsdp * size, size), size), :] = near[0]
        spot = pl.ds(pl.multiple_of((1 - fsdp) * size, size), size)
        if not gather:
            full[spot, :] = far[0]
            continue

        @pl.when(expert < early)
        def _(full=full, far=far, spot=spot):
            full[spot, :] = far[0]

        @pl.when(expert >= early)
        def _(full=full, landed=landed, spot=spot):
            full[spot, :] = landed[jnp.maximum(expert - early, 0)]
    gate_value = dot(rows, gate_full[...]) + dot(inner[:, :lanes], gate_out[0])
    up_value = dot(rows, up_full[...]) + dot(inner[:, lanes:], up_out[0])
    sigmoid = 1.0 / (1.0 + jnp.exp(-gate_value))
    silu = gate_value * sigmoid
    active = (silu * up_value).astype(BF16)
    down_inner = dot(active, down_in[0]).astype(BF16) * keep[:, :lanes]
    produced = (
        (dot(active, down_full[...]) + dot(down_inner, down_out[0])).astype(BF16).astype(F32)
    )
    slope = jnp.sum(upstream * produced, axis=1, keepdims=True)
    sent = (gate_column * produced).astype(BF16)
    slot_grad = (gate_column * upstream).astype(BF16)

    down_inner_grad = dot_nt(slot_grad, down_out[0]).astype(BF16) * keep[:, :lanes]
    active_grad = (
        (dot_nt(slot_grad, down_full[...]) + dot_nt(down_inner_grad, down_in[0]))
        .astype(BF16)
        .astype(F32)
    )
    gate_grad = (active_grad * up_value * (sigmoid + silu * (1.0 - sigmoid))).astype(BF16)
    up_grad = (active_grad * silu).astype(BF16)
    inner_grad = (
        jnp.concatenate([dot_nt(gate_grad, gate_out[0]), dot_nt(up_grad, up_out[0])], axis=1)
    ).astype(BF16) * keep
    row_grad = (
        dot_nt(gate_grad, gate_full[...])
        + dot_nt(up_grad, up_full[...])
        + dot_nt(inner_grad, firsts[...])
    ).astype(BF16)

    for s in range(sources):
        span = slice(s * slots, (s + 1) * slots)
        spot = pl.ds(s * each, each)
        mix[spot, :] += dot_tn(picks[s], sent[span, :])
        back[spot, :] += dot_tn(picks[s], row_grad[span, :])
        slope_rows[pl.ds(expert, 1), spot] = jnp.sum(
            jnp.where(picks[s] > 0.5, slope[span, :], 0.0), axis=0, keepdims=True
        )

    keep_at = expert if gather else 0

    def folded(start, width):
        total = tall_grad[pl.ds(start, RANK), :width]
        for shift in range(RANK, lanes, RANK):
            total += tall_grad[pl.ds(start + shift, RANK), :width]
        return total.astype(BF16)

    tall_grad[...] = dot_tn(inner_grad, rows)
    grads[keep_at, pl.ds(0, RANK), :] = folded(0, model)
    grads[keep_at, pl.ds(RANK, RANK), :] = folded(lanes, model)
    tall_grad[pl.ds(0, lanes), :hidden] = dot_tn(inner[:, :lanes], gate_grad)
    tall_grad[pl.ds(0, lanes), hidden:] = dot_tn(inner[:, lanes:], up_grad)
    grads[keep_at, pl.ds(2 * RANK, RANK), :] = folded(0, model)
    tall_grad[pl.ds(0, lanes), :] = dot_tn(down_inner, slot_grad)
    grads[keep_at, pl.ds(3 * RANK, RANK), :] = folded(0, model)
    tall_grad[pl.ds(0, lanes), :hidden] = dot_tn(down_inner_grad, active)
    grads[keep_at, pl.ds(4 * RANK, RANK), :hidden] = folded(0, hidden)
    grads[keep_at, pl.ds(4 * RANK, RANK), hidden:] = jnp.zeros((RANK, model - hidden), BF16)

    share = tall_grad.shape[1] // tp_count

    def grads_copy(n, k):
        where = ring(tp, k, tp_count)
        lanes = pl.ds(pl.multiple_of(where * share, share), share)
        return remote(
            grads.at[n, :, lanes], grads_in.at[k - 1, n], grads_sem.at[k - 1, n],
            arrive_sem.at[k - 1, n], {"tp": where},
        )

    def add_up(n):
        lanes = pl.ds(pl.multiple_of(tp * share, share), share)
        total = grads[n, :, lanes].astype(F32)
        for k in range(1, tp_count):
            grads_copy(n, k).wait()
            total += grads_in[k - 1, n].astype(F32)
        grad_out[n] = total.astype(BF16)

    if gather:
        for k in range(1, tp_count):
            grads_copy(expert, k).start()

        @pl.when(expert >= 2)
        def _():
            add_up(expert - 2)

    else:
        grad_out[0, 0] = grads[0]

    if gather:

        @pl.when(expert == pl.num_programs(1) - 1)
        def _():
            for n in range(late):
                for copy in cross(n):
                    copy.wait_send()
            for n in range(shared):
                for copy in hand_on(n):
                    copy.wait_send()

            @pl.when(rank == SPAN - 1)
            def _():
                query_copy().wait_send()

            @pl.when(rank == 0)
            def _():
                query_copy().wait_recv()

            for n in (2, 1):
                add_up(expert + 1 - n)

    @pl.when(expert == pl.num_programs(1) - 1)
    def _():
        mixed_out[...] = mix[...].astype(BF16)
        back_out[:, :model] = back[...].astype(BF16)
        turned = slope_rows[...].T
        high = turned.astype(BF16)
        low = (turned - high.astype(F32)).astype(BF16)
        local, lane = iota((LANES, LANES), 0), iota((LANES, LANES), 1)
        inside = local < pl.num_programs(1)
        first = (inside & (lane == local + first_row)).astype(BF16)
        later = (inside & (lane == local + first_row + experts)).astype(BF16)
        back_out[:, model:] = (dot(high, first) + dot(low, later)).astype(BF16)


def run_experts(
    sets, rows, upstream, routes, router, weights, far, queries, adapters, slots, sources, tp_count
):
    total, model = rows.shape
    experts = router.shape[0]
    local, half, hidden = weights[0].shape
    trees = sets.shape[0] // 2
    tokens = total // trees
    lanes = adapters[0].shape[2]
    tall = sources * slots
    piece = lambda c, e, *_: (c, 0)
    fixed = lambda c, e, *_: (0, 0)
    expert = lambda c, e, *_: (e, 0, 0)
    pairs, singles, shared, straight = transfer_plan(local, tp_count)
    early, late = pairs + singles, shared + straight
    arrived = lambda c, e, *_: (jnp.minimum(e, early - 1), 0, 0)
    hbm = pl.BlockSpec(memory_space=pl.ANY)
    dma = pltpu.SemaphoreType.DMA
    share = (local, 5 * RANK, model // tp_count)
    gradients = (
        (share, pl.BlockSpec(share, lambda c, e, *_: (0, 0, 0)))
        if late
        else (
            (trees, local, 5 * RANK, model),
            pl.BlockSpec((1, 1, 5 * RANK, model), lambda c, e, *_: (c, e, 0, 0)),
        )
    )
    return pl.pallas_call(
        functools.partial(
            expert_kernel, slots=slots, sources=sources, early=early, shared=shared,
            straight=straight, tp_count=tp_count,
        ),
        grid_spec=pltpu.PrefetchScalarGridSpec(
            num_scalar_prefetch=1,
            grid=(trees, local),
            in_specs=[
                pl.BlockSpec((tokens, model), piece),
                pl.BlockSpec((tokens, model), piece),
                pl.BlockSpec((routes.shape[0], tokens), lambda c, e, *_: (0, c)),
                pl.BlockSpec(router.shape, fixed),
                *[pl.BlockSpec((1,) + w.shape[1:], expert) for w in weights],
                *[pl.BlockSpec((1,) + w.shape[1:], arrived) for w in weights],
                *[hbm] * (len(weights) + 1),
                *[pl.BlockSpec((1,) + a.shape[1:], expert) for a in adapters],
            ],
            out_specs=[
                pl.BlockSpec((tokens, model + LANES), piece),
                pl.BlockSpec((tokens, model), piece),
                gradients[1],
                hbm,
            ],
            scratch_shapes=[
                pltpu.VMEM((experts, tokens), F32),
                pltpu.VMEM((experts, tokens), F32),
                pltpu.VMEM((LANES, tokens), F32),
                pltpu.VMEM((tokens, model), F32),
                pltpu.VMEM((tokens, model), F32),
                pltpu.VMEM((tall, model), BF16),
                pltpu.VMEM((model, 2 * lanes), BF16),
                pltpu.VMEM((2 * lanes, model), F32),
                pltpu.VMEM((2 * half, hidden), BF16),
                pltpu.VMEM((2 * half, hidden), BF16),
                pltpu.VMEM((hidden, model), BF16),
                *[pltpu.VMEM((max(late, 1),) + w.shape[1:], BF16) for w in weights],
                pltpu.VMEM((local if late else 1, 5 * RANK, model), BF16),
                pltpu.VMEM((tp_count - 1,) + (share if late else (1, 16, LANES)), BF16),
                dma((2, max(late, 1), 3)),
                dma((2, max(shared, 1), 3)),
                dma((tp_count - 1, local)),
                dma((tp_count - 1, local)),
                dma((2,)),
            ],
        ),
        out_shape=[
            jax.ShapeDtypeStruct((total, model + LANES), BF16),
            jax.ShapeDtypeStruct((total, model), BF16),
            jax.ShapeDtypeStruct(gradients[0], BF16),
            jax.ShapeDtypeStruct(queries.shape, BF16),
        ],
        compiler_params=(
            pltpu.CompilerParams(
                vmem_limit_bytes=60 * 1024 * 1024, collective_id=2, has_side_effects=True
            )
            if late
            else pltpu.CompilerParams(vmem_limit_bytes=60 * 1024 * 1024)
        ),
        name="experts",
        cost_estimate=pl.CostEstimate(
            flops=2 * local * total * model * model * 2,
            bytes_accessed=8 * 1024 * 1024,
            transcendentals=0,
        ),
    )(sets, rows, upstream, routes, router, *weights, *far, *weights, queries, *adapters)


def per_device(
    tokens,
    out_grad,
    routes,
    parents,
    adapter_set,
    gain_a,
    gain_b,
    w_query,
    key_projection_matrix,
    value_projection_matrix,
    w_output,
    w_router,
    w_gate,
    w_up,
    w_down,
    query_in,
    query_out,
    key_in,
    key_second_factor,
    value_in,
    value_second_factor,
    out_in,
    out_out,
    gate_in,
    gate_out,
    up_in,
    up_out,
    down_in,
    down_out,
):
    ctx_rank = lax.axis_index("ctx")
    fsdp_rank = lax.axis_index("fsdp")
    ctx_count = lax.axis_size("ctx")
    tp_count = lax.axis_size("tp")
    fsdp_count = lax.axis_size("fsdp")
    tok_rows, model = tokens.shape
    experts = w_router.shape[1]
    local_experts = w_gate.shape[0]
    slots = tok_rows * TOP * 3 // (2 * experts)
    trees = ctx_count // SPAN
    tree_index = (fsdp_rank * ctx_count + ctx_rank) // SPAN

    (
        attended, queries, kv_parts, lora, middle, o_reduced, attention_weights, normed_all,
        first, second, o_first, o_second, cos, sin, w_rows, att_rows,
        *far_weights, upstream_all, routes_all, rows_all,
    ) = forward(
        parents, adapter_set, tokens, (gain_a, gain_b),
        (w_query, key_projection_matrix, value_projection_matrix, w_output),
        (
            query_in, query_out, key_in, key_second_factor, value_in, value_second_factor,
            out_in, out_out,
        ),
        (w_gate, w_up, w_down), out_grad, routes.T, tp_count, ctx_count,
    )
    upstream_all = upstream_all.reshape(-1, model)
    rows_all = rows_all.reshape(-1, model)
    routes_all = routes_all.transpose(1, 0, 2).reshape(TOP, -1)

    back, mixed, expert_part, help_queries = run_experts(
        adapter_set,
        rows_all,
        upstream_all,
        routes_all,
        w_router.T,
        (w_gate, w_up, w_down),
        far_weights,
        queries,
        (gate_in, up_in, gate_out, up_out, down_in, down_out),
        slots,
        SPAN,
        tp_count,
    )
    direct = ctx_count == SPAN
    if direct:
        back = back.reshape(ctx_count, tok_rows, -1)
        mixed = mixed.reshape(ctx_count, tok_rows, -1)
    else:
        back = lax.psum_scatter(back, "ctx", scatter_dimension=0, tiled=True)
        mixed = lax.psum_scatter(mixed, "ctx", scatter_dimension=0, tiled=True)
    output, input_grad, packed, all_shares = backward(
        tokens, out_grad, routes.T, (gain_a, gain_b), w_router.T, middle, o_reduced, attention_weights,
        normed_all, lora, attended, queries, kv_parts, first, second, o_first, o_second,
        cos, sin, w_rows, att_rows, back, mixed, expert_part, help_queries, tp_count, ctx_count, experts, direct,
    )
    all_trees = fsdp_count * trees
    if not direct:
        mine = (jnp.arange(all_trees, dtype=jnp.int32) == tree_index)[:, None, None]
        packed = lax.psum(jnp.where(mine, packed, 0.0), ("fsdp", "ctx", "tp"))
    if direct:
        expert_part = all_shares
    else:
        expert_part = lax.all_gather(lax.psum(expert_part, "tp"), "fsdp")
        expert_part = expert_part.reshape(all_trees, local_experts, 5 * RANK, model)
    adapter_grads = place(
        adapter_set, packed, expert_part,
        (
            query_in, query_out, key_in, key_second_factor, value_in, value_second_factor,
            out_in, out_out,
        ),
        (gate_in, gate_out, up_in, up_out, down_in, down_out),
    )
    return (output, input_grad, *adapter_grads)


def solution(mesh):
    in_specs = (
        P(("fsdp", "ctx", "tp"), None),
        P(("fsdp", "ctx", "tp"), None),
        P(("fsdp", "ctx", "tp"), None),
        P(),
        P(),
        P(),
        P(),
        P("fsdp", "tp"),
        P("fsdp", "tp"),
        P("fsdp", "tp"),
        P("tp", "fsdp"),
        P(),
        P("ctx", "fsdp", None),
        P("ctx", "fsdp", None),
        P("ctx", "fsdp", None),
        P(),
        P(),
        P(),
        P(),
        P(),
        P(),
        P(),
        P(),
        P("ctx", None, None),
        P("ctx", None, None),
        P("ctx", None, None),
        P("ctx", None, None),
        P("ctx", None, None),
        P("ctx", None, None),
    )
    out_specs = (
        P(("fsdp", "ctx", "tp"), None),
        P(("fsdp", "ctx", "tp"), None),
        P(),
        P(),
        P(),
        P(),
        P(),
        P(),
        P(),
        P(),
        P("ctx", None, None),
        P("ctx", None, None),
        P("ctx", None, None),
        P("ctx", None, None),
        P("ctx", None, None),
        P("ctx", None, None),
    )
    return jax.shard_map(
        per_device, mesh=mesh, in_specs=in_specs, out_specs=out_specs, check_vma=False
    )
```

```python
import functools

import jax
import jax.numpy as jnp
import numpy as np
from jax import lax
from jax.experimental import pallas as pl
from jax.experimental.pallas import tpu as pltpu
from jax.sharding import PartitionSpec as P

HEAD = 64
TOP = 8
RANK = 16
SEG = 128
SEGS_DEV = 8
TREE_SEGS = 32
SPAN = TREE_SEGS // SEGS_DEV
LANES = 128

RESIDUAL_SCALE = 0.22
SCORE_SCALE = 0.015625
EPSILON = 1e-06
ROPE_BASE = 10000.0
MASKED = -1e30

F32 = jnp.float32
BF16 = jnp.bfloat16

CODE = HEAD
LSE = CODE + TREE_SEGS + 1
ONES = HEAD

VMEM_LIMIT = 56 * 1024 * 1024


def dot(a, b):
    return lax.dot_general(a, b, (((1,), (0,)), ((), ())), preferred_element_type=F32)


def dot_nt(a, b):
    return lax.dot_general(a, b, (((1,), (1,)), ((), ())), preferred_element_type=F32)


def dot_tn(a, b):
    return lax.dot_general(a, b, (((0,), (0,)), ((), ())), preferred_element_type=F32)


def iota(shape, dim):
    return lax.broadcasted_iota(jnp.int32, shape, dim)


def rms_scale(values, gain_row):
    return (
        values * lax.rsqrt(jnp.mean(values * values, axis=-1, keepdims=True) + EPSILON) * gain_row
    )


def rms_back(values, gain_row, grad):
    inv = lax.rsqrt(jnp.mean(values * values, axis=-1, keepdims=True) + EPSILON)
    scaled = grad * gain_row
    inner = jnp.mean(scaled * values, axis=-1, keepdims=True)
    return inv * scaled - values * (inv * inv * inv * inner)


def swap_halves(values):
    width = values.shape[-1]
    lane = iota(values.shape, 1) % HEAD
    ahead = pltpu.roll(values, width - HEAD // 2, 1)
    behind = pltpu.roll(values, HEAD // 2, 1)
    return jnp.where(lane < HEAD // 2, -ahead, behind)


def place_table(rows, source, target):
    r, c = iota((rows, LANES), 0), iota((rows, LANES), 1)
    return ((r - source == c - target) & (c >= target) & (c < target + HEAD)).astype(BF16)


def transfer_plan(local, tp_count):
    if local == 8 and tp_count % 2 == 0:
        return 3, 2, 2, 1
    return 0, local, 0, 0


BEGIN = {'start': (0, 1), 'proj': (2,), 'own': (3,), 'k1': (4,), 0: (0,), 2: (1,), 3: (2,)}
RELAY = {'k0': (0, 1), 'k3': (2,), 2: (0,), 4: (1,)}


def remote(src, dst, send, recv, where):
    return pltpu.make_async_remote_copy(
        src_ref=src,
        dst_ref=dst,
        send_sem=send,
        recv_sem=recv,
        device_id=where,
        device_id_type=pl.DeviceIdType.MESH,
    )


def far_moves(near, far, sems, pass_sems, shared, direct, first, land, other, tp):
    mate = {"tp": tp + 1 - 2 * lax.rem(tp, 2)}
    side = lax.rem(tp, 2)

    def piece(ref, rows, which):
        return ref.at[pl.ds(pl.multiple_of(which * rows, rows), rows)]

    def cross(n):
        moves = []
        for a, (source, target) in enumerate(zip(near, far)):
            src, dst = source.at[first + n], target.at[land + n]
            if n < shared:
                rows = src.shape[0] // 2
                src, dst = piece(src, rows, side), piece(dst, rows, side)
            moves.append(remote(src, dst, sems.at[0, n, a], sems.at[1, n, a], other))
        return moves

    def hand_on(n):
        moves = []
        for a, target in enumerate(far):
            dst = target.at[land + n]
            rows = dst.shape[0] // 2
            dst = piece(dst, rows, side)
            moves.append(remote(dst, dst, pass_sems.at[0, n, a], pass_sems.at[1, n, a], mate))
        return moves

    return cross, hand_on


class Line:
    def __init__(self, view, sems, me, count):
        self.view, self.sems, self.me, self.count = view, sems, me, count
        self.turns = 2 * count - 1

    def move(self, way, block):
        where = ring(self.me, 1 if way == 0 else -1, self.count)
        return remote(
            self.view(block), self.view(block),
            self.sems.at[way, 0, block], self.sems.at[way, 1, block], {"tp": where},
        )

    def goes(self, way):
        return self.me < self.count - 1 if way == 0 else self.me > 0

    def send(self, way, block):
        @pl.when(self.goes(way))
        def _():
            self.move(way, block).start()

    def start(self):
        self.send(0, self.me)
        self.send(1, self.me)

    def block(self, turn):
        step = (turn + 1) // 2
        block = jnp.where(lax.rem(turn, 2) == 1, self.me - step, self.me + step)
        valid = (block >= 0) & (block < self.count)
        return jnp.clip(block, 0, self.count - 1), valid

    def last(self):
        return jnp.maximum(2 * self.me - 1, 2 * (self.count - 1 - self.me))

    def arrive(self, turn, block):
        for way, odd in ((0, 1), (1, 0)):

            @pl.when((turn > 0) & (lax.rem(turn, 2) == odd))
            def _(way=way):
                self.move(way, block).wait_recv()
                self.send(way, block)

    def end(self):
        for block in range(self.count):
            for way, owned in ((0, block <= self.me), (1, block >= self.me)):

                @pl.when(owned & self.goes(way))
                def _(way=way):
                    self.move(way, block).wait_send()


def ring(me, step, count):
    return lax.rem(me + (step + count), count)


def aug_keys(kv, pair, pairs, first_seg, k_aug, v_aug, start):
    rows, width = kv.shape
    lane = iota((rows, LANES), 1)
    seg = first_seg + iota((rows, LANES), 0) // SEG
    key_code = ((lane - CODE == seg) | ((lane >= LSE) & (lane < LSE + 3))).astype(F32)
    one_code = ((lane == ONES) | (lane == ONES + 1)).astype(F32)
    span = pl.ds(start, rows)
    k_aug[pair, span, :] = (dot(kv, place_table(width, pair * HEAD, 0)) + key_code).astype(BF16)
    v_aug[pair, span, :] = (
        dot(kv, place_table(width, (pairs + pair) * HEAD, 0)) + one_code
    ).astype(BF16)


def forward_kernel(
    parents, adapter_set, tokens, gain_one, gain_two, freqs, w_query, w_key, w_value, w_output,
    query_in, query_out, key_in, key_out, value_in, value_out, out_in, out_out,
    w_gate, w_up, w_down, grads, routes,
    att_out, q_out, kv_out, lora_out, middle_out, low_out, weights, normed_all,
    first, second, o_first, o_second, cos, sin, w_rows, att_rows,
    gate_far, up_far, down_far, grads_all, routes_all, rows_all,
    q_aug, k_aug, v_aug, top, acc, rows_own, code_table, depth_table,
    shard_sem, normed_sem, kv_sem, part_sem, w_rows_sem, w_pass_sem, far_sem, pass_far_sem, grads_sem, routes_sem, rows_sem,
    pass_sem, local_sem,
    *, tp_count, ctx_count, shared, straight,
):
    tp, ctx, fsdp = (lax.axis_index(name) for name in ("tp", "ctx", "fsdp"))
    rank = lax.rem(ctx, SPAN)
    block, model = tokens.shape
    heads = q_aug.shape[0]
    pairs = k_aug.shape[0]
    group = heads // pairs
    tall = group * block
    half = model // 2
    q_cols = heads * HEAD
    kv_cols = pairs * HEAD
    turn = cos.shape[1]
    chips = ctx_count // 2
    partner = ctx + 1 - 2 * lax.rem(ctx, 2)
    other = {"fsdp": 1 - fsdp}

    barrier = pltpu.get_barrier_semaphore()
    pl.semaphore_signal(barrier, 1, device_id=other, device_id_type=pl.DeviceIdType.MESH)
    for k in range(1, tp_count):
        pl.semaphore_signal(
            barrier, 1, device_id={"tp": ring(tp, k, tp_count)},
            device_id_type=pl.DeviceIdType.MESH,
        )
    for k in range(1, ctx_count):
        pl.semaphore_signal(
            barrier, 1, device_id={"ctx": ring(ctx, k, ctx_count)},
            device_id_type=pl.DeviceIdType.MESH,
        )
    pl.semaphore_wait(barrier, tp_count + ctx_count - 1)

    corners = (
        (w_query, 0, 0),
        (w_key, 0, q_cols),
        (w_value, 0, q_cols + kv_cols),
        (w_output, half, 0),
    )
    shard_copies = []
    shard_passes = []
    core = lax.rem(ctx, 2)
    for n, (source, row, column) in enumerate(corners):
        size = source.shape[0] // 2
        start = pl.multiple_of(core * size, size)
        rows = pl.ds(pl.multiple_of(row + core * size, size), size)
        lanes = pl.ds(column, source.shape[1])
        shard_copies.append(
            remote(
                source.at[pl.ds(start, size)], weights.at[fsdp, rows, lanes],
                shard_sem.at[0, n], shard_sem.at[1, n], other,
            )
        )
        landed = weights.at[1 - fsdp, rows, lanes]
        shard_passes.append(
            remote(
                landed, landed, shard_sem.at[2, n], shard_sem.at[3, n], {"ctx": partner}
            )
        )
    for copy in shard_copies:
        copy.start()

    inputs = tokens[...].astype(F32)
    normed = rms_scale(inputs, gain_one[...].astype(F32).reshape(1, model)).astype(BF16)
    normed_all[tp] = normed

    line = Line(lambda b: normed_all.at[b], normed_sem, tp, tp_count)
    line.start()

    def side_copies(k):
        where = {"ctx": ring(ctx, k, ctx_count)}
        return (
            remote(grads, grads_all.at[ctx], grads_sem.at[0, k], grads_sem.at[1, k], where),
            remote(routes, routes_all.at[ctx], routes_sem.at[0, k], routes_sem.at[1, k], where),
        )

    own_copies = (
        pltpu.make_async_copy(grads, grads_all.at[ctx], local_sem.at[0]),
        pltpu.make_async_copy(routes, routes_all.at[ctx], local_sem.at[1]),
    )
    for copy in own_copies:
        copy.start()
    for k in range(1, ctx_count):
        for copy in side_copies(k):
            copy.start()

    for source, row, column in corners:
        weights[fsdp, pl.ds(row, source.shape[0]), pl.ds(column, source.shape[1])] = source[...]

    tree = (fsdp * ctx_count + ctx) // SPAN
    spot_row, spot_lane = iota((LANES, LANES), 0), iota((LANES, LANES), 1)
    linked = (spot_row == spot_lane) & (spot_row < TREE_SEGS)
    for n in range(TREE_SEGS):
        linked |= (spot_row == n) & (spot_lane == parents[tree * TREE_SEGS + n])
    reach = linked.astype(F32)
    for _ in range((TREE_SEGS - 1).bit_length()):
        reach = jnp.minimum(dot(reach.astype(BF16), reach.astype(BF16)), 1.0)
    depth_table[...] = jnp.broadcast_to(
        jnp.sum(reach, axis=1, keepdims=True) - 1.0, (LANES, LANES)
    ).astype(BF16)
    coded = (spot_lane >= CODE) & (spot_lane < CODE + TREE_SEGS)
    code_table[...] = jnp.where(
        coded & (pltpu.roll(reach, CODE, 1) < 0.5), MASKED, 0.0
    ).astype(BF16)

    chosen = adapter_set[tree]

    def pick(n):
        inside = (spot_lane >= n * RANK) & (spot_lane < (n + 1) * RANK)
        return (inside & (spot_row == spot_lane - n * RANK + chosen * RANK)).astype(BF16)

    first[...] = (
        dot(query_in[...], pick(0)) + dot(key_in[...], pick(1)) + dot(value_in[...], pick(2))
    ).astype(BF16)
    for n, (source, column, width) in enumerate(
        ((query_out, 0, q_cols), (key_out, q_cols, kv_cols), (value_out, q_cols + kv_cols, kv_cols))
    ):
        lanes = pl.ds(pl.multiple_of(tp * width, width), width)
        second[:, column : column + width] = dot_tn(pick(n), source[:, lanes]).astype(BF16)
    o_first[...] = dot(out_in[...], pick(0)).astype(BF16)
    o_second[...] = dot_tn(pick(0), out_out[...]).astype(BF16)

    for copy, onward in zip(shard_copies, shard_passes):
        copy.wait()
        onward.start()
    cross, hand_on = far_moves(
        (w_gate, w_up, w_down), (gate_far, up_far, down_far), far_sem, pass_far_sem,
        shared, straight, 0, 0, other, tp,
    )

    def point(name):
        if not shared:
            if name == "start":
                for n in range(straight):
                    for copy in cross(n):
                        copy.start()
            return
        for n in RELAY.get(name, ()):
            for copy in cross(n):
                copy.wait_recv()
            for copy in hand_on(n):
                copy.start()
        for n in BEGIN.get(name, ()):
            for copy in cross(n):
                copy.start()

    point("start")
    for onward in shard_passes:
        onward.wait()

    def kv_copy(distance, part):
        return remote(
            kv_out.at[0, part], kv_out.at[distance, part],
            kv_sem.at[0, distance - 1], kv_sem.at[1, distance - 1], {"ctx": ring(ctx, distance, ctx_count)},
        )

    def project(part):
        span = pl.ds(pl.multiple_of(part * block, block), block)
        rows = normed_all[part]
        seg = rank * SEGS_DEV + (part * block + iota((block, LANES), 0)) // SEG
        at_seg = (seg == iota((block, LANES), 1)).astype(BF16)
        offset = lax.rem(iota((block, LANES), 0), SEG).astype(F32)
        angles = (dot(at_seg, depth_table[...]) * SEG + offset) * freqs[...]
        cos[span, :] = jnp.cos(angles)
        sin[span, :] = jnp.sin(angles)
        codes = dot(at_seg, code_table[...])
        lora = dot(rows, first[...]).astype(BF16)
        lora_out[span, :] = lora
        pre = (
            dot(rows[:, :half], weights[0, pl.ds(0, half), :])
            + dot(rows[:, half:], weights[1, pl.ds(0, half), :])
            + dot(lora, second[...])
        )
        turned = []
        for start in range(0, pre.shape[1] // 4 * 3, turn):
            piece = pre[:, start : start + turn]
            turned.append(piece * cos[span, :] + swap_halves(piece) * sin[span, :])
        queries = (
            jnp.concatenate(turned[: q_cols // turn], axis=1) * SCORE_SCALE
        ).astype(BF16)
        for head in range(heads):
            q_aug[head, span, :] = (
                dot(queries, place_table(q_cols, head * HEAD, 0)) + codes
            ).astype(BF16)
        keys = jnp.concatenate(turned[q_cols // turn :], axis=1)
        kv = jnp.concatenate([keys, pre[:, q_cols + keys.shape[1] :]], axis=1).astype(BF16)
        kv_out[0, part] = kv
        for distance in range(1, SPAN):

            @pl.when(rank + distance < SPAN)
            def _(distance=distance):
                kv_copy(distance, part).start()

        for pair in range(pairs):
            aug_keys(
                kv, pair, pairs, rank * SEGS_DEV + part * (block // SEG), k_aug, v_aug,
                pl.multiple_of(part * block, block),
            )

    @pl.loop(0, line.turns)
    def _(turn):
        part, valid = line.block(turn)

        @pl.when(valid)
        def _():
            line.arrive(turn, part)
            project(part)

    w_line = Line(lambda b: w_rows.at[b, core], w_rows_sem, tp, tp_count)
    w_rows[tp, core] = weights[core, pl.ds(half, q_cols), :]
    w_line.start()
    w_pass = remote(
        w_rows.at[:, core], w_rows.at[:, core], w_pass_sem.at[0], w_pass_sem.at[1], {"ctx": partner}
    )
    point("proj")

    def advance(step):
        @pl.loop(2 * step - 1, 2 * step + 1)
        def _(turn):
            shard, valid = w_line.block(turn)

            @pl.when(valid)
            def _():
                w_line.arrive(turn, shard)

    def tile(part, pair, start, size, causal):
        index = part * pairs + pair
        rows = pl.ds(pl.multiple_of(part * block, block), block)
        queries = q_aug[pl.ds(pair * group, group), rows, :].reshape(tall, LANES)
        span = pl.ds(start, size)
        scores = dot_nt(queries, k_aug[pair, span, :])
        if causal:
            q_row = iota(scores.shape, 0) % block
            scores = jnp.where(iota(scores.shape, 1) <= q_row, scores, MASKED)
            now = jnp.broadcast_to(jnp.max(scores, axis=1, keepdims=True), (tall, LANES))
            probs = jnp.exp(scores - now[:, :1]).astype(BF16)
            acc[index] = dot(probs, v_aug[pair, span, :])
        else:
            before = top[index]
            now = jnp.maximum(before, jnp.max(scores, axis=1, keepdims=True))
            probs = jnp.exp(scores - now[:, :1]).astype(BF16)
            acc[index] = acc[index] * jnp.exp(before - now) + dot(probs, v_aug[pair, span, :])
        top[index] = now

    @pl.loop(0, tp_count * pairs)
    def _(index):
        part, pair = index // pairs, lax.rem(index, pairs)
        tile(part, pair, pl.multiple_of(part * block, block), block, True)

        @pl.loop(0, part)
        def _(j):
            tile(part, pair, pl.multiple_of(j * block, block), block, False)

    advance(1)
    point("own")
    group_rows = tp_count * block
    for distance in range(1, SPAN):

        @pl.when(distance <= rank)
        def _(distance=distance):
            remote(
                kv_out.at[0], kv_out.at[distance], kv_sem.at[0, distance - 1],
                kv_sem.at[1, distance - 1], {"ctx": ring(ctx, distance, ctx_count)},
            ).wait_recv()

            @pl.loop(0, tp_count)
            def _(part):
                kv = kv_out[distance, part]
                for pair in range(pairs):
                    aug_keys(
                        kv, pair, pairs,
                        (rank - distance) * SEGS_DEV + part * (block // SEG), k_aug, v_aug,
                        pl.multiple_of(distance * group_rows + part * block, block),
                    )

        @pl.when(distance > rank)
        def _(distance=distance):
            kv_out[distance] = jnp.zeros(kv_out.shape[1:], BF16)

    def part_copy(k):
        part = ring(tp, k + 1, tp_count)
        rows = pl.ds(pl.multiple_of(part * block, block), block)
        return remote(
            att_out.at[rows], att_rows.at[tp], part_sem.at[0, k], part_sem.at[1, k], {"tp": part}
        )

    @pl.loop(0, tp_count)
    def _(k):
        part = ring(tp, k + 1, tp_count)
        rows = pl.ds(pl.multiple_of(part * block, block), block)
        for pair in range(pairs):
            index = part * pairs + pair

            @pl.loop(1, rank + 1)
            def _(distance, pair=pair):
                tile(
                    part, pair, pl.multiple_of(distance * group_rows, group_rows), group_rows, False
                )

            summed = acc[index]
            total = summed[:, ONES : ONES + 1]
            result = (summed / total).astype(BF16)
            for member in range(group):
                head = pair * group + member
                att_out[rows, pl.ds(head * HEAD, HEAD)] = result[
                    member * block : (member + 1) * block, :HEAD
                ]
            minus = -(top[index] + jnp.log(total))
            high = minus.astype(BF16).astype(F32)
            middle = (minus - high).astype(BF16).astype(F32)
            lane = iota(minus.shape, 1)
            queries = q_aug[pl.ds(pair * group, group), rows, :].reshape(tall, LANES)
            coded = jnp.where(
                lane == LSE,
                high,
                jnp.where(
                    lane == LSE + 1,
                    middle,
                    jnp.where(lane == LSE + 2, minus - high - middle, queries.astype(F32)),
                ),
            )
            q_out[pl.ds(pair * group, group), rows, :] = coded.astype(BF16).reshape(
                group, block, LANES
            )

        @pl.when(k < tp_count - 1)
        def _():
            part_copy(k).start()

        @pl.when(k == tp_count - 1)
        def _():
            att_rows[tp] = att_out[rows, :]

        for step in range(2, tp_count):

            @pl.when(k == step - 2)
            def _(step=step):
                advance(step)
                if step == tp_count - 1:
                    w_pass.start()

        for n in range(tp_count):
            if f"k{n}" in BEGIN or f"k{n}" in RELAY:

                @pl.when(k == n)
                def _(n=n):
                    point(f"k{n}")

    for k in range(tp_count - 1):
        part_copy(k).wait_recv()
    point("sum")
    w_pass.wait_recv()
    low = sum(
        dot(att_rows[t], o_first[pl.ds(t * q_cols, q_cols), :]) for t in range(tp_count)
    ).astype(BF16)
    low_out[...] = low
    branch = dot(low, o_second[...]) + jnp.concatenate(
        [sum(dot(att_rows[t], w_rows[t, side]) for t in range(tp_count)) for side in range(2)],
        axis=1,
    )
    middle = inputs + RESIDUAL_SCALE * branch
    middle_out[...] = middle
    rows_own[...] = rms_scale(middle, gain_two[...].astype(F32).reshape(1, model)).astype(BF16)

    own_rows = pltpu.make_async_copy(rows_own, rows_all.at[ctx], local_sem.at[2])
    own_rows.start()
    to_partner = remote(
        rows_own, rows_all.at[ctx], rows_sem.at[0, 0], rows_sem.at[1, 0], {"ctx": partner}
    )
    to_partner.start()

    def rows_copy(k):
        return remote(
            rows_own, rows_all.at[ctx], rows_sem.at[0, k], rows_sem.at[1, k],
            {"ctx": ring(ctx, 2 * k, ctx_count)},
        )

    def pass_copy(k):
        source = ring(ctx, -2 * k, ctx_count)
        return remote(
            rows_all.at[source], rows_all.at[source], pass_sem.at[0, k], pass_sem.at[1, k],
            {"ctx": partner},
        )

    for k in range(1, chips):
        rows_copy(k).start()
    for k in range(1, chips):
        rows_copy(k).wait_recv()
        pass_copy(k).start()

    line.end()
    w_line.end()
    w_pass.wait_send()
    for k in range(tp_count - 1):
        part_copy(k).wait_send()
    for distance in range(1, SPAN):

        @pl.when(rank + distance < SPAN)
        def _(distance=distance):
            remote(
                kv_out.at[0], kv_out.at[distance], kv_sem.at[0, distance - 1],
                kv_sem.at[1, distance - 1], {"ctx": ring(ctx, distance, ctx_count)},
            ).wait_send()

    for k in range(1, ctx_count):
        for copy in side_copies(k):
            copy.wait()
    for copy in own_copies:
        copy.wait()
    own_rows.wait()
    to_partner.wait()
    for k in range(1, chips):
        rows_copy(k).wait_send()
        pass_copy(k).wait()
    for n in range(shared + straight):
        for copy in cross(n):
            copy.wait_send()
            if n >= shared:
                copy.wait_recv()
    for n in range(shared):
        for copy in hand_on(n):
            copy.wait()


def forward(
    parents, adapter_set, tokens, gains, attention, adapters, weights, grads, routes,
    tp_count, ctx_count,
):
    block, model = tokens.shape
    rows = tp_count * block
    q_cols, kv_cols = attention[0].shape[1], attention[1].shape[1]
    heads, pairs = q_cols // HEAD, kv_cols // HEAD
    cols = q_cols + 2 * kv_cols
    tall = heads // pairs * block
    chips = ctx_count // 2
    shared, straight, _, _ = transfer_plan(weights[0].shape[0], tp_count)
    vmem = pl.BlockSpec(memory_space=pltpu.VMEM)
    smem = pl.BlockSpec(memory_space=pltpu.SMEM)
    hbm = pl.BlockSpec(memory_space=pl.ANY)
    dma = pltpu.SemaphoreType.DMA
    half_head = HEAD // 2
    freqs = np.float32(ROPE_BASE) ** (-(np.arange(half_head, dtype=np.float32) * 2) / HEAD)
    freqs = jnp.asarray(np.tile(freqs.astype(np.float32), LANES // half_head)[None])
    return pl.pallas_call(
        functools.partial(
            forward_kernel, tp_count=tp_count, ctx_count=ctx_count, shared=shared, straight=straight
        ),
        in_specs=[smem] * 2 + [vmem] * 16 + [hbm] * 5,
        out_specs=[vmem] * 16 + [hbm] * 6,
        out_shape=[
            jax.ShapeDtypeStruct((rows, q_cols), BF16),
            jax.ShapeDtypeStruct((heads, rows, LANES), BF16),
            jax.ShapeDtypeStruct((SPAN, tp_count, block, 2 * kv_cols), BF16),
            jax.ShapeDtypeStruct((rows, LANES), BF16),
            jax.ShapeDtypeStruct((block, model), F32),
            jax.ShapeDtypeStruct((block, LANES), BF16),
            jax.ShapeDtypeStruct((2, model // 2 + q_cols, model // 2), BF16),
            jax.ShapeDtypeStruct((tp_count, block, model), BF16),
            jax.ShapeDtypeStruct((model, LANES), BF16),
            jax.ShapeDtypeStruct((LANES, cols), BF16),
            jax.ShapeDtypeStruct((tp_count * q_cols, LANES), BF16),
            jax.ShapeDtypeStruct((LANES, model), BF16),
            jax.ShapeDtypeStruct((rows, LANES), F32),
            jax.ShapeDtypeStruct((rows, LANES), F32),
            jax.ShapeDtypeStruct((tp_count, 2, q_cols, model // 2), BF16),
            jax.ShapeDtypeStruct((tp_count, block, q_cols), BF16),
            *[jax.ShapeDtypeStruct((shared + straight,) + w.shape[1:], BF16) for w in weights],
            jax.ShapeDtypeStruct((ctx_count,) + grads.shape, BF16),
            jax.ShapeDtypeStruct((ctx_count,) + routes.shape, jnp.int32),
            jax.ShapeDtypeStruct((ctx_count, block, model), BF16),
        ],
        scratch_shapes=[
            pltpu.VMEM((heads, rows, LANES), BF16),
            pltpu.VMEM((pairs, SPAN * rows, LANES), BF16),
            pltpu.VMEM((pairs, SPAN * rows, LANES), BF16),
            pltpu.VMEM((tp_count * pairs, tall, LANES), F32),
            pltpu.VMEM((tp_count * pairs, tall, LANES), F32),
            pltpu.VMEM((block, model), BF16),
            pltpu.VMEM((LANES, LANES), BF16),
            pltpu.VMEM((LANES, LANES), BF16),
            dma((4, 4)),
            dma((2, 2, tp_count)),
            dma((2, SPAN - 1)),
            dma((2, tp_count - 1)),
            dma((2, 2, tp_count)),
            dma((2,)),
            dma((2, shared + straight, 3)),
            dma((2, max(shared, 1), 3)),
            dma((2, ctx_count)),
            dma((2, ctx_count)),
            dma((2, chips)),
            dma((2, chips)),
            dma((3,)),
        ],
        compiler_params=pltpu.CompilerParams(
            vmem_limit_bytes=VMEM_LIMIT, collective_id=0, has_side_effects=True
        ),
        cost_estimate=pl.CostEstimate(
            flops=16 * SPAN * rows * rows * heads * LANES,
            bytes_accessed=32 * 1024 * 1024,
            transcendentals=0,
        ),
        name="forward",
    )(
        parents, adapter_set, tokens, *gains, freqs, *attention, *adapters, *weights, grads, routes,
    )


def joined(dk, dv, span):
    pairs = dk.shape[0]
    return jnp.concatenate(
        [dk[pair, span, :HEAD] for pair in range(pairs)]
        + [dv[pair, span, :HEAD] for pair in range(pairs)],
        axis=1,
    )


def backward_kernel(
    tokens, upstream_ref, routes, gain_one, gain_two, w_router, middle_ref, low_ref, weights,
    normed_all, lora, att, q_ref, kv_ref, first, second, o_first, o_second, cos, sin, w_rows, att_rows, back, mixed, shares, help_q,
    output, input_grad, packed_out, shares_out,
    k_aug, v_aug, up_aug, dk, dv, dq, help_up, help_dq, help_sum, do_out, do_all, far_out, far_in, own_kv, row_grads, low_grads, parts, parts_in,
    second_acc, first_acc, packed, ctx_in, tp_in, middle_grad, router,
    back_near, back_mine, back_pair, back_far, mixed_near, mixed_mine, mixed_pair, mixed_far,
    near_sem, mine_sem, far_sem, branch_sem, kv_sem, part_sem,
    ctx_sem, tp_sem, x_sem, ctx_all_sem, share_sem, swap_sem, own_sem,
    up_sem, sum_sem,
    *, tp_count, ctx_count, experts, direct,
):
    tp, ctx, fsdp = (lax.axis_index(name) for name in ("tp", "ctx", "fsdp"))
    rank = lax.rem(ctx, SPAN)
    block, model = tokens.shape
    heads, rows_all, _ = q_ref.shape
    pairs = k_aug.shape[0]
    group = heads // pairs
    tall = group * block
    half = weights.shape[2]
    q_cols = heads * HEAD
    kv_cols = pairs * HEAD
    turn = cos.shape[1]
    partner = ctx + 1 - 2 * lax.rem(ctx, 2)
    cross = ring(ctx, 2, ctx_count)
    cross_partner = ring(partner, 2, ctx_count)
    other = {"fsdp": 1 - fsdp}

    barrier = pltpu.get_barrier_semaphore()
    pl.semaphore_signal(barrier, 1, device_id=other, device_id_type=pl.DeviceIdType.MESH)
    for k in range(1, tp_count):
        pl.semaphore_signal(
            barrier, 1, device_id={"tp": ring(tp, k, tp_count)},
            device_id_type=pl.DeviceIdType.MESH,
        )
    for k in range(1, ctx_count):
        pl.semaphore_signal(
            barrier, 1, device_id={"ctx": ring(ctx, k, ctx_count)},
            device_id_type=pl.DeviceIdType.MESH,
        )
    pl.semaphore_wait(barrier, tp_count + ctx_count - 1)

    sums = (
        (back, back_near, back_mine, back_pair, back_far),
        (mixed, mixed_near, mixed_mine, mixed_pair, mixed_far),
    )

    def near_copy(n, slot):
        source, near = sums[n][:2]
        return remote(
            source.at[(partner, cross_partner)[slot]], near.at[slot],
            near_sem.at[0, 2 * n + slot], near_sem.at[1, 2 * n + slot], {"ctx": partner},
        )

    def mine_copy(n, slot):
        return pltpu.make_async_copy(
            sums[n][0].at[(ctx, cross)[slot]], sums[n][2].at[slot], mine_sem.at[2 * n + slot]
        )

    def pair_copy(n):
        return remote(sums[n][3], sums[n][4], far_sem.at[0, n], far_sem.at[1, n], {"ctx": cross})

    def start_sum(n):
        for slot in (1, 0):
            near_copy(n, slot).start()
            mine_copy(n, slot).start()

    def pass_sum(n):
        near_copy(n, 1).wait_recv()
        mine_copy(n, 1).wait()
        _, near, mine, pair, _ = sums[n]
        pair[...] = (near[1].astype(F32) + mine[1].astype(F32)).astype(BF16)
        pair_copy(n).start()

    def end_sum(n):
        near_copy(n, 0).wait_recv()
        mine_copy(n, 0).wait()
        pair_copy(n).wait_recv()
        _, near, mine, _, far = sums[n]
        return near[0].astype(F32) + mine[0].astype(F32) + far[...].astype(F32)

    if direct:
        share = shares.shape[2]
        own_lanes = pl.ds(pl.multiple_of(tp * share, share), share)

        def share_copy(k):
            return remote(
                shares, shares_out.at[fsdp, :, :, own_lanes],
                share_sem.at[0, k - 1], share_sem.at[1, k - 1], {"tp": ring(tp, k, tp_count)},
            )

        share_own = pltpu.make_async_copy(shares, shares_out.at[fsdp, :, :, own_lanes], own_sem.at[0])
        swap = remote(
            shares_out.at[fsdp], shares_out.at[fsdp], swap_sem.at[0], swap_sem.at[1], other
        )

        near_copy(0, 1).start()
        for slot in (1, 0):
            mine_copy(0, slot).start()
        pass_sum(0)
        near_copy(0, 0).start()
        start_sum(1)
        share_own.start()

    last_rank, first_rank = rank == SPAN - 1, rank == 0
    mirror = {"ctx": ctx + SPAN - 1 - 2 * rank}
    far_count = jnp.where(last_rank, rank - 1, rank) if direct else rank

    @pl.loop(0, far_count + 1)
    def _(distance):
        @pl.loop(0, tp_count)
        def _(part):
            kv = kv_ref[distance, part]
            for pair in range(pairs):
                aug_keys(
                    kv, pair, pairs, (rank - distance) * SEGS_DEV + part * (block // SEG),
                    k_aug, v_aug, pl.multiple_of(distance * rows_all + part * block, block),
                )

    dk[...] = jnp.zeros(dk.shape, F32)
    dv[...] = jnp.zeros(dv.shape, F32)
    dq[...] = jnp.zeros(dq.shape, F32)
    second_acc[...] = jnp.zeros(second_acc.shape, F32)
    first_acc[...] = jnp.zeros(first_acc.shape, F32)
    packed[...] = jnp.zeros(packed.shape, F32)

    middle = middle_ref[...]
    scale_one = gain_one[...].astype(F32).reshape(1, model)
    scale_two = gain_two[...].astype(F32).reshape(1, model)
    normed_two = rms_scale(middle, scale_two).astype(BF16)
    router[...] = jnp.zeros(router.shape, BF16)
    router[pl.ds(0, experts), :] = w_router[...]
    logits = dot_nt(normed_two, router[...])
    number = iota((LANES, block), 0)
    hit = jnp.zeros((LANES, block), F32)
    for k in range(routes.shape[0]):
        hit += (routes[k : k + 1, :] == number).astype(F32)
    hit = hit.T
    kept = jnp.where(hit > 0.5, logits, MASKED)
    gates = jnp.exp(kept - jnp.max(kept, axis=1, keepdims=True)) * hit
    gates = gates / jnp.sum(gates, axis=1, keepdims=True)

    if direct:
        back_sum = end_sum(0)
    else:
        back_sum = back[...].astype(F32)
    table = back_sum[:, model:]
    slopes = table + pltpu.roll(table, LANES - experts, 1)
    logits_grad = gates * (slopes - jnp.sum(gates * slopes, axis=1, keepdims=True))
    high = logits_grad.astype(BF16)
    low = (logits_grad - high.astype(F32)).astype(BF16)
    normed_two_grad = back_sum[:, :model] + dot(high, router[...]) + dot(low, router[...])
    middle_grad[...] = upstream_ref[...].astype(F32) + rms_back(
        middle, scale_two, normed_two_grad
    )
    branch = (RESIDUAL_SCALE * middle_grad[...]).astype(BF16)
    low_grad = dot_nt(branch, o_second[...]).astype(BF16)

    def do_copy(k):
        where = ring(tp, k, tp_count)
        return remote(
            do_out.at[where], do_all.at[tp], branch_sem.at[0, k - 1], branch_sem.at[1, k - 1],
            {"tp": where},
        )

    for t in range(tp_count):
        do_out[t] = (
            dot_nt(branch[:, :half], w_rows[t, 0])
            + dot_nt(branch[:, half:], w_rows[t, 1])
            + dot_nt(low_grad, o_first[pl.ds(t * q_cols, q_cols), :])
        ).astype(BF16)
    for k in range(1, tp_count):
        do_copy(k).start()
    do_all[tp] = do_out[tp]
    for t in range(tp_count):
        packed[pl.ds(3 * RANK, RANK), t * q_cols : (t + 1) * q_cols] = dot_tn(
            low_grad, att_rows[t]
        )[:RANK]
    packed[pl.ds(4 * RANK, RANK), :] = dot_tn(low_ref[...], branch)[:RANK]
    if direct:
        pass_sum(1)

    wide = heads * LANES
    r, c = iota((q_cols, wide), 0), iota((q_cols, wide), 1)
    same = r // HEAD == c // LANES
    place = (same & (r % HEAD == c % LANES)).astype(BF16)
    spread = (same & (c % LANES >= ONES) & (c % LANES < ONES + 2)).astype(BF16)

    def tile(part, pair, start, size, causal, from_q=q_ref, from_up=up_aug, into=dq):
        index = part * pairs + pair
        rows = pl.ds(pl.multiple_of(part * block, block), block)
        queries = from_q[pl.ds(pair * group, group), rows, :].reshape(tall, LANES)
        upstream = from_up[pl.ds(pair * group, group), rows, :].reshape(tall, LANES)
        span = pl.ds(start, size)
        keys = k_aug[pair, span, :]
        probs = jnp.exp(dot_nt(keys, queries))
        if causal:
            q_row = iota(probs.shape, 1) % block
            probs = jnp.where(iota(probs.shape, 0) <= q_row, probs, 0.0)
        steep = (probs * dot_nt(v_aug[pair, span, :], upstream)).astype(BF16)
        dv[pair, span, :] += dot(probs.astype(BF16), upstream)
        dk[pair, span, :] += dot(steep, queries)
        into[pair if into is help_dq else index] += dot_tn(steep, keys)

    def far_copy(distance):
        return remote(
            far_out.at[distance - 1], far_in.at[distance - 1],
            kv_sem.at[0, distance - 1], kv_sem.at[1, distance - 1],
            {"ctx": ring(ctx, -distance, ctx_count)},
        )

    size = min(rows_all, 1024)

    def take_block(part):
        rows = pl.ds(pl.multiple_of(part * block, block), block)
        grads = do_all[part]
        mixed_heads = att[rows, :]
        product = grads.astype(F32) * mixed_heads.astype(F32)
        minus = jnp.zeros((block, wide), F32)
        for _ in range(3):
            piece = product.astype(BF16)
            minus -= dot(piece, spread)
            product -= piece.astype(F32)
        top = minus.astype(BF16).astype(F32)
        lane = iota(minus.shape, 1) % LANES
        coded = dot(grads, place) + jnp.where(
            lane == ONES, top, jnp.where(lane == ONES + 1, minus - top, 0.0)
        )
        for head in range(heads):
            up_aug[head, rows, :] = coded[:, head * LANES : (head + 1) * LANES].astype(BF16)

    def up_copy(part):
        rows = pl.ds(pl.multiple_of(part * block, block), block)
        return remote(
            up_aug.at[:, rows], help_up.at[:, rows], up_sem.at[0, part], up_sem.at[1, part], mirror
        )

    def sum_copy(part):
        spot = pl.ds(part * pairs, pairs)
        return remote(
            help_sum.at[spot], help_sum.at[spot], sum_sem.at[0, part], sum_sem.at[1, part], mirror
        )

    @pl.loop(0, tp_count)
    def _(turn):
        part = ring(tp, -turn, tp_count)

        @pl.when(turn > 0)
        def _():
            do_copy(turn).wait_recv()

        @pl.when(turn >= 0)
        def _():
            take_block(part)
            if direct:

                @pl.when(last_rank)
                def _():
                    up_copy(part).start()

            @pl.loop(0, far_count)
            def _(step):
                distance = far_count - step
                start = distance * rows_all

                @pl.loop(0, pairs * (rows_all // size))
                def _(n):
                    pair, piece = n // (rows_all // size), lax.rem(n, rows_all // size)
                    tile(part, pair, pl.multiple_of(start + piece * size, size), size, False)

                @pl.when(turn == tp_count - 1)
                def _():
                    @pl.loop(0, tp_count)
                    def _(spot):
                        span = pl.ds(pl.multiple_of(start + spot * block, block), block)
                        rows = pl.ds(pl.multiple_of(spot * block, block), block)
                        far_out[distance - 1, rows, :] = joined(dk, dv, span).astype(BF16)

                    far_copy(distance).start()

            if direct:

                @pl.when(turn == 1)
                def _():
                    for k in range(1, tp_count):
                        share_copy(k).start()

            @pl.loop(0, pairs)
            def _(pair):
                tile(part, pair, pl.multiple_of(part * block, block), block, True)

                @pl.loop(0, part)
                def _(j):
                    tile(part, pair, pl.multiple_of(j * block, block), block, False)

            if direct:

                @pl.when(first_rank)
                def _():
                    up_copy(part).wait_recv()
                    help_dq[...] = jnp.zeros(help_dq.shape, F32)

                    @pl.loop(0, pairs)
                    def _(pair):
                        tile(part, pair, 0, rows_all, False, help_q, help_up, help_dq)

                    spot = pl.ds(part * pairs, pairs)
                    help_sum[spot] = help_dq[...].astype(BF16)
                    sum_copy(part).start()

    if direct:

        @pl.when(last_rank)
        def _():
            @pl.loop(0, tp_count)
            def _(part):
                sum_copy(part).wait_recv()
                spot = pl.ds(part * pairs, pairs)
                dq[spot] += help_sum[spot].astype(F32)

    own_kv[...] = joined(dk, dv, pl.ds(0, rows_all))
    far_steps = far_out.shape[0] + 1
    for distance in range(1, far_steps):

        @pl.when(rank + distance < SPAN)
        def _(distance=distance):
            far_copy(distance).wait_recv()
            own_kv[...] += far_in[distance - 1].astype(F32)

    def part_copy(k):
        return remote(
            parts.at[k], parts_in.at[k], part_sem.at[0, k], part_sem.at[1, k],
            {"tp": ring(tp, k + 1, tp_count)},
        )

    @pl.loop(0, tp_count)
    def _(part):
        rows = pl.ds(pl.multiple_of(part * block, block), block)
        pieces = []
        for pair in range(pairs):
            held = dq[part * pairs + pair]
            turned = SCORE_SCALE * jnp.concatenate(
                [held[member * block : (member + 1) * block, :HEAD] for member in range(group)],
                axis=1,
            )
            pieces.append(turned * cos[rows, :] - swap_halves(turned) * sin[rows, :])
        keys = own_kv[rows, :kv_cols]
        pieces.append(keys * cos[rows, :] - swap_halves(keys) * sin[rows, :])
        pieces.append(own_kv[rows, kv_cols:])
        grads = jnp.concatenate(pieces, axis=1).astype(BF16)
        row_grads[rows, :] = grads
        low_part = dot_nt(grads, second[...]).astype(BF16)
        low_grads[rows, :] = low_part
        second_acc[...] += dot_tn(lora[rows, :], grads)
        first_acc[...] += dot_tn(low_part, normed_all[part])

    packed[pl.ds(0, 3 * RANK), :] = first_acc[pl.ds(0, 3 * RANK), :]
    lanes = pl.ds(pl.multiple_of(tp * q_cols, q_cols), q_cols)
    packed[pl.ds(5 * RANK, RANK), lanes] = second_acc[pl.ds(0, RANK), :q_cols]
    lanes = pl.ds(pl.multiple_of(tp * kv_cols, kv_cols), kv_cols)
    packed[pl.ds(6 * RANK, RANK), lanes] = second_acc[pl.ds(RANK, RANK), q_cols : q_cols + kv_cols]
    lanes = pl.ds(pl.multiple_of(model // 2 + tp * kv_cols, kv_cols), kv_cols)
    packed[pl.ds(6 * RANK, RANK), lanes] = second_acc[pl.ds(2 * RANK, RANK), q_cols + kv_cols :]

    def make_parts():
        @pl.loop(0, tp_count)
        def _(k):
            part = ring(tp, k + 1, tp_count)
            rows = pl.ds(pl.multiple_of(part * block, block), block)
            grads = row_grads[rows, :]
            for side in range(2):
                columns = slice(side * half, (side + 1) * half)
                parts[k, :, columns] = (
                    dot_nt(grads, weights[side, pl.ds(0, half), :])
                    + dot_nt(low_grads[rows, :], first[columns, :])
                ).astype(BF16)

    def send_parts():
        for k in range(tp_count - 1):
            part_copy(k).start()

    if direct:
        tall_rows = packed.shape[0] // ctx_count

        def ctx_rows(index):
            return pl.ds(pl.multiple_of(index * tall_rows, tall_rows), tall_rows)

        def ctx_copy(k):
            where = ring(ctx, k, ctx_count)
            return remote(
                packed.at[ctx_rows(where)], ctx_in.at[k - 1],
                ctx_sem.at[0, k - 1], ctx_sem.at[1, k - 1], {"ctx": where},
            )

        def tp_copy(k):
            return remote(
                tp_in.at[tp], tp_in.at[tp], tp_sem.at[0, k - 1], tp_sem.at[1, k - 1],
                {"tp": ring(tp, k, tp_count)},
            )

        x_copy = remote(
            packed_out.at[fsdp, ctx_rows(ctx)], packed_out.at[fsdp, ctx_rows(ctx)],
            x_sem.at[0], x_sem.at[1], other,
        )

        def ctx_all_copy(k):
            return remote(
                packed_out.at[:, ctx_rows(ctx)], packed_out.at[:, ctx_rows(ctx)],
                ctx_all_sem.at[0, k - 1], ctx_all_sem.at[1, k - 1],
                {"ctx": ring(ctx, k, ctx_count)},
            )

        for k in range(1, ctx_count):
            ctx_copy(k).start()
        make_parts()
        for k in range(1, ctx_count):
            ctx_copy(k).wait()
        tp_in[tp] = (packed[ctx_rows(ctx), :] + sum(ctx_in[k] for k in range(ctx_count - 1))).astype(
            BF16
        )
        for k in range(1, tp_count):
            tp_copy(k).start()
        send_parts()
        for k in range(1, tp_count):
            tp_copy(k).wait()
        packed_out[fsdp, ctx_rows(ctx), :] = sum(tp_in[k].astype(F32) for k in range(tp_count))
        x_copy.start()
        x_copy.wait()
        for k in range(1, ctx_count):
            ctx_all_copy(k).start()
        share_own.wait()
        for k in range(1, tp_count):
            share_copy(k).wait()
        swap.start()
    else:
        packed_out[0] = packed[...]
        make_parts()
        send_parts()

    summed = parts[tp_count - 1].astype(F32)
    for k in range(tp_count - 1):
        part_copy(k).wait_recv()
        summed += parts_in[k].astype(F32)
    inputs = tokens[...].astype(F32)
    input_grad[...] = (middle_grad[...] + rms_back(inputs, scale_one, summed)).astype(BF16)
    mixture = end_sum(1) if direct else mixed[...].astype(F32)
    output[...] = (middle_ref[...] + RESIDUAL_SCALE * mixture).astype(BF16)

    if direct:
        swap.wait()
        for k in range(1, ctx_count):
            ctx_all_copy(k).wait()
        for n in range(2):
            for slot in range(2):
                near_copy(n, slot).wait_send()
            pair_copy(n).wait_send()
    for k in range(1, tp_count):
        do_copy(k).wait_send()
    if direct:
        for part in range(tp_count):

            @pl.when(last_rank)
            def _(part=part):
                up_copy(part).wait_send()

            @pl.when(first_rank)
            def _(part=part):
                sum_copy(part).wait_send()

    for k in range(tp_count - 1):
        part_copy(k).wait_send()
    for distance in range(1, far_steps):

        @pl.when(distance <= far_count)
        def _(distance=distance):
            far_copy(distance).wait_send()


def backward(
    tokens, upstream, routes, gains, router, middle, low, weights, normed, lora, att, queries, kv,
    first, second, o_first, o_second, cos, sin, w_rows, att_rows, back, mixed, shares, help_q,
    tp_count, ctx_count, experts, direct,
):
    block, model = tokens.shape
    heads, rows, _ = queries.shape
    pairs = kv.shape[3] // (2 * HEAD)
    tall = heads // pairs * block
    cols = second.shape[1]
    kv_width = kv.shape[3]
    vmem = pl.BlockSpec(memory_space=pltpu.VMEM)
    hbm = pl.BlockSpec(memory_space=pl.ANY)
    dma = pltpu.SemaphoreType.DMA
    part = (block, model)
    packed = (8 * RANK, model)
    copies = 2 if direct else 1
    slim = (8, LANES)

    def buffers(width):
        shapes = [(2, block, width), (2, block, width), (block, width), (block, width)]
        return [pltpu.VMEM(shape if direct else slim, BF16) for shape in shapes]

    return pl.pallas_call(
        functools.partial(
            backward_kernel, tp_count=tp_count, ctx_count=ctx_count, experts=experts, direct=direct
        ),
        in_specs=[vmem] * 22 + [hbm if direct else vmem] * 2 + [hbm, vmem if direct else hbm],
        out_specs=[vmem] * 3 + [hbm],
        out_shape=[
            jax.ShapeDtypeStruct((block, model), BF16),
            jax.ShapeDtypeStruct((block, model), BF16),
            jax.ShapeDtypeStruct((copies,) + packed, F32),
            jax.ShapeDtypeStruct(
                (2,) + shares.shape[:2] + (tp_count * shares.shape[2],) if direct else slim, BF16
            ),
        ],
        scratch_shapes=[
            pltpu.VMEM((pairs, SPAN * rows, LANES), BF16),
            pltpu.VMEM((pairs, SPAN * rows, LANES), BF16),
            pltpu.VMEM((heads, rows, LANES), BF16),
            pltpu.VMEM((pairs, SPAN * rows, LANES), F32),
            pltpu.VMEM((pairs, SPAN * rows, LANES), F32),
            pltpu.VMEM((tp_count * pairs, tall, LANES), F32),
            pltpu.VMEM((heads, rows, LANES) if direct else slim, BF16),
            pltpu.VMEM((pairs, tall, LANES) if direct else slim, F32),
            pltpu.VMEM((tp_count * pairs, tall, LANES) if direct else slim, BF16),
            pltpu.VMEM((tp_count, block, heads * HEAD), BF16),
            pltpu.VMEM((tp_count, block, heads * HEAD), BF16),
            pltpu.VMEM((SPAN - 2 if direct else SPAN - 1, rows, kv_width), BF16),
            pltpu.VMEM((SPAN - 2 if direct else SPAN - 1, rows, kv_width), BF16),
            pltpu.VMEM((rows, kv_width), F32),
            pltpu.VMEM((rows, cols), BF16),
            pltpu.VMEM((rows, LANES), BF16),
            pltpu.VMEM((tp_count,) + part, BF16),
            pltpu.VMEM((tp_count - 1,) + part, BF16),
            pltpu.VMEM((LANES, cols), F32),
            pltpu.VMEM((LANES, model), F32),
            pltpu.VMEM(packed, F32),
            pltpu.VMEM((ctx_count - 1, packed[0] // ctx_count, model) if direct else slim, F32),
            pltpu.VMEM((tp_count, packed[0] // ctx_count, model) if direct else slim, BF16),
            pltpu.VMEM((block, model), F32),
            pltpu.VMEM((LANES, model), BF16),
            *buffers(model + LANES),
            *buffers(model),
            dma((2, 4)),
            dma((4,)),
            dma((2, 2)),
            dma((2, tp_count - 1)),
            dma((2, SPAN - 1)),
            dma((2, tp_count - 1)),
            dma((2, ctx_count - 1)),
            dma((2, tp_count - 1)),
            dma((2,)),
            dma((2, ctx_count - 1)),
            dma((2, tp_count - 1)),
            dma((2,)),
            dma((1,)),
            dma((2, tp_count)),
            dma((2, tp_count)),
        ],
        compiler_params=pltpu.CompilerParams(
            vmem_limit_bytes=60 * 1024 * 1024, collective_id=1, has_side_effects=True
        ),
        cost_estimate=pl.CostEstimate(
            flops=32 * SPAN * rows * rows * heads * LANES,
            bytes_accessed=32 * 1024 * 1024,
            transcendentals=0,
        ),
        name="backward",
    )(
        tokens, upstream, routes, *gains, router, middle, low, weights, normed, lora, att, queries,
        kv, first, second, o_first, o_second, cos, sin, w_rows, att_rows, back, mixed, shares, help_q,
    )


def place_kernel(sets, packed, part, *outs):
    query_in, query_out, key_in, key_out, value_in, value_out, out_in, out_out = outs[:8]
    gate_in, gate_out, up_in, up_out, down_in, down_out = outs[8:]
    kv_cols, hidden = key_out.shape[1], gate_out.shape[2]
    trees = part.shape[0]
    spots = jnp.concatenate(
        [
            (iota((RANK, LANES), 1) == iota((RANK, LANES), 0) + sets[tree] * RANK).astype(BF16)
            for tree in range(trees)
        ],
        axis=0,
    )
    spots_twice = jnp.concatenate([spots, spots], axis=0)

    def block(rows):
        return slice(rows * RANK, (rows + 1) * RANK)

    @pl.when(pl.program_id(0) == 0)
    def _():
        def gathered(rows, lanes, turned):
            pieces = jnp.concatenate(
                [packed[tree, block(rows), lanes] for tree in range(trees)], axis=0
            )
            high = pieces.astype(BF16)
            both = jnp.concatenate([high, (pieces - high.astype(F32)).astype(BF16)], axis=0)
            return dot_tn(both, spots_twice) if turned else dot_tn(spots_twice, both)

        whole = slice(None)
        query_in[...] = gathered(0, whole, True)
        key_in[...] = gathered(1, whole, True)
        value_in[...] = gathered(2, whole, True)
        out_in[...] = gathered(3, whole, True)
        out_out[...] = gathered(4, whole, False)
        query_out[...] = gathered(5, whole, False)
        key_out[...] = gathered(6, slice(0, kv_cols), False)
        value_out[...] = gathered(6, slice(kv_cols, 2 * kv_cols), False)

    whole, left, right = slice(None), slice(0, hidden), slice(hidden, 2 * hidden)
    for n in range(part.shape[1]):

        def pieces(rows, lanes, n=n):
            return jnp.concatenate(
                [part[tree, n, block(rows), lanes] for tree in range(trees)], axis=0
            )

        gate_in[n] = dot_tn(pieces(0, whole), spots)
        up_in[n] = dot_tn(pieces(1, whole), spots)
        gate_out[n] = dot_tn(spots, pieces(2, left))
        up_out[n] = dot_tn(spots, pieces(2, right))
        down_out[n] = dot_tn(spots, pieces(3, whole))
        down_in[n] = dot_tn(pieces(4, left), spots)


def place(sets, packed, part, once, each):
    trees, local = part.shape[:2]
    batch = 2 if local % 2 == 0 else 1
    return pl.pallas_call(
        place_kernel,
        grid_spec=pltpu.PrefetchScalarGridSpec(
            num_scalar_prefetch=1,
            grid=(local // batch,),
            in_specs=[
                pl.BlockSpec(packed.shape, lambda e, s: (0, 0, 0)),
                pl.BlockSpec((trees, batch) + part.shape[2:], lambda e, s: (0, e, 0, 0)),
            ],
            out_specs=[
                *[pl.BlockSpec(o.shape, lambda e, s: (0, 0)) for o in once],
                *[pl.BlockSpec((batch,) + o.shape[1:], lambda e, s: (e, 0, 0)) for o in each],
            ],
        ),
        out_shape=[jax.ShapeDtypeStruct(o.shape, F32) for o in (*once, *each)],
        compiler_params=pltpu.CompilerParams(vmem_limit_bytes=VMEM_LIMIT),
        name="place",
    )(sets, packed, part)


def expert_kernel(
    sets, x_ref, g_ref, routes, router,
    w_gate, w_up, w_down, w_gate_far, w_up_far, w_down_far, all_gate, all_up, all_down, queries, gate_in, up_in, gate_out, up_out, down_in, down_out,
    back_out, mixed_out, grad_out, help_queries,
    rank_rows, gate_rows, slope_rows, mix, back, xs, firsts, tall_grad,
    gate_full, up_full, down_full, land_gate, land_up, land_down, grads, grads_in,
    far_sem, pass_far_sem, grads_sem, arrive_sem, query_sem,
    *, slots, sources, early, shared, straight, tp_count,
):
    chunk, expert = pl.program_id(0), pl.program_id(1)
    tp, fsdp = lax.axis_index("tp"), lax.axis_index("fsdp")
    late = shared + straight
    gather = late > 0
    other = {"fsdp": 1 - fsdp}
    cross, hand_on = far_moves(
        (all_gate, all_up, all_down), (land_gate, land_up, land_down), far_sem, pass_far_sem,
        shared, straight, early, 0, other, tp,
    )

    ctx = lax.axis_index("ctx")
    rank = lax.rem(ctx, SPAN)
    mirror = {"ctx": ctx + SPAN - 1 - 2 * rank}

    def query_copy():
        return remote(queries, help_queries, query_sem.at[0], query_sem.at[1], mirror)

    if gather:

        @pl.when(expert == 0)
        def _():
            barrier = pltpu.get_barrier_semaphore()
            for where in (other, mirror):
                pl.semaphore_signal(
                    barrier, 1, device_id=where, device_id_type=pl.DeviceIdType.MESH
                )
            for k in range(1, tp_count):
                pl.semaphore_signal(
                    barrier, 1, device_id={"tp": ring(tp, k, tp_count)},
                    device_id_type=pl.DeviceIdType.MESH,
                )
            pl.semaphore_wait(barrier, tp_count + 1)

            @pl.when(rank == SPAN - 1)
            def _():
                query_copy().start()

            for n in BEGIN[0]:
                for copy in cross(n):
                    copy.start()

        for step in range(1, early + late):
            if step in BEGIN or step in RELAY:

                @pl.when(expert == step)
                def _(step=step):
                    for n in RELAY.get(step, ()):
                        for copy in cross(n):
                            copy.wait_recv()
                        for copy in hand_on(n):
                            copy.start()
                    for n in BEGIN.get(step, ()):
                        for copy in cross(n):
                            copy.start()

        for n in range(late):

            @pl.when(expert == early + n)
            def _(n=n):
                for copy in hand_on(n) if n < shared else cross(n):
                    copy.wait_recv()

    experts = router.shape[0]
    tokens, model = x_ref.shape
    each = tokens // sources
    hidden = w_gate.shape[2]
    lanes = gate_in.shape[2]
    chosen = sets[fsdp * pl.num_programs(0) + chunk]

    @pl.when(expert == 0)
    def _():
        logits = dot_nt(router[...], x_ref[...])
        number = iota((experts, tokens), 0)
        hit = jnp.zeros((experts, tokens), F32)
        for k in range(routes.shape[0]):
            hit += (routes[k : k + 1, :] == number).astype(F32)
        kept = jnp.where(hit > 0.5, logits, MASKED)
        weights = jnp.exp(kept - jnp.max(kept, axis=0, keepdims=True)) * hit
        gate_rows[...] = weights / jnp.sum(weights, axis=0, keepdims=True)
        earlier = (iota((each, each), 0) < iota((each, each), 1)).astype(BF16)
        for s in range(sources):
            span = slice(s * each, (s + 1) * each)
            order = dot(hit[:, span].astype(BF16), earlier)
            rank_rows[:, span] = jnp.where(hit[:, span] > 0.5, order, -1.0)
        mix[...] = jnp.zeros(mix.shape, F32)
        back[...] = jnp.zeros(back.shape, F32)
        slope_rows[...] = jnp.zeros(slope_rows.shape, F32)

    first_row = lax.axis_index("ctx") * pl.num_programs(1)
    row = first_row + expert
    ranks = rank_rows[pl.ds(row, 1), :]
    gates = gate_rows[pl.ds(row, 1), :]
    slot_number = iota((slots, each), 0).astype(F32)
    picks, columns, upstreams = [], [], []
    for s in range(sources):
        span = slice(s * each, (s + 1) * each)
        pick = ranks[:, span] == slot_number
        columns.append(jnp.sum(jnp.where(pick, gates[:, span], 0.0), axis=1, keepdims=True))
        pick = pick.astype(BF16)
        picks.append(pick)
        xs[pl.ds(s * slots, slots), :] = dot(pick, x_ref[pl.ds(s * each, each), :]).astype(BF16)
        upstreams.append(dot(pick, g_ref[pl.ds(s * each, each), :]))
    gate_column = jnp.concatenate(columns, axis=0)
    upstream = RESIDUAL_SCALE * jnp.concatenate(upstreams, axis=0)

    firsts[:, :lanes] = gate_in[0]
    firsts[:, lanes:] = up_in[0]
    keep = (iota((1, 2 * lanes), 1) % lanes // RANK == chosen).astype(BF16)
    rows = xs[...]
    inner = dot(rows, firsts[...]).astype(BF16) * keep
    for full, near, far, landed in (
        (gate_full, w_gate, w_gate_far, land_gate),
        (up_full, w_up, w_up_far, land_up),
        (down_full, w_down, w_down_far, land_down),
    ):
        size = near.shape[1]
        full[pl.ds(pl.multiple_of(fsdp * size, size), size), :] = near[0]
        spot = pl.ds(pl.multiple_of((1 - fsdp) * size, size), size)
        if not gather:
            full[spot, :] = far[0]
            continue

        @pl.when(expert < early)
        def _(full=full, far=far, spot=spot):
            full[spot, :] = far[0]

        @pl.when(expert >= early)
        def _(full=full, landed=landed, spot=spot):
            full[spot, :] = landed[jnp.maximum(expert - early, 0)]
    gate_value = dot(rows, gate_full[...]) + dot(inner[:, :lanes], gate_out[0])
    up_value = dot(rows, up_full[...]) + dot(inner[:, lanes:], up_out[0])
    sigmoid = 1.0 / (1.0 + jnp.exp(-gate_value))
    silu = gate_value * sigmoid
    active = (silu * up_value).astype(BF16)
    down_inner = dot(active, down_in[0]).astype(BF16) * keep[:, :lanes]
    produced = (
        (dot(active, down_full[...]) + dot(down_inner, down_out[0])).astype(BF16).astype(F32)
    )
    slope = jnp.sum(upstream * produced, axis=1, keepdims=True)
    sent = (gate_column * produced).astype(BF16)
    slot_grad = (gate_column * upstream).astype(BF16)

    down_inner_grad = dot_nt(slot_grad, down_out[0]).astype(BF16) * keep[:, :lanes]
    active_grad = (
        (dot_nt(slot_grad, down_full[...]) + dot_nt(down_inner_grad, down_in[0]))
        .astype(BF16)
        .astype(F32)
    )
    gate_grad = (active_grad * up_value * (sigmoid + silu * (1.0 - sigmoid))).astype(BF16)
    up_grad = (active_grad * silu).astype(BF16)
    inner_grad = (
        jnp.concatenate([dot_nt(gate_grad, gate_out[0]), dot_nt(up_grad, up_out[0])], axis=1)
    ).astype(BF16) * keep
    row_grad = (
        dot_nt(gate_grad, gate_full[...])
        + dot_nt(up_grad, up_full[...])
        + dot_nt(inner_grad, firsts[...])
    ).astype(BF16)

    for s in range(sources):
        span = slice(s * slots, (s + 1) * slots)
        spot = pl.ds(s * each, each)
        mix[spot, :] += dot_tn(picks[s], sent[span, :])
        back[spot, :] += dot_tn(picks[s], row_grad[span, :])
        slope_rows[pl.ds(expert, 1), spot] = jnp.sum(
            jnp.where(picks[s] > 0.5, slope[span, :], 0.0), axis=0, keepdims=True
        )

    keep_at = expert if gather else 0

    def folded(start, width):
        total = tall_grad[pl.ds(start, RANK), :width]
        for shift in range(RANK, lanes, RANK):
            total += tall_grad[pl.ds(start + shift, RANK), :width]
        return total.astype(BF16)

    tall_grad[...] = dot_tn(inner_grad, rows)
    grads[keep_at, pl.ds(0, RANK), :] = folded(0, model)
    grads[keep_at, pl.ds(RANK, RANK), :] = folded(lanes, model)
    tall_grad[pl.ds(0, lanes), :hidden] = dot_tn(inner[:, :lanes], gate_grad)
    tall_grad[pl.ds(0, lanes), hidden:] = dot_tn(inner[:, lanes:], up_grad)
    grads[keep_at, pl.ds(2 * RANK, RANK), :] = folded(0, model)
    tall_grad[pl.ds(0, lanes), :] = dot_tn(down_inner, slot_grad)
    grads[keep_at, pl.ds(3 * RANK, RANK), :] = folded(0, model)
    tall_grad[pl.ds(0, lanes), :hidden] = dot_tn(down_inner_grad, active)
    grads[keep_at, pl.ds(4 * RANK, RANK), :hidden] = folded(0, hidden)
    grads[keep_at, pl.ds(4 * RANK, RANK), hidden:] = jnp.zeros((RANK, model - hidden), BF16)

    share = tall_grad.shape[1] // tp_count

    def grads_copy(n, k):
        where = ring(tp, k, tp_count)
        lanes = pl.ds(pl.multiple_of(where * share, share), share)
        return remote(
            grads.at[n, :, lanes], grads_in.at[k - 1, n], grads_sem.at[k - 1, n],
            arrive_sem.at[k - 1, n], {"tp": where},
        )

    def add_up(n):
        lanes = pl.ds(pl.multiple_of(tp * share, share), share)
        total = grads[n, :, lanes].astype(F32)
        for k in range(1, tp_count):
            grads_copy(n, k).wait()
            total += grads_in[k - 1, n].astype(F32)
        grad_out[n] = total.astype(BF16)

    if gather:
        for k in range(1, tp_count):
            grads_copy(expert, k).start()

        @pl.when(expert >= 2)
        def _():
            add_up(expert - 2)

    else:
        grad_out[0, 0] = grads[0]

    if gather:

        @pl.when(expert == pl.num_programs(1) - 1)
        def _():
            for n in range(late):
                for copy in cross(n):
                    copy.wait_send()
            for n in range(shared):
                for copy in hand_on(n):
                    copy.wait_send()

            @pl.when(rank == SPAN - 1)
            def _():
                query_copy().wait_send()

            @pl.when(rank == 0)
            def _():
                query_copy().wait_recv()

            for n in (2, 1):
                add_up(expert + 1 - n)

    @pl.when(expert == pl.num_programs(1) - 1)
    def _():
        mixed_out[...] = mix[...].astype(BF16)
        back_out[:, :model] = back[...].astype(BF16)
        turned = slope_rows[...].T
        high = turned.astype(BF16)
        low = (turned - high.astype(F32)).astype(BF16)
        local, lane = iota((LANES, LANES), 0), iota((LANES, LANES), 1)
        inside = local < pl.num_programs(1)
        first = (inside & (lane == local + first_row)).astype(BF16)
        later = (inside & (lane == local + first_row + experts)).astype(BF16)
        back_out[:, model:] = (dot(high, first) + dot(low, later)).astype(BF16)


def run_experts(
    sets, rows, upstream, routes, router, weights, far, queries, adapters, slots, sources, tp_count
):
    total, model = rows.shape
    experts = router.shape[0]
    local, half, hidden = weights[0].shape
    trees = sets.shape[0] // 2
    tokens = total // trees
    lanes = adapters[0].shape[2]
    tall = sources * slots
    piece = lambda c, e, *_: (c, 0)
    fixed = lambda c, e, *_: (0, 0)
    expert = lambda c, e, *_: (e, 0, 0)
    pairs, singles, shared, straight = transfer_plan(local, tp_count)
    early, late = pairs + singles, shared + straight
    arrived = lambda c, e, *_: (jnp.minimum(e, early - 1), 0, 0)
    hbm = pl.BlockSpec(memory_space=pl.ANY)
    dma = pltpu.SemaphoreType.DMA
    share = (local, 5 * RANK, model // tp_count)
    gradients = (
        (share, pl.BlockSpec(share, lambda c, e, *_: (0, 0, 0)))
        if late
        else (
            (trees, local, 5 * RANK, model),
            pl.BlockSpec((1, 1, 5 * RANK, model), lambda c, e, *_: (c, e, 0, 0)),
        )
    )
    return pl.pallas_call(
        functools.partial(
            expert_kernel, slots=slots, sources=sources, early=early, shared=shared,
            straight=straight, tp_count=tp_count,
        ),
        grid_spec=pltpu.PrefetchScalarGridSpec(
            num_scalar_prefetch=1,
            grid=(trees, local),
            in_specs=[
                pl.BlockSpec((tokens, model), piece),
                pl.BlockSpec((tokens, model), piece),
                pl.BlockSpec((routes.shape[0], tokens), lambda c, e, *_: (0, c)),
                pl.BlockSpec(router.shape, fixed),
                *[pl.BlockSpec((1,) + w.shape[1:], expert) for w in weights],
                *[pl.BlockSpec((1,) + w.shape[1:], arrived) for w in weights],
                *[hbm] * (len(weights) + 1),
                *[pl.BlockSpec((1,) + a.shape[1:], expert) for a in adapters],
            ],
            out_specs=[
                pl.BlockSpec((tokens, model + LANES), piece),
                pl.BlockSpec((tokens, model), piece),
                gradients[1],
                hbm,
            ],
            scratch_shapes=[
                pltpu.VMEM((experts, tokens), F32),
                pltpu.VMEM((experts, tokens), F32),
                pltpu.VMEM((LANES, tokens), F32),
                pltpu.VMEM((tokens, model), F32),
                pltpu.VMEM((tokens, model), F32),
                pltpu.VMEM((tall, model), BF16),
                pltpu.VMEM((model, 2 * lanes), BF16),
                pltpu.VMEM((2 * lanes, model), F32),
                pltpu.VMEM((2 * half, hidden), BF16),
                pltpu.VMEM((2 * half, hidden), BF16),
                pltpu.VMEM((hidden, model), BF16),
                *[pltpu.VMEM((max(late, 1),) + w.shape[1:], BF16) for w in weights],
                pltpu.VMEM((local if late else 1, 5 * RANK, model), BF16),
                pltpu.VMEM((tp_count - 1,) + (share if late else (1, 16, LANES)), BF16),
                dma((2, max(late, 1), 3)),
                dma((2, max(shared, 1), 3)),
                dma((tp_count - 1, local)),
                dma((tp_count - 1, local)),
                dma((2,)),
            ],
        ),
        out_shape=[
            jax.ShapeDtypeStruct((total, model + LANES), BF16),
            jax.ShapeDtypeStruct((total, model), BF16),
            jax.ShapeDtypeStruct(gradients[0], BF16),
            jax.ShapeDtypeStruct(queries.shape, BF16),
        ],
        compiler_params=(
            pltpu.CompilerParams(
                vmem_limit_bytes=60 * 1024 * 1024, collective_id=2, has_side_effects=True
            )
            if late
            else pltpu.CompilerParams(vmem_limit_bytes=60 * 1024 * 1024)
        ),
        name="experts",
        cost_estimate=pl.CostEstimate(
            flops=2 * local * total * model * model * 2,
            bytes_accessed=8 * 1024 * 1024,
            transcendentals=0,
        ),
    )(sets, rows, upstream, routes, router, *weights, *far, *weights, queries, *adapters)


def per_device(
    tokens,
    out_grad,
    routes,
    parents,
    adapter_set,
    gain_a,
    gain_b,
    w_query,
    key_projection_matrix,
    value_projection_matrix,
    w_output,
    w_router,
    w_gate,
    w_up,
    w_down,
    query_in,
    query_out,
    key_in,
    key_second_factor,
    value_in,
    value_second_factor,
    out_in,
    out_out,
    gate_in,
    gate_out,
    up_in,
    up_out,
    down_in,
    down_out,
):
    ctx_rank = lax.axis_index("ctx")
    fsdp_rank = lax.axis_index("fsdp")
    ctx_count = lax.axis_size("ctx")
    tp_count = lax.axis_size("tp")
    fsdp_count = lax.axis_size("fsdp")
    tok_rows, model = tokens.shape
    experts = w_router.shape[1]
    local_experts = w_gate.shape[0]
    slots = tok_rows * TOP * 3 // (2 * experts)
    trees = ctx_count // SPAN
    tree_index = (fsdp_rank * ctx_count + ctx_rank) // SPAN

    (
        attended, queries, kv_parts, lora, middle, o_reduced, attention_weights, normed_all,
        first, second, o_first, o_second, cos, sin, w_rows, att_rows,
        *far_weights, upstream_all, routes_all, rows_all,
    ) = forward(
        parents, adapter_set, tokens, (gain_a, gain_b),
        (w_query, key_projection_matrix, value_projection_matrix, w_output),
        (
            query_in, query_out, key_in, key_second_factor, value_in, value_second_factor,
            out_in, out_out,
        ),
        (w_gate, w_up, w_down), out_grad, routes.T, tp_count, ctx_count,
    )
    upstream_all = upstream_all.reshape(-1, model)
    rows_all = rows_all.reshape(-1, model)
    routes_all = routes_all.transpose(1, 0, 2).reshape(TOP, -1)

    back, mixed, expert_part, help_queries = run_experts(
        adapter_set,
        rows_all,
        upstream_all,
        routes_all,
        w_router.T,
        (w_gate, w_up, w_down),
        far_weights,
        queries,
        (gate_in, up_in, gate_out, up_out, down_in, down_out),
        slots,
        SPAN,
        tp_count,
    )
    direct = ctx_count == SPAN
    if direct:
        back = back.reshape(ctx_count, tok_rows, -1)
        mixed = mixed.reshape(ctx_count, tok_rows, -1)
    else:
        back = lax.psum_scatter(back, "ctx", scatter_dimension=0, tiled=True)
        mixed = lax.psum_scatter(mixed, "ctx", scatter_dimension=0, tiled=True)
    output, input_grad, packed, all_shares = backward(
        tokens, out_grad, routes.T, (gain_a, gain_b), w_router.T, middle, o_reduced, attention_weights,
        normed_all, lora, attended, queries, kv_parts, first, second, o_first, o_second,
        cos, sin, w_rows, att_rows, back, mixed, expert_part, help_queries, tp_count, ctx_count, experts, direct,
    )
    all_trees = fsdp_count * trees
    if not direct:
        mine = (jnp.arange(all_trees, dtype=jnp.int32) == tree_index)[:, None, None]
        packed = lax.psum(jnp.where(mine, packed, 0.0), ("fsdp", "ctx", "tp"))
    if direct:
        expert_part = all_shares
    else:
        expert_part = lax.all_gather(lax.psum(expert_part, "tp"), "fsdp")
        expert_part = expert_part.reshape(all_trees, local_experts, 5 * RANK, model)
    adapter_grads = place(
        adapter_set, packed, expert_part,
        (
            query_in, query_out, key_in, key_second_factor, value_in, value_second_factor,
            out_in, out_out,
        ),
        (gate_in, gate_out, up_in, up_out, down_in, down_out),
    )
    return (output, input_grad, *adapter_grads)


def solution(mesh):
    in_specs = (
        P(("fsdp", "ctx", "tp"), None),
        P(("fsdp", "ctx", "tp"), None),
        P(("fsdp", "ctx", "tp"), None),
        P(),
        P(),
        P(),
        P(),
        P("fsdp", "tp"),
        P("fsdp", "tp"),
        P("fsdp", "tp"),
        P("tp", "fsdp"),
        P(),
        P("ctx", "fsdp", None),
        P("ctx", "fsdp", None),
        P("ctx", "fsdp", None),
        P(),
        P(),
        P(),
        P(),
        P(),
        P(),
        P(),
        P(),
        P("ctx", None, None),
        P("ctx", None, None),
        P("ctx", None, None),
        P("ctx", None, None),
        P("ctx", None, None),
        P("ctx", None, None),
    )
    out_specs = (
        P(("fsdp", "ctx", "tp"), None),
        P(("fsdp", "ctx", "tp"), None),
        P(),
        P(),
        P(),
        P(),
        P(),
        P(),
        P(),
        P(),
        P("ctx", None, None),
        P("ctx", None, None),
        P("ctx", None, None),
        P("ctx", None, None),
        P("ctx", None, None),
        P("ctx", None, None),
    )
    return jax.shard_map(
        per_device, mesh=mesh, in_specs=in_specs, out_specs=out_specs, check_vma=False
    )
```
